32 devices in a mesh: dp: 8 (over z, x), expert: 4 (over y, core).
Axes of the slice: x: 2, y: 2, z: 4, core: 2. Of those that a mesh axis runs over, the one named last changes fastest.
Arguments:
- tokens: bfloat16 [2, 8, 256, 2048], P(None, 'dp', 'expert'), may hold values from -6 to 6
- w_query: bfloat16 [4, 2048, 2048], P('expert', 'dp'), may hold values from -0.125 to 0.125
- w_out: bfloat16 [4, 2048, 2048], P('expert', 'dp'), may hold values from -1.5 to 1.5
- w_key: bfloat16 [2048, 2048], P(('dp', 'expert')), may hold values from -0.125 to 0.125
- w_value: bfloat16 [2048, 2048], P(('dp', 'expert')), may hold values from -0.125 to 0.125
- gain_attn: bfloat16 [2048], P(('dp', 'expert')), may hold values from 0.5 to 1.5
- router_attn: bfloat16 [2048, 4], P(('dp', 'expert')), may hold values from -0.09375 to 0.09375
- gain_mlp: bfloat16 [2048], P(('dp', 'expert')), may hold values from 0.5 to 1.5
- router_mlp: bfloat16 [2048, 4], P(('dp', 'expert')), may hold values from -0.09375 to 0.09375
- w_gate: bfloat16 [4, 5632, 2048], P('expert', 'dp'), may hold values from -0.125 to 0.125
- w_up: bfloat16 [4, 5632, 2048], P('expert', 'dp'), may hold values from -0.125 to 0.125
- w_down: bfloat16 [4, 5632, 2048], P('expert', 'dp'), may hold values from -0.109375 to 0.109375
- attn_route: int32 [2, 8, 256, 2], P(None, 'dp'), may hold values from 0 to 3, all different within a row
- mlp_route: int32 [2, 8, 256, 2], P(None, 'dp', 'expert'), may hold values from 0 to 3, all different within a row
- fill_order: int32 [2, 8, 256], P(None, 'dp', 'expert'), may hold values from 0 to 255, each once within a row
- parents: int32 [2, 8, 13], P(None, 'dp'), may hold values from 0 to 4, as said below
- cotangent: bfloat16 [2, 8, 256, 2048], P(None, 'dp', 'expert'), may hold values from -6 to 6
Outputs:
- layer_out: bfloat16 [2, 8, 256, 2048], P(None, 'dp', 'expert')
- tokens_grad: float32 [2, 8, 256, 2048], P(None, 'dp', 'expert')
- w_query_grad: float32 [4, 2048, 2048], P('expert', 'dp')
- w_out_grad: float32 [4, 2048, 2048], P('expert', 'dp')
- w_key_grad: float32 [2048, 2048], P(('dp', 'expert'))
- w_value_grad: float32 [2048, 2048], P(('dp', 'expert'))
- gain_attn_grad: float32 [2048], P(('dp', 'expert'))
- router_attn_grad: float32 [2048, 4], P(('dp', 'expert'))
- gain_mlp_grad: float32 [2048], P(('dp', 'expert'))
- router_mlp_grad: float32 [2048, 4], P(('dp', 'expert'))
- w_gate_grad: float32 [4, 5632, 2048], P('expert', 'dp')
- w_up_grad: float32 [4, 5632, 2048], P('expert', 'dp')
- w_down_grad: float32 [4, 5632, 2048], P('expert', 'dp')
The draws below stay inside these ranges and needn't reach their ends.
Inputs may be any that keep to these rules, and one draw needn't show every extreme that they name: `parents`: in every tree segment 0 is the trunk, 1 to 4 the branches and 5 to 12 the leaves; the trunk's and each branch's parent is 0, and each branch is the parent of exactly two leaves. `attn_route`: each token names 2 different experts. `mlp_route`: each token names 2 different experts. `fill_order`: a permutation of the positions of each tree.
All inputs are finite; a program needn't handle non-finite values.
Results may differ from the reference program's by a relative error of at most 0.03.
Values may be sent and summed in bfloat16 or wider, within the bound.
A program may use at most 304 MiB of HBM per device.

```python
import math
from functools import partial
import jax
import jax.numpy as jnp
from jax import lax

D = 2048
HEADS = 16
HDIM = 128
FF = 5632
TOP = 2
SEG = 16
MB = 2
NSEG = 13
HQ = 2048
TOK = 64
TREE = 256
TREES = 8
EXPERTS = 4
CAP = 32
N_EXPERT = 4


def draw_parents(key, part):
    keys = jax.random.split(jax.random.fold_in(key, 17), MB * TREES)

    def one_tree(tree_key):
        order = jax.random.permutation(tree_key, jnp.arange(8, dtype=jnp.int32))
        leaves = (1 + order // 2).astype(jnp.int32)
        return jnp.concatenate([jnp.zeros((5,), jnp.int32), leaves])
    return jax.vmap(one_tree)(keys).reshape(MB, TREES, NSEG)


def level_of(key, shape, shards, low, high):
    def one(axis_at, shards_of):
        heights = jax.random.uniform(jax.random.fold_in(jax.random.fold_in(key, 6), axis_at), (shards_of,), jnp.float32, low / len(shards), high / len(shards))
        return jnp.repeat(jnp.exp(heights), shape[axis_at] // shards_of).reshape((-1,) + (1,) * (len(shape) - axis_at - 1))

    level = one(*shards[0])
    for cut in shards[1:]:
        level = level * one(*cut)
    return level


def different_ones(key, rows, count, top, lift):
    ranking = jax.random.permutation(jax.random.fold_in(key, 1), count)
    favour = ranking
    for power in range(3):
        favour = favour * favour // count
    favour = favour * lift // count
    lots = jax.random.randint(jax.random.fold_in(key, 2), (rows, count), 0, 4096) + favour
    fixed_rows = jax.random.permutation(jax.random.fold_in(key, 3), rows)[jnp.arange(count) % rows]
    lots = jnp.where(jnp.arange(rows)[:, None] == fixed_rows[None, :], 1 << 14, lots)
    merit = lots * count + jnp.arange(count)
    return lax.top_k(merit.astype(jnp.int32), top)[1].astype(jnp.int32)


def bell_draw(rng, shape, scale, most, cuts=(), kind=jnp.bfloat16):
    entries = scale * jax.random.normal(rng, shape, jnp.float32)
    if cuts:
        entries = entries * level_of(rng, shape, cuts, -0.22, 0.18)
    return jnp.clip(entries, -most, most).astype(kind)


def setup_inputs(seed: int = 0) -> dict:
    key_of = jax.random.split(jax.random.key(seed), 18)
    return {
        "tokens": bell_draw(key_of[0], (MB, TREES, TREE, D), 1.0, 6.0, ((1, 8), (2, 4))),
        "w_query": bell_draw(key_of[1], (EXPERTS, D, HQ), D ** -0.5, 0.125, ((0, 4), (1, 8))),
        "w_out": bell_draw(key_of[2], (EXPERTS, HQ, D), (max(HQ // 128, 1)) ** -0.5, 1.5, ((0, 4), (1, 8))),
        "w_key": bell_draw(key_of[3], (D, HQ), D ** -0.5, 0.125, ((0, 32),)),
        "w_value": bell_draw(key_of[4], (D, HQ), D ** -0.5, 0.125, ((0, 32),)),
        "gain_attn": jnp.clip(1.0 + 0.1 * jax.random.normal(key_of[5], (D,), jnp.float32), 0.5, 1.5).astype(jnp.bfloat16),
        "router_attn": bell_draw(key_of[6], (D, EXPERTS), (2 * D) ** -0.5, 0.09375, ((0, 32),)),
        "gain_mlp": jnp.clip(1.0 + 0.1 * jax.random.normal(key_of[7], (D,), jnp.float32), 0.5, 1.5).astype(jnp.bfloat16),
        "router_mlp": bell_draw(key_of[8], (D, EXPERTS), (2 * D) ** -0.5, 0.09375, ((0, 32),)),
        "w_gate": bell_draw(key_of[9], (EXPERTS, FF, D), D ** -0.5, 0.125, ((0, 4), (1, 8))),
        "w_up": bell_draw(key_of[10], (EXPERTS, FF, D), D ** -0.5, 0.125, ((0, 4), (1, 8))),
        "w_down": bell_draw(key_of[11], (EXPERTS, FF, D), (FF // 2) ** -0.5, 0.109375, ((0, 4), (1, 8))),
        "attn_route": different_ones(key_of[12], MB * TREES * TREE, EXPERTS, TOP, 0).reshape((MB, TREES, TREE, TOP)),
        "mlp_route": different_ones(key_of[13], MB * TREES * TREE, EXPERTS, TOP, 4096).reshape((MB, TREES, TREE, TOP)),
        "fill_order": jax.vmap(lambda own: jax.random.permutation(own, TREE))(jax.random.split(key_of[14], MB * TREES)).reshape((MB, TREES, TREE)).astype(jnp.int32),
        "parents": draw_parents(jax.random.fold_in(key_of[17], 71), 0),
        "cotangent": bell_draw(key_of[16], (MB, TREES, TREE, D), 1.0, 6.0, ((1, 8), (2, 4))),
    }


EPSILON = 1e-06
HIGHEST = lax.Precision.HIGHEST

@jax.custom_vjp
def low(v):
    return lax.optimization_barrier(v.astype(jnp.bfloat16)).astype(jnp.float32)

@jax.custom_vjp
def low_back(v):
    return v

def low_keep(v):
    return (low(v), None)

def low_pass(kept, grad):
    return (grad,)

def back_keep(v):
    return (v, None)

def back_low(kept, grad):
    return (low(grad),)
low.defvjp(low_keep, low_pass)
low_back.defvjp(back_keep, back_low)

def exact_product(left, right):
    return jnp.dot(left, right, precision=HIGHEST, preferred_element_type=jnp.float32)

def rms_scaled(values, gain):
    return values * lax.rsqrt(lax.optimization_barrier(jnp.mean(values * values, axis=-1, keepdims=True)) + EPSILON) * gain

def mixture_gates(picked, logits):
    labels = jnp.arange(logits.shape[1], dtype=jnp.int32)
    onehot = (picked[:, :, None] == labels[None, None, :]).astype(jnp.float32)
    chosen = lax.optimization_barrier(jnp.sum(onehot * logits[:, None, :], axis=-1))
    weights = jax.nn.softmax(chosen, axis=-1)
    return lax.optimization_barrier(jnp.sum(weights[:, :, None] * onehot, axis=1))

def tree_layout(segment_len, tree_len):
    places = jnp.arange(tree_len, dtype=jnp.int32)
    trunk_len = 4 * segment_len
    segment = jnp.where(places < trunk_len, 0, jnp.where(places < 2 * trunk_len, 1 + (places - trunk_len) // segment_len, 5 + (places - 2 * trunk_len) // segment_len)).astype(jnp.int32)
    depth = jnp.where(places < trunk_len, places, jnp.where(places < 2 * trunk_len, trunk_len + (places - trunk_len) % segment_len, trunk_len + segment_len + (places - 2 * trunk_len) % segment_len)).astype(jnp.int32)
    return (places, segment, depth)

def ancestors(parent, segment):
    labels = jnp.arange(parent.shape[0], dtype=jnp.int32)
    first = jnp.where(labels > 0, parent, -1).astype(jnp.int32)
    lookup = jnp.maximum(first, 0)[:, None] == labels[None, :]
    second = jnp.where(first > 0, lax.optimization_barrier(jnp.sum(jnp.where(lookup, parent[None, :], 0), axis=1)), -1).astype(jnp.int32)
    member = segment[:, None] == labels[None, :]
    up_one = lax.optimization_barrier(jnp.sum(jnp.where(member, first[None, :], 0), axis=1)).astype(jnp.int32)
    up_two = lax.optimization_barrier(jnp.sum(jnp.where(member, second[None, :], 0), axis=1)).astype(jnp.int32)
    return (up_one, up_two)

def visible(query_seg, query_place, query_up, query_top, key_seg, key_place):
    same = (key_seg[None, :] == query_seg[:, None]) & (key_place[None, :] <= query_place[:, None])
    return same | (key_seg[None, :] == query_up[:, None]) | (key_seg[None, :] == query_top[:, None])

def rotate(values, depth, sign):
    half = values.shape[-1] // 2
    rates = 10000.0 ** (-jnp.arange(half, dtype=jnp.float32) / half)
    angle = depth.astype(jnp.float32)[:, None] * rates[None, :]
    cosine = jnp.cos(angle)[:, None, :]
    sine = sign * jnp.sin(angle)[:, None, :]
    first = values[..., :half]
    second = values[..., half:]
    return jnp.concatenate([first * cosine - second * sine, second * cosine + first * sine], axis=-1)

def slot_table(picked, order, experts, capacity):
    labels = jnp.arange(experts, dtype=jnp.int32)
    chosen = lax.optimization_barrier(jnp.sum((picked[:, :, None] == labels[None, None, :]).astype(jnp.float32), axis=1))
    earlier = (order[None, :] < order[:, None]).astype(jnp.float32)
    ranks = jnp.dot(earlier, chosen, precision=HIGHEST, preferred_element_type=jnp.float32)
    slots = jnp.arange(capacity, dtype=jnp.float32)
    return jnp.transpose(chosen)[:, None, :] * (jnp.transpose(ranks)[:, None, :] == slots[None, :, None]).astype(jnp.float32)

def tree_pass(weights, tree_in, attn_pick, mlp_pick, order, parent):
    w_query, w_out, w_key, w_value, gain_attn, router_attn, gain_mlp, router_mlp, w_gate, w_up, w_down = weights
    scale = 1.0 / math.sqrt(HDIM)
    places, segment, depth = tree_layout(SEG, TREE)
    up_one, up_two = ancestors(parent, segment)
    allowed = visible(segment, places, up_one, up_two, segment, places)
    normed = low(rms_scaled(tree_in, gain_attn))
    total = jnp.zeros_like(tree_in)
    for expert in range(EXPERTS):
        expert_in = low_back(normed)
        queries = low(rotate(low_back(exact_product(expert_in, w_query[expert])).reshape(TREE, HEADS, HDIM), depth, 1.0))
        keys = low(rotate(low_back(exact_product(expert_in, w_key)).reshape(TREE, HEADS, HDIM), depth, 1.0))
        values = low(low_back(exact_product(expert_in, w_value))).reshape(TREE, HEADS, HDIM)
        raw = jnp.einsum('qhd,khd->hqk', queries, keys, precision=HIGHEST)
        scores = jnp.where(allowed[None], low_back(raw) * scale, -1e+30)
        probs = low(jax.nn.softmax(scores, axis=-1))
        heads = low(low_back(jnp.einsum('hqk,khd->qhd', probs, values, precision=HIGHEST))).reshape(TREE, HQ)
        gate = mixture_gates(attn_pick, exact_product(expert_in, router_attn))[:, expert]
        total = total + low(gate[:, None] * low_back(exact_product(heads, w_out[expert])))
    middle = tree_in + low_back(total)
    second = low(rms_scaled(middle, gain_mlp))
    mlp_gates = mixture_gates(mlp_pick, exact_product(second, router_mlp)).reshape(N_EXPERT, TOK, EXPERTS)
    pieces = second.reshape(N_EXPERT, TOK, D)
    tables = jax.vmap(partial(slot_table, experts=EXPERTS, capacity=CAP))(mlp_pick.reshape(N_EXPERT, TOK, TOP), order.reshape(N_EXPERT, TOK))
    sent = jnp.einsum('sect,std->secd', tables, pieces, precision=HIGHEST)
    mixed = jnp.zeros((N_EXPERT, TOK, D), jnp.float32)
    for expert in range(EXPERTS):
        expert_rows = low_back(sent[:, expert].reshape(N_EXPERT * CAP, D))
        gate_pre = low_back(exact_product(expert_rows, jnp.transpose(w_gate[expert])))
        up_pre = low_back(exact_product(expert_rows, jnp.transpose(w_up[expert])))
        inner = low(jax.nn.silu(gate_pre) * up_pre)
        result = low(low_back(exact_product(inner, w_down[expert]))).reshape(N_EXPERT, CAP, D)
        spread = jnp.einsum('sct,scd->std', tables[:, expert], result, precision=HIGHEST)
        mixed = mixed + mlp_gates[:, :, expert][:, :, None] * spread
    return middle + mixed.reshape(TREE, D)

def reference(tokens, w_query, w_out, w_key, w_value, gain_attn, router_attn, gain_mlp, router_mlp, w_gate, w_up, w_down, attn_route, mlp_route, fill_order, parents, cotangent):
    weights = tuple((w.astype(jnp.float32) for w in (w_query, w_out, w_key, w_value, gain_attn, router_attn, gain_mlp, router_mlp, w_gate, w_up, w_down)))
    count = MB * TREES
    inputs = tokens.astype(jnp.float32).reshape(count, TREE, D)
    integers = (attn_route.reshape(count, TREE, TOP), mlp_route.reshape(count, TREE, TOP), fill_order.reshape(count, TREE), parents.reshape(count, NSEG))
    checked = jax.checkpoint(tree_pass)

    def forward(weight_set, tree_inputs):

        def step(carry, item):
            return (carry, checked(weight_set, item[0], item[1], item[2], item[3], item[4]))
        _, result = lax.scan(step, jnp.zeros((), jnp.float32), (tree_inputs,) + integers)
        return result
    result, pull = jax.vjp(forward, weights, inputs)
    grads, input_grads = pull(cotangent.astype(jnp.float32).reshape(count, TREE, D))
    shape = (MB, TREES, TREE, D)
    return (result.astype(jnp.bfloat16).reshape(shape), input_grads.reshape(shape), grads[0], grads[1], grads[2], grads[3], grads[4], grads[5], grads[6], grads[7], grads[8], grads[9], grads[10])
```

```python
from functools import partial
import math

import jax
import jax.numpy as jnp
from jax import lax
from jax.experimental import pallas as pl
from jax.experimental.pallas import tpu as pltpu
from jax.sharding import Mesh, PartitionSpec as P

HEADS = 16
HDIM = 128
EPSILON = 1e-06
HIGHEST = lax.Precision.HIGHEST
BF16 = jnp.bfloat16
F32 = jnp.float32


def product(left, right):
    return jnp.dot(left, right, preferred_element_type=F32)


def product_tn(left, right):
    return lax.dot_general(left, right, (((0,), (0,)), ((), ())), preferred_element_type=F32)


def product_nt(left, right):
    return lax.dot_general(left, right, (((1,), (1,)), ((), ())), preferred_element_type=F32)


def rms_scaled(values, gain):
    return values * lax.rsqrt(jnp.mean(values * values, axis=-1, keepdims=True) + EPSILON) * gain


def mixture_gates(picked, logits):
    labels = jnp.arange(logits.shape[1], dtype=jnp.int32)
    onehot = (picked[:, :, None] == labels[None, None, :]).astype(F32)
    chosen = jnp.sum(onehot * logits[:, None, :], axis=-1)
    weights = jax.nn.softmax(chosen, axis=-1)
    return jnp.sum(weights[:, :, None] * onehot, axis=1)


def tree_layout(segment_len, tree_len):
    places = jnp.arange(tree_len, dtype=jnp.int32)
    trunk_len = 4 * segment_len
    segment = jnp.where(
        places < trunk_len,
        0,
        jnp.where(
            places < 2 * trunk_len,
            1 + (places - trunk_len) // segment_len,
            5 + (places - 2 * trunk_len) // segment_len,
        ),
    )
    depth = jnp.where(
        places < trunk_len,
        places,
        jnp.where(
            places < 2 * trunk_len,
            trunk_len + (places - trunk_len) % segment_len,
            trunk_len + segment_len + (places - 2 * trunk_len) % segment_len,
        ),
    )
    return (places, segment, depth)


def ancestors(parent, segment):
    labels = jnp.arange(parent.shape[0], dtype=jnp.int32)
    first = jnp.where(labels > 0, parent, -1)
    lookup = jnp.maximum(first, 0)[:, None] == labels[None, :]
    second = jnp.where(first > 0, jnp.sum(jnp.where(lookup, parent[None, :], 0), axis=1), -1)
    member = segment[:, None] == labels[None, :]
    up_one = jnp.sum(jnp.where(member, first[None, :], 0), axis=1)
    up_two = jnp.sum(jnp.where(member, second[None, :], 0), axis=1)
    return (up_one, up_two)


def score_bias(parent, segment, places):
    up_one, up_two = ancestors(parent, segment)
    same = (segment[None, :] == segment[:, None]) & (places[None, :] <= places[:, None])
    seen = same | (segment[None, :] == up_one[:, None]) | (segment[None, :] == up_two[:, None])
    return jnp.where(seen, 0.0, -1e30).astype(F32)


def slot_table(picked, order, experts, capacity):
    labels = jnp.arange(experts, dtype=jnp.int32)
    chosen = jnp.sum((picked[:, :, None] == labels[None, None, :]).astype(F32), axis=1)
    earlier = (order[None, :] < order[:, None]).astype(F32)
    ranks = jnp.dot(earlier, chosen, precision=HIGHEST, preferred_element_type=F32)
    slots = jnp.arange(capacity, dtype=F32)
    return jnp.transpose(chosen)[:, None, :] * (
        jnp.transpose(ranks)[:, None, :] == slots[None, :, None]
    ).astype(F32)


def turn(values, cosine, sine):
    half = values.shape[-1] // 2
    first = values[:, :half]
    second = values[:, half:]
    return jnp.concatenate(
        [first * cosine - second * sine, second * cosine + first * sine], axis=-1
    )


def softmax_rows(queries, keys, bias, scale):
    scores = product_nt(queries, keys) * scale + bias
    highest = jnp.max(scores, axis=-1, keepdims=True)
    weights = jnp.exp(scores - highest)
    return weights / jnp.sum(weights, axis=-1, keepdims=True)


def attend_kernel(heads, scale, raw_ref, kv_ref, cos_ref, sin_ref, bias_ref, query_ref, out_ref):
    quarter, tok = raw_ref.shape[1], raw_ref.shape[3]
    rows = quarter * tok
    cosine, sine, bias = cos_ref[...], sin_ref[...], bias_ref[0, 0]
    for head in range(heads):
        cols = slice(head * HDIM, (head + 1) * HDIM)
        raw = raw_ref[0, :, 0, :, cols].reshape(rows, HDIM)
        keys = kv_ref[0, 0, 0, :, 0, :, cols].reshape(rows, HDIM)
        values = kv_ref[0, 1, 0, :, 0, :, cols].reshape(rows, HDIM)
        queries = turn(raw, cosine, sine).astype(BF16)
        probs = softmax_rows(queries, keys, bias, scale).astype(BF16)
        query_ref[0, :, 0, :, cols] = queries.reshape(quarter, tok, HDIM)
        out_ref[0, :, 0, :, cols] = product(probs, values).astype(BF16).reshape(quarter, tok, HDIM)


def attend_back_kernel(
    heads, scale, query_ref, kv_ref, grad_ref, cos_ref, sin_ref, bias_ref, dq_ref, dkv_ref
):
    quarter, tok = query_ref.shape[1], query_ref.shape[3]
    rows = quarter * tok
    cosine, sine, bias = cos_ref[...], sin_ref[...], bias_ref[0, 0]
    for head in range(heads):
        cols = slice(head * HDIM, (head + 1) * HDIM)
        queries = query_ref[0, :, 0, :, cols].reshape(rows, HDIM)
        keys = kv_ref[0, 0, 0, :, 0, :, cols].reshape(rows, HDIM)
        values = kv_ref[0, 1, 0, :, 0, :, cols].reshape(rows, HDIM)
        grad = grad_ref[0, :, 0, :, cols].reshape(rows, HDIM)
        probs = softmax_rows(queries, keys, bias, scale)
        prob_grad = product_nt(grad, values)
        centre = jnp.sum(prob_grad * probs, axis=-1, keepdims=True)
        score_grad = (probs * (prob_grad - centre) * scale).astype(BF16)
        query_grad = turn(product(score_grad, keys), cosine, -sine).astype(BF16)
        key_grad = turn(product_tn(score_grad, queries), cosine, -sine).astype(BF16)
        value_grad = product_tn(probs.astype(BF16), grad).astype(BF16)
        dq_ref[0, :, 0, :, cols] = query_grad.reshape(quarter, tok, HDIM)
        dkv_ref[0, 0, 0, :, 0, :, cols] = key_grad.reshape(quarter, tok, HDIM)
        dkv_ref[0, 1, 0, :, 0, :, cols] = value_grad.reshape(quarter, tok, HDIM)


def attention_specs(shape, slices):
    pair, quarter, micro, tok, feats = shape
    part = feats // slices
    rows = quarter * tok
    grid = (pair, micro, slices)
    flat = pl.BlockSpec((1, quarter, 1, tok, part), lambda i, m, s: (i, 0, m, 0, s))
    both = pl.BlockSpec(
        (1, 2, 1, quarter, 1, tok, part), lambda i, m, s: (s, 0, i, 0, m, 0, 0)
    )
    angle = pl.BlockSpec((rows, HDIM // 2), lambda i, m, s: (0, 0))
    bias = pl.BlockSpec((1, 1, rows, rows), lambda i, m, s: (i, m, 0, 0))
    return grid, part, flat, both, angle, bias


def attend(raw, kv, cosine, sine, bias, scale):
    slices = kv.shape[0]
    grid, part, flat, both, angle, bias_spec = attention_specs(raw.shape, slices)
    out = jax.ShapeDtypeStruct(raw.shape, BF16)
    return pl.pallas_call(
        partial(attend_kernel, part // HDIM, scale),
        grid=grid,
        in_specs=[flat, both, angle, angle, bias_spec],
        out_specs=[flat, flat],
        out_shape=[out, out],
        cost_estimate=pl.CostEstimate(
            flops=4 * raw.size * cosine.shape[0],
            bytes_accessed=12 * raw.size,
            transcendentals=raw.size * 2,
        ),
        name="attend",
    )(raw, kv, cosine, sine, bias)


def attend_back(queries, kv, grad, cosine, sine, bias, scale):
    slices = kv.shape[0]
    grid, part, flat, both, angle, bias_spec = attention_specs(queries.shape, slices)
    return pl.pallas_call(
        partial(attend_back_kernel, part // HDIM, scale),
        grid=grid,
        in_specs=[flat, both, flat, angle, angle, bias_spec],
        out_specs=[flat, both],
        out_shape=[
            jax.ShapeDtypeStruct(queries.shape, BF16),
            jax.ShapeDtypeStruct(kv.shape, BF16),
        ],
        cost_estimate=pl.CostEstimate(
            flops=10 * queries.size * cosine.shape[0],
            bytes_accessed=14 * queries.size,
            transcendentals=queries.size * 2,
        ),
        name="attend_back",
    )(queries, kv, grad, cosine, sine, bias)


def gather(value, axes, axis=0):
    return lax.all_gather(value, axes, axis=axis, tiled=True)


def scatter(value, axes, axis=0):
    return lax.psum_scatter(value, axes, scatter_dimension=axis, tiled=True)


def swap(value, axes, split=0, concat=0):
    return lax.all_to_all(value, axes, split_axis=split, concat_axis=concat, tiled=True)


DP = ("line", "pair")
ALL = ("line", "pair", "expert")
TREES = ("pair", "expert")


def body(
    tokens,
    w_query,
    w_out,
    w_key,
    w_value,
    gain_attn,
    router_attn,
    gain_mlp,
    router_mlp,
    w_gate,
    w_up,
    w_down,
    attn_route,
    mlp_route,
    fill_order,
    parents,
    cotangent,
):
    experts = lax.axis_size("expert")
    pair = lax.axis_size("pair")
    line = lax.axis_size("line")
    position = lax.axis_index("expert")
    micro, _, tok, width = tokens.shape
    tree = experts * tok
    rows = pair * experts * micro * tok
    heads_total = w_query.shape[2]
    part = heads_total // (line * pair)
    feats = heads_total // pair
    piece = feats // experts
    own_in = w_query.shape[1]
    own_kv = w_key.shape[0]
    capacity = tok * mlp_route.shape[3] // experts
    scale = 1.0 / math.sqrt(HDIM)

    places, segment, depth = tree_layout(tree // 16, tree)
    half = HDIM // 2
    rates = 10000.0 ** (-jnp.arange(half, dtype=F32) / half)
    angle = depth.astype(F32)[:, None] * rates[None, :]
    cosine, sine = jnp.cos(angle), jnp.sin(angle)

    small = jnp.concatenate(
        [gain_attn[None], gain_mlp[None], router_attn.T, router_mlp.T], axis=0
    )
    small = jnp.transpose(lax.all_gather(small, ALL, axis=0), (1, 0, 2)).reshape(-1, width)
    first_gain = small[0].astype(F32)
    second_gain = small[1].astype(F32)
    first_router = small[2 : 2 + experts]
    second_router = small[2 + experts : 2 + 2 * experts]

    residual = tokens.reshape(micro * tok, width).astype(F32)
    normed, first_pull = jax.vjp(rms_scaled, residual, first_gain)
    normed = normed.astype(BF16)
    tree_input = gather(normed, TREES)

    integers = jnp.concatenate(
        [attn_route[:, 0].reshape(micro, -1), parents[:, 0]], axis=1
    )
    integers = lax.all_gather(integers, "pair", axis=0)
    routes = integers[..., : tree * 2].reshape(pair, micro, experts, tok, 2)
    routes = jnp.transpose(routes, (0, 2, 1, 3, 4)).reshape(rows, 2)
    family = integers[..., tree * 2 :]
    bias = jax.vmap(jax.vmap(lambda parent: score_bias(parent, segment, places)))(family)

    kv_mine = jnp.stack([w_key, w_value], axis=1).reshape(own_kv, 2, line, pair, part)
    kv_mine = jnp.transpose(kv_mine, (3, 2, 0, 1, 4)).reshape(
        pair, experts, line // experts, own_kv, 2, part
    )
    kv_mine = jnp.transpose(kv_mine, (0, 1, 3, 4, 2, 5)).reshape(
        pair * experts, own_kv, 2, piece
    )
    kv_mine = swap(kv_mine, TREES).reshape(pair * experts * own_kv, 2 * piece)
    kv_weight = gather(kv_mine, "line")
    query_weight = w_query[0].reshape(own_in, line, pair, part)
    query_weight = jnp.transpose(query_weight, (2, 0, 1, 3)).reshape(pair, own_in, feats)
    query_weight = swap(query_weight, "pair").reshape(pair * own_in, feats)
    query_weight = gather(query_weight, "line")
    out_weight = gather(w_out[0], "line")

    kv_raw = product(tree_input, kv_weight)
    spread_cos = jnp.broadcast_to(
        cosine.reshape(1, experts, 1, tok, 1, half), (pair, experts, micro, tok, 1, half)
    ).reshape(rows, 1, half)
    spread_sin = jnp.broadcast_to(
        sine.reshape(1, experts, 1, tok, 1, half), (pair, experts, micro, tok, 1, half)
    ).reshape(rows, 1, half)
    key_raw = kv_raw[:, :piece].reshape(rows, piece // HDIM, HDIM)
    key_one, key_two = key_raw[..., :half], key_raw[..., half:]
    keys = jnp.concatenate(
        [
            key_one * spread_cos - key_two * spread_sin,
            key_two * spread_cos + key_one * spread_sin,
        ],
        axis=-1,
    ).reshape(rows, piece)
    kv = jnp.stack([keys.astype(BF16), kv_raw[:, piece:].astype(BF16)])
    kv = lax.all_gather(kv, "expert", axis=0)
    shape = (pair, experts, micro, tok, feats)
    kv = kv.reshape(experts, 2, pair, experts, micro, tok, piece)

    first_gates, first_gate_pull = jax.vjp(
        partial(mixture_gates, routes), product_nt(tree_input, first_router)
    )
    column = (jnp.arange(experts, dtype=jnp.int32) == position).astype(F32)
    own_gate = jnp.sum(first_gates * column[None, :], axis=1)

    raw = product(tree_input, query_weight)
    queries, heads_out = attend(raw.reshape(shape), kv, cosine, sine, bias, scale)
    heads_flat = heads_out.reshape(rows, feats)
    projected = product(heads_flat, out_weight)
    attention = scatter((own_gate[:, None] * projected).astype(BF16), TREES).astype(F32)

    middle = residual + attention
    second_normed, second_pull = jax.vjp(rms_scaled, middle, second_gain)
    second_normed = second_normed.astype(BF16)
    picked = mlp_route[:, 0].reshape(micro * tok, 2)
    second_gates, second_gate_pull = jax.vjp(
        partial(mixture_gates, picked), product_nt(second_normed, second_router)
    )
    table = jax.vmap(partial(slot_table, experts=experts, capacity=capacity))(
        mlp_route[:, 0], fill_order[:, 0]
    )
    table_low = table.astype(BF16)
    grouped = second_normed.reshape(micro, tok, width)
    outgoing = jnp.einsum("mect,mtd->emcd", table_low, grouped, preferred_element_type=F32)
    top_grad = cotangent.reshape(micro, tok, width)
    slot_values = jnp.einsum("mect,mtd->emcd", table_low, top_grad, preferred_element_type=F32)
    slot_gates = jnp.einsum(
        "mect,mte->emc", table, second_gates.reshape(micro, tok, experts), precision=HIGHEST
    )
    slot_grad = (slot_gates[..., None] * slot_values).astype(BF16)
    slots = experts * micro * capacity
    arrived = gather(swap(outgoing.astype(BF16), "expert").reshape(slots, width), DP)
    result_grad = gather(swap(slot_grad, "expert").reshape(slots, width), DP)

    gate_weight, up_weight, down_weight = w_gate[0], w_up[0], w_down[0]
    gate_pre = product_nt(arrived, gate_weight)
    up_pre = product_nt(arrived, up_weight)
    sigma = jax.nn.sigmoid(gate_pre)
    inner = (gate_pre * sigma * up_pre).astype(BF16)
    returned = scatter(product(inner, down_weight).astype(BF16), DP)
    returned = swap(returned.reshape(experts, micro, capacity, width), "expert")
    inner_grad = product_nt(result_grad, down_weight)
    gate_grad = (inner_grad * up_pre * sigma * (1.0 + gate_pre * (1.0 - sigma))).astype(BF16)
    up_grad = (inner_grad * gate_pre * sigma).astype(BF16)
    came_back = scatter(
        (product(gate_grad, gate_weight) + product(up_grad, up_weight)).astype(BF16), DP
    )
    came_back = swap(came_back.reshape(experts, micro, capacity, width), "expert")
    grad_gate = product_tn(gate_grad, arrived)[None]
    grad_upward = product_tn(up_grad, arrived)[None]
    grad_downward = product_tn(inner, result_grad)[None]

    spread = jnp.einsum("mect,emcd->emtd", table_low, returned, preferred_element_type=F32)
    spread = spread.reshape(experts, micro * tok, width)
    mixed = jnp.sum(jnp.transpose(second_gates)[:, :, None] * spread, axis=0)
    layer_out = (middle + mixed).astype(BF16)
    dz = top_grad.reshape(micro * tok, width).astype(F32)
    second_gate_grad = jnp.transpose(jnp.sum(spread * dz[None], axis=-1))
    (second_logit_grad,) = second_gate_pull(second_gate_grad)
    hn_grad = jnp.einsum("mect,emcd->mtd", table_low, came_back, preferred_element_type=F32)
    hn_grad = hn_grad.reshape(micro * tok, width)
    second_router_wide = second_router.astype(F32)
    for expert in range(experts):
        hn_grad = hn_grad + second_logit_grad[:, expert : expert + 1] * second_router_wide[expert]
    grad_router_second = jnp.dot(
        jnp.transpose(second_logit_grad),
        second_normed.astype(F32),
        precision=HIGHEST,
        preferred_element_type=F32,
    )
    middle_grad, grad_gain_second = second_pull(hn_grad)
    middle_grad = middle_grad + dz

    mix_grad = gather(middle_grad.astype(BF16), TREES).astype(F32)
    own_gate_grad = jnp.sum(mix_grad * projected, axis=-1)
    projected_grad = (own_gate[:, None] * mix_grad).astype(BF16)
    heads_grad = product_nt(projected_grad, out_weight).astype(BF16).reshape(shape)
    grad_output = scatter(product_tn(heads_flat, projected_grad).astype(BF16), "line")
    query_pre, kv_pre = attend_back(queries, kv, heads_grad, cosine, sine, bias, scale)
    query_pre = query_pre.reshape(rows, feats)
    kv_sum = scatter(kv_pre.reshape(experts * 2, rows, piece), "expert")
    grad_query = scatter(product_tn(tree_input, query_pre).astype(BF16), "line")
    grad_query = swap(grad_query.reshape(own_in * pair, line, part)[None], "pair", 1, 0)
    grad_query = jnp.transpose(grad_query, (1, 2, 0, 3)).reshape(1, own_in, heads_total)

    (first_logit_grad,) = first_gate_pull(own_gate_grad[:, None] * column[None, :])
    key_pre, value_pre = kv_sum[0], kv_sum[1]
    input_term = (
        product_nt(query_pre, query_weight)
        + product_nt(key_pre, kv_weight[:, :piece])
        + product_nt(value_pre, kv_weight[:, piece:])
    )
    first_router_wide = first_router.astype(F32)
    for expert in range(experts):
        input_term = input_term + first_logit_grad[:, expert : expert + 1] * first_router_wide[expert]
    normed_grad = scatter(input_term.astype(BF16), TREES).astype(F32)
    grad_kv = jnp.stack(
        [product_tn(tree_input, key_pre), product_tn(tree_input, value_pre)], axis=1
    )
    grad_kv = scatter(grad_kv.astype(BF16), "line")
    grad_kv = swap(grad_kv.reshape(pair * experts, own_kv, 2, piece), TREES)
    grad_kv = grad_kv.reshape(pair, experts, own_kv, 2, line // experts, part)
    grad_kv = jnp.transpose(grad_kv, (2, 3, 1, 4, 0, 5)).reshape(own_kv, 2, heads_total)
    grad_kv = grad_kv.astype(F32)
    grad_router_first = jnp.dot(
        jnp.transpose(first_logit_grad),
        tree_input.astype(F32),
        precision=HIGHEST,
        preferred_element_type=F32,
    )
    token_grad, grad_gain_first = first_pull(normed_grad)
    tokens_grad = token_grad + middle_grad

    sums = jnp.concatenate(
        [grad_gain_first[None], grad_gain_second[None], grad_router_first, grad_router_second],
        axis=0,
    )
    sums = jnp.transpose(sums.reshape(sums.shape[0], -1, own_kv), (1, 0, 2))
    sums = scatter(sums, ALL)[0]
    return (
        layer_out.reshape(micro, 1, tok, width),
        tokens_grad.reshape(micro, 1, tok, width),
        grad_query.astype(F32),
        grad_output[None].astype(F32),
        grad_kv[:, 0],
        grad_kv[:, 1],
        sums[0],
        jnp.transpose(sums[2 : 2 + experts]),
        sums[1],
        jnp.transpose(sums[2 + experts :]),
        grad_gate,
        grad_upward,
        grad_downward,
    )


def solution(mesh):
    line, experts = mesh.devices.shape
    pair = 2 if line % 2 == 0 and (HEADS % line == 0) else 1
    shaped = Mesh(mesh.devices.reshape(line // pair, pair, experts), ALL)
    in_specs = (
        P(None, DP, "expert", None),
        P("expert", DP, None),
        P("expert", DP, None),
        P(ALL, None),
        P(ALL, None),
        P(ALL),
        P(ALL, None),
        P(ALL),
        P(ALL, None),
        P("expert", DP, None),
        P("expert", DP, None),
        P("expert", DP, None),
        P(None, DP, None, None),
        P(None, DP, "expert", None),
        P(None, DP, "expert"),
        P(None, DP, None),
        P(None, DP, "expert", None),
    )
    out_specs = (
        P(None, DP, "expert", None),
        P(None, DP, "expert", None),
        P("expert", DP, None),
        P("expert", DP, None),
        P(ALL, None),
        P(ALL, None),
        P(ALL),
        P(ALL, None),
        P(ALL),
        P(ALL, None),
        P("expert", DP, None),
        P("expert", DP, None),
        P("expert", DP, None),
    )
    return jax.shard_map(body, mesh=shaped, in_specs=in_specs, out_specs=out_specs, check_vma=False)
```

```python
from functools import partial
import math

import jax
import jax.numpy as jnp
from jax import lax
from jax.experimental import pallas as pl
from jax.experimental.pallas import tpu as pltpu
from jax.sharding import Mesh, PartitionSpec as P

HEADS = 16
HDIM = 128
EPSILON = 1e-06
HIGHEST = lax.Precision.HIGHEST
BF16 = jnp.bfloat16
F32 = jnp.float32


def product(left, right):
    return jnp.dot(left, right, preferred_element_type=F32)


def product_tn(left, right):
    return lax.dot_general(left, right, (((0,), (0,)), ((), ())), preferred_element_type=F32)


def product_nt(left, right):
    return lax.dot_general(left, right, (((1,), (1,)), ((), ())), preferred_element_type=F32)


def rms_scaled(values, gain):
    return values * lax.rsqrt(jnp.mean(values * values, axis=-1, keepdims=True) + EPSILON) * gain


def mixture_gates(picked, logits):
    labels = jnp.arange(logits.shape[1], dtype=jnp.int32)
    onehot = (picked[:, :, None] == labels[None, None, :]).astype(F32)
    chosen = jnp.sum(onehot * logits[:, None, :], axis=-1)
    weights = jax.nn.softmax(chosen, axis=-1)
    return jnp.sum(weights[:, :, None] * onehot, axis=1)


def tree_layout(segment_len, tree_len):
    places = jnp.arange(tree_len, dtype=jnp.int32)
    trunk_len = 4 * segment_len
    segment = jnp.where(
        places < trunk_len,
        0,
        jnp.where(
            places < 2 * trunk_len,
            1 + (places - trunk_len) // segment_len,
            5 + (places - 2 * trunk_len) // segment_len,
        ),
    )
    depth = jnp.where(
        places < trunk_len,
        places,
        jnp.where(
            places < 2 * trunk_len,
            trunk_len + (places - trunk_len) % segment_len,
            trunk_len + segment_len + (places - 2 * trunk_len) % segment_len,
        ),
    )
    return (places, segment, depth)


def ancestors(parent, segment):
    labels = jnp.arange(parent.shape[0], dtype=jnp.int32)
    first = jnp.where(labels > 0, parent, -1)
    lookup = jnp.maximum(first, 0)[:, None] == labels[None, :]
    second = jnp.where(first > 0, jnp.sum(jnp.where(lookup, parent[None, :], 0), axis=1), -1)
    member = segment[:, None] == labels[None, :]
    up_one = jnp.sum(jnp.where(member, first[None, :], 0), axis=1)
    up_two = jnp.sum(jnp.where(member, second[None, :], 0), axis=1)
    return (up_one, up_two)


def score_bias(parent, segment, places):
    up_one, up_two = ancestors(parent, segment)
    same = (segment[None, :] == segment[:, None]) & (places[None, :] <= places[:, None])
    seen = same | (segment[None, :] == up_one[:, None]) | (segment[None, :] == up_two[:, None])
    return jnp.where(seen, 0.0, -1e30).astype(F32)


def slot_table(picked, order, experts, capacity):
    labels = jnp.arange(experts, dtype=jnp.int32)
    chosen = jnp.sum((picked[:, :, None] == labels[None, None, :]).astype(F32), axis=1)
    earlier = (order[None, :] < order[:, None]).astype(F32)
    ranks = jnp.dot(earlier, chosen, precision=HIGHEST, preferred_element_type=F32)
    slots = jnp.arange(capacity, dtype=F32)
    return jnp.transpose(chosen)[:, None, :] * (
        jnp.transpose(ranks)[:, None, :] == slots[None, :, None]
    ).astype(F32)


def turn(values, cosine, sine):
    half = values.shape[-1] // 2
    first = values[:, :half]
    second = values[:, half:]
    return jnp.concatenate(
        [first * cosine - second * sine, second * cosine + first * sine], axis=-1
    )


def softmax_rows(queries, keys, bias, scale):
    scores = product_nt(queries, keys) * scale + bias
    highest = jnp.max(scores, axis=-1, keepdims=True)
    weights = jnp.exp(scores - highest)
    return weights / jnp.sum(weights, axis=-1, keepdims=True)


def attend_kernel(heads, scale, raw_ref, kv_ref, cos_ref, sin_ref, bias_ref, query_ref, out_ref):
    quarter, tok = raw_ref.shape[1], raw_ref.shape[3]
    rows = quarter * tok
    cosine, sine, bias = cos_ref[...], sin_ref[...], bias_ref[0, 0]
    for head in range(heads):
        cols = slice(head * HDIM, (head + 1) * HDIM)
        raw = raw_ref[0, :, 0, :, cols].reshape(rows, HDIM)
        keys = kv_ref[0, 0, 0, :, 0, :, cols].reshape(rows, HDIM)
        values = kv_ref[0, 1, 0, :, 0, :, cols].reshape(rows, HDIM)
        queries = turn(raw, cosine, sine).astype(BF16)
        probs = softmax_rows(queries, keys, bias, scale).astype(BF16)
        query_ref[0, :, 0, :, cols] = queries.reshape(quarter, tok, HDIM)
        out_ref[0, :, 0, :, cols] = product(probs, values).astype(BF16).reshape(quarter, tok, HDIM)


def attend_back_kernel(
    heads, scale, query_ref, kv_ref, grad_ref, cos_ref, sin_ref, bias_ref, dq_ref, dkv_ref
):
    quarter, tok = query_ref.shape[1], query_ref.shape[3]
    rows = quarter * tok
    cosine, sine, bias = cos_ref[...], sin_ref[...], bias_ref[0, 0]
    for head in range(heads):
        cols = slice(head * HDIM, (head + 1) * HDIM)
        queries = query_ref[0, :, 0, :, cols].reshape(rows, HDIM)
        keys = kv_ref[0, 0, 0, :, 0, :, cols].reshape(rows, HDIM)
        values = kv_ref[0, 1, 0, :, 0, :, cols].reshape(rows, HDIM)
        grad = grad_ref[0, :, 0, :, cols].reshape(rows, HDIM)
        probs = softmax_rows(queries, keys, bias, scale)
        prob_grad = product_nt(grad, values)
        centre = jnp.sum(prob_grad * probs, axis=-1, keepdims=True)
        score_grad = (probs * (prob_grad - centre) * scale).astype(BF16)
        query_grad = turn(product(score_grad, keys), cosine, -sine).astype(BF16)
        key_grad = turn(product_tn(score_grad, queries), cosine, -sine).astype(BF16)
        value_grad = product_tn(probs.astype(BF16), grad).astype(BF16)
        dq_ref[0, :, 0, :, cols] = query_grad.reshape(quarter, tok, HDIM)
        dkv_ref[0, 0, 0, :, 0, :, cols] = key_grad.reshape(quarter, tok, HDIM)
        dkv_ref[0, 1, 0, :, 0, :, cols] = value_grad.reshape(quarter, tok, HDIM)


def attention_specs(shape, slices):
    pair, quarter, micro, tok, feats = shape
    part = feats // slices
    rows = quarter * tok
    grid = (pair, micro, slices)
    flat = pl.BlockSpec((1, quarter, 1, tok, part), lambda i, m, s: (i, 0, m, 0, s))
    both = pl.BlockSpec(
        (1, 2, 1, quarter, 1, tok, part), lambda i, m, s: (s, 0, i, 0, m, 0, 0)
    )
    angle = pl.BlockSpec((rows, HDIM // 2), lambda i, m, s: (0, 0))
    bias = pl.BlockSpec((1, 1, rows, rows), lambda i, m, s: (i, m, 0, 0))
    return grid, part, flat, both, angle, bias


def attend(raw, kv, cosine, sine, bias, scale):
    slices = kv.shape[0]
    grid, part, flat, both, angle, bias_spec = attention_specs(raw.shape, slices)
    out = jax.ShapeDtypeStruct(raw.shape, BF16)
    return pl.pallas_call(
        partial(attend_kernel, part // HDIM, scale),
        grid=grid,
        in_specs=[flat, both, angle, angle, bias_spec],
        out_specs=[flat, flat],
        out_shape=[out, out],
        cost_estimate=pl.CostEstimate(
            flops=4 * raw.size * cosine.shape[0],
            bytes_accessed=12 * raw.size,
            transcendentals=raw.size * 2,
        ),
        name="attend",
    )(raw, kv, cosine, sine, bias)


def attend_back(queries, kv, grad, cosine, sine, bias, scale):
    slices = kv.shape[0]
    grid, part, flat, both, angle, bias_spec = attention_specs(queries.shape, slices)
    return pl.pallas_call(
        partial(attend_back_kernel, part // HDIM, scale),
        grid=grid,
        in_specs=[flat, both, flat, angle, angle, bias_spec],
        out_specs=[flat, both],
        out_shape=[
            jax.ShapeDtypeStruct(queries.shape, BF16),
            jax.ShapeDtypeStruct(kv.shape, BF16),
        ],
        cost_estimate=pl.CostEstimate(
            flops=10 * queries.size * cosine.shape[0],
            bytes_accessed=14 * queries.size,
            transcendentals=queries.size * 2,
        ),
        name="attend_back",
    )(queries, kv, grad, cosine, sine, bias)


MESH = pl.DeviceIdType.MESH
ANY = pl.BlockSpec(memory_space=pl.ANY)
VMEM = pl.BlockSpec(memory_space=pltpu.VMEM)
DMA = pltpu.SemaphoreType.DMA


def remote(src, dst, send, recv, target):
    return pltpu.make_async_remote_copy(
        src_ref=src, dst_ref=dst, send_sem=send, recv_sem=recv, device_id=target, device_id_type=MESH
    )


def greet(targets):
    barrier = pltpu.get_barrier_semaphore()
    for target in targets:
        pl.semaphore_signal(barrier, inc=1, device_id=target, device_id_type=MESH)
    pl.semaphore_wait(barrier, len(targets))


def params(number, limit=None):
    return pltpu.CompilerParams(
        collective_id=number, has_side_effects=True, vmem_limit_bytes=limit
    )


def add_into(target, sources, rows):
    step = 1
    while step * 2 <= rows and step * 2 * target.shape[-1] <= 65536 and rows % (step * 2) == 0:
        step *= 2

    def one(index, carry):
        where = pl.ds(pl.multiple_of(index * step, step), step)
        total = sources[0][where].astype(F32)
        for source in sources[1:]:
            total = total + source[where].astype(F32)
        target[where] = total.astype(target.dtype)
        return carry

    lax.fori_loop(0, rows // step, one, 0)


def cube_reduce_kernel(pairs, x_ref, o_ref, half, quarter, got_core, got_side, got_pair, send, recv):
    p = lax.axis_index("pair")
    e = lax.axis_index("expert")
    c, y = lax.rem(e, 2), lax.div(e, 2)
    core = {"expert": e + 1 - 2 * c}
    side = {"expert": e + 2 - 4 * y}
    other = {"pair": lax.rem(p + 1, pairs)}
    greet([core, side] + ([other] if pairs == 2 else []))
    rows = x_ref.shape[3]
    shifts = (1, 0) if pairs == 2 else (0,)
    order = [(dx, dy) for dy in (1, 0) for dx in shifts]
    first, second = [], {}
    for slot, (dx, dy) in enumerate(order):
        px, yy = lax.rem(p + dx, pairs), lax.rem(y + dy, 2)
        copy = remote(
            x_ref.at[px, yy, 1 - c], got_core.at[slot], send.at[slot], recv.at[slot], core
        )
        copy.start()
        first.append(copy)
    base = len(order)
    for slot, (dx, dy) in enumerate(order):
        px, yy = lax.rem(p + dx, pairs), lax.rem(y + dy, 2)
        first[slot].wait_recv()
        add_into(half.at[slot], [x_ref.at[px, yy, c], got_core.at[slot]], rows)
        if dy == 1:
            copy = remote(
                half.at[slot], got_side.at[dx], send.at[base + dx], recv.at[base + dx], side
            )
            copy.start()
            second[dx] = copy
    last = None
    for dx in shifts:
        second[dx].wait_recv()
        if dx == 1:
            add_into(quarter, [half.at[order.index((1, 0))], got_side.at[1]], rows)
            last = remote(quarter, got_pair, send.at[base + 2], recv.at[base + 2], other)
            last.start()
    if last is not None:
        last.wait_recv()
        add_into(o_ref, [half.at[order.index((0, 0))], got_side.at[0], got_pair], rows)
    else:
        add_into(o_ref, [half.at[order.index((0, 0))], got_side.at[0]], rows)
    for copy in first + list(second.values()) + ([last] if last is not None else []):
        copy.wait_send()


def cube_reduce(value, pairs, number):
    _, rows, cols = value.shape
    value = value.reshape(pairs, 2, 2, rows, cols)
    slots = 2 * pairs
    block = jax.ShapeDtypeStruct((rows, cols), value.dtype)
    return pl.pallas_call(
        partial(cube_reduce_kernel, pairs),
        in_specs=[VMEM],
        out_specs=VMEM,
        out_shape=block,
        scratch_shapes=[
            pltpu.VMEM((slots, rows, cols), value.dtype),
            pltpu.VMEM((rows, cols), value.dtype),
            pltpu.VMEM((slots, rows, cols), value.dtype),
            pltpu.VMEM((pairs, rows, cols), value.dtype),
            pltpu.VMEM((rows, cols), value.dtype),
            DMA((slots + 3,)),
            DMA((slots + 3,)),
        ],
        compiler_params=params(number, 48 * 2**20),
        cost_estimate=pl.CostEstimate(
            flops=value.size, bytes_accessed=24 * value.size, transcendentals=0
        ),
        name="cube_reduce",
    )(value)


def cube_gather_kernel(pairs, x_ref, o_ref, send, recv, local):
    p = lax.axis_index("pair") if pairs == 2 else 0
    e = lax.axis_index("expert")
    c, y = lax.rem(e, 2), lax.div(e, 2)
    core = {"expert": e + 1 - 2 * c}
    side = {"expert": e + 2 - 4 * y}
    other = {"pair": lax.rem(p + 1, pairs)}
    greet([core, side] + ([other] if pairs == 2 else []))
    q, w = lax.rem(p + 1, pairs), 1 - y
    own = o_ref.at[p, y, c]
    keep = pltpu.make_async_copy(x_ref, own, local)
    keep.start()
    copies = []

    def push(slot, source, place, target):
        copy = remote(source, place, send.at[slot], recv.at[slot], target)
        copy.start()
        copies.append(copy)
        return copy

    to_side = push(0, x_ref, own, side)
    to_other = push(1, x_ref, own, other) if pairs == 2 else None
    to_core = push(2, x_ref, own, core)
    waits = [to_core]
    if pairs == 2:
        to_other.wait_recv()
        block = o_ref.at[q, y, c]
        far = push(3, block, block, side)
        waits.append(push(4, block, block, core))
    to_side.wait_recv()
    block = o_ref.at[p, w, c]
    waits.append(push(5, block, block, core))
    if pairs == 2:
        far.wait_recv()
        block = o_ref.at[q, w, c]
        waits.append(push(6, block, block, core))
    for copy in waits:
        copy.wait_recv()
    for copy in copies:
        copy.wait_send()
    keep.wait()


def cube_gather(value, pairs, number):
    return pl.pallas_call(
        partial(cube_gather_kernel, pairs),
        in_specs=[VMEM],
        out_specs=VMEM,
        out_shape=jax.ShapeDtypeStruct((pairs, 2, 2) + value.shape, value.dtype),
        scratch_shapes=[DMA((7,)), DMA((7,)), DMA(())],
        compiler_params=params(number, 48 * 2**20),
        cost_estimate=pl.CostEstimate(
            flops=0, bytes_accessed=80 * value.size, transcendentals=0
        ),
        name="cube_gather",
    )(value)


def place_of(index, sizes):
    line, pairs, experts = sizes
    return {
        "line": index // (pairs * experts),
        "pair": (index // experts) % pairs,
        "expert": index % experts,
    }


def small_kernel(sizes, reduce, x_ref, o_ref, got, send, recv):
    line, pairs, experts = sizes
    count = line * pairs * experts
    me = (
        lax.axis_index("line") * (pairs * experts)
        + lax.axis_index("pair") * experts
        + lax.axis_index("expert")
    )
    barrier = pltpu.get_barrier_semaphore()

    def greet_one(offset, carry):
        target = place_of((me + offset) % count, sizes)
        pl.semaphore_signal(barrier, inc=1, device_id=target, device_id_type=MESH)
        return carry

    lax.fori_loop(1, count, greet_one, 0)
    pl.semaphore_wait(barrier, count - 1)

    def copy_to(offset):
        peer = (me + offset) % count
        source = x_ref.at[peer] if reduce else x_ref
        return remote(source, got.at[offset], send.at[offset], recv.at[offset], place_of(peer, sizes))

    def start(offset, carry):
        copy_to(offset).start()
        return carry

    lax.fori_loop(1, count, start, 0)
    got[0] = x_ref[me] if reduce else x_ref[...]

    def finish(offset, carry):
        copy_to(offset).wait()
        return carry

    lax.fori_loop(1, count, finish, 0)
    if reduce:
        o_ref[...] = jnp.sum(got[...], axis=0)
    else:

        def order(offset, carry):
            o_ref[(me - offset + count) % count] = got[offset]
            return carry

        lax.fori_loop(0, count, order, 0)


def small_exchange(value, sizes, reduce, number):
    count = sizes[0] * sizes[1] * sizes[2]
    block = value.shape[1:] if reduce else value.shape
    return pl.pallas_call(
        partial(small_kernel, sizes, reduce),
        in_specs=[VMEM],
        out_specs=VMEM,
        out_shape=jax.ShapeDtypeStruct(block if reduce else (count,) + block, value.dtype),
        scratch_shapes=[pltpu.VMEM((count,) + block, value.dtype), DMA((count,)), DMA((count,))],
        compiler_params=params(number),
        cost_estimate=pl.CostEstimate(flops=0, bytes_accessed=2**24, transcendentals=0),
        name="small_reduce" if reduce else "small_gather",
    )(value)


def ff_gather_kernel(line, a_in, b_in, a_hbm, b_hbm, a_out, b_out, send, recv, local, store):
    z, p, e = lax.axis_index("line"), lax.axis_index("pair"), lax.axis_index("expert")
    experts = a_in.shape[0]
    q = 1 - p
    up, down, other = {"line": z + 1}, {"line": z - 1}, {"pair": q}
    twin = z + 1 - 2 * lax.rem(z, 2)
    barrier = pltpu.get_barrier_semaphore()
    for shift in range(1, experts):
        pl.semaphore_signal(
            barrier, inc=1, device_id={"expert": lax.rem(e + shift, experts)}, device_id_type=MESH
        )
    pl.semaphore_signal(barrier, inc=1, device_id=other, device_id_type=MESH)

    @pl.when(z > 0)
    def _():
        pl.semaphore_signal(barrier, inc=1, device_id=down, device_id_type=MESH)

    @pl.when(z < line - 1)
    def _():
        pl.semaphore_signal(barrier, inc=1, device_id=up, device_id_type=MESH)

    below, above = (z + line - 1) // line, (2 * line - 2 - z) // line
    pl.semaphore_wait(barrier, experts + below + above)

    pairs = ((a_in, a_out), (b_in, b_out))
    UP, DOWN, SIDE = 3, 3 + line, 3 + 2 * line
    EXTRA = SIDE + line
    starts = []
    for kind, (src, dst) in enumerate(pairs):
        size = src.shape[1]
        home = dst.at[z, p, pl.ds(pl.multiple_of(e * size, size), size)]
        keep = pltpu.make_async_copy(src.at[e], home, local.at[kind])
        keep.start()
        group = []
        for shift in range(1, experts):
            peer = lax.rem(e + shift, experts)
            copy = remote(
                src.at[peer],
                home,
                send.at[kind, shift - 1],
                recv.at[kind, shift - 1],
                {"expert": peer},
            )
            copy.start()
            group.append(copy)
        starts.append((keep, group))

    def to_up(kind, j, d):
        ref = pairs[kind][1].at[j, p]
        return remote(ref, ref, send.at[kind, UP + d], recv.at[kind, UP + d], up)

    def to_down(kind, j, d):
        ref = pairs[kind][1].at[j, p]
        return remote(ref, ref, send.at[kind, DOWN + d], recv.at[kind, DOWN + d], down)

    def to_other(kind, j):
        ref = pairs[kind][1].at[j, p]
        return remote(ref, ref, send.at[kind, SIDE + j], recv.at[kind, SIDE + j], other)

    def to_twin(kind):
        ref = pairs[kind][1].at[z, q]
        return remote(ref, ref, send.at[kind, EXTRA], recv.at[kind, EXTRA], {"line": twin})

    for kind in range(2):
        keep, group = starts[kind]
        keep.wait()
        for copy in group:
            copy.wait_recv()

        @pl.when(z < line - 1)
        def _():
            to_up(kind, z, 1).start()

        @pl.when(z > 0)
        def _():
            to_down(kind, z, 1).start()

        to_other(kind, z).start()

    for d in range(1, line):
        for kind in range(2):

            @pl.when(z - d >= 0)
            def _():
                to_up(kind, z - d, d).wait_recv()

                @pl.when(z < line - 1)
                def _():
                    to_up(kind, z - d, d + 1).start()

                if kind == 0:
                    to_other(kind, z - d).start()
                else:

                    @pl.when(z - d != twin)
                    def _():
                        to_other(kind, z - d).start()

            @pl.when(z + d < line)
            def _():
                to_down(kind, z + d, d).wait_recv()

                @pl.when(z > 0)
                def _():
                    to_down(kind, z + d, d + 1).start()

                if kind == 0:
                    to_other(kind, z + d).start()
                else:

                    @pl.when(z + d != twin)
                    def _():
                        to_other(kind, z + d).start()

        if d == 1:
            to_other(1, z).wait_recv()
            to_twin(1).start()

    for j in range(line):
        to_other(0, j).wait_recv()

        @pl.when((j != twin) & (j != z))
        def _():
            to_other(1, j).wait_recv()

        to_other(0, j).wait_send()

        @pl.when(j != twin)
        def _():
            to_other(1, j).wait_send()

    to_twin(1).wait()
    saves = []
    for kind, target in enumerate((a_hbm, b_hbm)):
        save = pltpu.make_async_copy(pairs[kind][1], target, store.at[kind])
        save.start()
        saves.append(save)
    for save in saves:
        save.wait()
    for kind in range(2):
        for copy in starts[kind][1]:
            copy.wait_send()
        for d in range(1, line):

            @pl.when((z - d + 1 >= 0) & (z < line - 1))
            def _():
                to_up(kind, z - d + 1, d).wait_send()

            @pl.when((z + d - 1 < line) & (z > 0))
            def _():
                to_down(kind, z + d - 1, d).wait_send()


def ff_gather(first, second, line, pairs, number):
    uses = 3 + 3 * line + 1
    experts, rows, cols = first.shape
    out = jax.ShapeDtypeStruct((line, pairs, experts * rows, cols), first.dtype)
    return pl.pallas_call(
        partial(ff_gather_kernel, line),
        in_specs=[VMEM, VMEM],
        out_specs=[ANY, ANY],
        out_shape=[out, out],
        scratch_shapes=[
            pltpu.VMEM(out.shape, out.dtype),
            pltpu.VMEM(out.shape, out.dtype),
            DMA((2, uses)),
            DMA((2, uses)),
            DMA((2,)),
            DMA((2,)),
        ],
        compiler_params=params(number, 48 * 2**20),
        cost_estimate=pl.CostEstimate(
            flops=0, bytes_accessed=100 * first.size * line, transcendentals=0
        ),
        name="ff_gather",
    )(first, second)


def ff_reduce_kernel(
    line, a_in, b_in, a_out, b_out, mine, side, far, near, done, send, recv, load, local
):
    z, p, e = lax.axis_index("line"), lax.axis_index("pair"), lax.axis_index("expert")
    experts = a_out.shape[0]
    q = 1 - p
    up, down, other = {"line": z + 1}, {"line": z - 1}, {"pair": q}
    barrier = pltpu.get_barrier_semaphore()
    for shift in range(1, experts):
        pl.semaphore_signal(
            barrier, inc=1, device_id={"expert": lax.rem(e + shift, experts)}, device_id_type=MESH
        )
    pl.semaphore_signal(barrier, inc=1, device_id=other, device_id_type=MESH)

    @pl.when(z > 0)
    def _():
        pl.semaphore_signal(barrier, inc=1, device_id=down, device_id_type=MESH)

    @pl.when(z < line - 1)
    def _():
        pl.semaphore_signal(barrier, inc=1, device_id=up, device_id_type=MESH)

    below, above = (z + line - 1) // line, (2 * line - 2 - z) // line
    pl.semaphore_wait(barrier, experts + below + above)

    kinds = (a_in, b_in)
    outs = (a_out, b_out)
    UP, DOWN, SIDE, BACK = 0, line, 2 * line, 3 * line
    rows = mine.shape[2]

    def to_other(kind, j):
        return remote(
            kinds[kind].at[j, q],
            side.at[kind, j],
            send.at[kind, SIDE + j],
            recv.at[kind, SIDE + j],
            other,
        )

    def fetch(kind, j):
        return pltpu.make_async_copy(kinds[kind].at[j, p], mine.at[kind, j], load.at[kind, j])

    def to_up(kind, j):
        return remote(
            mine.at[kind, j], far.at[kind, j], send.at[kind, UP + j], recv.at[kind, UP + j], up
        )

    def to_down(kind, j, dst=None):
        return remote(
            mine.at[kind, j], near.at[kind, j], send.at[kind, DOWN + j], recv.at[kind, DOWN + j], down
        )

    for d in range(line - 1, -1, -1):
        for kind in range(2):

            @pl.when(z + d < line)
            def _():
                to_other(kind, z + d).start()
                fetch(kind, z + d).start()

            if d > 0:

                @pl.when(z - d >= 0)
                def _():
                    to_other(kind, z - d).start()
                    fetch(kind, z - d).start()

    for d in range(line - 1, 0, -1):
        for kind in range(2):

            @pl.when(z + d < line)
            def _():
                j = z + d
                fetch(kind, j).wait()
                to_other(kind, j).wait_recv()
                add_into(mine.at[kind, j], [mine.at[kind, j], side.at[kind, j]], rows)

                @pl.when(z > 0)
                def _():
                    to_up(kind, j).wait_recv()
                    add_into(mine.at[kind, j], [mine.at[kind, j], far.at[kind, j]], rows)

                to_up(kind, j).start()

            @pl.when(z - d >= 0)
            def _():
                j = z - d
                fetch(kind, j).wait()
                to_other(kind, j).wait_recv()
                add_into(mine.at[kind, j], [mine.at[kind, j], side.at[kind, j]], rows)

                @pl.when(z < line - 1)
                def _():
                    to_down(kind, j).wait_recv()
                    add_into(mine.at[kind, j], [mine.at[kind, j], near.at[kind, j]], rows)

                to_down(kind, j).start()

    back = []
    for kind in range(2):
        fetch(kind, z).wait()
        to_other(kind, z).wait_recv()

        @pl.when(z > 0)
        def _():
            to_up(kind, z).wait_recv()

        @pl.when(z < line - 1)
        def _():
            to_down(kind, z).wait_recv()

        total = done.at[kind]

        @pl.when((z > 0) & (z < line - 1))
        def _():
            add_into(
                total,
                [mine.at[kind, z], side.at[kind, z], far.at[kind, z], near.at[kind, z]],
                rows,
            )

        @pl.when(z == 0)
        def _():
            add_into(total, [mine.at[kind, z], side.at[kind, z], near.at[kind, z]], rows)

        @pl.when(z == line - 1)
        def _():
            add_into(total, [mine.at[kind, z], side.at[kind, z], far.at[kind, z]], rows)

        size = rows // experts
        keep = pltpu.make_async_copy(
            done.at[kind, pl.ds(pl.multiple_of(e * size, size), size)], outs[kind].at[e], local.at[kind]
        )
        keep.start()
        for shift in range(1, experts):
            peer = lax.rem(e + shift, experts)
            copy = remote(
                done.at[kind, pl.ds(pl.multiple_of(peer * size, size), size)],
                outs[kind].at[e],
                send.at[kind, BACK + shift],
                recv.at[kind, BACK + shift],
                {"expert": peer},
            )
            copy.start()
            back.append(copy)
        back.append(keep)
    for copy in back:
        copy.wait()
    for kind in range(2):
        for j in range(line):
            to_other(kind, j).wait_send()

            @pl.when(j > z)
            def _():
                to_up(kind, j).wait_send()

            @pl.when(j < z)
            def _():
                to_down(kind, j).wait_send()


def ff_reduce(first, second, line, pairs, experts, number):
    cols = first.shape[1]
    rows = first.shape[0] // (line * pairs)
    shape = (line, pairs, rows, cols)
    out = jax.ShapeDtypeStruct((experts, rows // experts, cols), first.dtype)
    uses = 3 * line + experts
    block = lambda: pltpu.VMEM((2, line, rows, cols), first.dtype)
    return pl.pallas_call(
        partial(ff_reduce_kernel, line),
        in_specs=[ANY, ANY],
        out_specs=[ANY, ANY],
        out_shape=[out, out],
        scratch_shapes=[
            block(),
            block(),
            block(),
            block(),
            pltpu.VMEM((2, rows, cols), first.dtype),
            DMA((2, uses)),
            DMA((2, uses)),
            DMA((2, line)),
            DMA((2,)),
        ],
        compiler_params=params(number, 56 * 2**20),
        cost_estimate=pl.CostEstimate(
            flops=0, bytes_accessed=40 * first.size, transcendentals=0
        ),
        name="ff_reduce",
    )(first.reshape(shape), second.reshape(shape))


def pair_swap_kernel(a_ref, b_ref, a_out, b_out, send, recv, local):
    p = lax.axis_index("pair")
    other = {"pair": 1 - p}
    greet([other])
    copies = []
    for slot, (src, dst) in enumerate(((a_ref.at[1 - p], a_out.at[p]), (b_ref, b_out.at[p]))):
        copy = remote(src, dst, send.at[slot], recv.at[slot], other)
        copy.start()
        copies.append(copy)
    for slot, (src, dst) in enumerate(((a_ref.at[p], a_out.at[p]), (b_ref, b_out.at[p]))):
        copy = pltpu.make_async_copy(src, dst, local.at[slot])
        copy.start()
        copies.append(copy)
    for copy in copies:
        copy.wait()


def pair_swap(value, shared, number):
    return pl.pallas_call(
        pair_swap_kernel,
        in_specs=[VMEM, VMEM],
        out_specs=[VMEM, VMEM],
        out_shape=[
            jax.ShapeDtypeStruct(value.shape, value.dtype),
            jax.ShapeDtypeStruct((2,) + shared.shape, shared.dtype),
        ],
        scratch_shapes=[DMA((2,)), DMA((2,)), DMA((2,))],
        compiler_params=params(number),
        cost_estimate=pl.CostEstimate(
            flops=0, bytes_accessed=20 * value.size, transcendentals=0
        ),
        name="pair_swap",
    )(value, shared)


def start_kernel(
    sizes, walk, tok_ref, small_ref, kv_ref, tok_out, small_out, kv_out, send, recv, peer_send, peer_recv, local
):
    line, pairs, experts = sizes
    z = lax.axis_index("line")
    p = lax.axis_index("pair") if pairs == 2 else 0
    e = lax.axis_index("expert")
    c, y = lax.rem(e, 2), lax.div(e, 2)
    core = {"expert": e + 1 - 2 * c}
    side = {"expert": e + 2 - 4 * y}
    other = {"pair": lax.rem(p + 1, pairs)}
    count = line * pairs * experts
    trees = pairs * experts
    local_me = p * experts + e
    me = z * trees + local_me
    barrier = pltpu.get_barrier_semaphore()

    def greet_one(offset, carry):
        target = place_of((me + offset) % count, sizes)
        pl.semaphore_signal(barrier, inc=1, device_id=target, device_id_type=MESH)
        return carry

    lax.fori_loop(1, count, greet_one, 0)
    pl.semaphore_wait(barrier, count - 1)

    size = kv_ref.shape[1]
    home = kv_out.at[z if walk else 0, pl.ds(pl.multiple_of(local_me * size, size), size)]
    keeps = [
        pltpu.make_async_copy(kv_ref.at[local_me], home, local.at[0]),
        pltpu.make_async_copy(tok_ref, tok_out.at[p, y, c], local.at[1]),
        pltpu.make_async_copy(small_ref, small_out.at[me], local.at[2]),
    ]
    for copy in keeps:
        copy.start()
    KV = 7
    pieces = []
    for shift in range(1, trees):
        peer = lax.rem(local_me + shift, trees)
        copy = remote(
            kv_ref.at[peer],
            home,
            send.at[KV + shift],
            recv.at[KV + shift],
            {"pair": peer // experts, "expert": peer % experts},
        )
        copy.start()
        pieces.append(copy)

    q, w = lax.rem(p + 1, pairs), 1 - y
    own = tok_out.at[p, y, c]
    copies = []

    def push(slot, source, place, target):
        copy = remote(source, place, send.at[slot], recv.at[slot], target)
        copy.start()
        copies.append(copy)
        return copy

    to_side = push(0, tok_ref, own, side)
    to_other = push(1, tok_ref, own, other) if pairs == 2 else None
    waits = [push(2, tok_ref, own, core)]

    def small_to(offset):
        return remote(
            small_ref,
            small_out.at[me],
            peer_send.at[offset],
            peer_recv.at[offset],
            place_of((me + offset) % count, sizes),
        )

    def small_start(offset, carry):
        small_to(offset).start()
        return carry

    lax.fori_loop(1, count, small_start, 0)

    base = KV + trees
    keeps[0].wait()
    for copy in pieces:
        copy.wait_recv()

    def to_up(j, d):
        ref = kv_out.at[j]
        return remote(ref, ref, send.at[base + d], recv.at[base + d], {"line": z + 1})

    def to_down(j, d):
        ref = kv_out.at[j]
        return remote(ref, ref, send.at[base + line + d], recv.at[base + line + d], {"line": z - 1})

    if walk:

        @pl.when(z < line - 1)
        def _():
            to_up(z, 1).start()

        @pl.when(z > 0)
        def _():
            to_down(z, 1).start()

    if pairs == 2:
        to_other.wait_recv()
        block = tok_out.at[q, y, c]
        far = push(3, block, block, side)
        waits.append(push(4, block, block, core))
    to_side.wait_recv()
    block = tok_out.at[p, w, c]
    waits.append(push(5, block, block, core))
    if pairs == 2:
        far.wait_recv()
        block = tok_out.at[q, w, c]
        waits.append(push(6, block, block, core))

    if walk:
        for d in range(1, line):

            @pl.when(z - d >= 0)
            def _():
                to_up(z - d, d).wait_recv()

                @pl.when(z < line - 1)
                def _():
                    to_up(z - d, d + 1).start()

            @pl.when(z + d < line)
            def _():
                to_down(z + d, d).wait_recv()

                @pl.when(z > 0)
                def _():
                    to_down(z + d, d + 1).start()

        for d in range(1, line):

            @pl.when((z - d + 1 >= 0) & (z < line - 1))
            def _():
                to_up(z - d + 1, d).wait_send()

            @pl.when((z + d - 1 < line) & (z > 0))
            def _():
                to_down(z + d - 1, d).wait_send()

    for copy in waits:
        copy.wait_recv()
    for copy in copies + pieces:
        copy.wait_send()
    for copy in keeps[1:]:
        copy.wait()

    def small_finish(offset, carry):
        small_to(offset).wait()
        return carry

    lax.fori_loop(1, count, small_finish, 0)


def start_exchange(tokens, small, kv, sizes, number):
    line, pairs, experts = sizes
    trees, rows, cols = kv.shape
    walk = line <= 4
    count = line * trees
    uses = 7 + trees + 2 * line + 2
    return pl.pallas_call(
        partial(start_kernel, sizes, walk),
        in_specs=[VMEM, VMEM, VMEM],
        out_specs=[VMEM, VMEM, VMEM],
        out_shape=[
            jax.ShapeDtypeStruct((pairs, 2, 2) + tokens.shape, tokens.dtype),
            jax.ShapeDtypeStruct((count,) + small.shape, small.dtype),
            jax.ShapeDtypeStruct((line if walk else 1, trees * rows, cols), kv.dtype),
        ],
        scratch_shapes=[DMA((uses,)), DMA((uses,)), DMA((count,)), DMA((count,)), DMA((3,))],
        compiler_params=params(number, 32 * 2**20),
        cost_estimate=pl.CostEstimate(
            flops=0, bytes_accessed=100 * kv.size, transcendentals=0
        ),
        name="start_exchange",
    )(tokens, small, kv)


def gather(value, axes, axis=0):
    return lax.all_gather(value, axes, axis=axis, tiled=True)


def scatter(value, axes, axis=0):
    return lax.psum_scatter(value, axes, scatter_dimension=axis, tiled=True)


def swap(value, axes, split=0, concat=0):
    return lax.all_to_all(value, axes, split_axis=split, concat_axis=concat, tiled=True)


DP = ("line", "pair")
ALL = ("line", "pair", "expert")
TREES = ("pair", "expert")


def body(
    tokens,
    w_query,
    w_out,
    w_key,
    w_value,
    gain_attn,
    router_attn,
    gain_mlp,
    router_mlp,
    w_gate,
    w_up,
    w_down,
    attn_route,
    mlp_route,
    fill_order,
    parents,
    cotangent,
):
    experts = lax.axis_size("expert")
    pair = lax.axis_size("pair")
    line = lax.axis_size("line")
    position = lax.axis_index("expert")
    micro, _, tok, width = tokens.shape
    tree = experts * tok
    rows = pair * experts * micro * tok
    heads_total = w_query.shape[2]
    part = heads_total // (line * pair)
    feats = heads_total // pair
    piece = feats // experts
    own_in = w_query.shape[1]
    own_kv = w_key.shape[0]
    capacity = tok * mlp_route.shape[3] // experts
    scale = 1.0 / math.sqrt(HDIM)

    places, segment, depth = tree_layout(tree // 16, tree)
    half = HDIM // 2
    rates = 10000.0 ** (-jnp.arange(half, dtype=F32) / half)
    angle = depth.astype(F32)[:, None] * rates[None, :]
    cosine, sine = jnp.cos(angle), jnp.sin(angle)

    sizes = (line, pair, experts)
    walk = line <= 4 and pair == 2
    query_mine = w_query[0].reshape(own_in, line, pair, part)
    query_mine = jnp.transpose(query_mine, (2, 0, 1, 3)).reshape(pair, own_in, feats)
    integers = jnp.concatenate([attn_route[:, 0].reshape(micro, -1), parents[:, 0]], axis=1)
    if pair == 2:
        flat = integers.reshape(-1)
        flat = jnp.pad(flat, (0, -flat.shape[0] % 1024)).reshape(-1, 128)
        query_mine, flat = pair_swap(query_mine, flat, 1)
        integers = flat.reshape(pair, -1)[:, : integers.size].reshape((pair,) + integers.shape)
    else:
        integers = integers[None]
    query_weight = gather(query_mine.reshape(pair * own_in, feats), "line")

    small = jnp.concatenate(
        [gain_attn[None], gain_mlp[None], router_attn.T, router_mlp.T], axis=0
    )
    kv_mine = jnp.stack([w_key, w_value], axis=1).reshape(
        own_kv, 2, experts, line // experts, pair, part
    )
    kv_mine = jnp.transpose(kv_mine, (4, 2, 0, 1, 3, 5)).reshape(
        pair * experts, own_kv, 2 * piece
    )
    own_tokens = tokens.reshape(micro * tok, width)
    tree_tokens, small, kv_weight = start_exchange(own_tokens, small, kv_mine, sizes, 2)
    kv_weight = kv_weight.reshape(-1, 2 * piece)
    if kv_weight.shape[0] < width:
        kv_weight = gather(kv_weight, "line")
    out_mine, small = lax.optimization_barrier((w_out[0], small))
    out_weight = gather(out_mine, "line")

    small = jnp.transpose(small, (1, 0, 2)).reshape(-1, width)
    first_gain = small[0].astype(F32)
    second_gain = small[1].astype(F32)
    first_router = small[2 : 2 + experts]
    second_router = small[2 + experts : 2 + 2 * experts]

    residual = own_tokens.astype(F32)
    _, first_pull = jax.vjp(rms_scaled, residual, first_gain)
    tree_input = rms_scaled(tree_tokens.reshape(rows, width).astype(F32), first_gain).astype(BF16)

    routes = integers[..., : tree * 2].reshape(pair, micro, experts, tok, 2)
    routes = jnp.transpose(routes, (0, 2, 1, 3, 4)).reshape(rows, 2)
    family = integers[..., tree * 2 :]
    bias = jax.vmap(jax.vmap(lambda parent: score_bias(parent, segment, places)))(family)

    kv_raw = product(tree_input, kv_weight)
    spread_cos = jnp.broadcast_to(
        cosine.reshape(1, experts, 1, tok, 1, half), (pair, experts, micro, tok, 1, half)
    ).reshape(rows, 1, half)
    spread_sin = jnp.broadcast_to(
        sine.reshape(1, experts, 1, tok, 1, half), (pair, experts, micro, tok, 1, half)
    ).reshape(rows, 1, half)
    key_raw = kv_raw[:, :piece].reshape(rows, piece // HDIM, HDIM)
    key_one, key_two = key_raw[..., :half], key_raw[..., half:]
    keys = jnp.concatenate(
        [
            key_one * spread_cos - key_two * spread_sin,
            key_two * spread_cos + key_one * spread_sin,
        ],
        axis=-1,
    ).reshape(rows, piece)
    kv = jnp.concatenate([keys.astype(BF16), kv_raw[:, piece:].astype(BF16)], axis=0)
    kv = cube_gather(kv, 1, 3)
    shape = (pair, experts, micro, tok, feats)
    kv = kv.reshape(experts, 2, pair, experts, micro, tok, piece)

    first_gates, first_gate_pull = jax.vjp(
        partial(mixture_gates, routes), product_nt(tree_input, first_router)
    )
    column = (jnp.arange(experts, dtype=jnp.int32) == position).astype(F32)
    own_gate = jnp.sum(first_gates * column[None, :], axis=1)

    raw = product(tree_input, query_weight)
    queries, heads_out = attend(raw.reshape(shape), kv, cosine, sine, bias, scale)
    heads_flat = heads_out.reshape(rows, feats)
    projected = product(heads_flat, out_weight)
    gated = (own_gate[:, None] * projected).astype(BF16)
    attention = cube_reduce(gated.reshape(pair * experts, micro * tok, width), pair, 4).astype(F32)

    middle = residual + attention
    second_normed, second_pull = jax.vjp(rms_scaled, middle, second_gain)
    second_normed = second_normed.astype(BF16)
    picked = mlp_route[:, 0].reshape(micro * tok, 2)
    second_gates, second_gate_pull = jax.vjp(
        partial(mixture_gates, picked), product_nt(second_normed, second_router)
    )
    table = jax.vmap(partial(slot_table, experts=experts, capacity=capacity))(
        mlp_route[:, 0], fill_order[:, 0]
    )
    table_low = table.astype(BF16)
    grouped = second_normed.reshape(micro, tok, width)
    outgoing = jnp.einsum("mect,mtd->emcd", table_low, grouped, preferred_element_type=F32)
    top_grad = cotangent.reshape(micro, tok, width)
    slot_values = jnp.einsum("mect,mtd->emcd", table_low, top_grad, preferred_element_type=F32)
    slot_gates = jnp.einsum(
        "mect,mte->emc", table, second_gates.reshape(micro, tok, experts), precision=HIGHEST
    )
    slot_grad = (slot_gates[..., None] * slot_values).astype(BF16)
    slots = experts * micro * capacity
    outgoing = outgoing.astype(BF16).reshape(experts, micro * capacity, width)
    slot_grad = slot_grad.reshape(experts, micro * capacity, width)
    if walk:
        arrived, result_grad = ff_gather(outgoing, slot_grad, line, pair, 5)
        arrived = arrived.reshape(-1, width)
        result_grad = result_grad.reshape(-1, width)
    else:
        arrived = gather(swap(outgoing, "expert").reshape(slots, width), DP)
        result_grad = gather(swap(slot_grad, "expert").reshape(slots, width), DP)

    gate_weight, up_weight, down_weight = w_gate[0], w_up[0], w_down[0]
    gate_pre = product_nt(arrived, gate_weight)
    up_pre = product_nt(arrived, up_weight)
    sigma = jax.nn.sigmoid(gate_pre)
    inner = (gate_pre * sigma * up_pre).astype(BF16)
    returned = product(inner, down_weight).astype(BF16)
    inner_grad = product_nt(result_grad, down_weight)
    gate_grad = (inner_grad * up_pre * sigma * (1.0 + gate_pre * (1.0 - sigma))).astype(BF16)
    up_grad = (inner_grad * gate_pre * sigma).astype(BF16)
    came_back = (product(gate_grad, gate_weight) + product(up_grad, up_weight)).astype(BF16)
    if walk:
        returned, came_back = ff_reduce(returned, came_back, line, pair, experts, 6)
    else:
        back = (experts, micro * capacity, width)
        returned = swap(scatter(returned, DP).reshape(back), "expert")
        came_back = swap(scatter(came_back, DP).reshape(back), "expert")
    gate_grad, up_grad, inner, arrived, result_grad, returned, came_back = lax.optimization_barrier(
        (gate_grad, up_grad, inner, arrived, result_grad, returned, came_back)
    )
    returned = returned.reshape(experts, micro, capacity, width)
    came_back = came_back.reshape(experts, micro, capacity, width)
    grad_gate = product_tn(gate_grad, arrived)[None]
    grad_upward = product_tn(up_grad, arrived)[None]
    grad_downward = product_tn(inner, result_grad)[None]

    spread = jnp.einsum("mect,emcd->emtd", table_low, returned, preferred_element_type=F32)
    spread = spread.reshape(experts, micro * tok, width)
    mixed = jnp.sum(jnp.transpose(second_gates)[:, :, None] * spread, axis=0)
    layer_out = (middle + mixed).astype(BF16)
    dz = top_grad.reshape(micro * tok, width).astype(F32)
    second_gate_grad = jnp.transpose(jnp.sum(spread * dz[None], axis=-1))
    (second_logit_grad,) = second_gate_pull(second_gate_grad)
    hn_grad = jnp.einsum("mect,emcd->mtd", table_low, came_back, preferred_element_type=F32)
    hn_grad = hn_grad.reshape(micro * tok, width)
    second_router_wide = second_router.astype(F32)
    for expert in range(experts):
        hn_grad = hn_grad + second_logit_grad[:, expert : expert + 1] * second_router_wide[expert]
    grad_router_second = jnp.dot(
        jnp.transpose(second_logit_grad),
        second_normed.astype(F32),
        precision=HIGHEST,
        preferred_element_type=F32,
    )
    middle_grad, grad_gain_second = second_pull(hn_grad)
    middle_grad = middle_grad + dz

    mix_grad = cube_gather(middle_grad.astype(BF16), pair, 7).reshape(rows, width).astype(F32)
    own_gate_grad = jnp.sum(mix_grad * projected, axis=-1)
    projected_grad = (own_gate[:, None] * mix_grad).astype(BF16)
    heads_grad = product_nt(projected_grad, out_weight).astype(BF16).reshape(shape)
    grad_output = scatter(product_tn(heads_flat, projected_grad).astype(BF16), "line")
    query_pre, kv_pre = attend_back(queries, kv, heads_grad, cosine, sine, bias, scale)
    query_pre = query_pre.reshape(rows, feats)
    kv_sum = cube_reduce(kv_pre.reshape(experts, 2 * rows, piece), 1, 8)
    grad_query = scatter(product_tn(tree_input, query_pre).astype(BF16), "line")
    grad_query = swap(grad_query.reshape(own_in * pair, line, part)[None], "pair", 1, 0)
    grad_query = jnp.transpose(grad_query, (1, 2, 0, 3)).reshape(1, own_in, heads_total)

    (first_logit_grad,) = first_gate_pull(own_gate_grad[:, None] * column[None, :])
    key_pre, value_pre = kv_sum[:rows], kv_sum[rows:]
    input_term = (
        product_nt(query_pre, query_weight)
        + product_nt(key_pre, kv_weight[:, :piece])
        + product_nt(value_pre, kv_weight[:, piece:])
    )
    first_router_wide = first_router.astype(F32)
    for expert in range(experts):
        input_term = input_term + first_logit_grad[:, expert : expert + 1] * first_router_wide[expert]
    input_term = input_term.astype(BF16).reshape(pair * experts, micro * tok, width)
    normed_grad = cube_reduce(input_term, pair, 9).astype(F32)
    grad_kv = jnp.stack(
        [product_tn(tree_input, key_pre), product_tn(tree_input, value_pre)], axis=1
    )
    grad_kv = scatter(grad_kv.astype(BF16), "line")
    grad_kv = swap(grad_kv.reshape(pair * experts, own_kv, 2, piece), TREES)
    grad_kv = grad_kv.reshape(pair, experts, own_kv, 2, line // experts, part)
    grad_kv = jnp.transpose(grad_kv, (2, 3, 1, 4, 0, 5)).reshape(own_kv, 2, heads_total)
    grad_kv = grad_kv.astype(F32)
    grad_router_first = jnp.dot(
        jnp.transpose(first_logit_grad),
        tree_input.astype(F32),
        precision=HIGHEST,
        preferred_element_type=F32,
    )
    token_grad, grad_gain_first = first_pull(normed_grad)
    tokens_grad = token_grad + middle_grad

    sums = jnp.concatenate(
        [grad_gain_first[None], grad_gain_second[None], grad_router_first, grad_router_second],
        axis=0,
    )
    sums = jnp.transpose(sums.reshape(sums.shape[0], -1, own_kv), (1, 0, 2))
    sums = small_exchange(sums, sizes, True, 10)
    return (
        layer_out.reshape(micro, 1, tok, width),
        tokens_grad.reshape(micro, 1, tok, width),
        grad_query.astype(F32),
        grad_output[None].astype(F32),
        grad_kv[:, 0],
        grad_kv[:, 1],
        sums[0],
        jnp.transpose(sums[2 : 2 + experts]),
        sums[1],
        jnp.transpose(sums[2 + experts :]),
        grad_gate,
        grad_upward,
        grad_downward,
    )


def solution(mesh):
    line, experts = mesh.devices.shape
    pair = 2 if line % 2 == 0 and (HEADS % line == 0) else 1
    shaped = Mesh(mesh.devices.reshape(line // pair, pair, experts), ALL)
    in_specs = (
        P(None, DP, "expert", None),
        P("expert", DP, None),
        P("expert", DP, None),
        P(ALL, None),
        P(ALL, None),
        P(ALL),
        P(ALL, None),
        P(ALL),
        P(ALL, None),
        P("expert", DP, None),
        P("expert", DP, None),
        P("expert", DP, None),
        P(None, DP, None, None),
        P(None, DP, "expert", None),
        P(None, DP, "expert"),
        P(None, DP, None),
        P(None, DP, "expert", None),
    )
    out_specs = (
        P(None, DP, "expert", None),
        P(None, DP, "expert", None),
        P("expert", DP, None),
        P("expert", DP, None),
        P(ALL, None),
        P(ALL, None),
        P(ALL),
        P(ALL, None),
        P(ALL),
        P(ALL, None),
        P("expert", DP, None),
        P("expert", DP, None),
        P("expert", DP, None),
    )
    return jax.shard_map(body, mesh=shaped, in_specs=in_specs, out_specs=out_specs, check_vma=False)
```

```python
from functools import partial
import math

import jax
import jax.numpy as jnp
from jax import lax
from jax.experimental import pallas as pl
from jax.experimental.pallas import tpu as pltpu
from jax.sharding import Mesh, PartitionSpec as P

HEADS = 16
HDIM = 128
EPSILON = 1e-06
HIGHEST = lax.Precision.HIGHEST
BF16 = jnp.bfloat16
F32 = jnp.float32


def product(left, right):
    return jnp.dot(left, right, preferred_element_type=F32)


def product_tn(left, right):
    return lax.dot_general(left, right, (((0,), (0,)), ((), ())), preferred_element_type=F32)


def product_nt(left, right):
    return lax.dot_general(left, right, (((1,), (1,)), ((), ())), preferred_element_type=F32)


def rms_scaled(values, gain):
    return values * lax.rsqrt(jnp.mean(values * values, axis=-1, keepdims=True) + EPSILON) * gain


def mixture_gates(picked, logits):
    labels = jnp.arange(logits.shape[1], dtype=jnp.int32)
    onehot = (picked[:, :, None] == labels[None, None, :]).astype(F32)
    chosen = jnp.sum(onehot * logits[:, None, :], axis=-1)
    weights = jax.nn.softmax(chosen, axis=-1)
    return jnp.sum(weights[:, :, None] * onehot, axis=1)


def tree_layout(segment_len, tree_len):
    places = jnp.arange(tree_len, dtype=jnp.int32)
    trunk_len = 4 * segment_len
    segment = jnp.where(
        places < trunk_len,
        0,
        jnp.where(
            places < 2 * trunk_len,
            1 + (places - trunk_len) // segment_len,
            5 + (places - 2 * trunk_len) // segment_len,
        ),
    )
    depth = jnp.where(
        places < trunk_len,
        places,
        jnp.where(
            places < 2 * trunk_len,
            trunk_len + (places - trunk_len) % segment_len,
            trunk_len + segment_len + (places - 2 * trunk_len) % segment_len,
        ),
    )
    return (places, segment, depth)


def ancestors(parent, segment):
    labels = jnp.arange(parent.shape[0], dtype=jnp.int32)
    first = jnp.where(labels > 0, parent, -1)
    lookup = jnp.maximum(first, 0)[:, None] == labels[None, :]
    second = jnp.where(first > 0, jnp.sum(jnp.where(lookup, parent[None, :], 0), axis=1), -1)
    member = segment[:, None] == labels[None, :]
    up_one = jnp.sum(jnp.where(member, first[None, :], 0), axis=1)
    up_two = jnp.sum(jnp.where(member, second[None, :], 0), axis=1)
    return (up_one, up_two)


def score_bias(parent, segment, places):
    up_one, up_two = ancestors(parent, segment)
    same = (segment[None, :] == segment[:, None]) & (places[None, :] <= places[:, None])
    seen = same | (segment[None, :] == up_one[:, None]) | (segment[None, :] == up_two[:, None])
    return jnp.where(seen, 0.0, -1e30).astype(F32)


def slot_table(picked, order, experts, capacity):
    labels = jnp.arange(experts, dtype=jnp.int32)
    chosen = jnp.sum((picked[:, :, None] == labels[None, None, :]).astype(F32), axis=1)
    earlier = (order[None, :] < order[:, None]).astype(F32)
    ranks = jnp.dot(earlier, chosen, precision=HIGHEST, preferred_element_type=F32)
    slots = jnp.arange(capacity, dtype=F32)
    return jnp.transpose(chosen)[:, None, :] * (
        jnp.transpose(ranks)[:, None, :] == slots[None, :, None]
    ).astype(F32)


def turn(values, cosine, sine):
    half = values.shape[-1] // 2
    first = values[:, :half]
    second = values[:, half:]
    return jnp.concatenate(
        [first * cosine - second * sine, second * cosine + first * sine], axis=-1
    )


def softmax_rows(queries, keys, bias, scale):
    scores = product_nt(queries, keys) * scale + bias
    highest = jnp.max(scores, axis=-1, keepdims=True)
    weights = jnp.exp(scores - highest)
    return weights / jnp.sum(weights, axis=-1, keepdims=True)


def attend_kernel(heads, scale, raw_ref, kv_ref, cos_ref, sin_ref, bias_ref, query_ref, out_ref):
    quarter, tok = raw_ref.shape[1], raw_ref.shape[3]
    rows = quarter * tok
    cosine, sine, bias = cos_ref[...], sin_ref[...], bias_ref[0, 0]
    for head in range(heads):
        cols = slice(head * HDIM, (head + 1) * HDIM)
        raw = raw_ref[0, :, 0, :, cols].reshape(rows, HDIM)
        keys = kv_ref[0, 0, 0, :, 0, :, cols].reshape(rows, HDIM)
        values = kv_ref[0, 1, 0, :, 0, :, cols].reshape(rows, HDIM)
        queries = turn(raw, cosine, sine).astype(BF16)
        probs = softmax_rows(queries, keys, bias, scale).astype(BF16)
        query_ref[0, :, 0, :, cols] = queries.reshape(quarter, tok, HDIM)
        out_ref[0, :, 0, :, cols] = product(probs, values).astype(BF16).reshape(quarter, tok, HDIM)


def attend_back_kernel(
    heads, scale, query_ref, kv_ref, grad_ref, cos_ref, sin_ref, bias_ref, dq_ref, dkv_ref
):
    quarter, tok = query_ref.shape[1], query_ref.shape[3]
    rows = quarter * tok
    cosine, sine, bias = cos_ref[...], sin_ref[...], bias_ref[0, 0]
    for head in range(heads):
        cols = slice(head * HDIM, (head + 1) * HDIM)
        queries = query_ref[0, :, 0, :, cols].reshape(rows, HDIM)
        keys = kv_ref[0, 0, 0, :, 0, :, cols].reshape(rows, HDIM)
        values = kv_ref[0, 1, 0, :, 0, :, cols].reshape(rows, HDIM)
        grad = grad_ref[0, :, 0, :, cols].reshape(rows, HDIM)
        probs = softmax_rows(queries, keys, bias, scale)
        prob_grad = product_nt(grad, values)
        centre = jnp.sum(prob_grad * probs, axis=-1, keepdims=True)
        score_grad = (probs * (prob_grad - centre) * scale).astype(BF16)
        query_grad = turn(product(score_grad, keys), cosine, -sine).astype(BF16)
        key_grad = turn(product_tn(score_grad, queries), cosine, -sine).astype(BF16)
        value_grad = product_tn(probs.astype(BF16), grad).astype(BF16)
        dq_ref[0, :, 0, :, cols] = query_grad.reshape(quarter, tok, HDIM)
        dkv_ref[0, 0, 0, :, 0, :, cols] = key_grad.reshape(quarter, tok, HDIM)
        dkv_ref[0, 1, 0, :, 0, :, cols] = value_grad.reshape(quarter, tok, HDIM)


def attention_specs(shape, slices):
    pair, quarter, micro, tok, feats = shape
    part = feats // slices
    rows = quarter * tok
    grid = (pair, micro, slices)
    flat = pl.BlockSpec((1, quarter, 1, tok, part), lambda i, m, s: (i, 0, m, 0, s))
    both = pl.BlockSpec(
        (1, 2, 1, quarter, 1, tok, part), lambda i, m, s: (s, 0, i, 0, m, 0, 0)
    )
    angle = pl.BlockSpec((rows, HDIM // 2), lambda i, m, s: (0, 0))
    bias = pl.BlockSpec((1, 1, rows, rows), lambda i, m, s: (i, m, 0, 0))
    return grid, part, flat, both, angle, bias


def attend(raw, kv, cosine, sine, bias, scale):
    slices = kv.shape[0]
    grid, part, flat, both, angle, bias_spec = attention_specs(raw.shape, slices)
    out = jax.ShapeDtypeStruct(raw.shape, BF16)
    return pl.pallas_call(
        partial(attend_kernel, part // HDIM, scale),
        grid=grid,
        in_specs=[flat, both, angle, angle, bias_spec],
        out_specs=[flat, flat],
        out_shape=[out, out],
        cost_estimate=pl.CostEstimate(
            flops=4 * raw.size * cosine.shape[0],
            bytes_accessed=12 * raw.size,
            transcendentals=raw.size * 2,
        ),
        name="attend",
    )(raw, kv, cosine, sine, bias)


def attend_back(queries, kv, grad, cosine, sine, bias, scale):
    slices = kv.shape[0]
    grid, part, flat, both, angle, bias_spec = attention_specs(queries.shape, slices)
    return pl.pallas_call(
        partial(attend_back_kernel, part // HDIM, scale),
        grid=grid,
        in_specs=[flat, both, flat, angle, angle, bias_spec],
        out_specs=[flat, both],
        out_shape=[
            jax.ShapeDtypeStruct(queries.shape, BF16),
            jax.ShapeDtypeStruct(kv.shape, BF16),
        ],
        cost_estimate=pl.CostEstimate(
            flops=10 * queries.size * cosine.shape[0],
            bytes_accessed=14 * queries.size,
            transcendentals=queries.size * 2,
        ),
        name="attend_back",
    )(queries, kv, grad, cosine, sine, bias)


MESH = pl.DeviceIdType.MESH
ANY = pl.BlockSpec(memory_space=pl.ANY)
VMEM = pl.BlockSpec(memory_space=pltpu.VMEM)
DMA = pltpu.SemaphoreType.DMA


def remote(src, dst, send, recv, target):
    return pltpu.make_async_remote_copy(
        src_ref=src, dst_ref=dst, send_sem=send, recv_sem=recv, device_id=target, device_id_type=MESH
    )


def greet(targets):
    barrier = pltpu.get_barrier_semaphore()
    for target in targets:
        pl.semaphore_signal(barrier, inc=1, device_id=target, device_id_type=MESH)
    pl.semaphore_wait(barrier, len(targets))


def params(number, limit=None):
    return pltpu.CompilerParams(
        collective_id=number, has_side_effects=True, vmem_limit_bytes=limit
    )


def add_into(target, sources, rows):
    step = 1
    while step * 2 <= rows and step * 2 * target.shape[-1] <= 65536 and rows % (step * 2) == 0:
        step *= 2

    def one(index, carry):
        where = pl.ds(pl.multiple_of(index * step, step), step)
        total = sources[0][where].astype(F32)
        for source in sources[1:]:
            total = total + source[where].astype(F32)
        target[where] = total.astype(target.dtype)
        return carry

    lax.fori_loop(0, rows // step, one, 0)


def cube_reduce_kernel(pairs, x_ref, o_ref, half, quarter, got_core, got_side, got_pair, send, recv):
    p = lax.axis_index("pair")
    e = lax.axis_index("expert")
    c, y = lax.rem(e, 2), lax.div(e, 2)
    core = {"expert": e + 1 - 2 * c}
    side = {"expert": e + 2 - 4 * y}
    other = {"pair": lax.rem(p + 1, pairs)}
    greet([core, side] + ([other] if pairs == 2 else []))
    rows = x_ref.shape[3]
    shifts = (1, 0) if pairs == 2 else (0,)
    order = [(dx, dy) for dy in (1, 0) for dx in shifts]
    first, second = [], {}
    for slot, (dx, dy) in enumerate(order):
        px, yy = lax.rem(p + dx, pairs), lax.rem(y + dy, 2)
        copy = remote(
            x_ref.at[px, yy, 1 - c], got_core.at[slot], send.at[slot], recv.at[slot], core
        )
        copy.start()
        first.append(copy)
    base = len(order)
    for slot, (dx, dy) in enumerate(order):
        px, yy = lax.rem(p + dx, pairs), lax.rem(y + dy, 2)
        first[slot].wait_recv()
        add_into(half.at[slot], [x_ref.at[px, yy, c], got_core.at[slot]], rows)
        if dy == 1:
            copy = remote(
                half.at[slot], got_side.at[dx], send.at[base + dx], recv.at[base + dx], side
            )
            copy.start()
            second[dx] = copy
    last = None
    for dx in shifts:
        second[dx].wait_recv()
        if dx == 1:
            add_into(quarter, [half.at[order.index((1, 0))], got_side.at[1]], rows)
            last = remote(quarter, got_pair, send.at[base + 2], recv.at[base + 2], other)
            last.start()
    if last is not None:
        last.wait_recv()
        add_into(o_ref, [half.at[order.index((0, 0))], got_side.at[0], got_pair], rows)
    else:
        add_into(o_ref, [half.at[order.index((0, 0))], got_side.at[0]], rows)
    for copy in first + list(second.values()) + ([last] if last is not None else []):
        copy.wait_send()


def cube_reduce(value, pairs, number):
    _, rows, cols = value.shape
    value = value.reshape(pairs, 2, 2, rows, cols)
    slots = 2 * pairs
    block = jax.ShapeDtypeStruct((rows, cols), value.dtype)
    return pl.pallas_call(
        partial(cube_reduce_kernel, pairs),
        in_specs=[VMEM],
        out_specs=VMEM,
        out_shape=block,
        scratch_shapes=[
            pltpu.VMEM((slots, rows, cols), value.dtype),
            pltpu.VMEM((rows, cols), value.dtype),
            pltpu.VMEM((slots, rows, cols), value.dtype),
            pltpu.VMEM((pairs, rows, cols), value.dtype),
            pltpu.VMEM((rows, cols), value.dtype),
            DMA((slots + 3,)),
            DMA((slots + 3,)),
        ],
        compiler_params=params(number, 48 * 2**20),
        cost_estimate=pl.CostEstimate(
            flops=value.size, bytes_accessed=24 * value.size, transcendentals=0
        ),
        name="cube_reduce",
    )(value)


def cube_gather_kernel(pairs, x_ref, o_ref, send, recv, local):
    p = lax.axis_index("pair") if pairs == 2 else 0
    e = lax.axis_index("expert")
    c, y = lax.rem(e, 2), lax.div(e, 2)
    core = {"expert": e + 1 - 2 * c}
    side = {"expert": e + 2 - 4 * y}
    other = {"pair": lax.rem(p + 1, pairs)}
    greet([core, side] + ([other] if pairs == 2 else []))
    q, w = lax.rem(p + 1, pairs), 1 - y
    own = o_ref.at[p, y, c]
    keep = pltpu.make_async_copy(x_ref, own, local)
    keep.start()
    copies = []

    def push(slot, source, place, target):
        copy = remote(source, place, send.at[slot], recv.at[slot], target)
        copy.start()
        copies.append(copy)
        return copy

    to_side = push(0, x_ref, own, side)
    to_other = push(1, x_ref, own, other) if pairs == 2 else None
    to_core = push(2, x_ref, own, core)
    waits = [to_core]
    if pairs == 2:
        to_other.wait_recv()
        block = o_ref.at[q, y, c]
        far = push(3, block, block, side)
        waits.append(push(4, block, block, core))
    to_side.wait_recv()
    block = o_ref.at[p, w, c]
    waits.append(push(5, block, block, core))
    if pairs == 2:
        far.wait_recv()
        block = o_ref.at[q, w, c]
        waits.append(push(6, block, block, core))
    for copy in waits:
        copy.wait_recv()
    for copy in copies:
        copy.wait_send()
    keep.wait()


def cube_gather(value, pairs, number):
    return pl.pallas_call(
        partial(cube_gather_kernel, pairs),
        in_specs=[VMEM],
        out_specs=VMEM,
        out_shape=jax.ShapeDtypeStruct((pairs, 2, 2) + value.shape, value.dtype),
        scratch_shapes=[DMA((7,)), DMA((7,)), DMA(())],
        compiler_params=params(number, 48 * 2**20),
        cost_estimate=pl.CostEstimate(
            flops=0, bytes_accessed=80 * value.size, transcendentals=0
        ),
        name="cube_gather",
    )(value)


def place_of(index, sizes):
    line, pairs, experts = sizes
    return {
        "line": index // (pairs * experts),
        "pair": (index // experts) % pairs,
        "expert": index % experts,
    }


def small_kernel(sizes, reduce, x_ref, o_ref, got, send, recv):
    line, pairs, experts = sizes
    count = line * pairs * experts
    me = (
        lax.axis_index("line") * (pairs * experts)
        + lax.axis_index("pair") * experts
        + lax.axis_index("expert")
    )
    barrier = pltpu.get_barrier_semaphore()

    def greet_one(offset, carry):
        target = place_of((me + offset) % count, sizes)
        pl.semaphore_signal(barrier, inc=1, device_id=target, device_id_type=MESH)
        return carry

    lax.fori_loop(1, count, greet_one, 0)
    pl.semaphore_wait(barrier, count - 1)

    def copy_to(offset):
        peer = (me + offset) % count
        source = x_ref.at[peer] if reduce else x_ref
        return remote(source, got.at[offset], send.at[offset], recv.at[offset], place_of(peer, sizes))

    def start(offset, carry):
        copy_to(offset).start()
        return carry

    lax.fori_loop(1, count, start, 0)
    got[0] = x_ref[me] if reduce else x_ref[...]

    def finish(offset, carry):
        copy_to(offset).wait()
        return carry

    lax.fori_loop(1, count, finish, 0)
    if reduce:
        o_ref[...] = jnp.sum(got[...], axis=0)
    else:

        def order(offset, carry):
            o_ref[(me - offset + count) % count] = got[offset]
            return carry

        lax.fori_loop(0, count, order, 0)


def small_exchange(value, sizes, reduce, number):
    count = sizes[0] * sizes[1] * sizes[2]
    block = value.shape[1:] if reduce else value.shape
    return pl.pallas_call(
        partial(small_kernel, sizes, reduce),
        in_specs=[VMEM],
        out_specs=VMEM,
        out_shape=jax.ShapeDtypeStruct(block if reduce else (count,) + block, value.dtype),
        scratch_shapes=[pltpu.VMEM((count,) + block, value.dtype), DMA((count,)), DMA((count,))],
        compiler_params=params(number),
        cost_estimate=pl.CostEstimate(flops=0, bytes_accessed=2**24, transcendentals=0),
        name="small_reduce" if reduce else "small_gather",
    )(value)


def pair_swap_kernel(a_ref, b_ref, a_out, b_out, send, recv, local):
    p = lax.axis_index("pair")
    other = {"pair": 1 - p}
    greet([other])
    copies = []
    for slot, (src, dst) in enumerate(((a_ref.at[1 - p], a_out.at[p]), (b_ref, b_out.at[p]))):
        copy = remote(src, dst, send.at[slot], recv.at[slot], other)
        copy.start()
        copies.append(copy)
    for slot, (src, dst) in enumerate(((a_ref.at[p], a_out.at[p]), (b_ref, b_out.at[p]))):
        copy = pltpu.make_async_copy(src, dst, local.at[slot])
        copy.start()
        copies.append(copy)
    for copy in copies:
        copy.wait()


def pair_swap(value, shared, number):
    return pl.pallas_call(
        pair_swap_kernel,
        in_specs=[VMEM, VMEM],
        out_specs=[VMEM, VMEM],
        out_shape=[
            jax.ShapeDtypeStruct(value.shape, value.dtype),
            jax.ShapeDtypeStruct((2,) + shared.shape, shared.dtype),
        ],
        scratch_shapes=[DMA((2,)), DMA((2,)), DMA((2,))],
        compiler_params=params(number),
        cost_estimate=pl.CostEstimate(
            flops=0, bytes_accessed=20 * value.size, transcendentals=0
        ),
        name="pair_swap",
    )(value, shared)


def start_kernel(
    sizes, walk, tok_ref, small_ref, kv_ref, tok_out, small_out, kv_out, send, recv, peer_send, peer_recv, local
):
    line, pairs, experts = sizes
    z = lax.axis_index("line")
    p = lax.axis_index("pair") if pairs == 2 else 0
    e = lax.axis_index("expert")
    c, y = lax.rem(e, 2), lax.div(e, 2)
    core = {"expert": e + 1 - 2 * c}
    side = {"expert": e + 2 - 4 * y}
    other = {"pair": lax.rem(p + 1, pairs)}
    count = line * pairs * experts
    trees = pairs * experts
    local_me = p * experts + e
    me = z * trees + local_me
    barrier = pltpu.get_barrier_semaphore()

    def greet_one(offset, carry):
        target = place_of((me + offset) % count, sizes)
        pl.semaphore_signal(barrier, inc=1, device_id=target, device_id_type=MESH)
        return carry

    lax.fori_loop(1, count, greet_one, 0)
    pl.semaphore_wait(barrier, count - 1)

    size = kv_ref.shape[1]
    home = kv_out.at[z if walk else 0, pl.ds(pl.multiple_of(local_me * size, size), size)]
    keeps = [
        pltpu.make_async_copy(kv_ref.at[local_me], home, local.at[0]),
        pltpu.make_async_copy(tok_ref, tok_out.at[p, y, c], local.at[1]),
        pltpu.make_async_copy(small_ref, small_out.at[me], local.at[2]),
    ]
    for copy in keeps:
        copy.start()
    KV = 7
    pieces = []
    for shift in range(1, trees):
        peer = lax.rem(local_me + shift, trees)
        copy = remote(
            kv_ref.at[peer],
            home,
            send.at[KV + shift],
            recv.at[KV + shift],
            {"pair": peer // experts, "expert": peer % experts},
        )
        copy.start()
        pieces.append(copy)

    q, w = lax.rem(p + 1, pairs), 1 - y
    own = tok_out.at[p, y, c]
    copies = []

    def push(slot, source, place, target):
        copy = remote(source, place, send.at[slot], recv.at[slot], target)
        copy.start()
        copies.append(copy)
        return copy

    to_side = push(0, tok_ref, own, side)
    to_other = push(1, tok_ref, own, other) if pairs == 2 else None
    waits = [push(2, tok_ref, own, core)]

    def small_to(offset):
        return remote(
            small_ref,
            small_out.at[me],
            peer_send.at[offset],
            peer_recv.at[offset],
            place_of((me + offset) % count, sizes),
        )

    def small_start(offset, carry):
        small_to(offset).start()
        return carry

    lax.fori_loop(1, count, small_start, 0)

    base = KV + trees
    keeps[0].wait()
    for copy in pieces:
        copy.wait_recv()

    def to_up(j, d):
        ref = kv_out.at[j]
        return remote(ref, ref, send.at[base + d], recv.at[base + d], {"line": z + 1})

    def to_down(j, d):
        ref = kv_out.at[j]
        return remote(ref, ref, send.at[base + line + d], recv.at[base + line + d], {"line": z - 1})

    if walk:

        @pl.when(z < line - 1)
        def _():
            to_up(z, 1).start()

        @pl.when(z > 0)
        def _():
            to_down(z, 1).start()

    if pairs == 2:
        to_other.wait_recv()
        block = tok_out.at[q, y, c]
        far = push(3, block, block, side)
        waits.append(push(4, block, block, core))
    to_side.wait_recv()
    block = tok_out.at[p, w, c]
    waits.append(push(5, block, block, core))
    if pairs == 2:
        far.wait_recv()
        block = tok_out.at[q, w, c]
        waits.append(push(6, block, block, core))

    if walk:
        for d in range(1, line):

            @pl.when(z - d >= 0)
            def _():
                to_up(z - d, d).wait_recv()

                @pl.when(z < line - 1)
                def _():
                    to_up(z - d, d + 1).start()

            @pl.when(z + d < line)
            def _():
                to_down(z + d, d).wait_recv()

                @pl.when(z > 0)
                def _():
                    to_down(z + d, d + 1).start()

        for d in range(1, line):

            @pl.when((z - d + 1 >= 0) & (z < line - 1))
            def _():
                to_up(z - d + 1, d).wait_send()

            @pl.when((z + d - 1 < line) & (z > 0))
            def _():
                to_down(z + d - 1, d).wait_send()

    for copy in waits:
        copy.wait_recv()
    for copy in copies + pieces:
        copy.wait_send()
    for copy in keeps[1:]:
        copy.wait()

    def small_finish(offset, carry):
        small_to(offset).wait()
        return carry

    lax.fori_loop(1, count, small_finish, 0)


def start_exchange(tokens, small, kv, sizes, number):
    line, pairs, experts = sizes
    trees, rows, cols = kv.shape
    walk = line <= 4
    count = line * trees
    uses = 7 + trees + 2 * line + 2
    return pl.pallas_call(
        partial(start_kernel, sizes, walk),
        in_specs=[VMEM, VMEM, VMEM],
        out_specs=[VMEM, VMEM, VMEM],
        out_shape=[
            jax.ShapeDtypeStruct((pairs, 2, 2) + tokens.shape, tokens.dtype),
            jax.ShapeDtypeStruct((count,) + small.shape, small.dtype),
            jax.ShapeDtypeStruct((line if walk else 1, trees * rows, cols), kv.dtype),
        ],
        scratch_shapes=[DMA((uses,)), DMA((uses,)), DMA((count,)), DMA((count,)), DMA((3,))],
        compiler_params=params(number, 32 * 2**20),
        cost_estimate=pl.CostEstimate(
            flops=0, bytes_accessed=100 * kv.size, transcendentals=0
        ),
        name="start_exchange",
    )(tokens, small, kv)


def ff_kernel(
    a_in, b_in, gate_hbm, up_hbm, down_hbm,
    a_out, b_out, a_save, b_save, inner_save, dgate_save, dup_save,
    a_buf, b_buf, side, hop, extra, w_gate, w_up, w_down, mid, acc,
    send, recv, load, store, local,
):
    z, p, e = lax.axis_index("line"), lax.axis_index("pair"), lax.axis_index("expert")
    line, _, rows, width = a_buf.shape
    experts, size = a_in.shape[0], a_in.shape[1]
    q = 1 - p
    twin = z + 1 - 2 * (z % 2)
    up, down, other, across = {"line": z + 1}, {"line": z - 1}, {"pair": q}, {"line": twin}
    ins, bufs, outs, saves = (a_in, b_in), (a_buf, b_buf), (a_out, b_out), (a_save, b_save)
    high = z // 2
    near = z + high * (line - 1 - 2 * z)

    def order(t):
        j = t + near * (1 - t // 2) * (1 - 2 * t)
        return j + high * (line - 1 - 2 * j)

    weights = [
        pltpu.make_async_copy(src, dst, load.at[i])
        for i, (src, dst) in enumerate(((gate_hbm, w_gate), (up_hbm, w_up), (down_hbm, w_down)))
    ]
    for copy in weights:
        copy.start()

    barrier = pltpu.get_barrier_semaphore()
    for shift in range(1, experts):
        pl.semaphore_signal(
            barrier, inc=1, device_id={"expert": (e + shift) % experts}, device_id_type=MESH
        )
    pl.semaphore_signal(barrier, inc=1, device_id=other, device_id_type=MESH)

    @pl.when(z > 0)
    def _():
        pl.semaphore_signal(barrier, inc=1, device_id=down, device_id_type=MESH)

    @pl.when(z < line - 1)
    def _():
        pl.semaphore_signal(barrier, inc=1, device_id=up, device_id_type=MESH)

    below, above = (z + line - 1) // line, (2 * line - 2 - z) // line
    pl.semaphore_wait(barrier, experts + below + above)

    UP, DOWN, SIDE, SUMUP, SUMDOWN, SUMSIDE = (i * line for i in range(6))
    TWIN, SUMTWIN, SWAP = 6 * line, 6 * line + 1, 6 * line + 2
    BACK = SWAP + experts

    def push(src, dst, kind, use, target):
        return remote(src, dst, send.at[kind, use], recv.at[kind, use], target)

    def to_up(kind, j):
        return push(bufs[kind].at[j, p], bufs[kind].at[j, p], kind, UP + j, up)

    def to_down(kind, j):
        return push(bufs[kind].at[j, p], bufs[kind].at[j, p], kind, DOWN + j, down)

    def to_other(kind, j):
        return push(bufs[kind].at[j, p], bufs[kind].at[j, p], kind, SIDE + j, other)

    def to_twin():
        return push(bufs[1].at[z, q], bufs[1].at[z, q], 1, TWIN, across)

    def sum_up(kind, j):
        return push(bufs[kind].at[j, p], hop.at[kind, j], kind, SUMUP + j, up)

    def sum_down(kind, j, slot):
        return push(bufs[kind].at[j, p], hop.at[kind, slot], kind, SUMDOWN + j, down)

    def sum_other(kind, j):
        return push(bufs[kind].at[j, q], side.at[kind, j], kind, SUMSIDE + j, other)

    def sum_twin():
        return push(bufs[1].at[twin, q], extra, 1, SUMTWIN, across)

    def piece(index):
        return pl.ds(pl.multiple_of(index * size, size), size)

    def save(kind, j, column):
        return pltpu.make_async_copy(
            bufs[kind].at[j, column], saves[kind].at[j, column], store.at[kind, j, column]
        )

    swaps = []
    for kind in range(2):
        home = bufs[kind].at[z, p, piece(e)]
        keep = pltpu.make_async_copy(ins[kind].at[e], home, local.at[kind])
        keep.start()
        group = []
        for shift in range(1, experts):
            peer = (e + shift) % experts
            copy = push(ins[kind].at[peer], home, kind, SWAP + shift, {"expert": peer})
            copy.start()
            group.append(copy)
        swaps.append((keep, group))

    def spread(t, first=False):
        j = order(t)
        for kind in range(2):
            if first:
                swaps[kind][0].wait()
                for copy in swaps[kind][1]:
                    copy.wait_recv()
            else:

                @pl.when(j < z)
                def _():
                    to_up(kind, j).wait_recv()

                @pl.when(j > z)
                def _():
                    to_down(kind, j).wait_recv()

            @pl.when((j <= z) & (z < line - 1))
            def _():
                to_up(kind, j).start()

            @pl.when((j >= z) & (z > 0))
            def _():
                to_down(kind, j).start()

            if kind == 0:
                to_other(kind, j).start()
            else:

                @pl.when(j != twin)
                def _():
                    to_other(kind, j).start()

            save(kind, j, p).start()

    chunk = 512
    steps = width // chunk

    def first_half(j, column):
        for index in range(3):
            acc[index] = jnp.zeros(acc.shape[1:], F32)

        def one(k, carry):
            where = pl.ds(pl.multiple_of(k * chunk, chunk), chunk)
            left = a_buf[j, column, :, where]
            acc[0] += product_nt(left, w_gate[:, where])
            acc[1] += product_nt(left, w_up[:, where])
            acc[2] += product_nt(b_buf[j, column, :, where], w_down[:, where])
            return carry

        lax.fori_loop(0, steps, one, 0)
        part = 32

        def two(i, carry):
            where = pl.ds(pl.multiple_of(i * part, part), part)
            gate, lift, grad = acc[0, where], acc[1, where], acc[2, where]
            sigma = jax.nn.sigmoid(gate)
            mid[j, column, 0, where] = (gate * sigma * lift).astype(BF16)
            mid[j, column, 1, where] = (
                grad * lift * sigma * (1.0 + gate * (1.0 - sigma))
            ).astype(BF16)
            mid[j, column, 2, where] = (grad * gate * sigma).astype(BF16)
            return carry

        lax.fori_loop(0, rows // part, two, 0)

    def second_half(j, column):
        def one(k, carry):
            where = pl.ds(pl.multiple_of(k * chunk, chunk), chunk)
            a_buf[j, column, :, where] = product(mid[j, column, 0], w_down[:, where]).astype(BF16)
            b_buf[j, column, :, where] = (
                product(mid[j, column, 1], w_gate[:, where])
                + product(mid[j, column, 2], w_up[:, where])
            ).astype(BF16)
            return carry

        lax.fori_loop(0, steps, one, 0)

    def arrive(j):
        for kind in range(2):
            if kind == 0:
                to_other(kind, j).wait_recv()
            else:

                @pl.when(j != twin)
                def _():
                    to_other(kind, j).wait_recv()

                @pl.when(j == twin)
                def _():
                    to_twin().wait_recv()

            save(kind, j, q).start()

        @pl.when(j == z)
        def _():
            to_twin().start()

    def step(s, carry):
        @pl.when(s == 0)
        def _():
            spread(0, True)
            for copy in weights:
                copy.wait()

        @pl.when(s == 1)
        def _():
            spread(1)
            spread(2)

        @pl.when(s == 3)
        def _():
            spread(3)

        def half(c, inner_carry):
            t = s - c
            column = p + c * (q - p)

            @pl.when((t >= 0) & (t < line))
            def _():
                j = order(t)

                @pl.when(c == 1)
                def _():
                    arrive(j)

                first_half(j, column)

                @pl.when(c == 1)
                def _():
                    @pl.when(j == z)
                    def _():
                        to_twin().wait_send()

                    for kind in range(2):
                        save(kind, j, q).wait()
                    second_half(j, column)

            return inner_carry

        return lax.fori_loop(0, 2, half, carry)

    lax.fori_loop(0, line + 1, step, 0)

    sum_twin().start()

    def emit(t, carry):
        j = order(line - 1 - t)
        sum_other(0, j).start()

        @pl.when((j != twin) & (j != z))
        def _():
            sum_other(1, j).start()

        return carry

    lax.fori_loop(0, line, emit, 0)

    for copy in (
        pltpu.make_async_copy(mid.at[:, :, 0], inner_save, local.at[2]),
        pltpu.make_async_copy(mid.at[:, :, 1], dgate_save, local.at[3]),
        pltpu.make_async_copy(mid.at[:, :, 2], dup_save, local.at[4]),
    ):
        copy.start()
    sum_twin().wait_recv()
    add_into(b_buf.at[z, q], [b_buf.at[z, q], extra], rows)
    sum_other(1, z).start()

    def fold(s, carry):
        t = line - 1 - s
        j = order(t)
        for kind in range(2):
            save(kind, j, p).wait()

            @pl.when((j <= z) & (z < line - 1))
            def _():
                to_up(kind, j).wait_send()

            @pl.when((j >= z) & (z > 0))
            def _():
                to_down(kind, j).wait_send()

            if kind == 0:
                to_other(kind, j).wait_send()
            else:

                @pl.when(j != twin)
                def _():
                    to_other(kind, j).wait_send()

        second_half(j, p)
        for kind in range(2):
            mine = bufs[kind].at[j, p]
            if kind == 0:
                sum_other(kind, j).wait_recv()
                add_into(mine, [mine, side.at[kind, j]], rows)
            else:

                @pl.when(j != twin)
                def _():
                    sum_other(kind, j).wait_recv()
                    add_into(mine, [mine, side.at[kind, j]], rows)

            @pl.when((j >= z) & (z > 0))
            def _():
                sum_up(kind, j).wait_recv()
                add_into(mine, [mine, hop.at[kind, j]], rows)

            @pl.when((j < z) & (z < line - 1))
            def _():
                sum_down(kind, j, j).wait_recv()
                add_into(mine, [mine, hop.at[kind, j]], rows)

            @pl.when((j == z) & (z < line - 1))
            def _():
                sum_down(kind, j, line).wait_recv()
                add_into(mine, [mine, hop.at[kind, line]], rows)

            @pl.when(j > z)
            def _():
                sum_up(kind, j).start()

            @pl.when((j < z) & (j != z - 1))
            def _():
                sum_down(kind, j, j).start()

            @pl.when((j < z) & (j == z - 1))
            def _():
                sum_down(kind, j, line).start()

        return carry

    lax.fori_loop(0, line, fold, 0)

    back = []
    for kind in range(2):
        keep = pltpu.make_async_copy(
            bufs[kind].at[z, p, piece(e)], outs[kind].at[e], local.at[kind]
        )
        keep.start()
        back.append(keep)
        for shift in range(1, experts):
            peer = (e + shift) % experts
            copy = push(
                bufs[kind].at[z, p, piece(peer)], outs[kind].at[e], kind, BACK + shift, {"expert": peer}
            )
            copy.start()
            back.append(copy)
    for copy in back:
        copy.wait()

    def drain(j, carry):
        for kind in range(2):
            if kind == 0:
                sum_other(kind, j).wait_send()
            else:

                @pl.when(j != twin)
                def _():
                    sum_other(kind, j).wait_send()

            @pl.when(j > z)
            def _():
                sum_up(kind, j).wait_send()

            @pl.when(j < z)
            def _():
                sum_down(kind, j, j).wait_send()

        return carry

    lax.fori_loop(0, line, drain, 0)
    sum_twin().wait_send()
    for copy in (
        pltpu.make_async_copy(mid.at[:, :, 0], inner_save, local.at[2]),
        pltpu.make_async_copy(mid.at[:, :, 1], dgate_save, local.at[3]),
        pltpu.make_async_copy(mid.at[:, :, 2], dup_save, local.at[4]),
    ):
        copy.wait()
    for keep, group in swaps:
        for copy in group:
            copy.wait_send()


def feed_forward(first, second, w_gate, w_up, w_down, line, pairs, number):
    experts, size, width = first.shape
    hidden = w_gate.shape[0]
    rows = experts * size
    blocks = (line, pairs, rows)
    back = jax.ShapeDtypeStruct(first.shape, BF16)
    wide = jax.ShapeDtypeStruct(blocks + (width,), BF16)
    thin = jax.ShapeDtypeStruct(blocks + (hidden,), BF16)
    uses = 6 * line + 2 + 2 * experts
    total = line * pairs * rows
    return pl.pallas_call(
        ff_kernel,
        in_specs=[ANY] * 5,
        out_specs=[ANY] * 7,
        out_shape=[back, back, wide, wide, thin, thin, thin],
        scratch_shapes=[
            pltpu.VMEM(blocks + (width,), BF16),
            pltpu.VMEM(blocks + (width,), BF16),
            pltpu.VMEM((2, line, rows, width), BF16),
            pltpu.VMEM((2, line + 1, rows, width), BF16),
            pltpu.VMEM((rows, width), BF16),
            pltpu.VMEM((hidden, width), BF16),
            pltpu.VMEM((hidden, width), BF16),
            pltpu.VMEM((hidden, width), BF16),
            pltpu.VMEM((line, pairs, 3, rows, hidden), BF16),
            pltpu.VMEM((3, rows, hidden), F32),
            DMA((2, uses)),
            DMA((2, uses)),
            DMA((3,)),
            DMA((2, line, pairs)),
            DMA((5,)),
        ],
        compiler_params=params(number, 63 * 2**20),
        cost_estimate=pl.CostEstimate(
            flops=12 * total * hidden * width,
            bytes_accessed=12 * total * width,
            transcendentals=total * hidden,
        ),
        name="feed_forward",
    )(first, second, w_gate, w_up, w_down)


def gather(value, axes, axis=0):
    return lax.all_gather(value, axes, axis=axis, tiled=True)


def scatter(value, axes, axis=0):
    return lax.psum_scatter(value, axes, scatter_dimension=axis, tiled=True)


def swap(value, axes, split=0, concat=0):
    return lax.all_to_all(value, axes, split_axis=split, concat_axis=concat, tiled=True)


DP = ("line", "pair")
ALL = ("line", "pair", "expert")
TREES = ("pair", "expert")


def body(
    tokens,
    w_query,
    w_out,
    w_key,
    w_value,
    gain_attn,
    router_attn,
    gain_mlp,
    router_mlp,
    w_gate,
    w_up,
    w_down,
    attn_route,
    mlp_route,
    fill_order,
    parents,
    cotangent,
):
    experts = lax.axis_size("expert")
    pair = lax.axis_size("pair")
    line = lax.axis_size("line")
    position = lax.axis_index("expert")
    micro, _, tok, width = tokens.shape
    tree = experts * tok
    rows = pair * experts * micro * tok
    heads_total = w_query.shape[2]
    part = heads_total // (line * pair)
    feats = heads_total // pair
    piece = feats // experts
    own_in = w_query.shape[1]
    own_kv = w_key.shape[0]
    capacity = tok * mlp_route.shape[3] // experts
    scale = 1.0 / math.sqrt(HDIM)

    places, segment, depth = tree_layout(tree // 16, tree)
    half = HDIM // 2
    rates = 10000.0 ** (-jnp.arange(half, dtype=F32) / half)
    angle = depth.astype(F32)[:, None] * rates[None, :]
    cosine, sine = jnp.cos(angle), jnp.sin(angle)

    sizes = (line, pair, experts)
    walk = line <= 4 and pair == 2
    query_mine = w_query[0].reshape(own_in, line, pair, part)
    query_mine = jnp.transpose(query_mine, (2, 0, 1, 3)).reshape(pair, own_in, feats)
    integers = jnp.concatenate([attn_route[:, 0].reshape(micro, -1), parents[:, 0]], axis=1)
    if pair == 2:
        flat = integers.reshape(-1)
        flat = jnp.pad(flat, (0, -flat.shape[0] % 1024)).reshape(-1, 128)
        query_mine, flat = pair_swap(query_mine, flat, 1)
        integers = flat.reshape(pair, -1)[:, : integers.size].reshape((pair,) + integers.shape)
    else:
        integers = integers[None]
    query_weight = gather(query_mine.reshape(pair * own_in, feats), "line")

    small = jnp.concatenate(
        [gain_attn[None], gain_mlp[None], router_attn.T, router_mlp.T], axis=0
    )
    kv_mine = jnp.stack([w_key, w_value], axis=1).reshape(
        own_kv, 2, experts, line // experts, pair, part
    )
    kv_mine = jnp.transpose(kv_mine, (4, 2, 0, 1, 3, 5)).reshape(
        pair * experts, own_kv, 2 * piece
    )
    own_tokens = tokens.reshape(micro * tok, width)
    tree_tokens, small, kv_weight = start_exchange(own_tokens, small, kv_mine, sizes, 2)
    kv_weight = kv_weight.reshape(-1, 2 * piece)
    if kv_weight.shape[0] < width:
        kv_weight = gather(kv_weight, "line")
    out_mine, small = lax.optimization_barrier((w_out[0], small))
    out_weight = gather(out_mine, "line")

    small = jnp.transpose(small, (1, 0, 2)).reshape(-1, width)
    first_gain = small[0].astype(F32)
    second_gain = small[1].astype(F32)
    first_router = small[2 : 2 + experts]
    second_router = small[2 + experts : 2 + 2 * experts]

    residual = own_tokens.astype(F32)
    _, first_pull = jax.vjp(rms_scaled, residual, first_gain)
    tree_input = rms_scaled(tree_tokens.reshape(rows, width).astype(F32), first_gain).astype(BF16)

    routes = integers[..., : tree * 2].reshape(pair, micro, experts, tok, 2)
    routes = jnp.transpose(routes, (0, 2, 1, 3, 4)).reshape(rows, 2)
    family = integers[..., tree * 2 :]
    bias = jax.vmap(jax.vmap(lambda parent: score_bias(parent, segment, places)))(family)

    kv_raw = product(tree_input, kv_weight)
    spread_cos = jnp.broadcast_to(
        cosine.reshape(1, experts, 1, tok, 1, half), (pair, experts, micro, tok, 1, half)
    ).reshape(rows, 1, half)
    spread_sin = jnp.broadcast_to(
        sine.reshape(1, experts, 1, tok, 1, half), (pair, experts, micro, tok, 1, half)
    ).reshape(rows, 1, half)
    key_raw = kv_raw[:, :piece].reshape(rows, piece // HDIM, HDIM)
    key_one, key_two = key_raw[..., :half], key_raw[..., half:]
    keys = jnp.concatenate(
        [
            key_one * spread_cos - key_two * spread_sin,
            key_two * spread_cos + key_one * spread_sin,
        ],
        axis=-1,
    ).reshape(rows, piece)
    kv = jnp.concatenate([keys.astype(BF16), kv_raw[:, piece:].astype(BF16)], axis=0)
    kv = cube_gather(kv, 1, 3)
    shape = (pair, experts, micro, tok, feats)
    kv = kv.reshape(experts, 2, pair, experts, micro, tok, piece)

    first_gates, first_gate_pull = jax.vjp(
        partial(mixture_gates, routes), product_nt(tree_input, first_router)
    )
    column = (jnp.arange(experts, dtype=jnp.int32) == position).astype(F32)
    own_gate = jnp.sum(first_gates * column[None, :], axis=1)

    raw = product(tree_input, query_weight)
    queries, heads_out = attend(raw.reshape(shape), kv, cosine, sine, bias, scale)
    heads_flat = heads_out.reshape(rows, feats)
    projected = product(heads_flat, out_weight)
    gated = (own_gate[:, None] * projected).astype(BF16)
    attention = cube_reduce(gated.reshape(pair * experts, micro * tok, width), pair, 4).astype(F32)

    middle = residual + attention
    second_normed, second_pull = jax.vjp(rms_scaled, middle, second_gain)
    second_normed = second_normed.astype(BF16)
    picked = mlp_route[:, 0].reshape(micro * tok, 2)
    second_gates, second_gate_pull = jax.vjp(
        partial(mixture_gates, picked), product_nt(second_normed, second_router)
    )
    table = jax.vmap(partial(slot_table, experts=experts, capacity=capacity))(
        mlp_route[:, 0], fill_order[:, 0]
    )
    table_low = table.astype(BF16)
    grouped = second_normed.reshape(micro, tok, width)
    outgoing = jnp.einsum("mect,mtd->emcd", table_low, grouped, preferred_element_type=F32)
    top_grad = cotangent.reshape(micro, tok, width)
    slot_values = jnp.einsum("mect,mtd->emcd", table_low, top_grad, preferred_element_type=F32)
    slot_gates = jnp.einsum(
        "mect,mte->emc", table, second_gates.reshape(micro, tok, experts), precision=HIGHEST
    )
    slot_grad = (slot_gates[..., None] * slot_values).astype(BF16)
    slots = experts * micro * capacity
    outgoing = outgoing.astype(BF16).reshape(experts, micro * capacity, width)
    slot_grad = slot_grad.reshape(experts, micro * capacity, width)
    gate_weight, up_weight, down_weight = w_gate[0], w_up[0], w_down[0]
    if walk:
        returned, came_back, arrived, result_grad, inner, gate_grad, up_grad = feed_forward(
            outgoing, slot_grad, gate_weight, up_weight, down_weight, line, pair, 5
        )
        arrived, result_grad, inner, gate_grad, up_grad = (
            value.reshape(-1, value.shape[-1])
            for value in (arrived, result_grad, inner, gate_grad, up_grad)
        )
    else:
        arrived = gather(swap(outgoing, "expert").reshape(slots, width), DP)
        result_grad = gather(swap(slot_grad, "expert").reshape(slots, width), DP)
        gate_pre = product_nt(arrived, gate_weight)
        up_pre = product_nt(arrived, up_weight)
        sigma = jax.nn.sigmoid(gate_pre)
        inner = (gate_pre * sigma * up_pre).astype(BF16)
        returned = product(inner, down_weight).astype(BF16)
        inner_grad = product_nt(result_grad, down_weight)
        gate_grad = (inner_grad * up_pre * sigma * (1.0 + gate_pre * (1.0 - sigma))).astype(BF16)
        up_grad = (inner_grad * gate_pre * sigma).astype(BF16)
        came_back = (product(gate_grad, gate_weight) + product(up_grad, up_weight)).astype(BF16)
        back = (experts, micro * capacity, width)
        returned = swap(scatter(returned, DP).reshape(back), "expert")
        came_back = swap(scatter(came_back, DP).reshape(back), "expert")
    returned = returned.reshape(experts, micro, capacity, width)
    came_back = came_back.reshape(experts, micro, capacity, width)
    grad_gate = product_tn(gate_grad, arrived)[None]
    grad_upward = product_tn(up_grad, arrived)[None]
    grad_downward = product_tn(inner, result_grad)[None]

    spread = jnp.einsum("mect,emcd->emtd", table_low, returned, preferred_element_type=F32)
    spread = spread.reshape(experts, micro * tok, width)
    mixed = jnp.sum(jnp.transpose(second_gates)[:, :, None] * spread, axis=0)
    layer_out = (middle + mixed).astype(BF16)
    dz = top_grad.reshape(micro * tok, width).astype(F32)
    second_gate_grad = jnp.transpose(jnp.sum(spread * dz[None], axis=-1))
    (second_logit_grad,) = second_gate_pull(second_gate_grad)
    hn_grad = jnp.einsum("mect,emcd->mtd", table_low, came_back, preferred_element_type=F32)
    hn_grad = hn_grad.reshape(micro * tok, width)
    second_router_wide = second_router.astype(F32)
    for expert in range(experts):
        hn_grad = hn_grad + second_logit_grad[:, expert : expert + 1] * second_router_wide[expert]
    grad_router_second = jnp.dot(
        jnp.transpose(second_logit_grad),
        second_normed.astype(F32),
        precision=HIGHEST,
        preferred_element_type=F32,
    )
    middle_grad, grad_gain_second = second_pull(hn_grad)
    middle_grad = middle_grad + dz

    mix_grad = cube_gather(middle_grad.astype(BF16), pair, 7).reshape(rows, width).astype(F32)
    own_gate_grad = jnp.sum(mix_grad * projected, axis=-1)
    projected_grad = (own_gate[:, None] * mix_grad).astype(BF16)
    grad_output = product_tn(heads_flat, projected_grad).astype(BF16)
    grad_output, projected_grad = lax.optimization_barrier((grad_output, projected_grad))
    grad_output = scatter(grad_output, "line")
    heads_grad = product_nt(projected_grad, out_weight).astype(BF16).reshape(shape)
    query_pre, kv_pre = attend_back(queries, kv, heads_grad, cosine, sine, bias, scale)
    query_pre = query_pre.reshape(rows, feats)
    grad_query = product_tn(tree_input, query_pre).astype(BF16)
    grad_query, kv_pre = lax.optimization_barrier((grad_query, kv_pre))
    kv_sum = cube_reduce(kv_pre.reshape(experts, 2 * rows, piece), 1, 8)
    (first_logit_grad,) = first_gate_pull(own_gate_grad[:, None] * column[None, :])
    key_pre, value_pre = kv_sum[:rows], kv_sum[rows:]
    grad_kv = jnp.stack(
        [product_tn(tree_input, key_pre), product_tn(tree_input, value_pre)], axis=1
    )
    grad_kv, key_pre, value_pre = lax.optimization_barrier(
        (grad_kv.astype(BF16), key_pre, value_pre)
    )
    input_term = (
        product_nt(query_pre, query_weight)
        + product_nt(key_pre, kv_weight[:, :piece])
        + product_nt(value_pre, kv_weight[:, piece:])
    )
    first_router_wide = first_router.astype(F32)
    for expert in range(experts):
        input_term = input_term + first_logit_grad[:, expert : expert + 1] * first_router_wide[expert]
    input_term = input_term.astype(BF16).reshape(pair * experts, micro * tok, width)
    grad_query, grad_output, input_term = lax.optimization_barrier(
        (grad_query, grad_output, input_term)
    )
    grad_query = scatter(grad_query, "line")
    normed_grad = cube_reduce(input_term, pair, 9).astype(F32)
    grad_kv, grad_query = lax.optimization_barrier((grad_kv, grad_query))
    grad_kv = scatter(grad_kv, "line")
    grad_query = swap(grad_query.reshape(own_in * pair, line, part)[None], "pair", 1, 0)
    grad_query = jnp.transpose(grad_query, (1, 2, 0, 3)).reshape(1, own_in, heads_total)
    grad_kv = swap(grad_kv.reshape(pair * experts, own_kv, 2, piece), TREES)
    grad_kv = grad_kv.reshape(pair, experts, own_kv, 2, line // experts, part)
    grad_kv = jnp.transpose(grad_kv, (2, 3, 1, 4, 0, 5)).reshape(own_kv, 2, heads_total)
    grad_kv = grad_kv.astype(F32)
    grad_router_first = jnp.dot(
        jnp.transpose(first_logit_grad),
        tree_input.astype(F32),
        precision=HIGHEST,
        preferred_element_type=F32,
    )
    token_grad, grad_gain_first = first_pull(normed_grad)
    tokens_grad = token_grad + middle_grad

    sums = jnp.concatenate(
        [grad_gain_first[None], grad_gain_second[None], grad_router_first, grad_router_second],
        axis=0,
    )
    sums = jnp.transpose(sums.reshape(sums.shape[0], -1, own_kv), (1, 0, 2))
    sums = small_exchange(sums, sizes, True, 10)
    return (
        layer_out.reshape(micro, 1, tok, width),
        tokens_grad.reshape(micro, 1, tok, width),
        grad_query.astype(F32),
        grad_output[None].astype(F32),
        grad_kv[:, 0],
        grad_kv[:, 1],
        sums[0],
        jnp.transpose(sums[2 : 2 + experts]),
        sums[1],
        jnp.transpose(sums[2 + experts :]),
        grad_gate,
        grad_upward,
        grad_downward,
    )


def solution(mesh):
    line, experts = mesh.devices.shape
    pair = 2 if line % 2 == 0 and (HEADS % line == 0) else 1
    shaped = Mesh(mesh.devices.reshape(line // pair, pair, experts), ALL)
    in_specs = (
        P(None, DP, "expert", None),
        P("expert", DP, None),
        P("expert", DP, None),
        P(ALL, None),
        P(ALL, None),
        P(ALL),
        P(ALL, None),
        P(ALL),
        P(ALL, None),
        P("expert", DP, None),
        P("expert", DP, None),
        P("expert", DP, None),
        P(None, DP, None, None),
        P(None, DP, "expert", None),
        P(None, DP, "expert"),
        P(None, DP, None),
        P(None, DP, "expert", None),
    )
    out_specs = (
        P(None, DP, "expert", None),
        P(None, DP, "expert", None),
        P("expert", DP, None),
        P("expert", DP, None),
        P(ALL, None),
        P(ALL, None),
        P(ALL),
        P(ALL, None),
        P(ALL),
        P(ALL, None),
        P("expert", DP, None),
        P("expert", DP, None),
        P("expert", DP, None),
    )
    return jax.shard_map(body, mesh=shaped, in_specs=in_specs, out_specs=out_specs, check_vma=False)
```

```python
from functools import partial
import math

import jax
import jax.numpy as jnp
from jax import lax
from jax.experimental import pallas as pl
from jax.experimental.pallas import tpu as pltpu
from jax.sharding import Mesh, PartitionSpec as P

HEADS = 16
HDIM = 128
EPSILON = 1e-06
HIGHEST = lax.Precision.HIGHEST
BF16 = jnp.bfloat16
F32 = jnp.float32


def product(left, right):
    return jnp.dot(left, right, preferred_element_type=F32)


def product_tn(left, right):
    return lax.dot_general(left, right, (((0,), (0,)), ((), ())), preferred_element_type=F32)


def product_nt(left, right):
    return lax.dot_general(left, right, (((1,), (1,)), ((), ())), preferred_element_type=F32)


def rms_scaled(values, gain):
    return values * lax.rsqrt(jnp.mean(values * values, axis=-1, keepdims=True) + EPSILON) * gain


def mixture_gates(picked, logits):
    labels = jnp.arange(logits.shape[1], dtype=jnp.int32)
    onehot = (picked[:, :, None] == labels[None, None, :]).astype(F32)
    chosen = jnp.sum(onehot * logits[:, None, :], axis=-1)
    weights = jax.nn.softmax(chosen, axis=-1)
    return jnp.sum(weights[:, :, None] * onehot, axis=1)


def tree_layout(segment_len, tree_len):
    places = jnp.arange(tree_len, dtype=jnp.int32)
    trunk_len = 4 * segment_len
    segment = jnp.where(
        places < trunk_len,
        0,
        jnp.where(
            places < 2 * trunk_len,
            1 + (places - trunk_len) // segment_len,
            5 + (places - 2 * trunk_len) // segment_len,
        ),
    )
    depth = jnp.where(
        places < trunk_len,
        places,
        jnp.where(
            places < 2 * trunk_len,
            trunk_len + (places - trunk_len) % segment_len,
            trunk_len + segment_len + (places - 2 * trunk_len) % segment_len,
        ),
    )
    return (places, segment, depth)


def ancestors(parent, segment):
    labels = jnp.arange(parent.shape[0], dtype=jnp.int32)
    first = jnp.where(labels > 0, parent, -1)
    lookup = jnp.maximum(first, 0)[:, None] == labels[None, :]
    second = jnp.where(first > 0, jnp.sum(jnp.where(lookup, parent[None, :], 0), axis=1), -1)
    member = segment[:, None] == labels[None, :]
    up_one = jnp.sum(jnp.where(member, first[None, :], 0), axis=1)
    up_two = jnp.sum(jnp.where(member, second[None, :], 0), axis=1)
    return (up_one, up_two)


def score_bias(parent, segment, places):
    up_one, up_two = ancestors(parent, segment)
    same = (segment[None, :] == segment[:, None]) & (places[None, :] <= places[:, None])
    seen = same | (segment[None, :] == up_one[:, None]) | (segment[None, :] == up_two[:, None])
    return jnp.where(seen, 0.0, -1e30).astype(F32)


def slot_table(picked, order, experts, capacity):
    labels = jnp.arange(experts, dtype=jnp.int32)
    chosen = jnp.sum((picked[:, :, None] == labels[None, None, :]).astype(F32), axis=1)
    earlier = (order[None, :] < order[:, None]).astype(F32)
    ranks = jnp.dot(earlier, chosen, precision=HIGHEST, preferred_element_type=F32)
    slots = jnp.arange(capacity, dtype=F32)
    return jnp.transpose(chosen)[:, None, :] * (
        jnp.transpose(ranks)[:, None, :] == slots[None, :, None]
    ).astype(F32)


def turn(values, cosine, sine):
    half = values.shape[-1] // 2
    first = values[:, :half]
    second = values[:, half:]
    return jnp.concatenate(
        [first * cosine - second * sine, second * cosine + first * sine], axis=-1
    )


def softmax_rows(queries, keys, bias, scale):
    scores = product_nt(queries, keys) * scale + bias
    highest = jnp.max(scores, axis=-1, keepdims=True)
    weights = jnp.exp(scores - highest)
    return weights / jnp.sum(weights, axis=-1, keepdims=True)


def attend_kernel(heads, scale, raw_ref, kv_ref, cos_ref, sin_ref, bias_ref, query_ref, out_ref):
    quarter, tok = raw_ref.shape[1], raw_ref.shape[3]
    rows = quarter * tok
    cosine, sine, bias = cos_ref[...], sin_ref[...], bias_ref[0, 0]
    for head in range(heads):
        cols = slice(head * HDIM, (head + 1) * HDIM)
        raw = raw_ref[0, :, 0, :, cols].reshape(rows, HDIM)
        keys = kv_ref[0, 0, 0, :, 0, :, cols].reshape(rows, HDIM)
        values = kv_ref[0, 1, 0, :, 0, :, cols].reshape(rows, HDIM)
        queries = turn(raw, cosine, sine).astype(BF16)
        probs = softmax_rows(queries, keys, bias, scale).astype(BF16)
        query_ref[0, :, 0, :, cols] = queries.reshape(quarter, tok, HDIM)
        out_ref[0, :, 0, :, cols] = product(probs, values).astype(BF16).reshape(quarter, tok, HDIM)


def attend_back_kernel(
    heads, scale, query_ref, kv_ref, grad_ref, cos_ref, sin_ref, bias_ref, dq_ref, dkv_ref
):
    quarter, tok = query_ref.shape[1], query_ref.shape[3]
    rows = quarter * tok
    cosine, sine, bias = cos_ref[...], sin_ref[...], bias_ref[0, 0]
    for head in range(heads):
        cols = slice(head * HDIM, (head + 1) * HDIM)
        queries = query_ref[0, :, 0, :, cols].reshape(rows, HDIM)
        keys = kv_ref[0, 0, 0, :, 0, :, cols].reshape(rows, HDIM)
        values = kv_ref[0, 1, 0, :, 0, :, cols].reshape(rows, HDIM)
        grad = grad_ref[0, :, 0, :, cols].reshape(rows, HDIM)
        probs = softmax_rows(queries, keys, bias, scale)
        prob_grad = product_nt(grad, values)
        centre = jnp.sum(prob_grad * probs, axis=-1, keepdims=True)
        score_grad = (probs * (prob_grad - centre) * scale).astype(BF16)
        query_grad = turn(product(score_grad, keys), cosine, -sine).astype(BF16)
        key_grad = turn(product_tn(score_grad, queries), cosine, -sine).astype(BF16)
        value_grad = product_tn(probs.astype(BF16), grad).astype(BF16)
        dq_ref[0, :, 0, :, cols] = query_grad.reshape(quarter, tok, HDIM)
        dkv_ref[0, 0, 0, :, 0, :, cols] = key_grad.reshape(quarter, tok, HDIM)
        dkv_ref[0, 1, 0, :, 0, :, cols] = value_grad.reshape(quarter, tok, HDIM)


def attention_specs(shape, slices):
    pair, quarter, micro, tok, feats = shape
    part = feats // slices
    rows = quarter * tok
    grid = (pair, micro, slices)
    flat = pl.BlockSpec((1, quarter, 1, tok, part), lambda i, m, s: (i, 0, m, 0, s))
    both = pl.BlockSpec(
        (1, 2, 1, quarter, 1, tok, part), lambda i, m, s: (s, 0, i, 0, m, 0, 0)
    )
    angle = pl.BlockSpec((rows, HDIM // 2), lambda i, m, s: (0, 0))
    bias = pl.BlockSpec((1, 1, rows, rows), lambda i, m, s: (i, m, 0, 0))
    return grid, part, flat, both, angle, bias


def attend(raw, kv, cosine, sine, bias, scale):
    slices = kv.shape[0]
    grid, part, flat, both, angle, bias_spec = attention_specs(raw.shape, slices)
    out = jax.ShapeDtypeStruct(raw.shape, BF16)
    return pl.pallas_call(
        partial(attend_kernel, part // HDIM, scale),
        grid=grid,
        in_specs=[flat, both, angle, angle, bias_spec],
        out_specs=[flat, flat],
        out_shape=[out, out],
        cost_estimate=pl.CostEstimate(
            flops=4 * raw.size * cosine.shape[0],
            bytes_accessed=12 * raw.size,
            transcendentals=raw.size * 2,
        ),
        name="attend",
    )(raw, kv, cosine, sine, bias)


def attend_back(queries, kv, grad, cosine, sine, bias, scale):
    slices = kv.shape[0]
    grid, part, flat, both, angle, bias_spec = attention_specs(queries.shape, slices)
    return pl.pallas_call(
        partial(attend_back_kernel, part // HDIM, scale),
        grid=grid,
        in_specs=[flat, both, flat, angle, angle, bias_spec],
        out_specs=[flat, both],
        out_shape=[
            jax.ShapeDtypeStruct(queries.shape, BF16),
            jax.ShapeDtypeStruct(kv.shape, BF16),
        ],
        cost_estimate=pl.CostEstimate(
            flops=10 * queries.size * cosine.shape[0],
            bytes_accessed=14 * queries.size,
            transcendentals=queries.size * 2,
        ),
        name="attend_back",
    )(queries, kv, grad, cosine, sine, bias)


MESH = pl.DeviceIdType.MESH
ANY = pl.BlockSpec(memory_space=pl.ANY)
VMEM = pl.BlockSpec(memory_space=pltpu.VMEM)
DMA = pltpu.SemaphoreType.DMA


def remote(src, dst, send, recv, target):
    return pltpu.make_async_remote_copy(
        src_ref=src, dst_ref=dst, send_sem=send, recv_sem=recv, device_id=target, device_id_type=MESH
    )


def greet(targets):
    barrier = pltpu.get_barrier_semaphore()
    for target in targets:
        pl.semaphore_signal(barrier, inc=1, device_id=target, device_id_type=MESH)
    pl.semaphore_wait(barrier, len(targets))


def params(number, limit=None):
    return pltpu.CompilerParams(
        collective_id=number, has_side_effects=True, vmem_limit_bytes=limit
    )


def add_into(target, sources, rows):
    step = 1
    while step * 2 <= rows and step * 2 * target.shape[-1] <= 65536 and rows % (step * 2) == 0:
        step *= 2

    def one(index, carry):
        where = pl.ds(pl.multiple_of(index * step, step), step)
        total = sources[0][where].astype(F32)
        for source in sources[1:]:
            total = total + source[where].astype(F32)
        target[where] = total.astype(target.dtype)
        return carry

    lax.fori_loop(0, rows // step, one, 0)


def cube_reduce_kernel(pairs, x_ref, o_ref, half, quarter, got_core, got_side, got_pair, send, recv):
    p = lax.axis_index("pair")
    e = lax.axis_index("expert")
    c, y = lax.rem(e, 2), lax.div(e, 2)
    core = {"expert": e + 1 - 2 * c}
    side = {"expert": e + 2 - 4 * y}
    other = {"pair": lax.rem(p + 1, pairs)}
    greet([core, side] + ([other] if pairs == 2 else []))
    rows = x_ref.shape[3]
    shifts = (1, 0) if pairs == 2 else (0,)
    order = [(dx, dy) for dy in (1, 0) for dx in shifts]
    first, second = [], {}
    for slot, (dx, dy) in enumerate(order):
        px, yy = lax.rem(p + dx, pairs), lax.rem(y + dy, 2)
        copy = remote(
            x_ref.at[px, yy, 1 - c], got_core.at[slot], send.at[slot], recv.at[slot], core
        )
        copy.start()
        first.append(copy)
    base = len(order)
    for slot, (dx, dy) in enumerate(order):
        px, yy = lax.rem(p + dx, pairs), lax.rem(y + dy, 2)
        first[slot].wait_recv()
        add_into(half.at[slot], [x_ref.at[px, yy, c], got_core.at[slot]], rows)
        if dy == 1:
            copy = remote(
                half.at[slot], got_side.at[dx], send.at[base + dx], recv.at[base + dx], side
            )
            copy.start()
            second[dx] = copy
    last = None
    for dx in shifts:
        second[dx].wait_recv()
        if dx == 1:
            add_into(quarter, [half.at[order.index((1, 0))], got_side.at[1]], rows)
            last = remote(quarter, got_pair, send.at[base + 2], recv.at[base + 2], other)
            last.start()
    if last is not None:
        last.wait_recv()
        add_into(o_ref, [half.at[order.index((0, 0))], got_side.at[0], got_pair], rows)
    else:
        add_into(o_ref, [half.at[order.index((0, 0))], got_side.at[0]], rows)
    for copy in first + list(second.values()) + ([last] if last is not None else []):
        copy.wait_send()


def cube_reduce(value, pairs, number):
    _, rows, cols = value.shape
    value = value.reshape(pairs, 2, 2, rows, cols)
    slots = 2 * pairs
    block = jax.ShapeDtypeStruct((rows, cols), value.dtype)
    return pl.pallas_call(
        partial(cube_reduce_kernel, pairs),
        in_specs=[VMEM],
        out_specs=VMEM,
        out_shape=block,
        scratch_shapes=[
            pltpu.VMEM((slots, rows, cols), value.dtype),
            pltpu.VMEM((rows, cols), value.dtype),
            pltpu.VMEM((slots, rows, cols), value.dtype),
            pltpu.VMEM((pairs, rows, cols), value.dtype),
            pltpu.VMEM((rows, cols), value.dtype),
            DMA((slots + 3,)),
            DMA((slots + 3,)),
        ],
        compiler_params=params(number, 48 * 2**20),
        cost_estimate=pl.CostEstimate(
            flops=value.size, bytes_accessed=24 * value.size, transcendentals=0
        ),
        name="cube_reduce",
    )(value)


def cube_gather_kernel(pairs, x_ref, o_ref, send, recv, local):
    p = lax.axis_index("pair") if pairs == 2 else 0
    e = lax.axis_index("expert")
    c, y = lax.rem(e, 2), lax.div(e, 2)
    core = {"expert": e + 1 - 2 * c}
    side = {"expert": e + 2 - 4 * y}
    other = {"pair": lax.rem(p + 1, pairs)}
    greet([core, side] + ([other] if pairs == 2 else []))
    q, w = lax.rem(p + 1, pairs), 1 - y
    own = o_ref.at[p, y, c]
    keep = pltpu.make_async_copy(x_ref, own, local)
    keep.start()
    copies = []

    def push(slot, source, place, target):
        copy = remote(source, place, send.at[slot], recv.at[slot], target)
        copy.start()
        copies.append(copy)
        return copy

    to_side = push(0, x_ref, own, side)
    to_other = push(1, x_ref, own, other) if pairs == 2 else None
    to_core = push(2, x_ref, own, core)
    waits = [to_core]
    if pairs == 2:
        to_other.wait_recv()
        block = o_ref.at[q, y, c]
        far = push(3, block, block, side)
        waits.append(push(4, block, block, core))
    to_side.wait_recv()
    block = o_ref.at[p, w, c]
    waits.append(push(5, block, block, core))
    if pairs == 2:
        far.wait_recv()
        block = o_ref.at[q, w, c]
        waits.append(push(6, block, block, core))
    for copy in waits:
        copy.wait_recv()
    for copy in copies:
        copy.wait_send()
    keep.wait()


def cube_gather(value, pairs, number):
    return pl.pallas_call(
        partial(cube_gather_kernel, pairs),
        in_specs=[VMEM],
        out_specs=VMEM,
        out_shape=jax.ShapeDtypeStruct((pairs, 2, 2) + value.shape, value.dtype),
        scratch_shapes=[DMA((7,)), DMA((7,)), DMA(())],
        compiler_params=params(number, 48 * 2**20),
        cost_estimate=pl.CostEstimate(
            flops=0, bytes_accessed=80 * value.size, transcendentals=0
        ),
        name="cube_gather",
    )(value)


def place_of(index, sizes):
    line, pairs, experts = sizes
    return {
        "line": index // (pairs * experts),
        "pair": (index // experts) % pairs,
        "expert": index % experts,
    }


def small_kernel(sizes, reduce, x_ref, o_ref, got, send, recv):
    line, pairs, experts = sizes
    count = line * pairs * experts
    me = (
        lax.axis_index("line") * (pairs * experts)
        + lax.axis_index("pair") * experts
        + lax.axis_index("expert")
    )
    barrier = pltpu.get_barrier_semaphore()

    def greet_one(offset, carry):
        target = place_of((me + offset) % count, sizes)
        pl.semaphore_signal(barrier, inc=1, device_id=target, device_id_type=MESH)
        return carry

    lax.fori_loop(1, count, greet_one, 0)
    pl.semaphore_wait(barrier, count - 1)

    def copy_to(offset):
        peer = (me + offset) % count
        source = x_ref.at[peer] if reduce else x_ref
        return remote(source, got.at[offset], send.at[offset], recv.at[offset], place_of(peer, sizes))

    def start(offset, carry):
        copy_to(offset).start()
        return carry

    lax.fori_loop(1, count, start, 0)
    got[0] = x_ref[me] if reduce else x_ref[...]

    def finish(offset, carry):
        copy_to(offset).wait()
        return carry

    lax.fori_loop(1, count, finish, 0)
    if reduce:
        o_ref[...] = jnp.sum(got[...], axis=0)
    else:

        def order(offset, carry):
            o_ref[(me - offset + count) % count] = got[offset]
            return carry

        lax.fori_loop(0, count, order, 0)


def small_exchange(value, sizes, reduce, number):
    count = sizes[0] * sizes[1] * sizes[2]
    block = value.shape[1:] if reduce else value.shape
    return pl.pallas_call(
        partial(small_kernel, sizes, reduce),
        in_specs=[VMEM],
        out_specs=VMEM,
        out_shape=jax.ShapeDtypeStruct(block if reduce else (count,) + block, value.dtype),
        scratch_shapes=[pltpu.VMEM((count,) + block, value.dtype), DMA((count,)), DMA((count,))],
        compiler_params=params(number),
        cost_estimate=pl.CostEstimate(flops=0, bytes_accessed=2**24, transcendentals=0),
        name="small_reduce" if reduce else "small_gather",
    )(value)


def pair_swap_kernel(a_ref, b_ref, a_out, b_out, send, recv, local):
    p = lax.axis_index("pair")
    other = {"pair": 1 - p}
    greet([other])
    copies = []
    for slot, (src, dst) in enumerate(((a_ref.at[1 - p], a_out.at[p]), (b_ref, b_out.at[p]))):
        copy = remote(src, dst, send.at[slot], recv.at[slot], other)
        copy.start()
        copies.append(copy)
    for slot, (src, dst) in enumerate(((a_ref.at[p], a_out.at[p]), (b_ref, b_out.at[p]))):
        copy = pltpu.make_async_copy(src, dst, local.at[slot])
        copy.start()
        copies.append(copy)
    for copy in copies:
        copy.wait()


def pair_swap(value, shared, number):
    return pl.pallas_call(
        pair_swap_kernel,
        in_specs=[VMEM, VMEM],
        out_specs=[VMEM, VMEM],
        out_shape=[
            jax.ShapeDtypeStruct(value.shape, value.dtype),
            jax.ShapeDtypeStruct((2,) + shared.shape, shared.dtype),
        ],
        scratch_shapes=[DMA((2,)), DMA((2,)), DMA((2,))],
        compiler_params=params(number),
        cost_estimate=pl.CostEstimate(
            flops=0, bytes_accessed=20 * value.size, transcendentals=0
        ),
        name="pair_swap",
    )(value, shared)


def start_kernel(
    sizes, walk, tok_ref, small_ref, kv_ref, tok_out, small_out, kv_out, send, recv, peer_send, peer_recv, local
):
    line, pairs, experts = sizes
    z = lax.axis_index("line")
    p = lax.axis_index("pair") if pairs == 2 else 0
    e = lax.axis_index("expert")
    c, y = lax.rem(e, 2), lax.div(e, 2)
    core = {"expert": e + 1 - 2 * c}
    side = {"expert": e + 2 - 4 * y}
    other = {"pair": lax.rem(p + 1, pairs)}
    count = line * pairs * experts
    trees = pairs * experts
    local_me = p * experts + e
    me = z * trees + local_me
    barrier = pltpu.get_barrier_semaphore()

    def greet_one(offset, carry):
        target = place_of((me + offset) % count, sizes)
        pl.semaphore_signal(barrier, inc=1, device_id=target, device_id_type=MESH)
        return carry

    lax.fori_loop(1, count, greet_one, 0)
    pl.semaphore_wait(barrier, count - 1)

    size = kv_ref.shape[1]
    home = kv_out.at[z if walk else 0, pl.ds(pl.multiple_of(local_me * size, size), size)]
    keeps = [
        pltpu.make_async_copy(kv_ref.at[local_me], home, local.at[0]),
        pltpu.make_async_copy(tok_ref, tok_out.at[p, y, c], local.at[1]),
        pltpu.make_async_copy(small_ref, small_out.at[me], local.at[2]),
    ]
    for copy in keeps:
        copy.start()
    KV = 7
    pieces = []
    for shift in range(1, trees):
        peer = lax.rem(local_me + shift, trees)
        copy = remote(
            kv_ref.at[peer],
            home,
            send.at[KV + shift],
            recv.at[KV + shift],
            {"pair": peer // experts, "expert": peer % experts},
        )
        copy.start()
        pieces.append(copy)

    q, w = lax.rem(p + 1, pairs), 1 - y
    own = tok_out.at[p, y, c]
    copies = []

    def push(slot, source, place, target):
        copy = remote(source, place, send.at[slot], recv.at[slot], target)
        copy.start()
        copies.append(copy)
        return copy

    to_side = push(0, tok_ref, own, side)
    to_other = push(1, tok_ref, own, other) if pairs == 2 else None
    waits = [push(2, tok_ref, own, core)]

    def small_to(offset):
        return remote(
            small_ref,
            small_out.at[me],
            peer_send.at[offset],
            peer_recv.at[offset],
            place_of((me + offset) % count, sizes),
        )

    def small_start(offset, carry):
        small_to(offset).start()
        return carry

    lax.fori_loop(1, count, small_start, 0)

    base = KV + trees
    keeps[0].wait()
    for copy in pieces:
        copy.wait_recv()

    def to_up(j, d):
        ref = kv_out.at[j]
        return remote(ref, ref, send.at[base + d], recv.at[base + d], {"line": z + 1})

    def to_down(j, d):
        ref = kv_out.at[j]
        return remote(ref, ref, send.at[base + line + d], recv.at[base + line + d], {"line": z - 1})

    if walk:

        @pl.when(z < line - 1)
        def _():
            to_up(z, 1).start()

        @pl.when(z > 0)
        def _():
            to_down(z, 1).start()

    if pairs == 2:
        to_other.wait_recv()
        block = tok_out.at[q, y, c]
        far = push(3, block, block, side)
        waits.append(push(4, block, block, core))
    to_side.wait_recv()
    block = tok_out.at[p, w, c]
    waits.append(push(5, block, block, core))
    if pairs == 2:
        far.wait_recv()
        block = tok_out.at[q, w, c]
        waits.append(push(6, block, block, core))

    if walk:
        for d in range(1, line):

            @pl.when(z - d >= 0)
            def _():
                to_up(z - d, d).wait_recv()

                @pl.when(z < line - 1)
                def _():
                    to_up(z - d, d + 1).start()

            @pl.when(z + d < line)
            def _():
                to_down(z + d, d).wait_recv()

                @pl.when(z > 0)
                def _():
                    to_down(z + d, d + 1).start()

        for d in range(1, line):

            @pl.when((z - d + 1 >= 0) & (z < line - 1))
            def _():
                to_up(z - d + 1, d).wait_send()

            @pl.when((z + d - 1 < line) & (z > 0))
            def _():
                to_down(z + d - 1, d).wait_send()

    for copy in waits:
        copy.wait_recv()
    for copy in copies + pieces:
        copy.wait_send()
    for copy in keeps[1:]:
        copy.wait()

    def small_finish(offset, carry):
        small_to(offset).wait()
        return carry

    lax.fori_loop(1, count, small_finish, 0)


def start_exchange(tokens, small, kv, sizes, number):
    line, pairs, experts = sizes
    trees, rows, cols = kv.shape
    walk = line <= 4
    count = line * trees
    uses = 7 + trees + 2 * line + 2
    return pl.pallas_call(
        partial(start_kernel, sizes, walk),
        in_specs=[VMEM, VMEM, VMEM],
        out_specs=[VMEM, VMEM, VMEM],
        out_shape=[
            jax.ShapeDtypeStruct((pairs, 2, 2) + tokens.shape, tokens.dtype),
            jax.ShapeDtypeStruct((count,) + small.shape, small.dtype),
            jax.ShapeDtypeStruct((line if walk else 1, trees * rows, cols), kv.dtype),
        ],
        scratch_shapes=[DMA((uses,)), DMA((uses,)), DMA((count,)), DMA((count,)), DMA((3,))],
        compiler_params=params(number, 32 * 2**20),
        cost_estimate=pl.CostEstimate(
            flops=0, bytes_accessed=100 * kv.size, transcendentals=0
        ),
        name="start_exchange",
    )(tokens, small, kv)


def ff_kernel(
    a_in, b_in, gate_hbm, up_hbm, down_hbm,
    a_out, b_out, a_save, b_save, inner_save, dgate_save, dup_save,
    a_buf, b_buf, side, hop, extra, w_gate, w_up, w_down, mid, acc,
    send, recv, load, store, local,
):
    z, p, e = lax.axis_index("line"), lax.axis_index("pair"), lax.axis_index("expert")
    line, _, rows, width = a_buf.shape
    experts, size = a_in.shape[0], a_in.shape[1]
    q = 1 - p
    twin = z + 1 - 2 * (z % 2)
    up, down, other, across = {"line": z + 1}, {"line": z - 1}, {"pair": q}, {"line": twin}
    ins, bufs, outs, saves = (a_in, b_in), (a_buf, b_buf), (a_out, b_out), (a_save, b_save)
    high = z // 2
    near = z + high * (line - 1 - 2 * z)

    def order(t):
        j = t + near * (1 - t // 2) * (1 - 2 * t)
        return j + high * (line - 1 - 2 * j)

    weights = [
        pltpu.make_async_copy(src, dst, load.at[i])
        for i, (src, dst) in enumerate(((gate_hbm, w_gate), (up_hbm, w_up), (down_hbm, w_down)))
    ]
    for copy in weights:
        copy.start()

    barrier = pltpu.get_barrier_semaphore()
    for shift in range(1, experts):
        pl.semaphore_signal(
            barrier, inc=1, device_id={"expert": (e + shift) % experts}, device_id_type=MESH
        )
    pl.semaphore_signal(barrier, inc=1, device_id=other, device_id_type=MESH)

    @pl.when(z > 0)
    def _():
        pl.semaphore_signal(barrier, inc=1, device_id=down, device_id_type=MESH)

    @pl.when(z < line - 1)
    def _():
        pl.semaphore_signal(barrier, inc=1, device_id=up, device_id_type=MESH)

    below, above = (z + line - 1) // line, (2 * line - 2 - z) // line
    pl.semaphore_wait(barrier, experts + below + above)

    UP, DOWN, SIDE, SUMUP, SUMDOWN, SUMSIDE = (i * line for i in range(6))
    TWIN, SUMTWIN, SWAP = 6 * line, 6 * line + 1, 6 * line + 2
    BACK = SWAP + experts

    def push(src, dst, kind, use, target):
        return remote(src, dst, send.at[kind, use], recv.at[kind, use], target)

    def to_up(kind, j):
        return push(bufs[kind].at[j, p], bufs[kind].at[j, p], kind, UP + j, up)

    def to_down(kind, j):
        return push(bufs[kind].at[j, p], bufs[kind].at[j, p], kind, DOWN + j, down)

    def to_other(kind, j):
        return push(bufs[kind].at[j, p], bufs[kind].at[j, p], kind, SIDE + j, other)

    def to_twin():
        return push(bufs[1].at[z, q], bufs[1].at[z, q], 1, TWIN, across)

    def sum_up(kind, j):
        return push(bufs[kind].at[j, p], hop.at[kind, j], kind, SUMUP + j, up)

    def sum_down(kind, j, slot):
        return push(bufs[kind].at[j, p], hop.at[kind, slot], kind, SUMDOWN + j, down)

    def sum_other(kind, j):
        return push(bufs[kind].at[j, q], side.at[kind, j], kind, SUMSIDE + j, other)

    def sum_twin():
        return push(bufs[1].at[twin, q], extra, 1, SUMTWIN, across)

    def piece(index):
        return pl.ds(pl.multiple_of(index * size, size), size)

    def save(kind, j, column):
        return pltpu.make_async_copy(
            bufs[kind].at[j, column], saves[kind].at[j, column], store.at[kind, j, column]
        )

    swaps = []
    for kind in range(2):
        home = bufs[kind].at[z, p, piece(e)]
        keep = pltpu.make_async_copy(ins[kind].at[e], home, local.at[kind])
        keep.start()
        group = []
        for shift in range(1, experts):
            peer = (e + shift) % experts
            copy = push(ins[kind].at[peer], home, kind, SWAP + shift, {"expert": peer})
            copy.start()
            group.append(copy)
        swaps.append((keep, group))

    def spread(t, first=False):
        j = order(t)
        for kind in range(2):
            if first:
                swaps[kind][0].wait()
                for copy in swaps[kind][1]:
                    copy.wait_recv()
            else:

                @pl.when(j < z)
                def _():
                    to_up(kind, j).wait_recv()

                @pl.when(j > z)
                def _():
                    to_down(kind, j).wait_recv()

            @pl.when((j <= z) & (z < line - 1))
            def _():
                to_up(kind, j).start()

            @pl.when((j >= z) & (z > 0))
            def _():
                to_down(kind, j).start()

            if kind == 0:
                to_other(kind, j).start()
            else:

                @pl.when(j != twin)
                def _():
                    to_other(kind, j).start()

            save(kind, j, p).start()

    chunk = 512
    steps = width // chunk

    def first_half(j, column):
        for index in range(3):
            acc[index] = jnp.zeros(acc.shape[1:], F32)

        def one(k, carry):
            where = pl.ds(pl.multiple_of(k * chunk, chunk), chunk)
            left = a_buf[j, column, :, where]
            acc[0] += product_nt(left, w_gate[:, where])
            acc[1] += product_nt(left, w_up[:, where])
            acc[2] += product_nt(b_buf[j, column, :, where], w_down[:, where])
            return carry

        lax.fori_loop(0, steps, one, 0)
        part = 32

        def two(i, carry):
            where = pl.ds(pl.multiple_of(i * part, part), part)
            gate, lift, grad = acc[0, where], acc[1, where], acc[2, where]
            sigma = jax.nn.sigmoid(gate)
            mid[j, column, 0, where] = (gate * sigma * lift).astype(BF16)
            mid[j, column, 1, where] = (
                grad * lift * sigma * (1.0 + gate * (1.0 - sigma))
            ).astype(BF16)
            mid[j, column, 2, where] = (grad * gate * sigma).astype(BF16)
            return carry

        lax.fori_loop(0, rows // part, two, 0)

    def second_half(j, column):
        def one(k, carry):
            where = pl.ds(pl.multiple_of(k * chunk, chunk), chunk)
            a_buf[j, column, :, where] = product(mid[j, column, 0], w_down[:, where]).astype(BF16)
            b_buf[j, column, :, where] = (
                product(mid[j, column, 1], w_gate[:, where])
                + product(mid[j, column, 2], w_up[:, where])
            ).astype(BF16)
            return carry

        lax.fori_loop(0, steps, one, 0)

    def arrive(j):
        for kind in range(2):
            if kind == 0:
                to_other(kind, j).wait_recv()
            else:

                @pl.when(j != twin)
                def _():
                    to_other(kind, j).wait_recv()

                @pl.when(j == twin)
                def _():
                    to_twin().wait_recv()

            save(kind, j, q).start()

        @pl.when(j == z)
        def _():
            to_twin().start()

    def emit(t):
        j = order(t)
        sum_other(0, j).start()

        @pl.when((j != twin) & (j != z))
        def _():
            sum_other(1, j).start()

    def step(s, carry):
        @pl.when(s == 0)
        def _():
            spread(0, True)
            for copy in weights:
                copy.wait()

        @pl.when(s == 1)
        def _():
            spread(1)
            spread(2)

        @pl.when(s == 3)
        def _():
            spread(3)

        @pl.when(s == line)
        def _():
            sum_twin().start()

        def half(c, inner_carry):
            t = s - c
            column = p + c * (q - p)

            @pl.when((t >= 0) & (t < line))
            def _():
                j = order(t)

                @pl.when(c == 1)
                def _():
                    arrive(j)

                first_half(j, column)

                @pl.when(c == 1)
                def _():
                    @pl.when(j == z)
                    def _():
                        to_twin().wait_send()

                    for kind in range(2):
                        save(kind, j, q).wait()
                    second_half(j, column)

            return inner_carry

        return lax.fori_loop(0, 2, half, carry)

    lax.fori_loop(0, line + 1, step, 0)

    for t in (3, 2, 1, 0):
        emit(t)

    for copy in (
        pltpu.make_async_copy(mid.at[:, :, 0], inner_save, local.at[2]),
        pltpu.make_async_copy(mid.at[:, :, 1], dgate_save, local.at[3]),
        pltpu.make_async_copy(mid.at[:, :, 2], dup_save, local.at[4]),
    ):
        copy.start()
    sum_twin().wait_recv()
    add_into(b_buf.at[z, q], [b_buf.at[z, q], extra], rows)
    sum_other(1, z).start()

    def back(kind):
        own = pltpu.make_async_copy(
            bufs[kind].at[z, p, piece(e)], outs[kind].at[e], local.at[kind]
        )
        return [own] + [
            push(
                bufs[kind].at[z, p, piece((e + shift) % experts)],
                outs[kind].at[e],
                kind,
                BACK + shift,
                {"expert": (e + shift) % experts},
            )
            for shift in range(1, experts)
        ]

    def fold(s, carry):
        t = line - 1 - s
        j = order(t)
        for kind in range(2):
            save(kind, j, p).wait()

            @pl.when((j <= z) & (z < line - 1))
            def _():
                to_up(kind, j).wait_send()

            @pl.when((j >= z) & (z > 0))
            def _():
                to_down(kind, j).wait_send()

            if kind == 0:
                to_other(kind, j).wait_send()
            else:

                @pl.when(j != twin)
                def _():
                    to_other(kind, j).wait_send()

        second_half(j, p)
        for kind in range(2):
            mine = bufs[kind].at[j, p]
            if kind == 0:
                sum_other(kind, j).wait_recv()
                add_into(mine, [mine, side.at[kind, j]], rows)
            else:

                @pl.when(j != twin)
                def _():
                    sum_other(kind, j).wait_recv()
                    add_into(mine, [mine, side.at[kind, j]], rows)

            @pl.when((j >= z) & (z > 0))
            def _():
                sum_up(kind, j).wait_recv()
                add_into(mine, [mine, hop.at[kind, j]], rows)

            @pl.when((j < z) & (z < line - 1))
            def _():
                sum_down(kind, j, j).wait_recv()
                add_into(mine, [mine, hop.at[kind, j]], rows)

            @pl.when((j == z) & (z < line - 1))
            def _():
                sum_down(kind, j, line).wait_recv()
                add_into(mine, [mine, hop.at[kind, line]], rows)

            @pl.when(j == z)
            def _():
                for copy in back(kind):
                    copy.start()

            @pl.when(j > z)
            def _():
                sum_up(kind, j).start()

            @pl.when((j < z) & (j != z - 1))
            def _():
                sum_down(kind, j, j).start()

            @pl.when((j < z) & (j == z - 1))
            def _():
                sum_down(kind, j, line).start()

        return carry

    lax.fori_loop(0, line, fold, 0)

    for kind in range(2):
        for copy in back(kind):
            copy.wait()

    def drain(j, carry):
        for kind in range(2):
            if kind == 0:
                sum_other(kind, j).wait_send()
            else:

                @pl.when(j != twin)
                def _():
                    sum_other(kind, j).wait_send()

            @pl.when(j > z)
            def _():
                sum_up(kind, j).wait_send()

            @pl.when(j < z)
            def _():
                sum_down(kind, j, j).wait_send()

        return carry

    lax.fori_loop(0, line, drain, 0)
    sum_twin().wait_send()
    for copy in (
        pltpu.make_async_copy(mid.at[:, :, 0], inner_save, local.at[2]),
        pltpu.make_async_copy(mid.at[:, :, 1], dgate_save, local.at[3]),
        pltpu.make_async_copy(mid.at[:, :, 2], dup_save, local.at[4]),
    ):
        copy.wait()
    for keep, group in swaps:
        for copy in group:
            copy.wait_send()


def feed_forward(first, second, w_gate, w_up, w_down, line, pairs, number):
    experts, size, width = first.shape
    hidden = w_gate.shape[0]
    rows = experts * size
    blocks = (line, pairs, rows)
    back = jax.ShapeDtypeStruct(first.shape, BF16)
    wide = jax.ShapeDtypeStruct(blocks + (width,), BF16)
    thin = jax.ShapeDtypeStruct(blocks + (hidden,), BF16)
    uses = 6 * line + 2 + 2 * experts
    total = line * pairs * rows
    return pl.pallas_call(
        ff_kernel,
        in_specs=[ANY] * 5,
        out_specs=[ANY] * 7,
        out_shape=[back, back, wide, wide, thin, thin, thin],
        scratch_shapes=[
            pltpu.VMEM(blocks + (width,), BF16),
            pltpu.VMEM(blocks + (width,), BF16),
            pltpu.VMEM((2, line, rows, width), BF16),
            pltpu.VMEM((2, line + 1, rows, width), BF16),
            pltpu.VMEM((rows, width), BF16),
            pltpu.VMEM((hidden, width), BF16),
            pltpu.VMEM((hidden, width), BF16),
            pltpu.VMEM((hidden, width), BF16),
            pltpu.VMEM((line, pairs, 3, rows, hidden), BF16),
            pltpu.VMEM((3, rows, hidden), F32),
            DMA((2, uses)),
            DMA((2, uses)),
            DMA((3,)),
            DMA((2, line, pairs)),
            DMA((5,)),
        ],
        compiler_params=params(number, 63 * 2**20),
        cost_estimate=pl.CostEstimate(
            flops=12 * total * hidden * width,
            bytes_accessed=12 * total * width,
            transcendentals=total * hidden,
        ),
        name="feed_forward",
    )(first, second, w_gate, w_up, w_down)


def end_kernel(
    pairs, x_ref, g_hbm, o_ref, k_ref,
    g_ref, half, quarter, got_core, got_side, got_pair, hop, send, recv, local,
):
    z, p, e = lax.axis_index("line"), lax.axis_index("pair"), lax.axis_index("expert")
    line, span, _ = g_ref.shape
    trees, piece, _ = k_ref.shape
    c, y = e % 2, e // 2
    core, side = {"expert": e + 1 - 2 * c}, {"expert": e + 2 - 4 * y}
    other, up, down = {"pair": 1 - p}, {"line": z + 1}, {"line": z - 1}
    experts = trees // pairs
    me = p * experts + e
    high = z // 2
    near = z + high * (line - 1 - 2 * z)

    def order(t):
        j = t + near * (1 - t // 2) * (1 - 2 * t)
        return j + high * (line - 1 - 2 * j)

    def place(index):
        return {"pair": index // experts, "expert": index % experts}

    fetch = pltpu.make_async_copy(g_hbm, g_ref, local)
    fetch.start()
    barrier = pltpu.get_barrier_semaphore()
    for shift in range(1, trees):
        pl.semaphore_signal(
            barrier, inc=1, device_id=place((me + shift) % trees), device_id_type=MESH
        )

    @pl.when(z > 0)
    def _():
        pl.semaphore_signal(barrier, inc=1, device_id=down, device_id_type=MESH)

    @pl.when(z < line - 1)
    def _():
        pl.semaphore_signal(barrier, inc=1, device_id=up, device_id_type=MESH)

    below, above = (z + line - 1) // line, (2 * line - 2 - z) // line
    pl.semaphore_wait(barrier, trees - 1 + below + above)
    UP, DOWN, SWAP = 7, 7 + line, 7 + 2 * line
    rows = x_ref.shape[3]

    def sum_up(j):
        return remote(g_ref.at[j], hop.at[j], send.at[UP + j], recv.at[UP + j], up)

    def sum_down(j, slot):
        return remote(g_ref.at[j], hop.at[slot], send.at[DOWN + j], recv.at[DOWN + j], down)

    def fold(t):
        j = order(t)
        mine = g_ref.at[j]

        @pl.when((j >= z) & (z > 0))
        def _():
            sum_up(j).wait_recv()
            add_into(mine, [mine, hop.at[j]], span)

        @pl.when((j < z) & (z < line - 1))
        def _():
            sum_down(j, j).wait_recv()
            add_into(mine, [mine, hop.at[j]], span)

        @pl.when((j == z) & (z < line - 1))
        def _():
            sum_down(j, line).wait_recv()
            add_into(mine, [mine, hop.at[line]], span)

        @pl.when(j > z)
        def _():
            sum_up(j).start()

        @pl.when((j < z) & (j != z - 1))
        def _():
            sum_down(j, j).start()

        @pl.when((j < z) & (j == z - 1))
        def _():
            sum_down(j, line).start()

    corners = [(1, 1), (0, 1), (1, 0), (0, 0)]
    first, second = [], {}
    for slot, (dx, dy) in enumerate(corners):
        copy = remote(
            x_ref.at[(p + dx) % 2, (y + dy) % 2, 1 - c],
            got_core.at[slot],
            send.at[slot],
            recv.at[slot],
            core,
        )
        copy.start()
        first.append(copy)
    fetch.wait()
    fold(3)
    for slot, (dx, dy) in enumerate(corners):
        first[slot].wait_recv()
        add_into(
            half.at[slot], [x_ref.at[(p + dx) % 2, (y + dy) % 2, c], got_core.at[slot]], rows
        )
        if dy == 1:
            second[dx] = remote(
                half.at[slot], got_side.at[dx], send.at[4 + dx], recv.at[4 + dx], side
            )
            second[dx].start()
    fold(2)
    second[1].wait_recv()
    add_into(quarter, [half.at[2], got_side.at[1]], rows)
    last = remote(quarter, got_pair, send.at[6], recv.at[6], other)
    last.start()
    fold(1)
    second[0].wait_recv()
    last.wait_recv()
    add_into(o_ref, [half.at[3], got_side.at[0], got_pair], rows)
    fold(0)

    def part(index):
        return g_ref.at[z, pl.ds(pl.multiple_of(index * piece, piece), piece)]

    keep = pltpu.make_async_copy(part(me), k_ref.at[me], local)
    keep.start()
    swaps = []
    for shift in range(1, trees):
        peer = (me + shift) % trees
        copy = remote(
            part(peer), k_ref.at[me], send.at[SWAP + shift], recv.at[SWAP + shift], place(peer)
        )
        copy.start()
        swaps.append(copy)
    for copy in swaps:
        copy.wait()
    keep.wait()
    for copy in first + list(second.values()) + [last]:
        copy.wait_send()

    def drain(j, carry):
        @pl.when(j > z)
        def _():
            sum_up(j).wait_send()

        @pl.when(j < z)
        def _():
            sum_down(j, j).wait_send()

        return carry

    lax.fori_loop(0, line, drain, 0)


def end_exchange(value, grads, line, pairs, number):
    trees, rows, cols = value.shape
    span, thin = grads.shape[0] // line, grads.shape[1]
    uses = 7 + 2 * line + trees
    block = pltpu.VMEM((rows, cols), BF16)
    return pl.pallas_call(
        partial(end_kernel, pairs),
        in_specs=[VMEM, ANY],
        out_specs=[VMEM, VMEM],
        out_shape=[
            jax.ShapeDtypeStruct((rows, cols), BF16),
            jax.ShapeDtypeStruct((trees, span // trees, thin), BF16),
        ],
        scratch_shapes=[
            pltpu.VMEM((line, span, thin), BF16),
            pltpu.VMEM((4, rows, cols), BF16),
            block,
            pltpu.VMEM((4, rows, cols), BF16),
            pltpu.VMEM((2, rows, cols), BF16),
            block,
            pltpu.VMEM((line + 1, span, thin), BF16),
            DMA((uses,)),
            DMA((uses,)),
            DMA(()),
        ],
        compiler_params=params(number, 48 * 2**20),
        cost_estimate=pl.CostEstimate(
            flops=value.size, bytes_accessed=32 * value.size, transcendentals=0
        ),
        name="end_exchange",
    )(value.reshape(pairs, 2, 2, rows, cols), grads.reshape(line, span, thin))


def gather(value, axes, axis=0):
    return lax.all_gather(value, axes, axis=axis, tiled=True)


def scatter(value, axes, axis=0):
    return lax.psum_scatter(value, axes, scatter_dimension=axis, tiled=True)


def swap(value, axes, split=0, concat=0):
    return lax.all_to_all(value, axes, split_axis=split, concat_axis=concat, tiled=True)


DP = ("line", "pair")
ALL = ("line", "pair", "expert")
TREES = ("pair", "expert")


def body(
    tokens,
    w_query,
    w_out,
    w_key,
    w_value,
    gain_attn,
    router_attn,
    gain_mlp,
    router_mlp,
    w_gate,
    w_up,
    w_down,
    attn_route,
    mlp_route,
    fill_order,
    parents,
    cotangent,
):
    experts = lax.axis_size("expert")
    pair = lax.axis_size("pair")
    line = lax.axis_size("line")
    position = lax.axis_index("expert")
    micro, _, tok, width = tokens.shape
    tree = experts * tok
    rows = pair * experts * micro * tok
    heads_total = w_query.shape[2]
    part = heads_total // (line * pair)
    feats = heads_total // pair
    piece = feats // experts
    own_in = w_query.shape[1]
    own_kv = w_key.shape[0]
    capacity = tok * mlp_route.shape[3] // experts
    scale = 1.0 / math.sqrt(HDIM)

    places, segment, depth = tree_layout(tree // 16, tree)
    half = HDIM // 2
    rates = 10000.0 ** (-jnp.arange(half, dtype=F32) / half)
    angle = depth.astype(F32)[:, None] * rates[None, :]
    cosine, sine = jnp.cos(angle), jnp.sin(angle)

    sizes = (line, pair, experts)
    walk = line <= 4 and pair == 2
    query_mine = w_query[0].reshape(own_in, line, pair, part)
    query_mine = jnp.transpose(query_mine, (2, 0, 1, 3)).reshape(pair, own_in, feats)
    integers = jnp.concatenate([attn_route[:, 0].reshape(micro, -1), parents[:, 0]], axis=1)
    if pair == 2:
        flat = integers.reshape(-1)
        flat = jnp.pad(flat, (0, -flat.shape[0] % 1024)).reshape(-1, 128)
        query_mine, flat = pair_swap(query_mine, flat, 1)
        integers = flat.reshape(pair, -1)[:, : integers.size].reshape((pair,) + integers.shape)
    else:
        integers = integers[None]
    query_weight = gather(query_mine.reshape(pair * own_in, feats), "line")

    small = jnp.concatenate(
        [gain_attn[None], gain_mlp[None], router_attn.T, router_mlp.T], axis=0
    )
    kv_mine = jnp.stack([w_key, w_value], axis=1).reshape(
        own_kv, 2, experts, line // experts, pair, part
    )
    kv_mine = jnp.transpose(kv_mine, (4, 2, 0, 1, 3, 5)).reshape(
        pair * experts, own_kv, 2 * piece
    )
    own_tokens = tokens.reshape(micro * tok, width)
    tree_tokens, small, kv_weight = start_exchange(own_tokens, small, kv_mine, sizes, 2)
    kv_weight = kv_weight.reshape(-1, 2 * piece)
    if kv_weight.shape[0] < width:
        kv_weight = gather(kv_weight, "line")
    out_mine, small = lax.optimization_barrier((w_out[0], small))
    out_weight = gather(out_mine, "line")

    small = jnp.transpose(small, (1, 0, 2)).reshape(-1, width)
    first_gain = small[0].astype(F32)
    second_gain = small[1].astype(F32)
    first_router = small[2 : 2 + experts]
    second_router = small[2 + experts : 2 + 2 * experts]

    residual = own_tokens.astype(F32)
    _, first_pull = jax.vjp(rms_scaled, residual, first_gain)
    tree_input = rms_scaled(tree_tokens.reshape(rows, width).astype(F32), first_gain).astype(BF16)

    routes = integers[..., : tree * 2].reshape(pair, micro, experts, tok, 2)
    routes = jnp.transpose(routes, (0, 2, 1, 3, 4)).reshape(rows, 2)
    family = integers[..., tree * 2 :]
    bias = jax.vmap(jax.vmap(lambda parent: score_bias(parent, segment, places)))(family)

    kv_raw = product(tree_input, kv_weight)
    spread_cos = jnp.broadcast_to(
        cosine.reshape(1, experts, 1, tok, 1, half), (pair, experts, micro, tok, 1, half)
    ).reshape(rows, 1, half)
    spread_sin = jnp.broadcast_to(
        sine.reshape(1, experts, 1, tok, 1, half), (pair, experts, micro, tok, 1, half)
    ).reshape(rows, 1, half)
    key_raw = kv_raw[:, :piece].reshape(rows, piece // HDIM, HDIM)
    key_one, key_two = key_raw[..., :half], key_raw[..., half:]
    keys = jnp.concatenate(
        [
            key_one * spread_cos - key_two * spread_sin,
            key_two * spread_cos + key_one * spread_sin,
        ],
        axis=-1,
    ).reshape(rows, piece)
    kv = jnp.concatenate([keys.astype(BF16), kv_raw[:, piece:].astype(BF16)], axis=0)
    kv = cube_gather(kv, 1, 3)
    shape = (pair, experts, micro, tok, feats)
    kv = kv.reshape(experts, 2, pair, experts, micro, tok, piece)

    first_gates, first_gate_pull = jax.vjp(
        partial(mixture_gates, routes), product_nt(tree_input, first_router)
    )
    column = (jnp.arange(experts, dtype=jnp.int32) == position).astype(F32)
    own_gate = jnp.sum(first_gates * column[None, :], axis=1)

    raw = product(tree_input, query_weight)
    queries, heads_out = attend(raw.reshape(shape), kv, cosine, sine, bias, scale)
    heads_flat = heads_out.reshape(rows, feats)
    projected = product(heads_flat, out_weight)
    gated = (own_gate[:, None] * projected).astype(BF16)
    attention = cube_reduce(gated.reshape(pair * experts, micro * tok, width), pair, 4).astype(F32)

    middle = residual + attention
    second_normed, second_pull = jax.vjp(rms_scaled, middle, second_gain)
    second_normed = second_normed.astype(BF16)
    picked = mlp_route[:, 0].reshape(micro * tok, 2)
    second_gates, second_gate_pull = jax.vjp(
        partial(mixture_gates, picked), product_nt(second_normed, second_router)
    )
    table = jax.vmap(partial(slot_table, experts=experts, capacity=capacity))(
        mlp_route[:, 0], fill_order[:, 0]
    )
    table_low = table.astype(BF16)
    grouped = second_normed.reshape(micro, tok, width)
    outgoing = jnp.einsum("mect,mtd->emcd", table_low, grouped, preferred_element_type=F32)
    top_grad = cotangent.reshape(micro, tok, width)
    slot_values = jnp.einsum("mect,mtd->emcd", table_low, top_grad, preferred_element_type=F32)
    slot_gates = jnp.einsum(
        "mect,mte->emc", table, second_gates.reshape(micro, tok, experts), precision=HIGHEST
    )
    slot_grad = (slot_gates[..., None] * slot_values).astype(BF16)
    slots = experts * micro * capacity
    outgoing = outgoing.astype(BF16).reshape(experts, micro * capacity, width)
    slot_grad = slot_grad.reshape(experts, micro * capacity, width)
    gate_weight, up_weight, down_weight = w_gate[0], w_up[0], w_down[0]
    if walk:
        returned, came_back, arrived, result_grad, inner, gate_grad, up_grad = feed_forward(
            outgoing, slot_grad, gate_weight, up_weight, down_weight, line, pair, 5
        )
        arrived, result_grad, inner, gate_grad, up_grad = (
            value.reshape(-1, value.shape[-1])
            for value in (arrived, result_grad, inner, gate_grad, up_grad)
        )
    else:
        arrived = gather(swap(outgoing, "expert").reshape(slots, width), DP)
        result_grad = gather(swap(slot_grad, "expert").reshape(slots, width), DP)
        gate_pre = product_nt(arrived, gate_weight)
        up_pre = product_nt(arrived, up_weight)
        sigma = jax.nn.sigmoid(gate_pre)
        inner = (gate_pre * sigma * up_pre).astype(BF16)
        returned = product(inner, down_weight).astype(BF16)
        inner_grad = product_nt(result_grad, down_weight)
        gate_grad = (inner_grad * up_pre * sigma * (1.0 + gate_pre * (1.0 - sigma))).astype(BF16)
        up_grad = (inner_grad * gate_pre * sigma).astype(BF16)
        came_back = (product(gate_grad, gate_weight) + product(up_grad, up_weight)).astype(BF16)
        back = (experts, micro * capacity, width)
        returned = swap(scatter(returned, DP).reshape(back), "expert")
        came_back = swap(scatter(came_back, DP).reshape(back), "expert")
    returned = returned.reshape(experts, micro, capacity, width)
    came_back = came_back.reshape(experts, micro, capacity, width)
    spread = jnp.einsum("mect,emcd->emtd", table_low, returned, preferred_element_type=F32)
    spread = spread.reshape(experts, micro * tok, width)
    mixed = jnp.sum(jnp.transpose(second_gates)[:, :, None] * spread, axis=0)
    layer_out = (middle + mixed).astype(BF16)
    dz = top_grad.reshape(micro * tok, width).astype(F32)
    second_gate_grad = jnp.transpose(jnp.sum(spread * dz[None], axis=-1))
    (second_logit_grad,) = second_gate_pull(second_gate_grad)
    hn_grad = jnp.einsum("mect,emcd->mtd", table_low, came_back, preferred_element_type=F32)
    hn_grad = hn_grad.reshape(micro * tok, width)
    second_router_wide = second_router.astype(F32)
    for expert in range(experts):
        hn_grad = hn_grad + second_logit_grad[:, expert : expert + 1] * second_router_wide[expert]
    grad_router_second = jnp.dot(
        jnp.transpose(second_logit_grad),
        second_normed.astype(F32),
        precision=HIGHEST,
        preferred_element_type=F32,
    )
    middle_grad, grad_gain_second = second_pull(hn_grad)
    middle_grad = middle_grad + dz

    mix_grad = cube_gather(middle_grad.astype(BF16), pair, 7).reshape(rows, width).astype(F32)
    own_gate_grad = jnp.sum(mix_grad * projected, axis=-1)
    projected_grad = (own_gate[:, None] * mix_grad).astype(BF16)
    grad_output = product_tn(heads_flat, projected_grad).astype(BF16)
    grad_output, projected_grad = lax.optimization_barrier((grad_output, projected_grad))
    grad_output = scatter(grad_output, "line")
    heads_grad = product_nt(projected_grad, out_weight).astype(BF16).reshape(shape)
    query_pre, kv_pre = attend_back(queries, kv, heads_grad, cosine, sine, bias, scale)
    query_pre = query_pre.reshape(rows, feats)
    grad_query = product_tn(tree_input, query_pre).astype(BF16)
    grad_query, kv_pre = lax.optimization_barrier((grad_query, kv_pre))
    kv_sum = cube_reduce(kv_pre.reshape(experts, 2 * rows, piece), 1, 8)
    grad_query, grad_output, kv_sum = lax.optimization_barrier((grad_query, grad_output, kv_sum))
    (first_logit_grad,) = first_gate_pull(own_gate_grad[:, None] * column[None, :])
    key_pre, value_pre = kv_sum[:rows], kv_sum[rows:]
    grad_kv = jnp.concatenate(
        [product_tn(tree_input, key_pre), product_tn(tree_input, value_pre)], axis=1
    )
    grad_kv, key_pre, value_pre = lax.optimization_barrier(
        (grad_kv.astype(BF16), key_pre, value_pre)
    )
    input_term = (
        product_nt(query_pre, query_weight)
        + product_nt(key_pre, kv_weight[:, :piece])
        + product_nt(value_pre, kv_weight[:, piece:])
    )
    first_router_wide = first_router.astype(F32)
    for expert in range(experts):
        input_term = input_term + first_logit_grad[:, expert : expert + 1] * first_router_wide[expert]
    input_term = input_term.astype(BF16).reshape(pair * experts, micro * tok, width)
    if walk:
        normed_grad, grad_kv = end_exchange(input_term, grad_kv, line, pair, 9)
    else:
        normed_grad = cube_reduce(input_term, pair, 9)
        grad_kv = scatter(grad_kv, "line")
        grad_kv = swap(grad_kv.reshape(pair * experts, own_kv, 2 * piece), TREES)
    gate_grad, up_grad, inner, arrived, result_grad, normed_grad = lax.optimization_barrier(
        (gate_grad, up_grad, inner, arrived, result_grad, normed_grad)
    )
    grad_gate = product_tn(gate_grad, arrived)[None]
    grad_upward = product_tn(up_grad, arrived)[None]
    grad_downward = product_tn(inner, result_grad)[None]
    normed_grad = normed_grad.astype(F32)
    grad_query = scatter(grad_query, "line")
    grad_query = swap(grad_query.reshape(own_in * pair, line, part)[None], "pair", 1, 0)
    grad_query = jnp.transpose(grad_query, (1, 2, 0, 3)).reshape(1, own_in, heads_total)
    grad_kv = grad_kv.reshape(pair, experts, own_kv, 2, line // experts, part)
    grad_kv = jnp.transpose(grad_kv, (2, 3, 1, 4, 0, 5)).reshape(own_kv, 2, heads_total)
    grad_kv = grad_kv.astype(F32)
    grad_router_first = jnp.dot(
        jnp.transpose(first_logit_grad),
        tree_input.astype(F32),
        precision=HIGHEST,
        preferred_element_type=F32,
    )
    token_grad, grad_gain_first = first_pull(normed_grad)
    tokens_grad = token_grad + middle_grad

    sums = jnp.concatenate(
        [grad_gain_first[None], grad_gain_second[None], grad_router_first, grad_router_second],
        axis=0,
    )
    sums = jnp.transpose(sums.reshape(sums.shape[0], -1, own_kv), (1, 0, 2))
    sums = small_exchange(sums, sizes, True, 10)
    return (
        layer_out.reshape(micro, 1, tok, width),
        tokens_grad.reshape(micro, 1, tok, width),
        grad_query.astype(F32),
        grad_output[None].astype(F32),
        grad_kv[:, 0],
        grad_kv[:, 1],
        sums[0],
        jnp.transpose(sums[2 : 2 + experts]),
        sums[1],
        jnp.transpose(sums[2 + experts :]),
        grad_gate,
        grad_upward,
        grad_downward,
    )


def solution(mesh):
    line, experts = mesh.devices.shape
    pair = 2 if line % 2 == 0 and (HEADS % line == 0) else 1
    shaped = Mesh(mesh.devices.reshape(line // pair, pair, experts), ALL)
    in_specs = (
        P(None, DP, "expert", None),
        P("expert", DP, None),
        P("expert", DP, None),
        P(ALL, None),
        P(ALL, None),
        P(ALL),
        P(ALL, None),
        P(ALL),
        P(ALL, None),
        P("expert", DP, None),
        P("expert", DP, None),
        P("expert", DP, None),
        P(None, DP, None, None),
        P(None, DP, "expert", None),
        P(None, DP, "expert"),
        P(None, DP, None),
        P(None, DP, "expert", None),
    )
    out_specs = (
        P(None, DP, "expert", None),
        P(None, DP, "expert", None),
        P("expert", DP, None),
        P("expert", DP, None),
        P(ALL, None),
        P(ALL, None),
        P(ALL),
        P(ALL, None),
        P(ALL),
        P(ALL, None),
        P("expert", DP, None),
        P("expert", DP, None),
        P("expert", DP, None),
    )
    return jax.shard_map(body, mesh=shaped, in_specs=in_specs, out_specs=out_specs, check_vma=False)
```

```python
from functools import partial
import math

import jax
import jax.numpy as jnp
from jax import lax
from jax.experimental import pallas as pl
from jax.experimental.pallas import tpu as pltpu
from jax.sharding import Mesh, PartitionSpec as P

HEADS = 16
HDIM = 128
EPSILON = 1e-06
HIGHEST = lax.Precision.HIGHEST
BF16 = jnp.bfloat16
F32 = jnp.float32


def product(left, right):
    return jnp.dot(left, right, preferred_element_type=F32)


def product_tn(left, right):
    return lax.dot_general(left, right, (((0,), (0,)), ((), ())), preferred_element_type=F32)


def product_nt(left, right):
    return lax.dot_general(left, right, (((1,), (1,)), ((), ())), preferred_element_type=F32)


def rms_scaled(values, gain):
    return values * lax.rsqrt(jnp.mean(values * values, axis=-1, keepdims=True) + EPSILON) * gain


def mixture_gates(picked, logits):
    labels = jnp.arange(logits.shape[1], dtype=jnp.int32)
    onehot = (picked[:, :, None] == labels[None, None, :]).astype(F32)
    chosen = jnp.sum(onehot * logits[:, None, :], axis=-1)
    weights = jax.nn.softmax(chosen, axis=-1)
    return jnp.sum(weights[:, :, None] * onehot, axis=1)


def tree_layout(segment_len, tree_len):
    places = jnp.arange(tree_len, dtype=jnp.int32)
    trunk_len = 4 * segment_len
    segment = jnp.where(
        places < trunk_len,
        0,
        jnp.where(
            places < 2 * trunk_len,
            1 + (places - trunk_len) // segment_len,
            5 + (places - 2 * trunk_len) // segment_len,
        ),
    )
    depth = jnp.where(
        places < trunk_len,
        places,
        jnp.where(
            places < 2 * trunk_len,
            trunk_len + (places - trunk_len) % segment_len,
            trunk_len + segment_len + (places - 2 * trunk_len) % segment_len,
        ),
    )
    return (places, segment, depth)


def ancestors(parent, segment):
    labels = jnp.arange(parent.shape[0], dtype=jnp.int32)
    first = jnp.where(labels > 0, parent, -1)
    lookup = jnp.maximum(first, 0)[:, None] == labels[None, :]
    second = jnp.where(first > 0, jnp.sum(jnp.where(lookup, parent[None, :], 0), axis=1), -1)
    member = segment[:, None] == labels[None, :]
    up_one = jnp.sum(jnp.where(member, first[None, :], 0), axis=1)
    up_two = jnp.sum(jnp.where(member, second[None, :], 0), axis=1)
    return (up_one, up_two)


def score_bias(parent, segment, places):
    up_one, up_two = ancestors(parent, segment)
    same = (segment[None, :] == segment[:, None]) & (places[None, :] <= places[:, None])
    seen = same | (segment[None, :] == up_one[:, None]) | (segment[None, :] == up_two[:, None])
    return jnp.where(seen, 0.0, -1e30).astype(F32)


def slot_table(picked, order, experts, capacity):
    labels = jnp.arange(experts, dtype=jnp.int32)
    chosen = jnp.sum((picked[:, :, None] == labels[None, None, :]).astype(F32), axis=1)
    earlier = (order[None, :] < order[:, None]).astype(F32)
    ranks = jnp.dot(earlier, chosen, precision=HIGHEST, preferred_element_type=F32)
    slots = jnp.arange(capacity, dtype=F32)
    return jnp.transpose(chosen)[:, None, :] * (
        jnp.transpose(ranks)[:, None, :] == slots[None, :, None]
    ).astype(F32)


def turn(values, cosine, sine):
    half = values.shape[-1] // 2
    first = values[:, :half]
    second = values[:, half:]
    return jnp.concatenate(
        [first * cosine - second * sine, second * cosine + first * sine], axis=-1
    )


def softmax_rows(queries, keys, bias, scale):
    scores = product_nt(queries, keys) * scale + bias
    highest = jnp.max(scores, axis=-1, keepdims=True)
    weights = jnp.exp(scores - highest)
    return weights / jnp.sum(weights, axis=-1, keepdims=True)


def attend_kernel(heads, scale, raw_ref, kv_ref, cos_ref, sin_ref, bias_ref, query_ref, out_ref):
    quarter, tok = raw_ref.shape[1], raw_ref.shape[3]
    rows = quarter * tok
    cosine, sine, bias = cos_ref[...], sin_ref[...], bias_ref[0, 0]
    for head in range(heads):
        cols = slice(head * HDIM, (head + 1) * HDIM)
        raw = raw_ref[0, :, 0, :, cols].reshape(rows, HDIM)
        keys = kv_ref[0, 0, 0, :, 0, :, cols].reshape(rows, HDIM)
        values = kv_ref[0, 1, 0, :, 0, :, cols].reshape(rows, HDIM)
        queries = turn(raw, cosine, sine).astype(BF16)
        probs = softmax_rows(queries, keys, bias, scale).astype(BF16)
        query_ref[0, :, 0, :, cols] = queries.reshape(quarter, tok, HDIM)
        out_ref[0, :, 0, :, cols] = product(probs, values).astype(BF16).reshape(quarter, tok, HDIM)


def attend_back_kernel(
    heads, scale, query_ref, kv_ref, grad_ref, cos_ref, sin_ref, bias_ref, dq_ref, dkv_ref
):
    quarter, tok = query_ref.shape[1], query_ref.shape[3]
    rows = quarter * tok
    cosine, sine, bias = cos_ref[...], sin_ref[...], bias_ref[0, 0]
    for head in range(heads):
        cols = slice(head * HDIM, (head + 1) * HDIM)
        queries = query_ref[0, :, 0, :, cols].reshape(rows, HDIM)
        keys = kv_ref[0, 0, 0, :, 0, :, cols].reshape(rows, HDIM)
        values = kv_ref[0, 1, 0, :, 0, :, cols].reshape(rows, HDIM)
        grad = grad_ref[0, :, 0, :, cols].reshape(rows, HDIM)
        probs = softmax_rows(queries, keys, bias, scale)
        prob_grad = product_nt(grad, values)
        centre = jnp.sum(prob_grad * probs, axis=-1, keepdims=True)
        score_grad = (probs * (prob_grad - centre) * scale).astype(BF16)
        query_grad = turn(product(score_grad, keys), cosine, -sine).astype(BF16)
        key_grad = turn(product_tn(score_grad, queries), cosine, -sine).astype(BF16)
        value_grad = product_tn(probs.astype(BF16), grad).astype(BF16)
        dq_ref[0, :, 0, :, cols] = query_grad.reshape(quarter, tok, HDIM)
        dkv_ref[0, 0, 0, :, 0, :, cols] = key_grad.reshape(quarter, tok, HDIM)
        dkv_ref[0, 1, 0, :, 0, :, cols] = value_grad.reshape(quarter, tok, HDIM)


def attention_specs(shape, slices):
    pair, quarter, micro, tok, feats = shape
    part = feats // slices
    rows = quarter * tok
    grid = (pair, micro, slices)
    flat = pl.BlockSpec((1, quarter, 1, tok, part), lambda i, m, s: (i, 0, m, 0, s))
    both = pl.BlockSpec(
        (1, 2, 1, quarter, 1, tok, part), lambda i, m, s: (s, 0, i, 0, m, 0, 0)
    )
    angle = pl.BlockSpec((rows, HDIM // 2), lambda i, m, s: (0, 0))
    bias = pl.BlockSpec((1, 1, rows, rows), lambda i, m, s: (i, m, 0, 0))
    return grid, part, flat, both, angle, bias


def attend(raw, kv, cosine, sine, bias, scale):
    slices = kv.shape[0]
    grid, part, flat, both, angle, bias_spec = attention_specs(raw.shape, slices)
    out = jax.ShapeDtypeStruct(raw.shape, BF16)
    return pl.pallas_call(
        partial(attend_kernel, part // HDIM, scale),
        grid=grid,
        in_specs=[flat, both, angle, angle, bias_spec],
        out_specs=[flat, flat],
        out_shape=[out, out],
        cost_estimate=pl.CostEstimate(
            flops=4 * raw.size * cosine.shape[0],
            bytes_accessed=12 * raw.size,
            transcendentals=raw.size * 2,
        ),
        name="attend",
    )(raw, kv, cosine, sine, bias)


def attend_back(queries, kv, grad, cosine, sine, bias, scale):
    slices = kv.shape[0]
    grid, part, flat, both, angle, bias_spec = attention_specs(queries.shape, slices)
    return pl.pallas_call(
        partial(attend_back_kernel, part // HDIM, scale),
        grid=grid,
        in_specs=[flat, both, flat, angle, angle, bias_spec],
        out_specs=[flat, both],
        out_shape=[
            jax.ShapeDtypeStruct(queries.shape, BF16),
            jax.ShapeDtypeStruct(kv.shape, BF16),
        ],
        cost_estimate=pl.CostEstimate(
            flops=10 * queries.size * cosine.shape[0],
            bytes_accessed=14 * queries.size,
            transcendentals=queries.size * 2,
        ),
        name="attend_back",
    )(queries, kv, grad, cosine, sine, bias)


MESH = pl.DeviceIdType.MESH
ANY = pl.BlockSpec(memory_space=pl.ANY)
VMEM = pl.BlockSpec(memory_space=pltpu.VMEM)
DMA = pltpu.SemaphoreType.DMA


def remote(src, dst, send, recv, target):
    return pltpu.make_async_remote_copy(
        src_ref=src, dst_ref=dst, send_sem=send, recv_sem=recv, device_id=target, device_id_type=MESH
    )


def greet(targets):
    barrier = pltpu.get_barrier_semaphore()
    for target in targets:
        pl.semaphore_signal(barrier, inc=1, device_id=target, device_id_type=MESH)
    pl.semaphore_wait(barrier, len(targets))


def params(number, limit=None):
    return pltpu.CompilerParams(
        collective_id=number, has_side_effects=True, vmem_limit_bytes=limit
    )


def add_into(target, sources, rows):
    step = 1
    while step * 2 <= rows and step * 2 * target.shape[-1] <= 65536 and rows % (step * 2) == 0:
        step *= 2

    def one(index, carry):
        where = pl.ds(pl.multiple_of(index * step, step), step)
        total = sources[0][where].astype(F32)
        for source in sources[1:]:
            total = total + source[where].astype(F32)
        target[where] = total.astype(target.dtype)
        return carry

    lax.fori_loop(0, rows // step, one, 0)


def cube_reduce_kernel(pairs, x_ref, o_ref, half, quarter, got_core, got_side, got_pair, send, recv):
    p = lax.axis_index("pair")
    e = lax.axis_index("expert")
    c, y = lax.rem(e, 2), lax.div(e, 2)
    core = {"expert": e + 1 - 2 * c}
    side = {"expert": e + 2 - 4 * y}
    other = {"pair": lax.rem(p + 1, pairs)}
    greet([core, side] + ([other] if pairs == 2 else []))
    rows = x_ref.shape[3]
    shifts = (1, 0) if pairs == 2 else (0,)
    order = [(dx, dy) for dy in (1, 0) for dx in shifts]
    first, second = [], {}
    for slot, (dx, dy) in enumerate(order):
        px, yy = lax.rem(p + dx, pairs), lax.rem(y + dy, 2)
        copy = remote(
            x_ref.at[px, yy, 1 - c], got_core.at[slot], send.at[slot], recv.at[slot], core
        )
        copy.start()
        first.append(copy)
    base = len(order)
    for slot, (dx, dy) in enumerate(order):
        px, yy = lax.rem(p + dx, pairs), lax.rem(y + dy, 2)
        first[slot].wait_recv()
        add_into(half.at[slot], [x_ref.at[px, yy, c], got_core.at[slot]], rows)
        if dy == 1:
            copy = remote(
                half.at[slot], got_side.at[dx], send.at[base + dx], recv.at[base + dx], side
            )
            copy.start()
            second[dx] = copy
    last = None
    for dx in shifts:
        second[dx].wait_recv()
        if dx == 1:
            add_into(quarter, [half.at[order.index((1, 0))], got_side.at[1]], rows)
            last = remote(quarter, got_pair, send.at[base + 2], recv.at[base + 2], other)
            last.start()
    if last is not None:
        last.wait_recv()
        add_into(o_ref, [half.at[order.index((0, 0))], got_side.at[0], got_pair], rows)
    else:
        add_into(o_ref, [half.at[order.index((0, 0))], got_side.at[0]], rows)
    for copy in first + list(second.values()) + ([last] if last is not None else []):
        copy.wait_send()


def cube_reduce(value, pairs, number):
    _, rows, cols = value.shape
    value = value.reshape(pairs, 2, 2, rows, cols)
    slots = 2 * pairs
    block = jax.ShapeDtypeStruct((rows, cols), value.dtype)
    return pl.pallas_call(
        partial(cube_reduce_kernel, pairs),
        in_specs=[VMEM],
        out_specs=VMEM,
        out_shape=block,
        scratch_shapes=[
            pltpu.VMEM((slots, rows, cols), value.dtype),
            pltpu.VMEM((rows, cols), value.dtype),
            pltpu.VMEM((slots, rows, cols), value.dtype),
            pltpu.VMEM((pairs, rows, cols), value.dtype),
            pltpu.VMEM((rows, cols), value.dtype),
            DMA((slots + 3,)),
            DMA((slots + 3,)),
        ],
        compiler_params=params(number, 48 * 2**20),
        cost_estimate=pl.CostEstimate(flops=0, bytes_accessed=0, transcendentals=0),
        name="cube_reduce",
    )(value)


def cube_gather_kernel(pairs, x_ref, o_ref, send, recv, local):
    p = lax.axis_index("pair") if pairs == 2 else 0
    e = lax.axis_index("expert")
    c, y = lax.rem(e, 2), lax.div(e, 2)
    core = {"expert": e + 1 - 2 * c}
    side = {"expert": e + 2 - 4 * y}
    other = {"pair": lax.rem(p + 1, pairs)}
    greet([core, side] + ([other] if pairs == 2 else []))
    q, w = lax.rem(p + 1, pairs), 1 - y
    own = o_ref.at[p, y, c]
    keep = pltpu.make_async_copy(x_ref, own, local)
    keep.start()
    copies = []

    def push(slot, source, place, target):
        copy = remote(source, place, send.at[slot], recv.at[slot], target)
        copy.start()
        copies.append(copy)
        return copy

    to_side = push(0, x_ref, own, side)
    to_other = push(1, x_ref, own, other) if pairs == 2 else None
    to_core = push(2, x_ref, own, core)
    waits = [to_core]
    if pairs == 2:
        to_other.wait_recv()
        block = o_ref.at[q, y, c]
        far = push(3, block, block, side)
        waits.append(push(4, block, block, core))
    to_side.wait_recv()
    block = o_ref.at[p, w, c]
    waits.append(push(5, block, block, core))
    if pairs == 2:
        far.wait_recv()
        block = o_ref.at[q, w, c]
        waits.append(push(6, block, block, core))
    for copy in waits:
        copy.wait_recv()
    for copy in copies:
        copy.wait_send()
    keep.wait()


def cube_gather(value, pairs, number):
    return pl.pallas_call(
        partial(cube_gather_kernel, pairs),
        in_specs=[VMEM],
        out_specs=VMEM,
        out_shape=jax.ShapeDtypeStruct((pairs, 2, 2) + value.shape, value.dtype),
        scratch_shapes=[DMA((7,)), DMA((7,)), DMA(())],
        compiler_params=params(number, 48 * 2**20),
        cost_estimate=pl.CostEstimate(
            flops=0, bytes_accessed=80 * value.size, transcendentals=0
        ),
        name="cube_gather",
    )(value)


def place_of(index, sizes):
    line, pairs, experts = sizes
    return {
        "line": index // (pairs * experts),
        "pair": (index // experts) % pairs,
        "expert": index % experts,
    }


def small_kernel(sizes, reduce, x_ref, o_ref, got, send, recv):
    line, pairs, experts = sizes
    count = line * pairs * experts
    me = (
        lax.axis_index("line") * (pairs * experts)
        + lax.axis_index("pair") * experts
        + lax.axis_index("expert")
    )
    barrier = pltpu.get_barrier_semaphore()

    def greet_one(offset, carry):
        target = place_of((me + offset) % count, sizes)
        pl.semaphore_signal(barrier, inc=1, device_id=target, device_id_type=MESH)
        return carry

    lax.fori_loop(1, count, greet_one, 0)
    pl.semaphore_wait(barrier, count - 1)

    def copy_to(offset):
        peer = (me + offset) % count
        source = x_ref.at[peer] if reduce else x_ref
        return remote(source, got.at[offset], send.at[offset], recv.at[offset], place_of(peer, sizes))

    def start(offset, carry):
        copy_to(offset).start()
        return carry

    lax.fori_loop(1, count, start, 0)
    got[0] = x_ref[me] if reduce else x_ref[...]

    def finish(offset, carry):
        copy_to(offset).wait()
        return carry

    lax.fori_loop(1, count, finish, 0)
    if reduce:
        o_ref[...] = jnp.sum(got[...], axis=0)
    else:

        def order(offset, carry):
            o_ref[(me - offset + count) % count] = got[offset]
            return carry

        lax.fori_loop(0, count, order, 0)


def small_exchange(value, sizes, reduce, number):
    count = sizes[0] * sizes[1] * sizes[2]
    block = value.shape[1:] if reduce else value.shape
    return pl.pallas_call(
        partial(small_kernel, sizes, reduce),
        in_specs=[VMEM],
        out_specs=VMEM,
        out_shape=jax.ShapeDtypeStruct(block if reduce else (count,) + block, value.dtype),
        scratch_shapes=[pltpu.VMEM((count,) + block, value.dtype), DMA((count,)), DMA((count,))],
        compiler_params=params(number),
        cost_estimate=pl.CostEstimate(flops=0, bytes_accessed=2**24, transcendentals=0),
        name="small_reduce" if reduce else "small_gather",
    )(value)


def ff_kernel(
    a_in, b_in, gate_hbm, up_hbm, down_hbm,
    a_out, b_out, a_save, b_save, inner_save, dgate_save, dup_save,
    a_buf, b_buf, side, hop, extra, w_gate, w_up, w_down, mid, acc,
    send, recv, load, store, local,
):
    z, p, e = lax.axis_index("line"), lax.axis_index("pair"), lax.axis_index("expert")
    line, _, rows, width = a_buf.shape
    experts, size = a_in.shape[0], a_in.shape[1]
    q = 1 - p
    twin = z + 1 - 2 * (z % 2)
    up, down, other, across = {"line": z + 1}, {"line": z - 1}, {"pair": q}, {"line": twin}
    ins, bufs, outs, saves = (a_in, b_in), (a_buf, b_buf), (a_out, b_out), (a_save, b_save)
    high = z // 2
    near = z + high * (line - 1 - 2 * z)

    def order(t):
        j = t + near * (1 - t // 2) * (1 - 2 * t)
        return j + high * (line - 1 - 2 * j)

    weights = [
        pltpu.make_async_copy(src, dst, load.at[i])
        for i, (src, dst) in enumerate(((gate_hbm, w_gate), (up_hbm, w_up), (down_hbm, w_down)))
    ]
    for copy in weights:
        copy.start()

    barrier = pltpu.get_barrier_semaphore()
    for shift in range(1, experts):
        pl.semaphore_signal(
            barrier, inc=1, device_id={"expert": (e + shift) % experts}, device_id_type=MESH
        )
    pl.semaphore_signal(barrier, inc=1, device_id=other, device_id_type=MESH)

    @pl.when(z > 0)
    def _():
        pl.semaphore_signal(barrier, inc=1, device_id=down, device_id_type=MESH)

    @pl.when(z < line - 1)
    def _():
        pl.semaphore_signal(barrier, inc=1, device_id=up, device_id_type=MESH)

    below, above = (z + line - 1) // line, (2 * line - 2 - z) // line
    pl.semaphore_wait(barrier, experts + below + above)

    UP, DOWN, SIDE, SUMUP, SUMDOWN, SUMSIDE = (i * line for i in range(6))
    TWIN, SUMTWIN, SWAP = 6 * line, 6 * line + 1, 6 * line + 2
    BACK = SWAP + experts

    def push(src, dst, kind, use, target):
        return remote(src, dst, send.at[kind, use], recv.at[kind, use], target)

    def to_up(kind, j):
        return push(bufs[kind].at[j, p], bufs[kind].at[j, p], kind, UP + j, up)

    def to_down(kind, j):
        return push(bufs[kind].at[j, p], bufs[kind].at[j, p], kind, DOWN + j, down)

    def to_other(kind, j):
        return push(bufs[kind].at[j, p], bufs[kind].at[j, p], kind, SIDE + j, other)

    def to_twin():
        return push(bufs[1].at[z, q], bufs[1].at[z, q], 1, TWIN, across)

    def sum_up(kind, j):
        return push(bufs[kind].at[j, p], hop.at[kind, j], kind, SUMUP + j, up)

    def sum_down(kind, j, slot):
        return push(bufs[kind].at[j, p], hop.at[kind, slot], kind, SUMDOWN + j, down)

    def sum_other(kind, j):
        return push(bufs[kind].at[j, q], side.at[kind, j], kind, SUMSIDE + j, other)

    def sum_twin():
        return push(bufs[1].at[twin, q], extra, 1, SUMTWIN, across)

    def piece(index):
        return pl.ds(pl.multiple_of(index * size, size), size)

    def save(kind, j, column):
        return pltpu.make_async_copy(
            bufs[kind].at[j, column], saves[kind].at[j, column], store.at[kind, j, column]
        )

    swaps = []
    for kind in range(2):
        home = bufs[kind].at[z, p, piece(e)]
        keep = pltpu.make_async_copy(ins[kind].at[e], home, local.at[kind])
        keep.start()
        group = []
        for shift in range(1, experts):
            peer = (e + shift) % experts
            copy = push(ins[kind].at[peer], home, kind, SWAP + shift, {"expert": peer})
            copy.start()
            group.append(copy)
        swaps.append((keep, group))

    def spread(t, first=False):
        j = order(t)
        for kind in range(2):
            if first:
                swaps[kind][0].wait()
                for copy in swaps[kind][1]:
                    copy.wait_recv()
            else:

                @pl.when(j < z)
                def _():
                    to_up(kind, j).wait_recv()

                @pl.when(j > z)
                def _():
                    to_down(kind, j).wait_recv()

            @pl.when((j <= z) & (z < line - 1))
            def _():
                to_up(kind, j).start()

            @pl.when((j >= z) & (z > 0))
            def _():
                to_down(kind, j).start()

            if kind == 0:
                to_other(kind, j).start()
            else:

                @pl.when(j != twin)
                def _():
                    to_other(kind, j).start()

            save(kind, j, p).start()

    chunk = 512
    steps = width // chunk

    def first_half(j, column):
        for index in range(3):
            acc[index] = jnp.zeros(acc.shape[1:], F32)

        def one(k, carry):
            where = pl.ds(pl.multiple_of(k * chunk, chunk), chunk)
            left = a_buf[j, column, :, where]
            acc[0] += product_nt(left, w_gate[:, where])
            acc[1] += product_nt(left, w_up[:, where])
            acc[2] += product_nt(b_buf[j, column, :, where], w_down[:, where])
            return carry

        lax.fori_loop(0, steps, one, 0)
        part = 32

        def two(i, carry):
            where = pl.ds(pl.multiple_of(i * part, part), part)
            gate, lift, grad = acc[0, where], acc[1, where], acc[2, where]
            sigma = jax.nn.sigmoid(gate)
            mid[j, column, 0, where] = (gate * sigma * lift).astype(BF16)
            mid[j, column, 1, where] = (
                grad * lift * sigma * (1.0 + gate * (1.0 - sigma))
            ).astype(BF16)
            mid[j, column, 2, where] = (grad * gate * sigma).astype(BF16)
            return carry

        lax.fori_loop(0, rows // part, two, 0)

    def second_half(j, column):
        def one(k, carry):
            where = pl.ds(pl.multiple_of(k * chunk, chunk), chunk)
            a_buf[j, column, :, where] = product(mid[j, column, 0], w_down[:, where]).astype(BF16)
            b_buf[j, column, :, where] = (
                product(mid[j, column, 1], w_gate[:, where])
                + product(mid[j, column, 2], w_up[:, where])
            ).astype(BF16)
            return carry

        lax.fori_loop(0, steps, one, 0)

    def arrive(j):
        for kind in range(2):
            if kind == 0:
                to_other(kind, j).wait_recv()
            else:

                @pl.when(j != twin)
                def _():
                    to_other(kind, j).wait_recv()

                @pl.when(j == twin)
                def _():
                    to_twin().wait_recv()

            save(kind, j, q).start()

        @pl.when(j == z)
        def _():
            to_twin().start()

    def emit(t):
        j = order(t)
        sum_other(0, j).start()

        @pl.when((j != twin) & (j != z))
        def _():
            sum_other(1, j).start()

    def step(s, carry):
        @pl.when(s == 0)
        def _():
            spread(0, True)
            for copy in weights:
                copy.wait()

        @pl.when(s == 1)
        def _():
            spread(1)
            spread(2)

        @pl.when(s == 3)
        def _():
            spread(3)

        @pl.when(s == line)
        def _():
            sum_twin().start()

        def half(c, inner_carry):
            t = s - c
            column = p + c * (q - p)

            @pl.when((t >= 0) & (t < line))
            def _():
                j = order(t)

                @pl.when(c == 1)
                def _():
                    arrive(j)

                first_half(j, column)

                @pl.when(c == 1)
                def _():
                    @pl.when(j == z)
                    def _():
                        to_twin().wait_send()

                    for kind in range(2):
                        save(kind, j, q).wait()
                    second_half(j, column)

            return inner_carry

        return lax.fori_loop(0, 2, half, carry)

    lax.fori_loop(0, line + 1, step, 0)

    for t in (3, 2, 1, 0):
        emit(t)

    for copy in (
        pltpu.make_async_copy(mid.at[:, :, 0], inner_save, local.at[2]),
        pltpu.make_async_copy(mid.at[:, :, 1], dgate_save, local.at[3]),
        pltpu.make_async_copy(mid.at[:, :, 2], dup_save, local.at[4]),
    ):
        copy.start()
    sum_twin().wait_recv()
    add_into(b_buf.at[z, q], [b_buf.at[z, q], extra], rows)
    sum_other(1, z).start()

    def back(kind):
        own = pltpu.make_async_copy(
            bufs[kind].at[z, p, piece(e)], outs[kind].at[e], local.at[kind]
        )
        return [own] + [
            push(
                bufs[kind].at[z, p, piece((e + shift) % experts)],
                outs[kind].at[e],
                kind,
                BACK + shift,
                {"expert": (e + shift) % experts},
            )
            for shift in range(1, experts)
        ]

    def fold(s, carry):
        t = line - 1 - s
        j = order(t)
        for kind in range(2):
            save(kind, j, p).wait()

            @pl.when((j <= z) & (z < line - 1))
            def _():
                to_up(kind, j).wait_send()

            @pl.when((j >= z) & (z > 0))
            def _():
                to_down(kind, j).wait_send()

            if kind == 0:
                to_other(kind, j).wait_send()
            else:

                @pl.when(j != twin)
                def _():
                    to_other(kind, j).wait_send()

        second_half(j, p)
        for kind in range(2):
            mine = bufs[kind].at[j, p]
            if kind == 0:
                sum_other(kind, j).wait_recv()
                add_into(mine, [mine, side.at[kind, j]], rows)
            else:

                @pl.when(j != twin)
                def _():
                    sum_other(kind, j).wait_recv()
                    add_into(mine, [mine, side.at[kind, j]], rows)

            @pl.when((j >= z) & (z > 0))
            def _():
                sum_up(kind, j).wait_recv()
                add_into(mine, [mine, hop.at[kind, j]], rows)

            @pl.when((j < z) & (z < line - 1))
            def _():
                sum_down(kind, j, j).wait_recv()
                add_into(mine, [mine, hop.at[kind, j]], rows)

            @pl.when((j == z) & (z < line - 1))
            def _():
                sum_down(kind, j, line).wait_recv()
                add_into(mine, [mine, hop.at[kind, line]], rows)

            @pl.when(j == z)
            def _():
                for copy in back(kind):
                    copy.start()

            @pl.when(j > z)
            def _():
                sum_up(kind, j).start()

            @pl.when((j < z) & (j != z - 1))
            def _():
                sum_down(kind, j, j).start()

            @pl.when((j < z) & (j == z - 1))
            def _():
                sum_down(kind, j, line).start()

        return carry

    lax.fori_loop(0, line, fold, 0)

    for kind in range(2):
        for copy in back(kind):
            copy.wait()

    def drain(j, carry):
        for kind in range(2):
            if kind == 0:
                sum_other(kind, j).wait_send()
            else:

                @pl.when(j != twin)
                def _():
                    sum_other(kind, j).wait_send()

            @pl.when(j > z)
            def _():
                sum_up(kind, j).wait_send()

            @pl.when(j < z)
            def _():
                sum_down(kind, j, j).wait_send()

        return carry

    lax.fori_loop(0, line, drain, 0)
    sum_twin().wait_send()
    for copy in (
        pltpu.make_async_copy(mid.at[:, :, 0], inner_save, local.at[2]),
        pltpu.make_async_copy(mid.at[:, :, 1], dgate_save, local.at[3]),
        pltpu.make_async_copy(mid.at[:, :, 2], dup_save, local.at[4]),
    ):
        copy.wait()
    for keep, group in swaps:
        for copy in group:
            copy.wait_send()


def feed_forward(first, second, w_gate, w_up, w_down, line, pairs, number):
    experts, size, width = first.shape
    hidden = w_gate.shape[0]
    rows = experts * size
    blocks = (line, pairs, rows)
    back = jax.ShapeDtypeStruct(first.shape, BF16)
    wide = jax.ShapeDtypeStruct(blocks + (width,), BF16)
    thin = jax.ShapeDtypeStruct(blocks + (hidden,), BF16)
    uses = 6 * line + 2 + 2 * experts
    total = line * pairs * rows
    return pl.pallas_call(
        ff_kernel,
        in_specs=[ANY] * 5,
        out_specs=[ANY] * 7,
        out_shape=[back, back, wide, wide, thin, thin, thin],
        scratch_shapes=[
            pltpu.VMEM(blocks + (width,), BF16),
            pltpu.VMEM(blocks + (width,), BF16),
            pltpu.VMEM((2, line, rows, width), BF16),
            pltpu.VMEM((2, line + 1, rows, width), BF16),
            pltpu.VMEM((rows, width), BF16),
            pltpu.VMEM((hidden, width), BF16),
            pltpu.VMEM((hidden, width), BF16),
            pltpu.VMEM((hidden, width), BF16),
            pltpu.VMEM((line, pairs, 3, rows, hidden), BF16),
            pltpu.VMEM((3, rows, hidden), F32),
            DMA((2, uses)),
            DMA((2, uses)),
            DMA((3,)),
            DMA((2, line, pairs)),
            DMA((5,)),
        ],
        compiler_params=params(number, 63 * 2**20),
        cost_estimate=pl.CostEstimate(
            flops=12 * total * hidden * width,
            bytes_accessed=12 * total * width,
            transcendentals=total * hidden,
        ),
        name="feed_forward",
    )(first, second, w_gate, w_up, w_down)


def end_kernel(
    pairs, x_ref, g_hbm, o_ref, key_ref, value_ref,
    g_ref, k_ref, half, quarter, got_core, got_side, got_pair, hop, send, recv, local,
):
    z, p, e = lax.axis_index("line"), lax.axis_index("pair"), lax.axis_index("expert")
    line, span, _ = g_ref.shape
    trees, piece, _ = k_ref.shape
    c, y = e % 2, e // 2
    core, side = {"expert": e + 1 - 2 * c}, {"expert": e + 2 - 4 * y}
    other, up, down = {"pair": 1 - p}, {"line": z + 1}, {"line": z - 1}
    experts = trees // pairs
    me = p * experts + e
    high = z // 2
    near = z + high * (line - 1 - 2 * z)

    def order(t):
        j = t + near * (1 - t // 2) * (1 - 2 * t)
        return j + high * (line - 1 - 2 * j)

    def place(index):
        return {"pair": index // experts, "expert": index % experts}

    fetch = pltpu.make_async_copy(g_hbm, g_ref, local)
    fetch.start()
    barrier = pltpu.get_barrier_semaphore()
    for shift in range(1, trees):
        pl.semaphore_signal(
            barrier, inc=1, device_id=place((me + shift) % trees), device_id_type=MESH
        )

    @pl.when(z > 0)
    def _():
        pl.semaphore_signal(barrier, inc=1, device_id=down, device_id_type=MESH)

    @pl.when(z < line - 1)
    def _():
        pl.semaphore_signal(barrier, inc=1, device_id=up, device_id_type=MESH)

    below, above = (z + line - 1) // line, (2 * line - 2 - z) // line
    pl.semaphore_wait(barrier, trees - 1 + below + above)
    UP, DOWN, SWAP = 7, 7 + line, 7 + 2 * line
    rows = x_ref.shape[3]

    def sum_up(j):
        return remote(g_ref.at[j], hop.at[j], send.at[UP + j], recv.at[UP + j], up)

    def sum_down(j, slot):
        return remote(g_ref.at[j], hop.at[slot], send.at[DOWN + j], recv.at[DOWN + j], down)

    def fold(t):
        j = order(t)
        mine = g_ref.at[j]

        @pl.when((j >= z) & (z > 0))
        def _():
            sum_up(j).wait_recv()
            add_into(mine, [mine, hop.at[j]], span)

        @pl.when((j < z) & (z < line - 1))
        def _():
            sum_down(j, j).wait_recv()
            add_into(mine, [mine, hop.at[j]], span)

        @pl.when((j == z) & (z < line - 1))
        def _():
            sum_down(j, line).wait_recv()
            add_into(mine, [mine, hop.at[line]], span)

        @pl.when(j > z)
        def _():
            sum_up(j).start()

        @pl.when((j < z) & (j != z - 1))
        def _():
            sum_down(j, j).start()

        @pl.when((j < z) & (j == z - 1))
        def _():
            sum_down(j, line).start()

    corners = [(1, 1), (0, 1), (1, 0), (0, 0)]
    first, second = [], {}
    for slot, (dx, dy) in enumerate(corners):
        copy = remote(
            x_ref.at[(p + dx) % 2, (y + dy) % 2, 1 - c],
            got_core.at[slot],
            send.at[slot],
            recv.at[slot],
            core,
        )
        copy.start()
        first.append(copy)
    fetch.wait()
    fold(3)
    for slot, (dx, dy) in enumerate(corners):
        first[slot].wait_recv()
        add_into(
            half.at[slot], [x_ref.at[(p + dx) % 2, (y + dy) % 2, c], got_core.at[slot]], rows
        )
        if dy == 1:
            second[dx] = remote(
                half.at[slot], got_side.at[dx], send.at[4 + dx], recv.at[4 + dx], side
            )
            second[dx].start()
    fold(2)
    second[1].wait_recv()
    add_into(quarter, [half.at[2], got_side.at[1]], rows)
    last = remote(quarter, got_pair, send.at[6], recv.at[6], other)
    last.start()
    fold(1)
    second[0].wait_recv()
    last.wait_recv()
    add_into(o_ref, [half.at[3], got_side.at[0], got_pair], rows)
    fold(0)

    def part(index):
        return g_ref.at[z, pl.ds(pl.multiple_of(index * piece, piece), piece)]

    keep = pltpu.make_async_copy(part(me), k_ref.at[me], local)
    keep.start()
    swaps = []
    for shift in range(1, trees):
        peer = (me + shift) % trees
        copy = remote(
            part(peer), k_ref.at[me], send.at[SWAP + shift], recv.at[SWAP + shift], place(peer)
        )
        copy.start()
        swaps.append(copy)
    for copy in swaps:
        copy.wait()
    keep.wait()
    share = k_ref.shape[2] // 2
    for source in range(trees):
        column = ((source % experts) * pairs + source // experts) * share
        for index, target in enumerate((key_ref, value_ref)):
            target[:, column : column + share] = k_ref[
                source, :, index * share : (index + 1) * share
            ].astype(F32)
    for copy in first + list(second.values()) + [last]:
        copy.wait_send()

    def drain(j, carry):
        @pl.when(j > z)
        def _():
            sum_up(j).wait_send()

        @pl.when(j < z)
        def _():
            sum_down(j, j).wait_send()

        return carry

    lax.fori_loop(0, line, drain, 0)


def end_exchange(value, grads, line, pairs, number):
    trees, rows, cols = value.shape
    span, thin = grads.shape[0] // line, grads.shape[1]
    uses = 7 + 2 * line + trees
    block = pltpu.VMEM((rows, cols), BF16)
    return pl.pallas_call(
        partial(end_kernel, pairs),
        in_specs=[VMEM, ANY],
        out_specs=[VMEM] * 3,
        out_shape=[jax.ShapeDtypeStruct((rows, cols), BF16)]
        + [jax.ShapeDtypeStruct((span // trees, trees * thin // 2), F32)] * 2,
        scratch_shapes=[
            pltpu.VMEM((line, span, thin), BF16),
            pltpu.VMEM((trees, span // trees, thin), BF16),
            pltpu.VMEM((4, rows, cols), BF16),
            block,
            pltpu.VMEM((4, rows, cols), BF16),
            pltpu.VMEM((2, rows, cols), BF16),
            block,
            pltpu.VMEM((line + 1, span, thin), BF16),
            DMA((uses,)),
            DMA((uses,)),
            DMA(()),
        ],
        compiler_params=params(number, 48 * 2**20),
        cost_estimate=pl.CostEstimate(flops=0, bytes_accessed=0, transcendentals=0),
        name="end_exchange",
    )(value.reshape(pairs, 2, 2, rows, cols), grads.reshape(line, span, thin))


def final_kernel(sizes, x_ref, q_ref, o_ref, w_ref, got, side, send, recv, pair_send, pair_recv):
    line, pairs, experts = sizes
    count = line * pairs * experts
    p = lax.axis_index("pair")
    me = lax.axis_index("line") * (pairs * experts) + p * experts + lax.axis_index("expert")
    barrier = pltpu.get_barrier_semaphore()

    def greet_one(offset, carry):
        target = place_of((me + offset) % count, sizes)
        pl.semaphore_signal(barrier, inc=1, device_id=target, device_id_type=MESH)
        return carry

    lax.fori_loop(1, count, greet_one, 0)
    pl.semaphore_wait(barrier, count - 1)
    swap = remote(q_ref.at[1 - p], side, pair_send, pair_recv, {"pair": 1 - p})
    swap.start()

    def copy_to(offset):
        peer = (me + offset) % count
        return remote(
            x_ref.at[peer], got.at[offset], send.at[offset], recv.at[offset], place_of(peer, sizes)
        )

    def start(offset, carry):
        copy_to(offset).start()
        return carry

    lax.fori_loop(1, count, start, 0)
    got[0] = x_ref[me]
    part = q_ref.shape[2] // line

    def lay(block, source):
        for index in range(line):
            column = pl.multiple_of((index * pairs + source) * part, part)
            w_ref[:, pl.ds(column, part)] = block[:, index * part : (index + 1) * part].astype(F32)

    lay(q_ref.at[p], p)
    swap.wait_recv()
    lay(side, 1 - p)

    def finish(offset, carry):
        copy_to(offset).wait()
        return carry

    lax.fori_loop(1, count, finish, 0)
    o_ref[...] = jnp.sum(got[...], axis=0)
    swap.wait_send()


def final_exchange(sums, grads, sizes, number):
    count, block = sums.shape[0], sums.shape[1:]
    pairs, rows, cols = grads.shape
    return pl.pallas_call(
        partial(final_kernel, sizes),
        in_specs=[VMEM, VMEM],
        out_specs=[VMEM, VMEM],
        out_shape=[
            jax.ShapeDtypeStruct(block, F32),
            jax.ShapeDtypeStruct((rows, pairs * cols), F32),
        ],
        scratch_shapes=[
            pltpu.VMEM((count,) + block, F32),
            pltpu.VMEM((rows, cols), BF16),
            DMA((count,)),
            DMA((count,)),
            DMA(()),
            DMA(()),
        ],
        compiler_params=params(number, 32 * 2**20),
        name="final_exchange",
    )(sums, grads)


def start_all_kernel(
    sizes, tok_ref, wq_ref, wk_ref, wv_ref, small_ref, int_ref,
    tok_out, q_out, kv_out, small_out, int_out,
    q_cut, kv_cut, send, recv, peer_send, peer_recv, local,
):
    line, pairs, experts = sizes
    z, p, e = lax.axis_index("line"), lax.axis_index("pair"), lax.axis_index("expert")
    c, y = e % 2, e // 2
    core, side = {"expert": e + 1 - 2 * c}, {"expert": e + 2 - 4 * y}
    other = {"pair": 1 - p}
    trees = pairs * experts
    count = line * trees
    mine = p * experts + e
    me = z * trees + mine
    barrier = pltpu.get_barrier_semaphore()

    def greet_one(offset, carry):
        target = place_of((me + offset) % count, sizes)
        pl.semaphore_signal(barrier, inc=1, device_id=target, device_id_type=MESH)
        return carry

    lax.fori_loop(1, count, greet_one, 0)
    part = wq_ref.shape[1] // (line * pairs)
    for q in range(pairs):
        for index in range(line):
            column = (index * pairs + q) * part
            q_cut[q, :, index * part : (index + 1) * part] = wq_ref[:, column : column + part]
    sub = line // experts
    for q in range(pairs):
        for d in range(experts):
            for index, ref in enumerate((wk_ref, wv_ref)):
                for h in range(sub):
                    column = ((d * sub + h) * pairs + q) * part
                    place = (index * sub + h) * part
                    kv_cut[q * experts + d, :, place : place + part] = ref[
                        :, column : column + part
                    ]
    pl.semaphore_wait(barrier, count - 1)

    copies, TOK, QSWAP, INTS, KV = [], 0, 7, 8, 9
    WALK = KV + trees

    def push(slot, source, place, target):
        copy = remote(source, place, send.at[slot], recv.at[slot], target)
        copy.start()
        copies.append(copy)
        return copy

    rows = q_cut.shape[1]
    q_home = q_out.at[z, pl.ds(pl.multiple_of(p * rows, rows), rows)]
    q_swap = push(QSWAP, q_cut.at[1 - p], q_home, other)
    size = kv_cut.shape[1]
    kv_home = kv_out.at[z, pl.ds(pl.multiple_of(mine * size, size), size)]
    pieces = []
    for shift in range(1, trees):
        peer = (mine + shift) % trees
        pieces.append(
            push(
                KV + shift,
                kv_cut.at[peer],
                kv_home,
                {"pair": peer // experts, "expert": peer % experts},
            )
        )
    keeps = [
        pltpu.make_async_copy(q_cut.at[p], q_home, local.at[0]),
        pltpu.make_async_copy(kv_cut.at[mine], kv_home, local.at[1]),
        pltpu.make_async_copy(tok_ref, tok_out.at[p, y, c], local.at[2]),
        pltpu.make_async_copy(small_ref, small_out.at[me], local.at[3]),
        pltpu.make_async_copy(int_ref, int_out.at[p], local.at[4]),
    ]
    for copy in keeps:
        copy.start()
    own = tok_out.at[p, y, c]
    to_side = push(TOK, tok_ref, own, side)
    to_other = push(TOK + 1, tok_ref, own, other)
    waits = [push(TOK + 2, tok_ref, own, core), push(INTS, int_ref, int_out.at[p], other)]

    def small_to(offset):
        return remote(
            small_ref,
            small_out.at[me],
            peer_send.at[offset],
            peer_recv.at[offset],
            place_of((me + offset) % count, sizes),
        )

    def small_start(offset, carry):
        small_to(offset).start()
        return carry

    lax.fori_loop(1, count, small_start, 0)

    def walker(ref, base):
        def to_up(j, d):
            return remote(
                ref.at[j], ref.at[j], send.at[base + d], recv.at[base + d], {"line": z + 1}
            )

        def to_down(j, d):
            at = base + line + d
            return remote(ref.at[j], ref.at[j], send.at[at], recv.at[at], {"line": z - 1})

        return to_up, to_down

    walkers = [walker(q_out, WALK), walker(kv_out, WALK + 2 * line + 2)]

    def begin(which):
        to_up, to_down = walkers[which]

        @pl.when(z < line - 1)
        def _():
            to_up(z, 1).start()

        @pl.when(z > 0)
        def _():
            to_down(z, 1).start()

    keeps[0].wait()
    q_swap.wait_recv()
    begin(0)
    keeps[1].wait()
    for copy in pieces:
        copy.wait_recv()
    begin(1)
    to_other.wait_recv()
    block = tok_out.at[1 - p, y, c]
    far = push(TOK + 3, block, block, side)
    waits.append(push(TOK + 4, block, block, core))
    to_side.wait_recv()
    block = tok_out.at[p, 1 - y, c]
    waits.append(push(TOK + 5, block, block, core))
    far.wait_recv()
    block = tok_out.at[1 - p, 1 - y, c]
    waits.append(push(TOK + 6, block, block, core))

    for d in range(1, line):
        for to_up, to_down in walkers:

            @pl.when(z - d >= 0)
            def _():
                to_up(z - d, d).wait_recv()

                @pl.when(z < line - 1)
                def _():
                    to_up(z - d, d + 1).start()

            @pl.when(z + d < line)
            def _():
                to_down(z + d, d).wait_recv()

                @pl.when(z > 0)
                def _():
                    to_down(z + d, d + 1).start()

    for d in range(1, line):
        for to_up, to_down in walkers:

            @pl.when((z - d + 1 >= 0) & (z < line - 1))
            def _():
                to_up(z - d + 1, d).wait_send()

            @pl.when((z + d - 1 < line) & (z > 0))
            def _():
                to_down(z + d - 1, d).wait_send()

    for copy in waits:
        copy.wait_recv()
    for copy in copies:
        copy.wait_send()
    for copy in keeps[2:]:
        copy.wait()

    def small_finish(offset, carry):
        small_to(offset).wait()
        return carry

    lax.fori_loop(1, count, small_finish, 0)


def start_all(tokens, w_query, w_key, w_value, small, integers, sizes, number):
    line, pairs, experts = sizes
    trees = pairs * experts
    count = line * trees
    rows, width = w_query.shape
    size = w_key.shape[0]
    feats = width // pairs
    thin = 2 * feats // experts
    uses = 9 + trees + 4 * line + 4
    return pl.pallas_call(
        partial(start_all_kernel, sizes),
        in_specs=[VMEM] * 6,
        out_specs=[VMEM] * 5,
        out_shape=[
            jax.ShapeDtypeStruct((pairs, 2, 2) + tokens.shape, BF16),
            jax.ShapeDtypeStruct((line, pairs * rows, feats), BF16),
            jax.ShapeDtypeStruct((line, trees * size, thin), BF16),
            jax.ShapeDtypeStruct((count,) + small.shape, BF16),
            jax.ShapeDtypeStruct((pairs,) + integers.shape, jnp.int32),
        ],
        scratch_shapes=[
            pltpu.VMEM((pairs, rows, feats), BF16),
            pltpu.VMEM((trees, size, thin), BF16),
            DMA((uses,)),
            DMA((uses,)),
            DMA((count,)),
            DMA((count,)),
            DMA((5,)),
        ],
        compiler_params=params(number, 48 * 2**20),
        name="start_all",
    )(tokens, w_query, w_key, w_value, small, integers)


def project_kernel(micro, x_ref, w_ref, gain_ref, router_ref, cos_ref, sin_ref, n_ref, kv_ref, l_ref):
    x = x_ref[...].astype(F32)
    scale = lax.rsqrt(jnp.mean(x * x, axis=-1, keepdims=True) + EPSILON)
    normed = (x * scale * gain_ref[...]).astype(BF16)
    n_ref[...] = normed
    l_ref[...] = product_nt(normed, router_ref[...])
    raw = product(normed, w_ref[...])
    piece = kv_ref.shape[2]
    spread = lambda ref: jnp.concatenate(
        [ref[i] for i in range(ref.shape[0]) for _ in range(micro)], axis=0
    )
    cosine, sine = spread(cos_ref), spread(sin_ref)
    for head in range(piece // HDIM):
        cols = slice(head * HDIM, (head + 1) * HDIM)
        kv_ref[0, :, cols] = turn(raw[:, cols], cosine, sine).astype(BF16)
    kv_ref[1] = raw[:, piece:].astype(BF16)


def project(tokens, weight, gain, router, cosine, sine, micro):
    rows, width = tokens.shape
    piece = weight.shape[1] // 2
    experts, tok, half = cosine.shape
    block = 2 * micro * tok
    loops = experts // 2
    return pl.pallas_call(
        partial(project_kernel, micro),
        grid=(rows // block,),
        in_specs=[
            pl.BlockSpec((block, width), lambda i: (i, 0)),
            pl.BlockSpec(weight.shape, lambda i: (0, 0)),
            pl.BlockSpec((1, width), lambda i: (0, 0)),
            pl.BlockSpec(router.shape, lambda i: (0, 0)),
            pl.BlockSpec((2, tok, half), lambda i: (i % loops, 0, 0)),
            pl.BlockSpec((2, tok, half), lambda i: (i % loops, 0, 0)),
        ],
        out_specs=[
            pl.BlockSpec((block, width), lambda i: (i, 0)),
            pl.BlockSpec((2, block, piece), lambda i: (0, i, 0)),
            pl.BlockSpec((block, experts), lambda i: (i, 0)),
        ],
        out_shape=[
            jax.ShapeDtypeStruct((rows, width), BF16),
            jax.ShapeDtypeStruct((2, rows, piece), BF16),
            jax.ShapeDtypeStruct((rows, experts), F32),
        ],
        compiler_params=pltpu.CompilerParams(vmem_limit_bytes=40 * 2**20),
        cost_estimate=pl.CostEstimate(
            flops=2 * rows * width * weight.shape[1], bytes_accessed=5 * rows * width, transcendentals=0
        ),
        name="project",
    )(tokens, weight, gain, router, cosine, sine)


def gather(value, axes, axis=0):
    return lax.all_gather(value, axes, axis=axis, tiled=True)


def scatter(value, axes, axis=0):
    return lax.psum_scatter(value, axes, scatter_dimension=axis, tiled=True)


def swap(value, axes, split=0, concat=0):
    return lax.all_to_all(value, axes, split_axis=split, concat_axis=concat, tiled=True)


DP = ("line", "pair")
ALL = ("line", "pair", "expert")
TREES = ("pair", "expert")


def body(
    tokens,
    w_query,
    w_out,
    w_key,
    w_value,
    gain_attn,
    router_attn,
    gain_mlp,
    router_mlp,
    w_gate,
    w_up,
    w_down,
    attn_route,
    mlp_route,
    fill_order,
    parents,
    cotangent,
):
    experts = lax.axis_size("expert")
    pair = lax.axis_size("pair")
    line = lax.axis_size("line")
    position = lax.axis_index("expert")
    micro, _, tok, width = tokens.shape
    tree = experts * tok
    rows = pair * experts * micro * tok
    heads_total = w_query.shape[2]
    part = heads_total // (line * pair)
    feats = heads_total // pair
    piece = feats // experts
    own_in = w_query.shape[1]
    own_kv = w_key.shape[0]
    capacity = tok * mlp_route.shape[3] // experts
    scale = 1.0 / math.sqrt(HDIM)

    places, segment, depth = tree_layout(tree // 16, tree)
    half = HDIM // 2
    rates = 10000.0 ** (-jnp.arange(half, dtype=F32) / half)
    angle = depth.astype(F32)[:, None] * rates[None, :]
    cosine, sine = jnp.cos(angle), jnp.sin(angle)

    sizes = (line, pair, experts)
    walk = line == 4 and pair == 2 and experts == 4
    own_tokens = tokens.reshape(micro * tok, width)
    small = jnp.concatenate(
        [gain_attn[None], gain_mlp[None], router_attn.T, router_mlp.T], axis=0
    )
    integers = jnp.concatenate([attn_route[:, 0].reshape(micro, -1), parents[:, 0]], axis=1)
    if walk:
        flat = integers.reshape(-1)
        flat = jnp.pad(flat, (0, -flat.shape[0] % 1024)).reshape(-1, 128)
        tree_tokens, query_weight, kv_weight, small, flat = start_all(
            own_tokens, w_query[0], w_key, w_value, small, flat, sizes, 1
        )
        query_weight = query_weight.reshape(width, feats)
        kv_weight = kv_weight.reshape(width, 2 * piece)
        integers = flat.reshape(pair, -1)[:, : integers.size].reshape((pair,) + integers.shape)
    else:
        query_mine = w_query[0].reshape(own_in, line, pair, part)
        query_mine = jnp.transpose(query_mine, (2, 0, 1, 3)).reshape(pair, own_in, feats)
        if pair == 2:
            query_mine = swap(query_mine, "pair")
            integers = lax.all_gather(integers, "pair", axis=0)
        else:
            integers = integers[None]
        query_weight = gather(query_mine.reshape(pair * own_in, feats), "line")
        kv_mine = jnp.stack([w_key, w_value], axis=1).reshape(
            own_kv, 2, experts, line // experts, pair, part
        )
        kv_mine = jnp.transpose(kv_mine, (4, 2, 0, 1, 3, 5)).reshape(
            pair * experts, own_kv, 2 * piece
        )
        tree_tokens = cube_gather(own_tokens, pair, 1)
        small = small_exchange(small, sizes, False, 2)
        kv_mine = swap(kv_mine, TREES).reshape(pair * experts * own_kv, 2 * piece)
        kv_weight = gather(kv_mine, "line")
    out_mine, small = lax.optimization_barrier((w_out[0], small))
    out_weight = gather(out_mine, "line")

    small = jnp.transpose(small, (1, 0, 2)).reshape(-1, width)
    first_gain = small[0].astype(F32)
    second_gain = small[1].astype(F32)
    first_router = small[2 : 2 + experts]
    second_router = small[2 + experts : 2 + 2 * experts]

    residual = own_tokens.astype(F32)
    _, first_pull = jax.vjp(rms_scaled, residual, first_gain)
    table_shape = (experts, tok, half)
    tree_input, kv, first_logits = project(
        tree_tokens.reshape(rows, width),
        kv_weight,
        first_gain[None],
        first_router,
        cosine.reshape(table_shape),
        sine.reshape(table_shape),
        micro,
    )

    routes = integers[..., : tree * 2].reshape(pair, micro, experts, tok, 2)
    routes = jnp.transpose(routes, (0, 2, 1, 3, 4)).reshape(rows, 2)
    family = integers[..., tree * 2 :]
    bias = jax.vmap(jax.vmap(lambda parent: score_bias(parent, segment, places)))(family)

    kv = cube_gather(kv.reshape(2 * rows, piece), 1, 3)
    shape = (pair, experts, micro, tok, feats)
    kv = kv.reshape(experts, 2, pair, experts, micro, tok, piece)

    first_gates, first_gate_pull = jax.vjp(partial(mixture_gates, routes), first_logits)
    column = (jnp.arange(experts, dtype=jnp.int32) == position).astype(F32)
    own_gate = jnp.sum(first_gates * column[None, :], axis=1)

    raw = product(tree_input, query_weight)
    queries, heads_out = attend(raw.reshape(shape), kv, cosine, sine, bias, scale)
    heads_flat = heads_out.reshape(rows, feats)
    projected = product(heads_flat, out_weight)
    gated = (own_gate[:, None] * projected).astype(BF16)
    attention = cube_reduce(gated.reshape(pair * experts, micro * tok, width), pair, 4).astype(F32)

    middle = residual + attention
    second_normed, second_pull = jax.vjp(rms_scaled, middle, second_gain)
    second_normed = second_normed.astype(BF16)
    picked = mlp_route[:, 0].reshape(micro * tok, 2)
    second_gates, second_gate_pull = jax.vjp(
        partial(mixture_gates, picked), product_nt(second_normed, second_router)
    )
    table = jax.vmap(partial(slot_table, experts=experts, capacity=capacity))(
        mlp_route[:, 0], fill_order[:, 0]
    )
    table_low = table.astype(BF16)
    grouped = second_normed.reshape(micro, tok, width)
    outgoing = jnp.einsum("mect,mtd->emcd", table_low, grouped, preferred_element_type=F32)
    top_grad = cotangent.reshape(micro, tok, width)
    slot_values = jnp.einsum("mect,mtd->emcd", table_low, top_grad, preferred_element_type=F32)
    slot_gates = jnp.einsum(
        "mect,mte->emc", table, second_gates.reshape(micro, tok, experts), precision=HIGHEST
    )
    slot_grad = (slot_gates[..., None] * slot_values).astype(BF16)
    slots = experts * micro * capacity
    outgoing = outgoing.astype(BF16).reshape(experts, micro * capacity, width)
    slot_grad = slot_grad.reshape(experts, micro * capacity, width)
    gate_weight, up_weight, down_weight = w_gate[0], w_up[0], w_down[0]
    if walk:
        returned, came_back, arrived, result_grad, inner, gate_grad, up_grad = feed_forward(
            outgoing, slot_grad, gate_weight, up_weight, down_weight, line, pair, 5
        )
        arrived, result_grad, inner, gate_grad, up_grad = (
            value.reshape(-1, value.shape[-1])
            for value in (arrived, result_grad, inner, gate_grad, up_grad)
        )
    else:
        arrived = gather(swap(outgoing, "expert").reshape(slots, width), DP)
        result_grad = gather(swap(slot_grad, "expert").reshape(slots, width), DP)
        gate_pre = product_nt(arrived, gate_weight)
        up_pre = product_nt(arrived, up_weight)
        sigma = jax.nn.sigmoid(gate_pre)
        inner = (gate_pre * sigma * up_pre).astype(BF16)
        returned = product(inner, down_weight).astype(BF16)
        inner_grad = product_nt(result_grad, down_weight)
        gate_grad = (inner_grad * up_pre * sigma * (1.0 + gate_pre * (1.0 - sigma))).astype(BF16)
        up_grad = (inner_grad * gate_pre * sigma).astype(BF16)
        came_back = (product(gate_grad, gate_weight) + product(up_grad, up_weight)).astype(BF16)
        back = (experts, micro * capacity, width)
        returned = swap(scatter(returned, DP).reshape(back), "expert")
        came_back = swap(scatter(came_back, DP).reshape(back), "expert")
    returned = returned.reshape(experts, micro, capacity, width)
    came_back = came_back.reshape(experts, micro, capacity, width)
    spread = jnp.einsum("mect,emcd->emtd", table_low, returned, preferred_element_type=F32)
    spread = spread.reshape(experts, micro * tok, width)
    mixed = jnp.sum(jnp.transpose(second_gates)[:, :, None] * spread, axis=0)
    layer_out = (middle + mixed).astype(BF16)
    dz = top_grad.reshape(micro * tok, width).astype(F32)
    second_gate_grad = jnp.transpose(jnp.sum(spread * dz[None], axis=-1))
    (second_logit_grad,) = second_gate_pull(second_gate_grad)
    hn_grad = jnp.einsum("mect,emcd->mtd", table_low, came_back, preferred_element_type=F32)
    hn_grad = hn_grad.reshape(micro * tok, width)
    second_router_wide = second_router.astype(F32)
    for expert in range(experts):
        hn_grad = hn_grad + second_logit_grad[:, expert : expert + 1] * second_router_wide[expert]
    grad_router_second = jnp.dot(
        jnp.transpose(second_logit_grad),
        second_normed.astype(F32),
        precision=HIGHEST,
        preferred_element_type=F32,
    )
    middle_grad, grad_gain_second = second_pull(hn_grad)
    middle_grad = middle_grad + dz

    mix_grad = gather(middle_grad.astype(BF16), TREES)
    grad_gate = product_tn(gate_grad, arrived)[None]
    grad_upward = product_tn(up_grad, arrived)[None]
    grad_downward = product_tn(inner, result_grad)[None]
    mix_grad, grad_gate, grad_upward, grad_downward = lax.optimization_barrier(
        (mix_grad, grad_gate, grad_upward, grad_downward)
    )
    mix_grad = mix_grad.astype(F32)
    own_gate_grad = jnp.sum(mix_grad * projected, axis=-1)
    projected_grad = (own_gate[:, None] * mix_grad).astype(BF16)
    grad_output = product_tn(heads_flat, projected_grad).astype(BF16)
    grad_output, projected_grad = lax.optimization_barrier((grad_output, projected_grad))
    grad_output = scatter(grad_output, "line")
    heads_grad = product_nt(projected_grad, out_weight).astype(BF16).reshape(shape)
    query_pre, kv_pre = attend_back(queries, kv, heads_grad, cosine, sine, bias, scale)
    query_pre = query_pre.reshape(rows, feats)
    grad_query = product_tn(tree_input, query_pre).astype(BF16)
    grad_query, kv_pre = lax.optimization_barrier((grad_query, kv_pre))
    kv_sum = cube_reduce(kv_pre.reshape(experts, 2 * rows, piece), 1, 8)
    grad_query, grad_output, kv_sum = lax.optimization_barrier((grad_query, grad_output, kv_sum))
    (first_logit_grad,) = first_gate_pull(own_gate_grad[:, None] * column[None, :])
    key_pre, value_pre = kv_sum[:rows], kv_sum[rows:]
    grad_kv = jnp.concatenate(
        [product_tn(tree_input, key_pre), product_tn(tree_input, value_pre)], axis=1
    )
    grad_kv, key_pre, value_pre = lax.optimization_barrier(
        (grad_kv.astype(BF16), key_pre, value_pre)
    )
    input_term = (
        product_nt(query_pre, query_weight)
        + product_nt(key_pre, kv_weight[:, :piece])
        + product_nt(value_pre, kv_weight[:, piece:])
    )
    first_router_wide = first_router.astype(F32)
    for expert in range(experts):
        input_term = input_term + first_logit_grad[:, expert : expert + 1] * first_router_wide[expert]
    input_term = input_term.astype(BF16).reshape(pair * experts, micro * tok, width)
    if walk:
        normed_grad, grad_key, grad_value = end_exchange(input_term, grad_kv, line, pair, 9)
    else:
        normed_grad = cube_reduce(input_term, pair, 9)
        grad_kv = scatter(grad_kv, "line")
        grad_kv = swap(grad_kv.reshape(pair * experts, own_kv, 2 * piece), TREES)
        grad_kv = grad_kv.reshape(pair, experts, own_kv, 2, line // experts, part)
        grad_kv = jnp.transpose(grad_kv, (2, 3, 1, 4, 0, 5)).reshape(own_kv, 2, heads_total)
        grad_key, grad_value = grad_kv[:, 0].astype(F32), grad_kv[:, 1].astype(F32)
    grad_query = scatter(grad_query, "line")
    normed_grad = normed_grad.astype(F32)
    grad_router_first = jnp.dot(
        jnp.transpose(first_logit_grad),
        tree_input.astype(F32),
        precision=HIGHEST,
        preferred_element_type=F32,
    )
    token_grad, grad_gain_first = first_pull(normed_grad)
    tokens_grad = token_grad + middle_grad

    sums = jnp.concatenate(
        [grad_gain_first[None], grad_gain_second[None], grad_router_first, grad_router_second],
        axis=0,
    )
    sums = jnp.transpose(sums.reshape(sums.shape[0], -1, own_kv), (1, 0, 2))
    if walk:
        sums, grad_query = final_exchange(sums, grad_query.reshape(pair, own_in, feats), sizes, 10)
        grad_query = grad_query[None]
    else:
        sums = small_exchange(sums, sizes, True, 10)
        grad_query = swap(grad_query.reshape(own_in * pair, line, part)[None], "pair", 1, 0)
        grad_query = jnp.transpose(grad_query, (1, 2, 0, 3)).reshape(1, own_in, heads_total)
    return (
        layer_out.reshape(micro, 1, tok, width),
        tokens_grad.reshape(micro, 1, tok, width),
        grad_query.astype(F32),
        grad_output[None].astype(F32),
        grad_key,
        grad_value,
        sums[0],
        jnp.transpose(sums[2 : 2 + experts]),
        sums[1],
        jnp.transpose(sums[2 + experts :]),
        grad_gate,
        grad_upward,
        grad_downward,
    )


def solution(mesh):
    line, experts = mesh.devices.shape
    pair = 2 if line % 2 == 0 and (HEADS % line == 0) else 1
    shaped = Mesh(mesh.devices.reshape(line // pair, pair, experts), ALL)
    in_specs = (
        P(None, DP, "expert", None),
        P("expert", DP, None),
        P("expert", DP, None),
        P(ALL, None),
        P(ALL, None),
        P(ALL),
        P(ALL, None),
        P(ALL),
        P(ALL, None),
        P("expert", DP, None),
        P("expert", DP, None),
        P("expert", DP, None),
        P(None, DP, None, None),
        P(None, DP, "expert", None),
        P(None, DP, "expert"),
        P(None, DP, None),
        P(None, DP, "expert", None),
    )
    out_specs = (
        P(None, DP, "expert", None),
        P(None, DP, "expert", None),
        P("expert", DP, None),
        P("expert", DP, None),
        P(ALL, None),
        P(ALL, None),
        P(ALL),
        P(ALL, None),
        P(ALL),
        P(ALL, None),
        P("expert", DP, None),
        P("expert", DP, None),
        P("expert", DP, None),
    )
    return jax.shard_map(body, mesh=shaped, in_specs=in_specs, out_specs=out_specs, check_vma=False)
```

```python
from functools import partial
import math

import jax
import jax.numpy as jnp
from jax import lax
from jax.experimental import pallas as pl
from jax.experimental.pallas import tpu as pltpu
from jax.sharding import Mesh, PartitionSpec as P

HEADS = 16
HDIM = 128
EPSILON = 1e-06
HIGHEST = lax.Precision.HIGHEST
BF16 = jnp.bfloat16
F32 = jnp.float32


def product(left, right):
    return jnp.dot(left, right, preferred_element_type=F32)


def product_tn(left, right):
    return lax.dot_general(left, right, (((0,), (0,)), ((), ())), preferred_element_type=F32)


def product_nt(left, right):
    return lax.dot_general(left, right, (((1,), (1,)), ((), ())), preferred_element_type=F32)


def split_product(values, rows):
    parts, rest = [], values
    for _ in range(3):
        parts.append(lax.reduce_precision(rest, 8, 7))
        rest = rest - parts[-1]
    count = values.shape[1]
    total = product_tn(jnp.concatenate(parts, axis=1).astype(BF16), rows)
    return total[:count] + total[count : 2 * count] + total[2 * count :]


def rms_scaled(values, gain):
    return values * lax.rsqrt(jnp.mean(values * values, axis=-1, keepdims=True) + EPSILON) * gain


def mixture_gates(picked, logits):
    labels = jnp.arange(logits.shape[1], dtype=jnp.int32)
    onehot = (picked[:, :, None] == labels[None, None, :]).astype(F32)
    chosen = jnp.sum(onehot * logits[:, None, :], axis=-1)
    weights = jax.nn.softmax(chosen, axis=-1)
    return jnp.sum(weights[:, :, None] * onehot, axis=1)


def tree_layout(segment_len, tree_len):
    places = jnp.arange(tree_len, dtype=jnp.int32)
    trunk_len = 4 * segment_len
    segment = jnp.where(
        places < trunk_len,
        0,
        jnp.where(
            places < 2 * trunk_len,
            1 + (places - trunk_len) // segment_len,
            5 + (places - 2 * trunk_len) // segment_len,
        ),
    )
    depth = jnp.where(
        places < trunk_len,
        places,
        jnp.where(
            places < 2 * trunk_len,
            trunk_len + (places - trunk_len) % segment_len,
            trunk_len + segment_len + (places - 2 * trunk_len) % segment_len,
        ),
    )
    return (places, segment, depth)


def ancestors(parent, segment):
    labels = jnp.arange(parent.shape[0], dtype=jnp.int32)
    first = jnp.where(labels > 0, parent, -1)
    lookup = jnp.maximum(first, 0)[:, None] == labels[None, :]
    second = jnp.where(first > 0, jnp.sum(jnp.where(lookup, parent[None, :], 0), axis=1), -1)
    member = segment[:, None] == labels[None, :]
    up_one = jnp.sum(jnp.where(member, first[None, :], 0), axis=1)
    up_two = jnp.sum(jnp.where(member, second[None, :], 0), axis=1)
    return (up_one, up_two)


def score_bias(parent, segment, places):
    up_one, up_two = ancestors(parent, segment)
    same = (segment[None, :] == segment[:, None]) & (places[None, :] <= places[:, None])
    seen = same | (segment[None, :] == up_one[:, None]) | (segment[None, :] == up_two[:, None])
    return jnp.where(seen, 0.0, -1e30).astype(F32)


def slot_table(picked, order, experts, capacity):
    labels = jnp.arange(experts, dtype=jnp.int32)
    chosen = jnp.sum((picked[:, :, None] == labels[None, None, :]).astype(F32), axis=1)
    earlier = (order[None, :] < order[:, None]).astype(F32)
    ranks = jnp.dot(earlier, chosen, precision=HIGHEST, preferred_element_type=F32)
    slots = jnp.arange(capacity, dtype=F32)
    return jnp.transpose(chosen)[:, None, :] * (
        jnp.transpose(ranks)[:, None, :] == slots[None, :, None]
    ).astype(F32)


def turn(values, cosine, sine):
    half = values.shape[-1] // 2
    first = values[:, :half]
    second = values[:, half:]
    return jnp.concatenate(
        [first * cosine - second * sine, second * cosine + first * sine], axis=-1
    )


def softmax_rows(queries, keys, bias, scale):
    scores = product_nt(queries, keys) * scale + bias
    highest = jnp.max(scores, axis=-1, keepdims=True)
    weights = jnp.exp(scores - highest)
    return weights / jnp.sum(weights, axis=-1, keepdims=True)


def attend_kernel(heads, scale, raw_ref, kv_ref, cos_ref, sin_ref, bias_ref, query_ref, out_ref):
    quarter, tok = raw_ref.shape[1], raw_ref.shape[3]
    rows = quarter * tok
    cosine, sine, bias = cos_ref[...], sin_ref[...], bias_ref[0, 0]
    for head in range(heads):
        cols = slice(head * HDIM, (head + 1) * HDIM)
        raw = raw_ref[0, :, 0, :, cols].reshape(rows, HDIM)
        keys = kv_ref[0, 0, 0, :, 0, :, cols].reshape(rows, HDIM)
        values = kv_ref[0, 1, 0, :, 0, :, cols].reshape(rows, HDIM)
        queries = turn(raw, cosine, sine).astype(BF16)
        probs = softmax_rows(queries, keys, bias, scale).astype(BF16)
        query_ref[0, :, 0, :, cols] = queries.reshape(quarter, tok, HDIM)
        out_ref[0, :, 0, :, cols] = product(probs, values).astype(BF16).reshape(quarter, tok, HDIM)


def attend_back_kernel(
    heads, scale, query_ref, kv_ref, grad_ref, cos_ref, sin_ref, bias_ref, dq_ref, dkv_ref
):
    quarter, tok = query_ref.shape[1], query_ref.shape[3]
    rows = quarter * tok
    cosine, sine, bias = cos_ref[...], sin_ref[...], bias_ref[0, 0]
    for head in range(heads):
        cols = slice(head * HDIM, (head + 1) * HDIM)
        queries = query_ref[0, :, 0, :, cols].reshape(rows, HDIM)
        keys = kv_ref[0, 0, 0, :, 0, :, cols].reshape(rows, HDIM)
        values = kv_ref[0, 1, 0, :, 0, :, cols].reshape(rows, HDIM)
        grad = grad_ref[0, :, 0, :, cols].reshape(rows, HDIM)
        probs = softmax_rows(queries, keys, bias, scale)
        prob_grad = product_nt(grad, values)
        centre = jnp.sum(prob_grad * probs, axis=-1, keepdims=True)
        score_grad = (probs * (prob_grad - centre) * scale).astype(BF16)
        query_grad = turn(product(score_grad, keys), cosine, -sine).astype(BF16)
        key_grad = turn(product_tn(score_grad, queries), cosine, -sine).astype(BF16)
        value_grad = product_tn(probs.astype(BF16), grad).astype(BF16)
        dq_ref[0, :, 0, :, cols] = query_grad.reshape(quarter, tok, HDIM)
        dkv_ref[0, 0, 0, :, 0, :, cols] = key_grad.reshape(quarter, tok, HDIM)
        dkv_ref[0, 1, 0, :, 0, :, cols] = value_grad.reshape(quarter, tok, HDIM)


def attention_specs(shape, slices):
    pair, quarter, micro, tok, feats = shape
    part = feats // slices
    rows = quarter * tok
    grid = (pair, micro, slices)
    flat = pl.BlockSpec((1, quarter, 1, tok, part), lambda i, m, s: (i, 0, m, 0, s))
    both = pl.BlockSpec(
        (1, 2, 1, quarter, 1, tok, part), lambda i, m, s: (s, 0, i, 0, m, 0, 0)
    )
    angle = pl.BlockSpec((rows, HDIM // 2), lambda i, m, s: (0, 0))
    bias = pl.BlockSpec((1, 1, rows, rows), lambda i, m, s: (i, m, 0, 0))
    return grid, part, flat, both, angle, bias


def attend(raw, kv, cosine, sine, bias, scale):
    slices = kv.shape[0]
    grid, part, flat, both, angle, bias_spec = attention_specs(raw.shape, slices)
    out = jax.ShapeDtypeStruct(raw.shape, BF16)
    return pl.pallas_call(
        partial(attend_kernel, part // HDIM, scale),
        grid=grid,
        in_specs=[flat, both, angle, angle, bias_spec],
        out_specs=[flat, flat],
        out_shape=[out, out],
        cost_estimate=pl.CostEstimate(
            flops=4 * raw.size * cosine.shape[0],
            bytes_accessed=12 * raw.size,
            transcendentals=raw.size * 2,
        ),
        name="attend",
    )(raw, kv, cosine, sine, bias)


def attend_back(queries, kv, grad, cosine, sine, bias, scale):
    slices = kv.shape[0]
    grid, part, flat, both, angle, bias_spec = attention_specs(queries.shape, slices)
    return pl.pallas_call(
        partial(attend_back_kernel, part // HDIM, scale),
        grid=grid,
        in_specs=[flat, both, flat, angle, angle, bias_spec],
        out_specs=[flat, both],
        out_shape=[
            jax.ShapeDtypeStruct(queries.shape, BF16),
            jax.ShapeDtypeStruct(kv.shape, BF16),
        ],
        cost_estimate=pl.CostEstimate(
            flops=10 * queries.size * cosine.shape[0],
            bytes_accessed=14 * queries.size,
            transcendentals=queries.size * 2,
        ),
        name="attend_back",
    )(queries, kv, grad, cosine, sine, bias)


MESH = pl.DeviceIdType.MESH
ANY = pl.BlockSpec(memory_space=pl.ANY)
VMEM = pl.BlockSpec(memory_space=pltpu.VMEM)
DMA = pltpu.SemaphoreType.DMA


def remote(src, dst, send, recv, target):
    return pltpu.make_async_remote_copy(
        src_ref=src, dst_ref=dst, send_sem=send, recv_sem=recv, device_id=target, device_id_type=MESH
    )


def greet(targets):
    barrier = pltpu.get_barrier_semaphore()
    for target in targets:
        pl.semaphore_signal(barrier, inc=1, device_id=target, device_id_type=MESH)
    pl.semaphore_wait(barrier, len(targets))


def params(number, limit=None):
    return pltpu.CompilerParams(
        collective_id=number, has_side_effects=True, vmem_limit_bytes=limit
    )


def add_into(target, sources, rows):
    step = 1
    while step * 2 <= rows and step * 2 * target.shape[-1] <= 65536 and rows % (step * 2) == 0:
        step *= 2

    def one(index, carry):
        where = pl.ds(pl.multiple_of(index * step, step), step)
        total = sources[0][where].astype(F32)
        for source in sources[1:]:
            total = total + source[where].astype(F32)
        target[where] = total.astype(target.dtype)
        return carry

    lax.fori_loop(0, rows // step, one, 0)


def cube_reduce_kernel(pairs, x_ref, o_ref, half, quarter, got_core, got_side, got_pair, send, recv):
    p = lax.axis_index("pair")
    e = lax.axis_index("expert")
    c, y = lax.rem(e, 2), lax.div(e, 2)
    core = {"expert": e + 1 - 2 * c}
    side = {"expert": e + 2 - 4 * y}
    other = {"pair": lax.rem(p + 1, pairs)}
    greet([core, side] + ([other] if pairs == 2 else []))
    rows = x_ref.shape[3]
    shifts = (1, 0) if pairs == 2 else (0,)
    order = [(dx, dy) for dy in (1, 0) for dx in shifts]
    first, second = [], {}
    for slot, (dx, dy) in enumerate(order):
        px, yy = lax.rem(p + dx, pairs), lax.rem(y + dy, 2)
        copy = remote(
            x_ref.at[px, yy, 1 - c], got_core.at[slot], send.at[slot], recv.at[slot], core
        )
        copy.start()
        first.append(copy)
    base = len(order)
    for slot, (dx, dy) in enumerate(order):
        px, yy = lax.rem(p + dx, pairs), lax.rem(y + dy, 2)
        first[slot].wait_recv()
        add_into(half.at[slot], [x_ref.at[px, yy, c], got_core.at[slot]], rows)
        if dy == 1:
            copy = remote(
                half.at[slot], got_side.at[dx], send.at[base + dx], recv.at[base + dx], side
            )
            copy.start()
            second[dx] = copy
    last = None
    for dx in shifts:
        second[dx].wait_recv()
        if dx == 1:
            add_into(quarter, [half.at[order.index((1, 0))], got_side.at[1]], rows)
            last = remote(quarter, got_pair, send.at[base + 2], recv.at[base + 2], other)
            last.start()
    if last is not None:
        last.wait_recv()
        add_into(o_ref, [half.at[order.index((0, 0))], got_side.at[0], got_pair], rows)
    else:
        add_into(o_ref, [half.at[order.index((0, 0))], got_side.at[0]], rows)
    for copy in first + list(second.values()) + ([last] if last is not None else []):
        copy.wait_send()


def cube_reduce(value, pairs, number):
    _, rows, cols = value.shape
    value = value.reshape(pairs, 2, 2, rows, cols)
    slots = 2 * pairs
    block = jax.ShapeDtypeStruct((rows, cols), value.dtype)
    return pl.pallas_call(
        partial(cube_reduce_kernel, pairs),
        in_specs=[VMEM],
        out_specs=VMEM,
        out_shape=block,
        scratch_shapes=[
            pltpu.VMEM((slots, rows, cols), value.dtype),
            pltpu.VMEM((rows, cols), value.dtype),
            pltpu.VMEM((slots, rows, cols), value.dtype),
            pltpu.VMEM((pairs, rows, cols), value.dtype),
            pltpu.VMEM((rows, cols), value.dtype),
            DMA((slots + 3,)),
            DMA((slots + 3,)),
        ],
        compiler_params=params(number, 48 * 2**20),
        cost_estimate=pl.CostEstimate(flops=0, bytes_accessed=0, transcendentals=0),
        name="cube_reduce",
    )(value)


def cube_gather_kernel(pairs, x_ref, o_ref, send, recv, local):
    p = lax.axis_index("pair") if pairs == 2 else 0
    e = lax.axis_index("expert")
    c, y = lax.rem(e, 2), lax.div(e, 2)
    core = {"expert": e + 1 - 2 * c}
    side = {"expert": e + 2 - 4 * y}
    other = {"pair": lax.rem(p + 1, pairs)}
    greet([core, side] + ([other] if pairs == 2 else []))
    q, w = lax.rem(p + 1, pairs), 1 - y
    own = o_ref.at[p, y, c]
    keep = pltpu.make_async_copy(x_ref, own, local)
    keep.start()
    copies = []

    def push(slot, source, place, target):
        copy = remote(source, place, send.at[slot], recv.at[slot], target)
        copy.start()
        copies.append(copy)
        return copy

    to_side = push(0, x_ref, own, side)
    to_other = push(1, x_ref, own, other) if pairs == 2 else None
    to_core = push(2, x_ref, own, core)
    waits = [to_core]
    if pairs == 2:
        to_other.wait_recv()
        block = o_ref.at[q, y, c]
        far = push(3, block, block, side)
        waits.append(push(4, block, block, core))
    to_side.wait_recv()
    block = o_ref.at[p, w, c]
    waits.append(push(5, block, block, core))
    if pairs == 2:
        far.wait_recv()
        block = o_ref.at[q, w, c]
        waits.append(push(6, block, block, core))
    for copy in waits:
        copy.wait_recv()
    for copy in copies:
        copy.wait_send()
    keep.wait()


def cube_gather(value, pairs, number):
    return pl.pallas_call(
        partial(cube_gather_kernel, pairs),
        in_specs=[VMEM],
        out_specs=VMEM,
        out_shape=jax.ShapeDtypeStruct((pairs, 2, 2) + value.shape, value.dtype),
        scratch_shapes=[DMA((7,)), DMA((7,)), DMA(())],
        compiler_params=params(number, 48 * 2**20),
        cost_estimate=pl.CostEstimate(
            flops=0, bytes_accessed=80 * value.size, transcendentals=0
        ),
        name="cube_gather",
    )(value)


def place_of(index, sizes):
    line, pairs, experts = sizes
    return {
        "line": index // (pairs * experts),
        "pair": (index // experts) % pairs,
        "expert": index % experts,
    }


def small_kernel(sizes, reduce, x_ref, o_ref, got, send, recv):
    line, pairs, experts = sizes
    count = line * pairs * experts
    me = (
        lax.axis_index("line") * (pairs * experts)
        + lax.axis_index("pair") * experts
        + lax.axis_index("expert")
    )
    barrier = pltpu.get_barrier_semaphore()

    def greet_one(offset, carry):
        target = place_of((me + offset) % count, sizes)
        pl.semaphore_signal(barrier, inc=1, device_id=target, device_id_type=MESH)
        return carry

    lax.fori_loop(1, count, greet_one, 0)
    pl.semaphore_wait(barrier, count - 1)

    def copy_to(offset):
        peer = (me + offset) % count
        source = x_ref.at[peer] if reduce else x_ref
        return remote(source, got.at[offset], send.at[offset], recv.at[offset], place_of(peer, sizes))

    def start(offset, carry):
        copy_to(offset).start()
        return carry

    lax.fori_loop(1, count, start, 0)
    got[0] = x_ref[me] if reduce else x_ref[...]

    def finish(offset, carry):
        copy_to(offset).wait()
        return carry

    lax.fori_loop(1, count, finish, 0)
    if reduce:
        o_ref[...] = jnp.sum(got[...], axis=0)
    else:

        def order(offset, carry):
            o_ref[(me - offset + count) % count] = got[offset]
            return carry

        lax.fori_loop(0, count, order, 0)


def small_exchange(value, sizes, reduce, number):
    count = sizes[0] * sizes[1] * sizes[2]
    block = value.shape[1:] if reduce else value.shape
    return pl.pallas_call(
        partial(small_kernel, sizes, reduce),
        in_specs=[VMEM],
        out_specs=VMEM,
        out_shape=jax.ShapeDtypeStruct(block if reduce else (count,) + block, value.dtype),
        scratch_shapes=[pltpu.VMEM((count,) + block, value.dtype), DMA((count,)), DMA((count,))],
        compiler_params=params(number),
        cost_estimate=pl.CostEstimate(flops=0, bytes_accessed=2**24, transcendentals=0),
        name="small_reduce" if reduce else "small_gather",
    )(value)


def ff_kernel(
    a_in, b_in, gate_hbm, up_hbm, down_hbm,
    a_out, b_out, a_save, b_save, inner_save, dgate_save, dup_save,
    a_buf, b_buf, side, hop, extra, w_gate, w_up, w_down, mid, acc,
    send, recv, load, store, local,
):
    z, p, e = lax.axis_index("line"), lax.axis_index("pair"), lax.axis_index("expert")
    line, _, rows, width = a_buf.shape
    experts, size = a_in.shape[0], a_in.shape[1]
    q = 1 - p
    twin = z + 1 - 2 * (z % 2)
    up, down, other, across = {"line": z + 1}, {"line": z - 1}, {"pair": q}, {"line": twin}
    ins, bufs, outs, saves = (a_in, b_in), (a_buf, b_buf), (a_out, b_out), (a_save, b_save)
    high = z // 2
    near = z + high * (line - 1 - 2 * z)

    def order(t):
        j = t + near * (1 - t // 2) * (1 - 2 * t)
        return j + high * (line - 1 - 2 * j)

    weights = [
        pltpu.make_async_copy(src, dst, load.at[i])
        for i, (src, dst) in enumerate(((gate_hbm, w_gate), (up_hbm, w_up), (down_hbm, w_down)))
    ]
    for copy in weights:
        copy.start()

    barrier = pltpu.get_barrier_semaphore()
    for shift in range(1, experts):
        pl.semaphore_signal(
            barrier, inc=1, device_id={"expert": (e + shift) % experts}, device_id_type=MESH
        )
    pl.semaphore_signal(barrier, inc=1, device_id=other, device_id_type=MESH)

    @pl.when(z > 0)
    def _():
        pl.semaphore_signal(barrier, inc=1, device_id=down, device_id_type=MESH)

    @pl.when(z < line - 1)
    def _():
        pl.semaphore_signal(barrier, inc=1, device_id=up, device_id_type=MESH)

    below, above = (z + line - 1) // line, (2 * line - 2 - z) // line
    pl.semaphore_wait(barrier, experts + below + above)

    UP, DOWN, SIDE, SUMUP, SUMDOWN, SUMSIDE = (i * line for i in range(6))
    TWIN, SUMTWIN, SWAP = 6 * line, 6 * line + 1, 6 * line + 2
    BACK = SWAP + experts

    def push(src, dst, kind, use, target):
        return remote(src, dst, send.at[kind, use], recv.at[kind, use], target)

    def to_up(kind, j):
        return push(bufs[kind].at[j, p], bufs[kind].at[j, p], kind, UP + j, up)

    def to_down(kind, j):
        return push(bufs[kind].at[j, p], bufs[kind].at[j, p], kind, DOWN + j, down)

    def to_other(kind, j):
        return push(bufs[kind].at[j, p], bufs[kind].at[j, p], kind, SIDE + j, other)

    def to_twin():
        return push(bufs[1].at[z, q], bufs[1].at[z, q], 1, TWIN, across)

    def sum_up(kind, j):
        return push(bufs[kind].at[j, p], hop.at[kind, j], kind, SUMUP + j, up)

    def sum_down(kind, j, slot):
        return push(bufs[kind].at[j, p], hop.at[kind, slot], kind, SUMDOWN + j, down)

    def sum_other(kind, j):
        return push(bufs[kind].at[j, q], side.at[kind, j], kind, SUMSIDE + j, other)

    def sum_twin():
        return push(bufs[1].at[twin, q], extra, 1, SUMTWIN, across)

    def piece(index):
        return pl.ds(pl.multiple_of(index * size, size), size)

    def save(kind, j, column):
        return pltpu.make_async_copy(
            bufs[kind].at[j, column], saves[kind].at[j, column], store.at[kind, j, column]
        )

    swaps = []
    for kind in range(2):
        home = bufs[kind].at[z, p, piece(e)]
        keep = pltpu.make_async_copy(ins[kind].at[e], home, local.at[kind])
        keep.start()
        group = []
        for shift in range(1, experts):
            peer = (e + shift) % experts
            copy = push(ins[kind].at[peer], home, kind, SWAP + shift, {"expert": peer})
            copy.start()
            group.append(copy)
        swaps.append((keep, group))

    def spread(t, first=False):
        j = order(t)
        for kind in range(2):
            if first:
                swaps[kind][0].wait()
                for copy in swaps[kind][1]:
                    copy.wait_recv()
            else:

                @pl.when(j < z)
                def _():
                    to_up(kind, j).wait_recv()

                @pl.when(j > z)
                def _():
                    to_down(kind, j).wait_recv()

            @pl.when((j <= z) & (z < line - 1))
            def _():
                to_up(kind, j).start()

            @pl.when((j >= z) & (z > 0))
            def _():
                to_down(kind, j).start()

            if kind == 0:
                to_other(kind, j).start()
            else:

                @pl.when(j != twin)
                def _():
                    to_other(kind, j).start()

            save(kind, j, p).start()

    chunk = 512
    steps = width // chunk

    def first_half(j, column):
        for index in range(3):
            acc[index] = jnp.zeros(acc.shape[1:], F32)

        def one(k, carry):
            where = pl.ds(pl.multiple_of(k * chunk, chunk), chunk)
            left = a_buf[j, column, :, where]
            acc[0] += product_nt(left, w_gate[:, where])
            acc[1] += product_nt(left, w_up[:, where])
            acc[2] += product_nt(b_buf[j, column, :, where], w_down[:, where])
            return carry

        lax.fori_loop(0, steps, one, 0)
        part = 32

        def two(i, carry):
            where = pl.ds(pl.multiple_of(i * part, part), part)
            gate, lift, grad = acc[0, where], acc[1, where], acc[2, where]
            sigma = jax.nn.sigmoid(gate)
            mid[j, column, 0, where] = (gate * sigma * lift).astype(BF16)
            mid[j, column, 1, where] = (
                grad * lift * sigma * (1.0 + gate * (1.0 - sigma))
            ).astype(BF16)
            mid[j, column, 2, where] = (grad * gate * sigma).astype(BF16)
            return carry

        lax.fori_loop(0, rows // part, two, 0)

    def second_half(j, column):
        def one(k, carry):
            where = pl.ds(pl.multiple_of(k * chunk, chunk), chunk)
            a_buf[j, column, :, where] = product(mid[j, column, 0], w_down[:, where]).astype(BF16)
            b_buf[j, column, :, where] = (
                product(mid[j, column, 1], w_gate[:, where])
                + product(mid[j, column, 2], w_up[:, where])
            ).astype(BF16)
            return carry

        lax.fori_loop(0, steps, one, 0)

    def arrive(j):
        for kind in range(2):
            if kind == 0:
                to_other(kind, j).wait_recv()
            else:

                @pl.when(j != twin)
                def _():
                    to_other(kind, j).wait_recv()

                @pl.when(j == twin)
                def _():
                    to_twin().wait_recv()

            save(kind, j, q).start()

        @pl.when(j == z)
        def _():
            to_twin().start()

    def emit(t):
        j = order(t)
        sum_other(0, j).start()

        @pl.when((j != twin) & (j != z))
        def _():
            sum_other(1, j).start()

    def step(s, carry):
        @pl.when(s == 0)
        def _():
            spread(0, True)
            for copy in weights:
                copy.wait()

        @pl.when(s == 1)
        def _():
            spread(1)
            spread(2)

        @pl.when(s == 3)
        def _():
            spread(3)

        @pl.when(s == line)
        def _():
            sum_twin().start()

        def half(c, inner_carry):
            t = s - c
            column = p + c * (q - p)

            @pl.when((t >= 0) & (t < line))
            def _():
                j = order(t)

                @pl.when(c == 1)
                def _():
                    arrive(j)

                first_half(j, column)

                @pl.when(c == 1)
                def _():
                    @pl.when(j == z)
                    def _():
                        to_twin().wait_send()

                    for kind in range(2):
                        save(kind, j, q).wait()
                    second_half(j, column)

            return inner_carry

        return lax.fori_loop(0, 2, half, carry)

    lax.fori_loop(0, line + 1, step, 0)

    for t in (3, 2, 1, 0):
        emit(t)

    for copy in (
        pltpu.make_async_copy(mid.at[:, :, 0], inner_save, local.at[2]),
        pltpu.make_async_copy(mid.at[:, :, 1], dgate_save, local.at[3]),
        pltpu.make_async_copy(mid.at[:, :, 2], dup_save, local.at[4]),
    ):
        copy.start()
    sum_twin().wait_recv()
    add_into(b_buf.at[z, q], [b_buf.at[z, q], extra], rows)
    sum_other(1, z).start()

    def back(kind):
        own = pltpu.make_async_copy(
            bufs[kind].at[z, p, piece(e)], outs[kind].at[e], local.at[kind]
        )
        return [own] + [
            push(
                bufs[kind].at[z, p, piece((e + shift) % experts)],
                outs[kind].at[e],
                kind,
                BACK + shift,
                {"expert": (e + shift) % experts},
            )
            for shift in range(1, experts)
        ]

    def fold(s, carry):
        t = line - 1 - s
        j = order(t)
        for kind in range(2):
            save(kind, j, p).wait()

            @pl.when((j <= z) & (z < line - 1))
            def _():
                to_up(kind, j).wait_send()

            @pl.when((j >= z) & (z > 0))
            def _():
                to_down(kind, j).wait_send()

            if kind == 0:
                to_other(kind, j).wait_send()
            else:

                @pl.when(j != twin)
                def _():
                    to_other(kind, j).wait_send()

        second_half(j, p)
        for kind in range(2):
            mine = bufs[kind].at[j, p]
            if kind == 0:
                sum_other(kind, j).wait_recv()
                add_into(mine, [mine, side.at[kind, j]], rows)
            else:

                @pl.when(j != twin)
                def _():
                    sum_other(kind, j).wait_recv()
                    add_into(mine, [mine, side.at[kind, j]], rows)

            @pl.when((j >= z) & (z > 0))
            def _():
                sum_up(kind, j).wait_recv()
                add_into(mine, [mine, hop.at[kind, j]], rows)

            @pl.when((j < z) & (z < line - 1))
            def _():
                sum_down(kind, j, j).wait_recv()
                add_into(mine, [mine, hop.at[kind, j]], rows)

            @pl.when((j == z) & (z < line - 1))
            def _():
                sum_down(kind, j, line).wait_recv()
                add_into(mine, [mine, hop.at[kind, line]], rows)

            @pl.when(j == z)
            def _():
                for copy in back(kind):
                    copy.start()

            @pl.when(j > z)
            def _():
                sum_up(kind, j).start()

            @pl.when((j < z) & (j != z - 1))
            def _():
                sum_down(kind, j, j).start()

            @pl.when((j < z) & (j == z - 1))
            def _():
                sum_down(kind, j, line).start()

        return carry

    lax.fori_loop(0, line, fold, 0)

    for kind in range(2):
        for copy in back(kind):
            copy.wait()

    def drain(j, carry):
        for kind in range(2):
            if kind == 0:
                sum_other(kind, j).wait_send()
            else:

                @pl.when(j != twin)
                def _():
                    sum_other(kind, j).wait_send()

            @pl.when(j > z)
            def _():
                sum_up(kind, j).wait_send()

            @pl.when(j < z)
            def _():
                sum_down(kind, j, j).wait_send()

        return carry

    lax.fori_loop(0, line, drain, 0)
    sum_twin().wait_send()
    for copy in (
        pltpu.make_async_copy(mid.at[:, :, 0], inner_save, local.at[2]),
        pltpu.make_async_copy(mid.at[:, :, 1], dgate_save, local.at[3]),
        pltpu.make_async_copy(mid.at[:, :, 2], dup_save, local.at[4]),
    ):
        copy.wait()
    for keep, group in swaps:
        for copy in group:
            copy.wait_send()


def feed_forward(first, second, w_gate, w_up, w_down, line, pairs, number):
    experts, size, width = first.shape
    hidden = w_gate.shape[0]
    rows = experts * size
    blocks = (line, pairs, rows)
    back = jax.ShapeDtypeStruct(first.shape, BF16)
    wide = jax.ShapeDtypeStruct(blocks + (width,), BF16)
    thin = jax.ShapeDtypeStruct(blocks + (hidden,), BF16)
    uses = 6 * line + 2 + 2 * experts
    total = line * pairs * rows
    return pl.pallas_call(
        ff_kernel,
        in_specs=[ANY] * 5,
        out_specs=[ANY] * 7,
        out_shape=[back, back, wide, wide, thin, thin, thin],
        scratch_shapes=[
            pltpu.VMEM(blocks + (width,), BF16),
            pltpu.VMEM(blocks + (width,), BF16),
            pltpu.VMEM((2, line, rows, width), BF16),
            pltpu.VMEM((2, line + 1, rows, width), BF16),
            pltpu.VMEM((rows, width), BF16),
            pltpu.VMEM((hidden, width), BF16),
            pltpu.VMEM((hidden, width), BF16),
            pltpu.VMEM((hidden, width), BF16),
            pltpu.VMEM((line, pairs, 3, rows, hidden), BF16),
            pltpu.VMEM((3, rows, hidden), F32),
            DMA((2, uses)),
            DMA((2, uses)),
            DMA((3,)),
            DMA((2, line, pairs)),
            DMA((5,)),
        ],
        compiler_params=params(number, 63 * 2**20),
        cost_estimate=pl.CostEstimate(
            flops=12 * total * hidden * width,
            bytes_accessed=12 * total * width,
            transcendentals=total * hidden,
        ),
        name="feed_forward",
    )(first, second, w_gate, w_up, w_down)


def last_kernel(
    sizes, x_ref, q_ref, g_hbm, o_ref, w_ref, key_ref, value_ref,
    got, side, g_ref, k_ref, hop, send, recv, peer_send, peer_recv, local,
):
    line, pairs, experts = sizes
    trees = pairs * experts
    count = line * trees
    z, p, e = lax.axis_index("line"), lax.axis_index("pair"), lax.axis_index("expert")
    mine = p * experts + e
    me = z * trees + mine
    span, piece = g_ref.shape[1], k_ref.shape[1]
    up, down = {"line": z + 1}, {"line": z - 1}
    high = z // 2
    near = z + high * (line - 1 - 2 * z)

    def order(t):
        j = t + near * (1 - t // 2) * (1 - 2 * t)
        return j + high * (line - 1 - 2 * j)

    fetch = pltpu.make_async_copy(g_hbm, g_ref, local)
    fetch.start()
    barrier = pltpu.get_barrier_semaphore()

    def greet_one(offset, carry):
        target = place_of((me + offset) % count, sizes)
        pl.semaphore_signal(barrier, inc=1, device_id=target, device_id_type=MESH)
        return carry

    lax.fori_loop(1, count, greet_one, 0)
    pl.semaphore_wait(barrier, count - 1)
    UP, DOWN, SWAP, PAIR = 0, line, 2 * line, 2 * line + trees

    def sum_up(j):
        return remote(g_ref.at[j], hop.at[j], send.at[UP + j], recv.at[UP + j], up)

    def sum_down(j, slot):
        return remote(g_ref.at[j], hop.at[slot], send.at[DOWN + j], recv.at[DOWN + j], down)

    def fold(t):
        j = order(t)
        own = g_ref.at[j]

        @pl.when((j >= z) & (z > 0))
        def _():
            sum_up(j).wait_recv()
            add_into(own, [own, hop.at[j]], span)

        @pl.when((j < z) & (z < line - 1))
        def _():
            sum_down(j, j).wait_recv()
            add_into(own, [own, hop.at[j]], span)

        @pl.when((j == z) & (z < line - 1))
        def _():
            sum_down(j, line).wait_recv()
            add_into(own, [own, hop.at[line]], span)

        @pl.when(j > z)
        def _():
            sum_up(j).start()

        @pl.when((j < z) & (j != z - 1))
        def _():
            sum_down(j, j).start()

        @pl.when((j < z) & (j == z - 1))
        def _():
            sum_down(j, line).start()

    fetch.wait()
    fold(3)
    swap = remote(q_ref.at[1 - p], side, send.at[PAIR], recv.at[PAIR], {"pair": 1 - p})
    swap.start()

    def copy_to(offset):
        peer = (me + offset) % count
        return remote(
            x_ref.at[peer],
            got.at[offset],
            peer_send.at[offset],
            peer_recv.at[offset],
            place_of(peer, sizes),
        )

    def start(offset, carry):
        copy_to(offset).start()
        return carry

    lax.fori_loop(1, count, start, 0)
    got[0] = x_ref[me]
    fold(2)
    part = q_ref.shape[2] // line

    def lay(block, source):
        for index in range(line):
            column = pl.multiple_of((index * pairs + source) * part, part)
            w_ref[:, pl.ds(column, part)] = block[:, index * part : (index + 1) * part].astype(F32)

    lay(q_ref.at[p], p)
    fold(1)
    swap.wait_recv()
    lay(side, 1 - p)

    def finish(offset, carry):
        copy_to(offset).wait()
        return carry

    lax.fori_loop(1, count, finish, 0)
    o_ref[...] = jnp.sum(got[...], axis=0)
    fold(0)

    def share_of(index):
        return g_ref.at[z, pl.ds(pl.multiple_of(index * piece, piece), piece)]

    keep = pltpu.make_async_copy(share_of(mine), k_ref.at[mine], local)
    keep.start()
    swaps = []
    for shift in range(1, trees):
        peer = (mine + shift) % trees
        copy = remote(
            share_of(peer),
            k_ref.at[mine],
            send.at[SWAP + shift],
            recv.at[SWAP + shift],
            {"pair": peer // experts, "expert": peer % experts},
        )
        copy.start()
        swaps.append(copy)
    keep.wait()
    for copy in swaps:
        copy.wait()
    share = k_ref.shape[2] // 2
    for source in range(trees):
        column = ((source % experts) * pairs + source // experts) * share
        for index, target in enumerate((key_ref, value_ref)):
            target[:, column : column + share] = k_ref[
                source, :, index * share : (index + 1) * share
            ].astype(F32)
    swap.wait_send()

    def drain(j, carry):
        @pl.when(j > z)
        def _():
            sum_up(j).wait_send()

        @pl.when(j < z)
        def _():
            sum_down(j, j).wait_send()

        return carry

    lax.fori_loop(0, line, drain, 0)


def last_exchange(sums, query, grads, sizes, number):
    line, pairs, experts = sizes
    trees = pairs * experts
    count, block = sums.shape[0], sums.shape[1:]
    _, rows, cols = query.shape
    span, thin = grads.shape[0] // line, grads.shape[1]
    uses = 2 * line + trees + 1
    wide = jax.ShapeDtypeStruct((span // trees, trees * thin // 2), F32)
    return pl.pallas_call(
        partial(last_kernel, sizes),
        in_specs=[VMEM, VMEM, ANY],
        out_specs=[VMEM] * 4,
        out_shape=[
            jax.ShapeDtypeStruct(block, F32),
            jax.ShapeDtypeStruct((rows, pairs * cols), F32),
            wide,
            wide,
        ],
        scratch_shapes=[
            pltpu.VMEM((count,) + block, F32),
            pltpu.VMEM((rows, cols), BF16),
            pltpu.VMEM((line, span, thin), BF16),
            pltpu.VMEM((trees, span // trees, thin), BF16),
            pltpu.VMEM((line + 1, span, thin), BF16),
            DMA((uses,)),
            DMA((uses,)),
            DMA((count,)),
            DMA((count,)),
            DMA(()),
        ],
        compiler_params=params(number, 48 * 2**20),
        cost_estimate=pl.CostEstimate(flops=0, bytes_accessed=0, transcendentals=0),
        name="last_exchange",
    )(sums, query, grads.reshape(line, span, thin))


def start_all_kernel(
    sizes, tok_ref, wq_ref, wk_ref, wv_ref, small_ref, int_ref,
    tok_out, q_out, kv_out, small_out, int_out,
    q_cut, kv_cut, send, recv, peer_send, peer_recv, local,
):
    line, pairs, experts = sizes
    z, p, e = lax.axis_index("line"), lax.axis_index("pair"), lax.axis_index("expert")
    c, y = e % 2, e // 2
    core, side = {"expert": e + 1 - 2 * c}, {"expert": e + 2 - 4 * y}
    other = {"pair": 1 - p}
    trees = pairs * experts
    count = line * trees
    mine = p * experts + e
    me = z * trees + mine
    barrier = pltpu.get_barrier_semaphore()

    def greet_one(offset, carry):
        target = place_of((me + offset) % count, sizes)
        pl.semaphore_signal(barrier, inc=1, device_id=target, device_id_type=MESH)
        return carry

    lax.fori_loop(1, count, greet_one, 0)
    part = wq_ref.shape[1] // (line * pairs)
    for q in range(pairs):
        for index in range(line):
            column = (index * pairs + q) * part
            q_cut[q, :, index * part : (index + 1) * part] = wq_ref[:, column : column + part]
    sub = line // experts
    for q in range(pairs):
        for d in range(experts):
            for index, ref in enumerate((wk_ref, wv_ref)):
                for h in range(sub):
                    column = ((d * sub + h) * pairs + q) * part
                    place = (index * sub + h) * part
                    kv_cut[q * experts + d, :, place : place + part] = ref[
                        :, column : column + part
                    ]
    pl.semaphore_wait(barrier, count - 1)

    copies, TOK, QSWAP, INTS, KV = [], 0, 7, 8, 9
    WALK = KV + trees

    def push(slot, source, place, target):
        copy = remote(source, place, send.at[slot], recv.at[slot], target)
        copy.start()
        copies.append(copy)
        return copy

    rows = q_cut.shape[1]
    q_home = q_out.at[z, pl.ds(pl.multiple_of(p * rows, rows), rows)]
    q_swap = push(QSWAP, q_cut.at[1 - p], q_home, other)
    size = kv_cut.shape[1]
    kv_home = kv_out.at[z, pl.ds(pl.multiple_of(mine * size, size), size)]
    pieces = []
    for shift in range(1, trees):
        peer = (mine + shift) % trees
        pieces.append(
            push(
                KV + shift,
                kv_cut.at[peer],
                kv_home,
                {"pair": peer // experts, "expert": peer % experts},
            )
        )
    keeps = [
        pltpu.make_async_copy(q_cut.at[p], q_home, local.at[0]),
        pltpu.make_async_copy(kv_cut.at[mine], kv_home, local.at[1]),
        pltpu.make_async_copy(tok_ref, tok_out.at[p, y, c], local.at[2]),
        pltpu.make_async_copy(small_ref, small_out.at[me], local.at[3]),
        pltpu.make_async_copy(int_ref, int_out.at[p], local.at[4]),
    ]
    for copy in keeps:
        copy.start()
    own = tok_out.at[p, y, c]
    to_side = push(TOK, tok_ref, own, side)
    to_other = push(TOK + 1, tok_ref, own, other)
    waits = [push(TOK + 2, tok_ref, own, core), push(INTS, int_ref, int_out.at[p], other)]

    def small_to(offset):
        return remote(
            small_ref,
            small_out.at[me],
            peer_send.at[offset],
            peer_recv.at[offset],
            place_of((me + offset) % count, sizes),
        )

    def small_start(offset, carry):
        small_to(offset).start()
        return carry

    lax.fori_loop(1, count, small_start, 0)

    def walker(ref, base):
        def to_up(j, d):
            return remote(
                ref.at[j], ref.at[j], send.at[base + d], recv.at[base + d], {"line": z + 1}
            )

        def to_down(j, d):
            at = base + line + d
            return remote(ref.at[j], ref.at[j], send.at[at], recv.at[at], {"line": z - 1})

        return to_up, to_down

    walkers = [walker(q_out, WALK), walker(kv_out, WALK + 2 * line + 2)]

    def begin(which):
        to_up, to_down = walkers[which]

        @pl.when(z < line - 1)
        def _():
            to_up(z, 1).start()

        @pl.when(z > 0)
        def _():
            to_down(z, 1).start()

    keeps[0].wait()
    q_swap.wait_recv()
    begin(0)
    keeps[1].wait()
    for copy in pieces:
        copy.wait_recv()
    begin(1)
    to_other.wait_recv()
    block = tok_out.at[1 - p, y, c]
    far = push(TOK + 3, block, block, side)
    waits.append(push(TOK + 4, block, block, core))
    to_side.wait_recv()
    block = tok_out.at[p, 1 - y, c]
    waits.append(push(TOK + 5, block, block, core))
    far.wait_recv()
    block = tok_out.at[1 - p, 1 - y, c]
    waits.append(push(TOK + 6, block, block, core))

    for d in range(1, line):
        for to_up, to_down in walkers:

            @pl.when(z - d >= 0)
            def _():
                to_up(z - d, d).wait_recv()

                @pl.when(z < line - 1)
                def _():
                    to_up(z - d, d + 1).start()

            @pl.when(z + d < line)
            def _():
                to_down(z + d, d).wait_recv()

                @pl.when(z > 0)
                def _():
                    to_down(z + d, d + 1).start()

    for d in range(1, line):
        for to_up, to_down in walkers:

            @pl.when((z - d + 1 >= 0) & (z < line - 1))
            def _():
                to_up(z - d + 1, d).wait_send()

            @pl.when((z + d - 1 < line) & (z > 0))
            def _():
                to_down(z + d - 1, d).wait_send()

    for copy in waits:
        copy.wait_recv()
    for copy in copies:
        copy.wait_send()
    for copy in keeps[2:]:
        copy.wait()

    def small_finish(offset, carry):
        small_to(offset).wait()
        return carry

    lax.fori_loop(1, count, small_finish, 0)


def start_all(tokens, w_query, w_key, w_value, small, integers, sizes, number):
    line, pairs, experts = sizes
    trees = pairs * experts
    count = line * trees
    rows, width = w_query.shape
    size = w_key.shape[0]
    feats = width // pairs
    thin = 2 * feats // experts
    uses = 9 + trees + 4 * line + 4
    return pl.pallas_call(
        partial(start_all_kernel, sizes),
        in_specs=[VMEM] * 6,
        out_specs=[VMEM] * 5,
        out_shape=[
            jax.ShapeDtypeStruct((pairs, 2, 2) + tokens.shape, BF16),
            jax.ShapeDtypeStruct((line, pairs * rows, feats), BF16),
            jax.ShapeDtypeStruct((line, trees * size, thin), BF16),
            jax.ShapeDtypeStruct((count,) + small.shape, BF16),
            jax.ShapeDtypeStruct((pairs,) + integers.shape, jnp.int32),
        ],
        scratch_shapes=[
            pltpu.VMEM((pairs, rows, feats), BF16),
            pltpu.VMEM((trees, size, thin), BF16),
            DMA((uses,)),
            DMA((uses,)),
            DMA((count,)),
            DMA((count,)),
            DMA((5,)),
        ],
        compiler_params=params(number, 48 * 2**20),
        name="start_all",
    )(tokens, w_query, w_key, w_value, small, integers)


def input_kernel(dq_ref, wq_ref, kv_ref, wkv_ref, dl_ref, router_ref, o_ref):
    piece = kv_ref.shape[2]
    total = product_nt(dq_ref[...], wq_ref[...])
    total = total + product_nt(kv_ref[0], wkv_ref[:, :piece])
    total = total + product_nt(kv_ref[1], wkv_ref[:, piece:])
    for expert in range(router_ref.shape[0]):
        total = total + dl_ref[:, expert : expert + 1] * router_ref[expert : expert + 1, :]
    o_ref[...] = total.astype(BF16)


def input_gradient(query_pre, query_weight, kv_sum, kv_weight, logit_grad, router):
    rows, feats = query_pre.shape
    width = query_weight.shape[0]
    piece = kv_sum.shape[2]
    experts = router.shape[0]
    block, lanes = min(512, rows), 512
    return pl.pallas_call(
        input_kernel,
        grid=(width // lanes, rows // block),
        in_specs=[
            pl.BlockSpec((block, feats), lambda n, i: (i, 0)),
            pl.BlockSpec((lanes, feats), lambda n, i: (n, 0)),
            pl.BlockSpec((2, block, piece), lambda n, i: (0, i, 0)),
            pl.BlockSpec((lanes, 2 * piece), lambda n, i: (n, 0)),
            pl.BlockSpec((block, experts), lambda n, i: (i, 0)),
            pl.BlockSpec((experts, lanes), lambda n, i: (0, n)),
        ],
        out_specs=pl.BlockSpec((block, lanes), lambda n, i: (i, n)),
        out_shape=jax.ShapeDtypeStruct((rows, width), BF16),
        compiler_params=pltpu.CompilerParams(vmem_limit_bytes=40 * 2**20),
        cost_estimate=pl.CostEstimate(
            flops=2 * rows * width * (feats + 2 * piece), bytes_accessed=6 * rows * width, transcendentals=0
        ),
        name="input_gradient",
    )(query_pre, query_weight, kv_sum, kv_weight, logit_grad, router)


def project_kernel(micro, x_ref, w_ref, gain_ref, router_ref, cos_ref, sin_ref, n_ref, kv_ref, l_ref):
    x = x_ref[...].astype(F32)
    scale = lax.rsqrt(jnp.mean(x * x, axis=-1, keepdims=True) + EPSILON)
    normed = (x * scale * gain_ref[...]).astype(BF16)
    n_ref[...] = normed
    l_ref[...] = product_nt(normed, router_ref[...])
    raw = product(normed, w_ref[...])
    piece = kv_ref.shape[2]
    spread = lambda ref: jnp.concatenate(
        [ref[i] for i in range(ref.shape[0]) for _ in range(micro)], axis=0
    )
    cosine, sine = spread(cos_ref), spread(sin_ref)
    for head in range(piece // HDIM):
        cols = slice(head * HDIM, (head + 1) * HDIM)
        kv_ref[0, :, cols] = turn(raw[:, cols], cosine, sine).astype(BF16)
    kv_ref[1] = raw[:, piece:].astype(BF16)


def project(tokens, weight, gain, router, cosine, sine, micro):
    rows, width = tokens.shape
    piece = weight.shape[1] // 2
    experts, tok, half = cosine.shape
    block = 2 * micro * tok
    loops = experts // 2
    return pl.pallas_call(
        partial(project_kernel, micro),
        grid=(rows // block,),
        in_specs=[
            pl.BlockSpec((block, width), lambda i: (i, 0)),
            pl.BlockSpec(weight.shape, lambda i: (0, 0)),
            pl.BlockSpec((1, width), lambda i: (0, 0)),
            pl.BlockSpec(router.shape, lambda i: (0, 0)),
            pl.BlockSpec((2, tok, half), lambda i: (i % loops, 0, 0)),
            pl.BlockSpec((2, tok, half), lambda i: (i % loops, 0, 0)),
        ],
        out_specs=[
            pl.BlockSpec((block, width), lambda i: (i, 0)),
            pl.BlockSpec((2, block, piece), lambda i: (0, i, 0)),
            pl.BlockSpec((block, experts), lambda i: (i, 0)),
        ],
        out_shape=[
            jax.ShapeDtypeStruct((rows, width), BF16),
            jax.ShapeDtypeStruct((2, rows, piece), BF16),
            jax.ShapeDtypeStruct((rows, experts), F32),
        ],
        compiler_params=pltpu.CompilerParams(vmem_limit_bytes=40 * 2**20),
        cost_estimate=pl.CostEstimate(
            flops=2 * rows * width * weight.shape[1], bytes_accessed=5 * rows * width, transcendentals=0
        ),
        name="project",
    )(tokens, weight, gain, router, cosine, sine)


def gather(value, axes, axis=0):
    return lax.all_gather(value, axes, axis=axis, tiled=True)


def scatter(value, axes, axis=0):
    return lax.psum_scatter(value, axes, scatter_dimension=axis, tiled=True)


def swap(value, axes, split=0, concat=0):
    return lax.all_to_all(value, axes, split_axis=split, concat_axis=concat, tiled=True)


DP = ("line", "pair")
ALL = ("line", "pair", "expert")
TREES = ("pair", "expert")


def body(
    tokens,
    w_query,
    w_out,
    w_key,
    w_value,
    gain_attn,
    router_attn,
    gain_mlp,
    router_mlp,
    w_gate,
    w_up,
    w_down,
    attn_route,
    mlp_route,
    fill_order,
    parents,
    cotangent,
):
    experts = lax.axis_size("expert")
    pair = lax.axis_size("pair")
    line = lax.axis_size("line")
    position = lax.axis_index("expert")
    micro, _, tok, width = tokens.shape
    tree = experts * tok
    rows = pair * experts * micro * tok
    heads_total = w_query.shape[2]
    part = heads_total // (line * pair)
    feats = heads_total // pair
    piece = feats // experts
    own_in = w_query.shape[1]
    own_kv = w_key.shape[0]
    capacity = tok * mlp_route.shape[3] // experts
    scale = 1.0 / math.sqrt(HDIM)

    places, segment, depth = tree_layout(tree // 16, tree)
    half = HDIM // 2
    rates = 10000.0 ** (-jnp.arange(half, dtype=F32) / half)
    angle = depth.astype(F32)[:, None] * rates[None, :]
    cosine, sine = jnp.cos(angle), jnp.sin(angle)

    sizes = (line, pair, experts)
    walk = line == 4 and pair == 2 and experts == 4
    own_tokens = tokens.reshape(micro * tok, width)
    small = jnp.concatenate(
        [gain_attn[None], gain_mlp[None], router_attn.T, router_mlp.T], axis=0
    )
    integers = jnp.concatenate([attn_route[:, 0].reshape(micro, -1), parents[:, 0]], axis=1)
    if walk:
        flat = integers.reshape(-1)
        flat = jnp.pad(flat, (0, -flat.shape[0] % 1024)).reshape(-1, 128)
        tree_tokens, query_weight, kv_weight, small, flat = start_all(
            own_tokens, w_query[0], w_key, w_value, small, flat, sizes, 1
        )
        query_weight = query_weight.reshape(width, feats)
        kv_weight = kv_weight.reshape(width, 2 * piece)
        integers = flat.reshape(pair, -1)[:, : integers.size].reshape((pair,) + integers.shape)
    else:
        query_mine = w_query[0].reshape(own_in, line, pair, part)
        query_mine = jnp.transpose(query_mine, (2, 0, 1, 3)).reshape(pair, own_in, feats)
        if pair == 2:
            query_mine = swap(query_mine, "pair")
            integers = lax.all_gather(integers, "pair", axis=0)
        else:
            integers = integers[None]
        query_weight = gather(query_mine.reshape(pair * own_in, feats), "line")
        kv_mine = jnp.stack([w_key, w_value], axis=1).reshape(
            own_kv, 2, experts, line // experts, pair, part
        )
        kv_mine = jnp.transpose(kv_mine, (4, 2, 0, 1, 3, 5)).reshape(
            pair * experts, own_kv, 2 * piece
        )
        tree_tokens = cube_gather(own_tokens, pair, 1)
        small = small_exchange(small, sizes, False, 2)
        kv_mine = swap(kv_mine, TREES).reshape(pair * experts * own_kv, 2 * piece)
        kv_weight = gather(kv_mine, "line")
    out_mine, small = lax.optimization_barrier((w_out[0], small))
    out_weight = gather(out_mine, "line")

    small = jnp.transpose(small, (1, 0, 2)).reshape(-1, width)
    first_gain = small[0].astype(F32)
    second_gain = small[1].astype(F32)
    first_router = small[2 : 2 + experts]
    second_router = small[2 + experts : 2 + 2 * experts]

    residual = own_tokens.astype(F32)
    _, first_pull = jax.vjp(rms_scaled, residual, first_gain)
    table_shape = (experts, tok, half)
    tree_input, kv, first_logits = project(
        tree_tokens.reshape(rows, width),
        kv_weight,
        first_gain[None],
        first_router,
        cosine.reshape(table_shape),
        sine.reshape(table_shape),
        micro,
    )

    routes = integers[..., : tree * 2].reshape(pair, micro, experts, tok, 2)
    routes = jnp.transpose(routes, (0, 2, 1, 3, 4)).reshape(rows, 2)
    family = integers[..., tree * 2 :]
    bias = jax.vmap(jax.vmap(lambda parent: score_bias(parent, segment, places)))(family)

    kv = cube_gather(kv.reshape(2 * rows, piece), 1, 3)
    shape = (pair, experts, micro, tok, feats)
    kv = kv.reshape(experts, 2, pair, experts, micro, tok, piece)

    first_gates, first_gate_pull = jax.vjp(partial(mixture_gates, routes), first_logits)
    column = (jnp.arange(experts, dtype=jnp.int32) == position).astype(F32)
    own_gate = jnp.sum(first_gates * column[None, :], axis=1)

    raw = product(tree_input, query_weight)
    queries, heads_out = attend(raw.reshape(shape), kv, cosine, sine, bias, scale)
    heads_flat = heads_out.reshape(rows, feats)
    projected = product(heads_flat, out_weight)
    gated = (own_gate[:, None] * projected).astype(BF16)
    projected = projected.astype(BF16)
    attention = cube_reduce(gated.reshape(pair * experts, micro * tok, width), pair, 4).astype(F32)

    middle = residual + attention
    second_normed, second_pull = jax.vjp(rms_scaled, middle, second_gain)
    second_normed = second_normed.astype(BF16)
    picked = mlp_route[:, 0].reshape(micro * tok, 2)
    second_gates, second_gate_pull = jax.vjp(
        partial(mixture_gates, picked), product_nt(second_normed, second_router)
    )
    table = jax.vmap(partial(slot_table, experts=experts, capacity=capacity))(
        mlp_route[:, 0], fill_order[:, 0]
    )
    table_low = table.astype(BF16)
    grouped = second_normed.reshape(micro, tok, width)
    outgoing = jnp.einsum("mect,mtd->emcd", table_low, grouped, preferred_element_type=F32)
    top_grad = cotangent.reshape(micro, tok, width)
    slot_values = jnp.einsum("mect,mtd->emcd", table_low, top_grad, preferred_element_type=F32)
    slot_gates = jnp.einsum(
        "mect,mte->emc", table, second_gates.reshape(micro, tok, experts), precision=HIGHEST
    )
    slot_grad = (slot_gates[..., None] * slot_values).astype(BF16)
    slots = experts * micro * capacity
    outgoing = outgoing.astype(BF16).reshape(experts, micro * capacity, width)
    slot_grad = slot_grad.reshape(experts, micro * capacity, width)
    gate_weight, up_weight, down_weight = w_gate[0], w_up[0], w_down[0]
    if walk:
        returned, came_back, arrived, result_grad, inner, gate_grad, up_grad = feed_forward(
            outgoing, slot_grad, gate_weight, up_weight, down_weight, line, pair, 5
        )
        arrived, result_grad, inner, gate_grad, up_grad = (
            value.reshape(-1, value.shape[-1])
            for value in (arrived, result_grad, inner, gate_grad, up_grad)
        )
    else:
        arrived = gather(swap(outgoing, "expert").reshape(slots, width), DP)
        result_grad = gather(swap(slot_grad, "expert").reshape(slots, width), DP)
        gate_pre = product_nt(arrived, gate_weight)
        up_pre = product_nt(arrived, up_weight)
        sigma = jax.nn.sigmoid(gate_pre)
        inner = (gate_pre * sigma * up_pre).astype(BF16)
        returned = product(inner, down_weight).astype(BF16)
        inner_grad = product_nt(result_grad, down_weight)
        gate_grad = (inner_grad * up_pre * sigma * (1.0 + gate_pre * (1.0 - sigma))).astype(BF16)
        up_grad = (inner_grad * gate_pre * sigma).astype(BF16)
        came_back = (product(gate_grad, gate_weight) + product(up_grad, up_weight)).astype(BF16)
        back = (experts, micro * capacity, width)
        returned = swap(scatter(returned, DP).reshape(back), "expert")
        came_back = swap(scatter(came_back, DP).reshape(back), "expert")
    returned = returned.reshape(experts, micro, capacity, width)
    came_back = came_back.reshape(experts, micro, capacity, width)
    spread = jnp.einsum("mect,emcd->emtd", table_low, returned, preferred_element_type=F32)
    spread = spread.reshape(experts, micro * tok, width)
    mixed = jnp.sum(jnp.transpose(second_gates)[:, :, None] * spread, axis=0)
    layer_out = (middle + mixed).astype(BF16)
    dz = top_grad.reshape(micro * tok, width).astype(F32)
    second_gate_grad = jnp.transpose(jnp.sum(spread * dz[None], axis=-1))
    (second_logit_grad,) = second_gate_pull(second_gate_grad)
    hn_grad = jnp.einsum("mect,emcd->mtd", table_low, came_back, preferred_element_type=F32)
    hn_grad = hn_grad.reshape(micro * tok, width)
    second_router_wide = second_router.astype(F32)
    for expert in range(experts):
        hn_grad = hn_grad + second_logit_grad[:, expert : expert + 1] * second_router_wide[expert]
    grad_router_second = split_product(second_logit_grad, second_normed)
    middle_grad, grad_gain_second = second_pull(hn_grad)
    middle_grad = middle_grad + dz

    mix_grad = cube_gather(middle_grad.astype(BF16), pair, 7).reshape(rows, width).astype(F32)
    own_gate_grad = jnp.sum(mix_grad * projected.astype(F32), axis=-1)
    projected_grad = (own_gate[:, None] * mix_grad).astype(BF16)
    grad_output = product_tn(heads_flat, projected_grad).astype(BF16)
    grad_output, projected_grad = lax.optimization_barrier((grad_output, projected_grad))
    grad_output = scatter(grad_output, "line")
    heads_grad = product_nt(projected_grad, out_weight).astype(BF16).reshape(shape)
    query_pre, kv_pre = attend_back(queries, kv, heads_grad, cosine, sine, bias, scale)
    query_pre = query_pre.reshape(rows, feats)
    grad_query = product_tn(tree_input, query_pre).astype(BF16)
    grad_query, kv_pre = lax.optimization_barrier((grad_query, kv_pre))
    kv_sum = cube_reduce(kv_pre.reshape(experts, 2 * rows, piece), 1, 8)
    grad_query, grad_output, kv_sum = lax.optimization_barrier((grad_query, grad_output, kv_sum))
    (first_logit_grad,) = first_gate_pull(own_gate_grad[:, None] * column[None, :])
    kv_sum = kv_sum.reshape(2, rows, piece)
    grad_kv = jnp.concatenate(
        [product_tn(tree_input, kv_sum[0]), product_tn(tree_input, kv_sum[1])], axis=1
    ).astype(BF16)
    input_term = input_gradient(
        query_pre, query_weight, kv_sum, kv_weight, first_logit_grad, first_router.astype(F32)
    ).reshape(pair * experts, micro * tok, width)
    normed_grad = cube_reduce(input_term, pair, 9)
    if not walk:
        grad_kv = scatter(grad_kv, "line")
        grad_kv = swap(grad_kv.reshape(pair * experts, own_kv, 2 * piece), TREES)
        grad_kv = grad_kv.reshape(pair, experts, own_kv, 2, line // experts, part)
        grad_kv = jnp.transpose(grad_kv, (2, 3, 1, 4, 0, 5)).reshape(own_kv, 2, heads_total)
        grad_key, grad_value = grad_kv[:, 0].astype(F32), grad_kv[:, 1].astype(F32)
    grad_query = scatter(grad_query, "line")
    gate_grad, up_grad, inner, arrived, result_grad, normed_grad = lax.optimization_barrier(
        (gate_grad, up_grad, inner, arrived, result_grad, normed_grad)
    )
    grad_gate = product_tn(gate_grad, arrived)[None]
    grad_upward = product_tn(up_grad, arrived)[None]
    grad_downward = product_tn(inner, result_grad)[None]
    normed_grad = normed_grad.astype(F32)
    grad_router_first = split_product(first_logit_grad, tree_input)
    token_grad, grad_gain_first = first_pull(normed_grad)
    tokens_grad = token_grad + middle_grad

    sums = jnp.concatenate(
        [grad_gain_first[None], grad_gain_second[None], grad_router_first, grad_router_second],
        axis=0,
    )
    sums = jnp.transpose(sums.reshape(sums.shape[0], -1, own_kv), (1, 0, 2))
    if walk:
        sums, grad_query, grad_key, grad_value = last_exchange(
            sums, grad_query.reshape(pair, own_in, feats), grad_kv, sizes, 10
        )
        grad_query = grad_query[None]
    else:
        sums = small_exchange(sums, sizes, True, 10)
        grad_query = swap(grad_query.reshape(own_in * pair, line, part)[None], "pair", 1, 0)
        grad_query = jnp.transpose(grad_query, (1, 2, 0, 3)).reshape(1, own_in, heads_total)
    return (
        layer_out.reshape(micro, 1, tok, width),
        tokens_grad.reshape(micro, 1, tok, width),
        grad_query.astype(F32),
        grad_output[None].astype(F32),
        grad_key,
        grad_value,
        sums[0],
        jnp.transpose(sums[2 : 2 + experts]),
        sums[1],
        jnp.transpose(sums[2 + experts :]),
        grad_gate,
        grad_upward,
        grad_downward,
    )


def solution(mesh):
    line, experts = mesh.devices.shape
    pair = 2 if line % 2 == 0 and (HEADS % line == 0) else 1
    shaped = Mesh(mesh.devices.reshape(line // pair, pair, experts), ALL)
    in_specs = (
        P(None, DP, "expert", None),
        P("expert", DP, None),
        P("expert", DP, None),
        P(ALL, None),
        P(ALL, None),
        P(ALL),
        P(ALL, None),
        P(ALL),
        P(ALL, None),
        P("expert", DP, None),
        P("expert", DP, None),
        P("expert", DP, None),
        P(None, DP, None, None),
        P(None, DP, "expert", None),
        P(None, DP, "expert"),
        P(None, DP, None),
        P(None, DP, "expert", None),
    )
    out_specs = (
        P(None, DP, "expert", None),
        P(None, DP, "expert", None),
        P("expert", DP, None),
        P("expert", DP, None),
        P(ALL, None),
        P(ALL, None),
        P(ALL),
        P(ALL, None),
        P(ALL),
        P(ALL, None),
        P("expert", DP, None),
        P("expert", DP, None),
        P("expert", DP, None),
    )
    return jax.shard_map(body, mesh=shaped, in_specs=in_specs, out_specs=out_specs, check_vma=False)
```

```python
from functools import partial
import math

import jax
import jax.numpy as jnp
from jax import lax
from jax.experimental import pallas as pl
from jax.experimental.pallas import tpu as pltpu
from jax.sharding import Mesh, PartitionSpec as P

HEADS = 16
HDIM = 128
EPSILON = 1e-06
HIGHEST = lax.Precision.HIGHEST
BF16 = jnp.bfloat16
F32 = jnp.float32


def product(left, right):
    return jnp.dot(left, right, preferred_element_type=F32)


def product_tn(left, right):
    return lax.dot_general(left, right, (((0,), (0,)), ((), ())), preferred_element_type=F32)


def product_nt(left, right):
    return lax.dot_general(left, right, (((1,), (1,)), ((), ())), preferred_element_type=F32)


def split_product(values, rows):
    parts, rest = [], values
    for _ in range(3):
        parts.append(lax.reduce_precision(rest, 8, 7))
        rest = rest - parts[-1]
    count = values.shape[1]
    total = product_tn(jnp.concatenate(parts, axis=1).astype(BF16), rows)
    return total[:count] + total[count : 2 * count] + total[2 * count :]


def rms_scaled(values, gain):
    return values * lax.rsqrt(jnp.mean(values * values, axis=-1, keepdims=True) + EPSILON) * gain


def mixture_gates(picked, logits):
    labels = jnp.arange(logits.shape[1], dtype=jnp.int32)
    onehot = (picked[:, :, None] == labels[None, None, :]).astype(F32)
    chosen = jnp.sum(onehot * logits[:, None, :], axis=-1)
    weights = jax.nn.softmax(chosen, axis=-1)
    return jnp.sum(weights[:, :, None] * onehot, axis=1)


def tree_layout(segment_len, tree_len):
    places = jnp.arange(tree_len, dtype=jnp.int32)
    trunk_len = 4 * segment_len
    segment = jnp.where(
        places < trunk_len,
        0,
        jnp.where(
            places < 2 * trunk_len,
            1 + (places - trunk_len) // segment_len,
            5 + (places - 2 * trunk_len) // segment_len,
        ),
    )
    depth = jnp.where(
        places < trunk_len,
        places,
        jnp.where(
            places < 2 * trunk_len,
            trunk_len + (places - trunk_len) % segment_len,
            trunk_len + segment_len + (places - 2 * trunk_len) % segment_len,
        ),
    )
    return (places, segment, depth)


def ancestors(parent, segment):
    labels = jnp.arange(parent.shape[0], dtype=jnp.int32)
    first = jnp.where(labels > 0, parent, -1)
    lookup = jnp.maximum(first, 0)[:, None] == labels[None, :]
    second = jnp.where(first > 0, jnp.sum(jnp.where(lookup, parent[None, :], 0), axis=1), -1)
    member = segment[:, None] == labels[None, :]
    up_one = jnp.sum(jnp.where(member, first[None, :], 0), axis=1)
    up_two = jnp.sum(jnp.where(member, second[None, :], 0), axis=1)
    return (up_one, up_two)


def score_bias(parent, segment, places):
    up_one, up_two = ancestors(parent, segment)
    same = (segment[None, :] == segment[:, None]) & (places[None, :] <= places[:, None])
    seen = same | (segment[None, :] == up_one[:, None]) | (segment[None, :] == up_two[:, None])
    return jnp.where(seen, 0.0, -1e30).astype(F32)


def slot_table(picked, order, experts, capacity):
    labels = jnp.arange(experts, dtype=jnp.int32)
    chosen = jnp.sum((picked[:, :, None] == labels[None, None, :]).astype(F32), axis=1)
    earlier = (order[None, :] < order[:, None]).astype(F32)
    ranks = jnp.dot(earlier, chosen, precision=HIGHEST, preferred_element_type=F32)
    slots = jnp.arange(capacity, dtype=F32)
    return jnp.transpose(chosen)[:, None, :] * (
        jnp.transpose(ranks)[:, None, :] == slots[None, :, None]
    ).astype(F32)


def turn(values, cosine, sine):
    half = values.shape[-1] // 2
    first = values[:, :half]
    second = values[:, half:]
    return jnp.concatenate(
        [first * cosine - second * sine, second * cosine + first * sine], axis=-1
    )


def softmax_rows(queries, keys, bias, scale):
    scores = product_nt(queries, keys) * scale + bias
    highest = jnp.max(scores, axis=-1, keepdims=True)
    weights = jnp.exp(scores - highest)
    return weights / jnp.sum(weights, axis=-1, keepdims=True)


def attend_kernel(heads, scale, raw_ref, kv_ref, cos_ref, sin_ref, bias_ref, query_ref, out_ref):
    quarter, tok = raw_ref.shape[1], raw_ref.shape[3]
    rows = quarter * tok
    cosine, sine, bias = cos_ref[...], sin_ref[...], bias_ref[0, 0]
    for head in range(heads):
        cols = slice(head * HDIM, (head + 1) * HDIM)
        raw = raw_ref[0, :, 0, :, cols].reshape(rows, HDIM)
        keys = kv_ref[0, 0, 0, :, 0, :, cols].reshape(rows, HDIM)
        values = kv_ref[0, 1, 0, :, 0, :, cols].reshape(rows, HDIM)
        queries = turn(raw, cosine, sine).astype(BF16)
        probs = softmax_rows(queries, keys, bias, scale).astype(BF16)
        query_ref[0, :, 0, :, cols] = queries.reshape(quarter, tok, HDIM)
        out_ref[0, :, 0, :, cols] = product(probs, values).astype(BF16).reshape(quarter, tok, HDIM)


def attend_back_kernel(
    heads, scale, query_ref, kv_ref, grad_ref, cos_ref, sin_ref, bias_ref, dq_ref, dkv_ref
):
    quarter, tok = query_ref.shape[1], query_ref.shape[3]
    rows = quarter * tok
    cosine, sine, bias = cos_ref[...], sin_ref[...], bias_ref[0, 0]
    for head in range(heads):
        cols = slice(head * HDIM, (head + 1) * HDIM)
        queries = query_ref[0, :, 0, :, cols].reshape(rows, HDIM)
        keys = kv_ref[0, 0, 0, :, 0, :, cols].reshape(rows, HDIM)
        values = kv_ref[0, 1, 0, :, 0, :, cols].reshape(rows, HDIM)
        grad = grad_ref[0, :, 0, :, cols].reshape(rows, HDIM)
        probs = softmax_rows(queries, keys, bias, scale)
        prob_grad = product_nt(grad, values)
        centre = jnp.sum(prob_grad * probs, axis=-1, keepdims=True)
        score_grad = (probs * (prob_grad - centre) * scale).astype(BF16)
        query_grad = turn(product(score_grad, keys), cosine, -sine).astype(BF16)
        key_grad = turn(product_tn(score_grad, queries), cosine, -sine).astype(BF16)
        value_grad = product_tn(probs.astype(BF16), grad).astype(BF16)
        dq_ref[0, :, 0, :, cols] = query_grad.reshape(quarter, tok, HDIM)
        dkv_ref[0, 0, 0, :, 0, :, cols] = key_grad.reshape(quarter, tok, HDIM)
        dkv_ref[0, 1, 0, :, 0, :, cols] = value_grad.reshape(quarter, tok, HDIM)


def attention_specs(shape, slices):
    pair, quarter, micro, tok, feats = shape
    part = feats // slices
    rows = quarter * tok
    grid = (pair, micro, slices)
    flat = pl.BlockSpec((1, quarter, 1, tok, part), lambda i, m, s: (i, 0, m, 0, s))
    both = pl.BlockSpec(
        (1, 2, 1, quarter, 1, tok, part), lambda i, m, s: (s, 0, i, 0, m, 0, 0)
    )
    angle = pl.BlockSpec((rows, HDIM // 2), lambda i, m, s: (0, 0))
    bias = pl.BlockSpec((1, 1, rows, rows), lambda i, m, s: (i, m, 0, 0))
    return grid, part, flat, both, angle, bias


def attend(raw, kv, cosine, sine, bias, scale):
    slices = kv.shape[0]
    grid, part, flat, both, angle, bias_spec = attention_specs(raw.shape, slices)
    out = jax.ShapeDtypeStruct(raw.shape, BF16)
    return pl.pallas_call(
        partial(attend_kernel, part // HDIM, scale),
        grid=grid,
        in_specs=[flat, both, angle, angle, bias_spec],
        out_specs=[flat, flat],
        out_shape=[out, out],
        cost_estimate=pl.CostEstimate(
            flops=4 * raw.size * cosine.shape[0],
            bytes_accessed=12 * raw.size,
            transcendentals=raw.size * 2,
        ),
        name="attend",
    )(raw, kv, cosine, sine, bias)


def attend_back(queries, kv, grad, cosine, sine, bias, scale):
    slices = kv.shape[0]
    grid, part, flat, both, angle, bias_spec = attention_specs(queries.shape, slices)
    return pl.pallas_call(
        partial(attend_back_kernel, part // HDIM, scale),
        grid=grid,
        in_specs=[flat, both, flat, angle, angle, bias_spec],
        out_specs=[flat, both],
        out_shape=[
            jax.ShapeDtypeStruct(queries.shape, BF16),
            jax.ShapeDtypeStruct(kv.shape, BF16),
        ],
        cost_estimate=pl.CostEstimate(
            flops=10 * queries.size * cosine.shape[0],
            bytes_accessed=14 * queries.size,
            transcendentals=queries.size * 2,
        ),
        name="attend_back",
    )(queries, kv, grad, cosine, sine, bias)


MESH = pl.DeviceIdType.MESH
ANY = pl.BlockSpec(memory_space=pl.ANY)
VMEM = pl.BlockSpec(memory_space=pltpu.VMEM)
DMA = pltpu.SemaphoreType.DMA


def remote(src, dst, send, recv, target):
    return pltpu.make_async_remote_copy(
        src_ref=src, dst_ref=dst, send_sem=send, recv_sem=recv, device_id=target, device_id_type=MESH
    )


def greet(targets):
    barrier = pltpu.get_barrier_semaphore()
    for target in targets:
        pl.semaphore_signal(barrier, inc=1, device_id=target, device_id_type=MESH)
    pl.semaphore_wait(barrier, len(targets))


def params(number, limit=None):
    return pltpu.CompilerParams(
        collective_id=number, has_side_effects=True, vmem_limit_bytes=limit
    )


def add_into(target, sources, rows):
    step = 1
    while step * 2 <= rows and step * 2 * target.shape[-1] <= 65536 and rows % (step * 2) == 0:
        step *= 2

    def one(index, carry):
        where = pl.ds(pl.multiple_of(index * step, step), step)
        total = sources[0][where].astype(F32)
        for source in sources[1:]:
            total = total + source[where].astype(F32)
        target[where] = total.astype(target.dtype)
        return carry

    lax.fori_loop(0, rows // step, one, 0)


def cube_reduce_kernel(pairs, x_ref, o_ref, half, quarter, got_core, got_side, got_pair, send, recv):
    p = lax.axis_index("pair")
    e = lax.axis_index("expert")
    c, y = lax.rem(e, 2), lax.div(e, 2)
    core = {"expert": e + 1 - 2 * c}
    side = {"expert": e + 2 - 4 * y}
    other = {"pair": lax.rem(p + 1, pairs)}
    greet([core, side] + ([other] if pairs == 2 else []))
    rows = x_ref.shape[3]
    shifts = (1, 0) if pairs == 2 else (0,)
    order = [(dx, dy) for dy in (1, 0) for dx in shifts]
    first, second = [], {}
    for slot, (dx, dy) in enumerate(order):
        px, yy = lax.rem(p + dx, pairs), lax.rem(y + dy, 2)
        copy = remote(
            x_ref.at[px, yy, 1 - c], got_core.at[slot], send.at[slot], recv.at[slot], core
        )
        copy.start()
        first.append(copy)
    base = len(order)
    for slot, (dx, dy) in enumerate(order):
        px, yy = lax.rem(p + dx, pairs), lax.rem(y + dy, 2)
        first[slot].wait_recv()
        add_into(half.at[slot], [x_ref.at[px, yy, c], got_core.at[slot]], rows)
        if dy == 1:
            copy = remote(
                half.at[slot], got_side.at[dx], send.at[base + dx], recv.at[base + dx], side
            )
            copy.start()
            second[dx] = copy
    last = None
    for dx in shifts:
        second[dx].wait_recv()
        if dx == 1:
            add_into(quarter, [half.at[order.index((1, 0))], got_side.at[1]], rows)
            last = remote(quarter, got_pair, send.at[base + 2], recv.at[base + 2], other)
            last.start()
    if last is not None:
        last.wait_recv()
        add_into(o_ref, [half.at[order.index((0, 0))], got_side.at[0], got_pair], rows)
    else:
        add_into(o_ref, [half.at[order.index((0, 0))], got_side.at[0]], rows)
    for copy in first + list(second.values()) + ([last] if last is not None else []):
        copy.wait_send()


def cube_reduce(value, pairs, number):
    _, rows, cols = value.shape
    value = value.reshape(pairs, 2, 2, rows, cols)
    slots = 2 * pairs
    block = jax.ShapeDtypeStruct((rows, cols), value.dtype)
    return pl.pallas_call(
        partial(cube_reduce_kernel, pairs),
        in_specs=[VMEM],
        out_specs=VMEM,
        out_shape=block,
        scratch_shapes=[
            pltpu.VMEM((slots, rows, cols), value.dtype),
            pltpu.VMEM((rows, cols), value.dtype),
            pltpu.VMEM((slots, rows, cols), value.dtype),
            pltpu.VMEM((pairs, rows, cols), value.dtype),
            pltpu.VMEM((rows, cols), value.dtype),
            DMA((slots + 3,)),
            DMA((slots + 3,)),
        ],
        compiler_params=params(number, 48 * 2**20),
        cost_estimate=pl.CostEstimate(flops=0, bytes_accessed=0, transcendentals=0),
        name="cube_reduce",
    )(value)


def cube_gather_kernel(pairs, x_ref, o_ref, send, recv, local):
    p = lax.axis_index("pair") if pairs == 2 else 0
    e = lax.axis_index("expert")
    c, y = lax.rem(e, 2), lax.div(e, 2)
    core = {"expert": e + 1 - 2 * c}
    side = {"expert": e + 2 - 4 * y}
    other = {"pair": lax.rem(p + 1, pairs)}
    greet([core, side] + ([other] if pairs == 2 else []))
    q, w = lax.rem(p + 1, pairs), 1 - y
    own = o_ref.at[p, y, c]
    keep = pltpu.make_async_copy(x_ref, own, local)
    keep.start()
    copies = []

    def push(slot, source, place, target):
        copy = remote(source, place, send.at[slot], recv.at[slot], target)
        copy.start()
        copies.append(copy)
        return copy

    to_side = push(0, x_ref, own, side)
    to_other = push(1, x_ref, own, other) if pairs == 2 else None
    to_core = push(2, x_ref, own, core)
    waits = [to_core]
    if pairs == 2:
        to_other.wait_recv()
        block = o_ref.at[q, y, c]
        far = push(3, block, block, side)
        waits.append(push(4, block, block, core))
    to_side.wait_recv()
    block = o_ref.at[p, w, c]
    waits.append(push(5, block, block, core))
    if pairs == 2:
        far.wait_recv()
        block = o_ref.at[q, w, c]
        waits.append(push(6, block, block, core))
    for copy in waits:
        copy.wait_recv()
    for copy in copies:
        copy.wait_send()
    keep.wait()


def cube_gather(value, pairs, number):
    return pl.pallas_call(
        partial(cube_gather_kernel, pairs),
        in_specs=[VMEM],
        out_specs=VMEM,
        out_shape=jax.ShapeDtypeStruct((pairs, 2, 2) + value.shape, value.dtype),
        scratch_shapes=[DMA((7,)), DMA((7,)), DMA(())],
        compiler_params=params(number, 48 * 2**20),
        cost_estimate=pl.CostEstimate(
            flops=0, bytes_accessed=80 * value.size, transcendentals=0
        ),
        name="cube_gather",
    )(value)


def place_of(index, sizes):
    line, pairs, experts = sizes
    return {
        "line": index // (pairs * experts),
        "pair": (index // experts) % pairs,
        "expert": index % experts,
    }


def small_kernel(sizes, reduce, x_ref, o_ref, got, send, recv):
    line, pairs, experts = sizes
    count = line * pairs * experts
    me = (
        lax.axis_index("line") * (pairs * experts)
        + lax.axis_index("pair") * experts
        + lax.axis_index("expert")
    )
    barrier = pltpu.get_barrier_semaphore()

    def greet_one(offset, carry):
        target = place_of((me + offset) % count, sizes)
        pl.semaphore_signal(barrier, inc=1, device_id=target, device_id_type=MESH)
        return carry

    lax.fori_loop(1, count, greet_one, 0)
    pl.semaphore_wait(barrier, count - 1)

    def copy_to(offset):
        peer = (me + offset) % count
        source = x_ref.at[peer] if reduce else x_ref
        return remote(source, got.at[offset], send.at[offset], recv.at[offset], place_of(peer, sizes))

    def start(offset, carry):
        copy_to(offset).start()
        return carry

    lax.fori_loop(1, count, start, 0)
    got[0] = x_ref[me] if reduce else x_ref[...]

    def finish(offset, carry):
        copy_to(offset).wait()
        return carry

    lax.fori_loop(1, count, finish, 0)
    if reduce:
        o_ref[...] = jnp.sum(got[...], axis=0)
    else:

        def order(offset, carry):
            o_ref[(me - offset + count) % count] = got[offset]
            return carry

        lax.fori_loop(0, count, order, 0)


def small_exchange(value, sizes, reduce, number):
    count = sizes[0] * sizes[1] * sizes[2]
    block = value.shape[1:] if reduce else value.shape
    return pl.pallas_call(
        partial(small_kernel, sizes, reduce),
        in_specs=[VMEM],
        out_specs=VMEM,
        out_shape=jax.ShapeDtypeStruct(block if reduce else (count,) + block, value.dtype),
        scratch_shapes=[pltpu.VMEM((count,) + block, value.dtype), DMA((count,)), DMA((count,))],
        compiler_params=params(number),
        cost_estimate=pl.CostEstimate(flops=0, bytes_accessed=2**24, transcendentals=0),
        name="small_reduce" if reduce else "small_gather",
    )(value)


def ff_kernel(
    a_in, b_in, gate_hbm, up_hbm, down_hbm,
    a_out, b_out, a_save, b_save, inner_save, dgate_save, dup_save,
    a_buf, b_buf, side, hop, extra, w_gate, w_up, w_down, mid, acc,
    send, recv, load, store, local,
):
    z, p, e = lax.axis_index("line"), lax.axis_index("pair"), lax.axis_index("expert")
    line, _, rows, width = a_buf.shape
    experts, size = a_in.shape[0], a_in.shape[1]
    q = 1 - p
    twin = z + 1 - 2 * (z % 2)
    up, down, other, across = {"line": z + 1}, {"line": z - 1}, {"pair": q}, {"line": twin}
    ins, bufs, outs, saves = (a_in, b_in), (a_buf, b_buf), (a_out, b_out), (a_save, b_save)
    high = z // 2
    near = z + high * (line - 1 - 2 * z)

    def order(t):
        j = t + near * (1 - t // 2) * (1 - 2 * t)
        return j + high * (line - 1 - 2 * j)

    weights = [
        pltpu.make_async_copy(src, dst, load.at[i])
        for i, (src, dst) in enumerate(((gate_hbm, w_gate), (up_hbm, w_up), (down_hbm, w_down)))
    ]
    for copy in weights:
        copy.start()

    barrier = pltpu.get_barrier_semaphore()
    for shift in range(1, experts):
        pl.semaphore_signal(
            barrier, inc=1, device_id={"expert": (e + shift) % experts}, device_id_type=MESH
        )
    pl.semaphore_signal(barrier, inc=1, device_id=other, device_id_type=MESH)

    @pl.when(z > 0)
    def _():
        pl.semaphore_signal(barrier, inc=1, device_id=down, device_id_type=MESH)

    @pl.when(z < line - 1)
    def _():
        pl.semaphore_signal(barrier, inc=1, device_id=up, device_id_type=MESH)

    below, above = (z + line - 1) // line, (2 * line - 2 - z) // line
    pl.semaphore_wait(barrier, experts + below + above)

    UP, DOWN, SIDE, SUMUP, SUMDOWN, SUMSIDE = (i * line for i in range(6))
    SUMTWIN, SWAP = 6 * line, 6 * line + 1
    BACK = SWAP + experts

    def push(src, dst, kind, use, target):
        return remote(src, dst, send.at[kind, use], recv.at[kind, use], target)

    def to_up(kind, j):
        return push(bufs[kind].at[j, p], bufs[kind].at[j, p], kind, UP + j, up)

    def to_down(kind, j):
        return push(bufs[kind].at[j, p], bufs[kind].at[j, p], kind, DOWN + j, down)

    def to_other(kind, j):
        return push(bufs[kind].at[j, p], bufs[kind].at[j, p], kind, SIDE + j, other)

    def sum_up(kind, j):
        return push(bufs[kind].at[j, p], hop.at[kind, j], kind, SUMUP + j, up)

    def sum_down(kind, j, slot):
        return push(bufs[kind].at[j, p], hop.at[kind, slot], kind, SUMDOWN + j, down)

    def sum_other(kind, j):
        return push(bufs[kind].at[j, q], side.at[kind, j], kind, SUMSIDE + j, other)

    def sum_twin():
        return push(bufs[1].at[twin, q], extra, 1, SUMTWIN, across)

    def piece(index):
        return pl.ds(pl.multiple_of(index * size, size), size)

    def save(kind, j, column):
        return pltpu.make_async_copy(
            bufs[kind].at[j, column], saves[kind].at[j, column], store.at[kind, j, column]
        )

    swaps = []
    for kind in range(2):
        home = bufs[kind].at[z, p, piece(e)]
        keep = pltpu.make_async_copy(ins[kind].at[e], home, local.at[kind])
        keep.start()
        group = []
        for shift in range(1, experts):
            peer = (e + shift) % experts
            copy = push(ins[kind].at[peer], home, kind, SWAP + shift, {"expert": peer})
            copy.start()
            group.append(copy)
        swaps.append((keep, group))

    def spread(t, first=False):
        j = order(t)
        for kind in range(2):
            if first:
                swaps[kind][0].wait()
                for copy in swaps[kind][1]:
                    copy.wait_recv()
            else:

                @pl.when(j < z)
                def _():
                    to_up(kind, j).wait_recv()

                @pl.when(j > z)
                def _():
                    to_down(kind, j).wait_recv()

            @pl.when((j <= z) & (z < line - 1))
            def _():
                to_up(kind, j).start()

            @pl.when((j >= z) & (z > 0))
            def _():
                to_down(kind, j).start()

            to_other(kind, j).start()
            save(kind, j, p).start()

    chunk = 512
    steps = width // chunk

    def first_half(j, column):
        for index in range(3):
            acc[index] = jnp.zeros(acc.shape[1:], F32)

        def one(k, carry):
            where = pl.ds(pl.multiple_of(k * chunk, chunk), chunk)
            left = a_buf[j, column, :, where]
            acc[0] += product_nt(left, w_gate[:, where])
            acc[1] += product_nt(left, w_up[:, where])
            acc[2] += product_nt(b_buf[j, column, :, where], w_down[:, where])
            return carry

        lax.fori_loop(0, steps, one, 0)
        part = 32

        def two(i, carry):
            where = pl.ds(pl.multiple_of(i * part, part), part)
            gate, lift, grad = acc[0, where], acc[1, where], acc[2, where]
            sigma = jax.nn.sigmoid(gate)
            mid[j, column, 0, where] = (gate * sigma * lift).astype(BF16)
            mid[j, column, 1, where] = (
                grad * lift * sigma * (1.0 + gate * (1.0 - sigma))
            ).astype(BF16)
            mid[j, column, 2, where] = (grad * gate * sigma).astype(BF16)
            return carry

        lax.fori_loop(0, rows // part, two, 0)

    def second_half(j, column):
        def one(k, carry):
            where = pl.ds(pl.multiple_of(k * chunk, chunk), chunk)
            a_buf[j, column, :, where] = product(mid[j, column, 0], w_down[:, where]).astype(BF16)
            b_buf[j, column, :, where] = (
                product(mid[j, column, 1], w_gate[:, where])
                + product(mid[j, column, 2], w_up[:, where])
            ).astype(BF16)
            return carry

        lax.fori_loop(0, steps, one, 0)

    def arrive(j):
        for kind in range(2):
            to_other(kind, j).wait_recv()
            save(kind, j, q).start()

    def emit(t):
        j = order(t)
        sum_other(0, j).start()

        @pl.when((j != twin) & (j != z))
        def _():
            sum_other(1, j).start()

    def step(s, carry):
        @pl.when(s == 0)
        def _():
            spread(0, True)
            for copy in weights:
                copy.wait()

        @pl.when(s == 1)
        def _():
            spread(1)
            spread(2)

        @pl.when(s == 3)
        def _():
            spread(3)

        @pl.when(s == line)
        def _():
            sum_twin().start()

        def half(c, inner_carry):
            t = s - c
            column = p + c * (q - p)

            @pl.when((t >= 0) & (t < line))
            def _():
                j = order(t)

                @pl.when(c == 1)
                def _():
                    arrive(j)

                first_half(j, column)

                @pl.when(c == 1)
                def _():
                    for kind in range(2):
                        save(kind, j, q).wait()
                    second_half(j, column)

            return inner_carry

        return lax.fori_loop(0, 2, half, carry)

    lax.fori_loop(0, line + 1, step, 0)

    for t in (3, 2, 1, 0):
        emit(t)

    for copy in (
        pltpu.make_async_copy(mid.at[:, :, 0], inner_save, local.at[2]),
        pltpu.make_async_copy(mid.at[:, :, 1], dgate_save, local.at[3]),
        pltpu.make_async_copy(mid.at[:, :, 2], dup_save, local.at[4]),
    ):
        copy.start()
    sum_twin().wait_recv()
    add_into(b_buf.at[z, q], [b_buf.at[z, q], extra], rows)
    sum_other(1, z).start()

    def back(kind):
        own = pltpu.make_async_copy(
            bufs[kind].at[z, p, piece(e)], outs[kind].at[e], local.at[kind]
        )
        return [own] + [
            push(
                bufs[kind].at[z, p, piece((e + shift) % experts)],
                outs[kind].at[e],
                kind,
                BACK + shift,
                {"expert": (e + shift) % experts},
            )
            for shift in range(1, experts)
        ]

    def fold(s, carry):
        t = line - 1 - s
        j = order(t)
        for kind in range(2):
            save(kind, j, p).wait()

            @pl.when((j <= z) & (z < line - 1))
            def _():
                to_up(kind, j).wait_send()

            @pl.when((j >= z) & (z > 0))
            def _():
                to_down(kind, j).wait_send()

            to_other(kind, j).wait_send()

        second_half(j, p)
        for kind in range(2):
            mine = bufs[kind].at[j, p]
            if kind == 0:
                sum_other(kind, j).wait_recv()
                add_into(mine, [mine, side.at[kind, j]], rows)
            else:

                @pl.when(j != twin)
                def _():
                    sum_other(kind, j).wait_recv()
                    add_into(mine, [mine, side.at[kind, j]], rows)

            @pl.when((j >= z) & (z > 0))
            def _():
                sum_up(kind, j).wait_recv()
                add_into(mine, [mine, hop.at[kind, j]], rows)

            @pl.when((j < z) & (z < line - 1))
            def _():
                sum_down(kind, j, j).wait_recv()
                add_into(mine, [mine, hop.at[kind, j]], rows)

            @pl.when((j == z) & (z < line - 1))
            def _():
                sum_down(kind, j, line).wait_recv()
                add_into(mine, [mine, hop.at[kind, line]], rows)

            @pl.when(j == z)
            def _():
                for copy in back(kind):
                    copy.start()

            @pl.when(j > z)
            def _():
                sum_up(kind, j).start()

            @pl.when((j < z) & (j != z - 1))
            def _():
                sum_down(kind, j, j).start()

            @pl.when((j < z) & (j == z - 1))
            def _():
                sum_down(kind, j, line).start()

        return carry

    lax.fori_loop(0, line, fold, 0)

    for kind in range(2):
        for copy in back(kind):
            copy.wait()

    def drain(j, carry):
        for kind in range(2):
            if kind == 0:
                sum_other(kind, j).wait_send()
            else:

                @pl.when(j != twin)
                def _():
                    sum_other(kind, j).wait_send()

            @pl.when(j > z)
            def _():
                sum_up(kind, j).wait_send()

            @pl.when(j < z)
            def _():
                sum_down(kind, j, j).wait_send()

        return carry

    lax.fori_loop(0, line, drain, 0)
    sum_twin().wait_send()
    for copy in (
        pltpu.make_async_copy(mid.at[:, :, 0], inner_save, local.at[2]),
        pltpu.make_async_copy(mid.at[:, :, 1], dgate_save, local.at[3]),
        pltpu.make_async_copy(mid.at[:, :, 2], dup_save, local.at[4]),
    ):
        copy.wait()
    for keep, group in swaps:
        for copy in group:
            copy.wait_send()


def feed_forward(first, second, w_gate, w_up, w_down, line, pairs, number):
    experts, size, width = first.shape
    hidden = w_gate.shape[0]
    rows = experts * size
    blocks = (line, pairs, rows)
    back = jax.ShapeDtypeStruct(first.shape, BF16)
    wide = jax.ShapeDtypeStruct(blocks + (width,), BF16)
    thin = jax.ShapeDtypeStruct(blocks + (hidden,), BF16)
    uses = 6 * line + 2 + 2 * experts
    total = line * pairs * rows
    return pl.pallas_call(
        ff_kernel,
        in_specs=[ANY] * 5,
        out_specs=[ANY] * 7,
        out_shape=[back, back, wide, wide, thin, thin, thin],
        scratch_shapes=[
            pltpu.VMEM(blocks + (width,), BF16),
            pltpu.VMEM(blocks + (width,), BF16),
            pltpu.VMEM((2, line, rows, width), BF16),
            pltpu.VMEM((2, line + 1, rows, width), BF16),
            pltpu.VMEM((rows, width), BF16),
            pltpu.VMEM((hidden, width), BF16),
            pltpu.VMEM((hidden, width), BF16),
            pltpu.VMEM((hidden, width), BF16),
            pltpu.VMEM((line, pairs, 3, rows, hidden), BF16),
            pltpu.VMEM((3, rows, hidden), F32),
            DMA((2, uses)),
            DMA((2, uses)),
            DMA((3,)),
            DMA((2, line, pairs)),
            DMA((5,)),
        ],
        compiler_params=params(number, 63 * 2**20),
        cost_estimate=pl.CostEstimate(
            flops=12 * total * hidden * width,
            bytes_accessed=12 * total * width,
            transcendentals=total * hidden,
        ),
        name="feed_forward",
    )(first, second, w_gate, w_up, w_down)


def last_kernel(
    sizes, x_ref, q_ref, g_hbm, o_ref, w_ref, key_ref, value_ref,
    got, side, g_ref, k_ref, hop, send, recv, peer_send, peer_recv, local,
):
    line, pairs, experts = sizes
    trees = pairs * experts
    count = line * trees
    z, p, e = lax.axis_index("line"), lax.axis_index("pair"), lax.axis_index("expert")
    mine = p * experts + e
    me = z * trees + mine
    span, piece = g_ref.shape[1], k_ref.shape[1]
    up, down = {"line": z + 1}, {"line": z - 1}
    high = z // 2
    near = z + high * (line - 1 - 2 * z)

    def order(t):
        j = t + near * (1 - t // 2) * (1 - 2 * t)
        return j + high * (line - 1 - 2 * j)

    fetch = pltpu.make_async_copy(g_hbm, g_ref, local)
    fetch.start()
    barrier = pltpu.get_barrier_semaphore()

    def greet_one(offset, carry):
        target = place_of((me + offset) % count, sizes)
        pl.semaphore_signal(barrier, inc=1, device_id=target, device_id_type=MESH)
        return carry

    lax.fori_loop(1, count, greet_one, 0)
    pl.semaphore_wait(barrier, count - 1)
    UP, DOWN, SWAP, PAIR = 0, line, 2 * line, 2 * line + trees

    def sum_up(j):
        return remote(g_ref.at[j], hop.at[j], send.at[UP + j], recv.at[UP + j], up)

    def sum_down(j, slot):
        return remote(g_ref.at[j], hop.at[slot], send.at[DOWN + j], recv.at[DOWN + j], down)

    def fold(t):
        j = order(t)
        own = g_ref.at[j]

        @pl.when((j >= z) & (z > 0))
        def _():
            sum_up(j).wait_recv()
            add_into(own, [own, hop.at[j]], span)

        @pl.when((j < z) & (z < line - 1))
        def _():
            sum_down(j, j).wait_recv()
            add_into(own, [own, hop.at[j]], span)

        @pl.when((j == z) & (z < line - 1))
        def _():
            sum_down(j, line).wait_recv()
            add_into(own, [own, hop.at[line]], span)

        @pl.when(j > z)
        def _():
            sum_up(j).start()

        @pl.when((j < z) & (j != z - 1))
        def _():
            sum_down(j, j).start()

        @pl.when((j < z) & (j == z - 1))
        def _():
            sum_down(j, line).start()

    fetch.wait()
    fold(3)
    swap = remote(q_ref.at[1 - p], side, send.at[PAIR], recv.at[PAIR], {"pair": 1 - p})
    swap.start()

    def copy_to(offset):
        peer = (me + offset) % count
        return remote(
            x_ref.at[peer],
            got.at[offset],
            peer_send.at[offset],
            peer_recv.at[offset],
            place_of(peer, sizes),
        )

    def start(offset, carry):
        copy_to(offset).start()
        return carry

    lax.fori_loop(1, count, start, 0)
    got[0] = x_ref[me]
    fold(2)
    part = q_ref.shape[2] // line

    def lay(block, source):
        for index in range(line):
            column = pl.multiple_of((index * pairs + source) * part, part)
            w_ref[:, pl.ds(column, part)] = block[:, index * part : (index + 1) * part].astype(F32)

    lay(q_ref.at[p], p)
    fold(1)
    swap.wait_recv()
    lay(side, 1 - p)

    def finish(offset, carry):
        copy_to(offset).wait()
        return carry

    lax.fori_loop(1, count, finish, 0)
    o_ref[...] = jnp.sum(got[...], axis=0)
    fold(0)

    def share_of(index):
        return g_ref.at[z, pl.ds(pl.multiple_of(index * piece, piece), piece)]

    keep = pltpu.make_async_copy(share_of(mine), k_ref.at[mine], local)
    keep.start()
    swaps = []
    for shift in range(1, trees):
        peer = (mine + shift) % trees
        copy = remote(
            share_of(peer),
            k_ref.at[mine],
            send.at[SWAP + shift],
            recv.at[SWAP + shift],
            {"pair": peer // experts, "expert": peer % experts},
        )
        copy.start()
        swaps.append(copy)
    keep.wait()
    for copy in swaps:
        copy.wait()
    share = k_ref.shape[2] // 2
    for source in range(trees):
        column = ((source % experts) * pairs + source // experts) * share
        for index, target in enumerate((key_ref, value_ref)):
            target[:, column : column + share] = k_ref[
                source, :, index * share : (index + 1) * share
            ].astype(F32)
    swap.wait_send()

    def drain(j, carry):
        @pl.when(j > z)
        def _():
            sum_up(j).wait_send()

        @pl.when(j < z)
        def _():
            sum_down(j, j).wait_send()

        return carry

    lax.fori_loop(0, line, drain, 0)


def last_exchange(sums, query, grads, sizes, number):
    line, pairs, experts = sizes
    trees = pairs * experts
    count, block = sums.shape[0], sums.shape[1:]
    _, rows, cols = query.shape
    span, thin = grads.shape[0] // line, grads.shape[1]
    uses = 2 * line + trees + 1
    wide = jax.ShapeDtypeStruct((span // trees, trees * thin // 2), F32)
    return pl.pallas_call(
        partial(last_kernel, sizes),
        in_specs=[VMEM, VMEM, ANY],
        out_specs=[VMEM] * 4,
        out_shape=[
            jax.ShapeDtypeStruct(block, F32),
            jax.ShapeDtypeStruct((rows, pairs * cols), F32),
            wide,
            wide,
        ],
        scratch_shapes=[
            pltpu.VMEM((count,) + block, F32),
            pltpu.VMEM((rows, cols), BF16),
            pltpu.VMEM((line, span, thin), BF16),
            pltpu.VMEM((trees, span // trees, thin), BF16),
            pltpu.VMEM((line + 1, span, thin), BF16),
            DMA((uses,)),
            DMA((uses,)),
            DMA((count,)),
            DMA((count,)),
            DMA(()),
        ],
        compiler_params=params(number, 48 * 2**20),
        cost_estimate=pl.CostEstimate(flops=0, bytes_accessed=0, transcendentals=0),
        name="last_exchange",
    )(sums, query, grads.reshape(line, span, thin))


def start_all_kernel(
    sizes, tok_ref, wq_ref, wk_ref, wv_ref, small_ref, int_ref,
    tok_out, q_out, kv_out, small_out, int_out,
    q_cut, kv_cut, send, recv, peer_send, peer_recv, local,
):
    line, pairs, experts = sizes
    z, p, e = lax.axis_index("line"), lax.axis_index("pair"), lax.axis_index("expert")
    c, y = e % 2, e // 2
    core, side = {"expert": e + 1 - 2 * c}, {"expert": e + 2 - 4 * y}
    other = {"pair": 1 - p}
    trees = pairs * experts
    count = line * trees
    mine = p * experts + e
    me = z * trees + mine
    barrier = pltpu.get_barrier_semaphore()

    def greet_one(offset, carry):
        target = place_of((me + offset) % count, sizes)
        pl.semaphore_signal(barrier, inc=1, device_id=target, device_id_type=MESH)
        return carry

    lax.fori_loop(1, count, greet_one, 0)
    part = wq_ref.shape[1] // (line * pairs)
    sub = line // experts
    for q in range(pairs):
        for d in range(experts):
            for index, ref in enumerate((wk_ref, wv_ref)):
                for h in range(sub):
                    column = ((d * sub + h) * pairs + q) * part
                    place = (index * sub + h) * part
                    kv_cut[q * experts + d, :, place : place + part] = ref[
                        :, column : column + part
                    ]
    for q in range(pairs):
        for index in range(line):
            column = (index * pairs + q) * part
            q_cut[q, :, index * part : (index + 1) * part] = wq_ref[:, column : column + part]
    pl.semaphore_wait(barrier, count - 1)

    copies, TOK, QSWAP, INTS, KV = [], 0, 7, 8, 9
    WALK = KV + trees

    def push(slot, source, place, target):
        copy = remote(source, place, send.at[slot], recv.at[slot], target)
        copy.start()
        copies.append(copy)
        return copy

    size = kv_cut.shape[1]
    kv_home = kv_out.at[z, pl.ds(pl.multiple_of(mine * size, size), size)]
    pieces = []
    for shift in range(1, trees):
        peer = (mine + shift) % trees
        pieces.append(
            push(
                KV + shift,
                kv_cut.at[peer],
                kv_home,
                {"pair": peer // experts, "expert": peer % experts},
            )
        )
    rows = q_cut.shape[1]
    q_home = q_out.at[z, pl.ds(pl.multiple_of(p * rows, rows), rows)]
    q_swap = push(QSWAP, q_cut.at[1 - p], q_home, other)
    keeps = [
        pltpu.make_async_copy(q_cut.at[p], q_home, local.at[0]),
        pltpu.make_async_copy(kv_cut.at[mine], kv_home, local.at[1]),
        pltpu.make_async_copy(tok_ref, tok_out.at[p, y, c], local.at[2]),
        pltpu.make_async_copy(small_ref, small_out.at[me], local.at[3]),
        pltpu.make_async_copy(int_ref, int_out.at[p], local.at[4]),
    ]
    for copy in keeps:
        copy.start()
    own = tok_out.at[p, y, c]
    to_side = push(TOK, tok_ref, own, side)
    to_other = push(TOK + 1, tok_ref, own, other)
    waits = [push(TOK + 2, tok_ref, own, core), push(INTS, int_ref, int_out.at[p], other)]

    def small_to(offset):
        return remote(
            small_ref,
            small_out.at[me],
            peer_send.at[offset],
            peer_recv.at[offset],
            place_of((me + offset) % count, sizes),
        )

    def small_start(offset, carry):
        small_to(offset).start()
        return carry

    lax.fori_loop(1, count, small_start, 0)

    def walker(ref, base):
        def to_up(j, d):
            return remote(
                ref.at[j], ref.at[j], send.at[base + d], recv.at[base + d], {"line": z + 1}
            )

        def to_down(j, d):
            at = base + line + d
            return remote(ref.at[j], ref.at[j], send.at[at], recv.at[at], {"line": z - 1})

        return to_up, to_down

    walkers = [walker(q_out, WALK), walker(kv_out, WALK + 2 * line + 2)]

    def begin(which):
        to_up, to_down = walkers[which]

        @pl.when(z < line - 1)
        def _():
            to_up(z, 1).start()

        @pl.when(z > 0)
        def _():
            to_down(z, 1).start()

    keeps[1].wait()
    for copy in pieces:
        copy.wait_recv()
    begin(1)
    keeps[0].wait()
    q_swap.wait_recv()
    begin(0)
    to_other.wait_recv()
    block = tok_out.at[1 - p, y, c]
    far = push(TOK + 3, block, block, side)
    waits.append(push(TOK + 4, block, block, core))
    to_side.wait_recv()
    block = tok_out.at[p, 1 - y, c]
    waits.append(push(TOK + 5, block, block, core))
    far.wait_recv()
    block = tok_out.at[1 - p, 1 - y, c]
    waits.append(push(TOK + 6, block, block, core))

    for d in range(1, line):
        for to_up, to_down in walkers[::-1]:

            @pl.when(z - d >= 0)
            def _():
                to_up(z - d, d).wait_recv()

                @pl.when(z < line - 1)
                def _():
                    to_up(z - d, d + 1).start()

            @pl.when(z + d < line)
            def _():
                to_down(z + d, d).wait_recv()

                @pl.when(z > 0)
                def _():
                    to_down(z + d, d + 1).start()

    for d in range(1, line):
        for to_up, to_down in walkers:

            @pl.when((z - d + 1 >= 0) & (z < line - 1))
            def _():
                to_up(z - d + 1, d).wait_send()

            @pl.when((z + d - 1 < line) & (z > 0))
            def _():
                to_down(z + d - 1, d).wait_send()

    for copy in waits:
        copy.wait_recv()
    for copy in copies:
        copy.wait_send()
    for copy in keeps[2:]:
        copy.wait()

    def small_finish(offset, carry):
        small_to(offset).wait()
        return carry

    lax.fori_loop(1, count, small_finish, 0)


def start_all(tokens, w_query, w_key, w_value, small, integers, sizes, number):
    line, pairs, experts = sizes
    trees = pairs * experts
    count = line * trees
    rows, width = w_query.shape
    size = w_key.shape[0]
    feats = width // pairs
    thin = 2 * feats // experts
    uses = 9 + trees + 4 * line + 4
    return pl.pallas_call(
        partial(start_all_kernel, sizes),
        in_specs=[VMEM] * 6,
        out_specs=[VMEM] * 5,
        out_shape=[
            jax.ShapeDtypeStruct((pairs, 2, 2) + tokens.shape, BF16),
            jax.ShapeDtypeStruct((line, pairs * rows, feats), BF16),
            jax.ShapeDtypeStruct((line, trees * size, thin), BF16),
            jax.ShapeDtypeStruct((count,) + small.shape, BF16),
            jax.ShapeDtypeStruct((pairs,) + integers.shape, jnp.int32),
        ],
        scratch_shapes=[
            pltpu.VMEM((pairs, rows, feats), BF16),
            pltpu.VMEM((trees, size, thin), BF16),
            DMA((uses,)),
            DMA((uses,)),
            DMA((count,)),
            DMA((count,)),
            DMA((5,)),
        ],
        compiler_params=params(number, 48 * 2**20),
        name="start_all",
    )(tokens, w_query, w_key, w_value, small, integers)


def input_kernel(dq_ref, wq_ref, kv_ref, wkv_ref, dl_ref, router_ref, o_ref):
    piece = kv_ref.shape[2]
    total = product_nt(dq_ref[...], wq_ref[...])
    total = total + product_nt(kv_ref[0], wkv_ref[:, :piece])
    total = total + product_nt(kv_ref[1], wkv_ref[:, piece:])
    for expert in range(router_ref.shape[0]):
        total = total + dl_ref[:, expert : expert + 1] * router_ref[expert : expert + 1, :]
    o_ref[...] = total.astype(BF16)


def input_gradient(query_pre, query_weight, kv_sum, kv_weight, logit_grad, router):
    rows, feats = query_pre.shape
    width = query_weight.shape[0]
    piece = kv_sum.shape[2]
    experts = router.shape[0]
    block, lanes = min(512, rows), 512
    return pl.pallas_call(
        input_kernel,
        grid=(width // lanes, rows // block),
        in_specs=[
            pl.BlockSpec((block, feats), lambda n, i: (i, 0)),
            pl.BlockSpec((lanes, feats), lambda n, i: (n, 0)),
            pl.BlockSpec((2, block, piece), lambda n, i: (0, i, 0)),
            pl.BlockSpec((lanes, 2 * piece), lambda n, i: (n, 0)),
            pl.BlockSpec((block, experts), lambda n, i: (i, 0)),
            pl.BlockSpec((experts, lanes), lambda n, i: (0, n)),
        ],
        out_specs=pl.BlockSpec((block, lanes), lambda n, i: (i, n)),
        out_shape=jax.ShapeDtypeStruct((rows, width), BF16),
        compiler_params=pltpu.CompilerParams(vmem_limit_bytes=40 * 2**20),
        cost_estimate=pl.CostEstimate(
            flops=2 * rows * width * (feats + 2 * piece), bytes_accessed=6 * rows * width, transcendentals=0
        ),
        name="input_gradient",
    )(query_pre, query_weight, kv_sum, kv_weight, logit_grad, router)


def project_kernel(micro, x_ref, w_ref, gain_ref, router_ref, cos_ref, sin_ref, n_ref, kv_ref, l_ref):
    x = x_ref[...].astype(F32)
    scale = lax.rsqrt(jnp.mean(x * x, axis=-1, keepdims=True) + EPSILON)
    normed = (x * scale * gain_ref[...]).astype(BF16)
    n_ref[...] = normed
    l_ref[...] = product_nt(normed, router_ref[...])
    raw = product(normed, w_ref[...])
    piece = kv_ref.shape[2]
    spread = lambda ref: jnp.concatenate(
        [ref[i] for i in range(ref.shape[0]) for _ in range(micro)], axis=0
    )
    cosine, sine = spread(cos_ref), spread(sin_ref)
    for head in range(piece // HDIM):
        cols = slice(head * HDIM, (head + 1) * HDIM)
        kv_ref[0, :, cols] = turn(raw[:, cols], cosine, sine).astype(BF16)
    kv_ref[1] = raw[:, piece:].astype(BF16)


def project(tokens, weight, gain, router, cosine, sine, micro):
    rows, width = tokens.shape
    piece = weight.shape[1] // 2
    experts, tok, half = cosine.shape
    block = 2 * micro * tok
    loops = experts // 2
    return pl.pallas_call(
        partial(project_kernel, micro),
        grid=(rows // block,),
        in_specs=[
            pl.BlockSpec((block, width), lambda i: (i, 0)),
            pl.BlockSpec(weight.shape, lambda i: (0, 0)),
            pl.BlockSpec((1, width), lambda i: (0, 0)),
            pl.BlockSpec(router.shape, lambda i: (0, 0)),
            pl.BlockSpec((2, tok, half), lambda i: (i % loops, 0, 0)),
            pl.BlockSpec((2, tok, half), lambda i: (i % loops, 0, 0)),
        ],
        out_specs=[
            pl.BlockSpec((block, width), lambda i: (i, 0)),
            pl.BlockSpec((2, block, piece), lambda i: (0, i, 0)),
            pl.BlockSpec((block, experts), lambda i: (i, 0)),
        ],
        out_shape=[
            jax.ShapeDtypeStruct((rows, width), BF16),
            jax.ShapeDtypeStruct((2, rows, piece), BF16),
            jax.ShapeDtypeStruct((rows, experts), F32),
        ],
        compiler_params=pltpu.CompilerParams(vmem_limit_bytes=40 * 2**20),
        cost_estimate=pl.CostEstimate(
            flops=2 * rows * width * weight.shape[1], bytes_accessed=5 * rows * width, transcendentals=0
        ),
        name="project",
    )(tokens, weight, gain, router, cosine, sine)


def gather(value, axes, axis=0):
    return lax.all_gather(value, axes, axis=axis, tiled=True)


def scatter(value, axes, axis=0):
    return lax.psum_scatter(value, axes, scatter_dimension=axis, tiled=True)


def swap(value, axes, split=0, concat=0):
    return lax.all_to_all(value, axes, split_axis=split, concat_axis=concat, tiled=True)


DP = ("line", "pair")
ALL = ("line", "pair", "expert")
TREES = ("pair", "expert")


def body(
    tokens,
    w_query,
    w_out,
    w_key,
    w_value,
    gain_attn,
    router_attn,
    gain_mlp,
    router_mlp,
    w_gate,
    w_up,
    w_down,
    attn_route,
    mlp_route,
    fill_order,
    parents,
    cotangent,
):
    experts = lax.axis_size("expert")
    pair = lax.axis_size("pair")
    line = lax.axis_size("line")
    position = lax.axis_index("expert")
    micro, _, tok, width = tokens.shape
    tree = experts * tok
    rows = pair * experts * micro * tok
    heads_total = w_query.shape[2]
    part = heads_total // (line * pair)
    feats = heads_total // pair
    piece = feats // experts
    own_in = w_query.shape[1]
    own_kv = w_key.shape[0]
    capacity = tok * mlp_route.shape[3] // experts
    scale = 1.0 / math.sqrt(HDIM)

    places, segment, depth = tree_layout(tree // 16, tree)
    half = HDIM // 2
    rates = 10000.0 ** (-jnp.arange(half, dtype=F32) / half)
    angle = depth.astype(F32)[:, None] * rates[None, :]
    cosine, sine = jnp.cos(angle), jnp.sin(angle)

    sizes = (line, pair, experts)
    walk = line == 4 and pair == 2 and experts == 4
    own_tokens = tokens.reshape(micro * tok, width)
    small = jnp.concatenate(
        [gain_attn[None], gain_mlp[None], router_attn.T, router_mlp.T], axis=0
    )
    integers = jnp.concatenate([attn_route[:, 0].reshape(micro, -1), parents[:, 0]], axis=1)
    if walk:
        flat = integers.reshape(-1)
        flat = jnp.pad(flat, (0, -flat.shape[0] % 1024)).reshape(-1, 128)
        tree_tokens, query_weight, kv_weight, small, flat = start_all(
            own_tokens, w_query[0], w_key, w_value, small, flat, sizes, 1
        )
        query_weight = query_weight.reshape(width, feats)
        kv_weight = kv_weight.reshape(width, 2 * piece)
        integers = flat.reshape(pair, -1)[:, : integers.size].reshape((pair,) + integers.shape)
    else:
        query_mine = w_query[0].reshape(own_in, line, pair, part)
        query_mine = jnp.transpose(query_mine, (2, 0, 1, 3)).reshape(pair, own_in, feats)
        if pair == 2:
            query_mine = swap(query_mine, "pair")
            integers = lax.all_gather(integers, "pair", axis=0)
        else:
            integers = integers[None]
        query_weight = gather(query_mine.reshape(pair * own_in, feats), "line")
        kv_mine = jnp.stack([w_key, w_value], axis=1).reshape(
            own_kv, 2, experts, line // experts, pair, part
        )
        kv_mine = jnp.transpose(kv_mine, (4, 2, 0, 1, 3, 5)).reshape(
            pair * experts, own_kv, 2 * piece
        )
        tree_tokens = cube_gather(own_tokens, pair, 1)
        small = small_exchange(small, sizes, False, 2)
        kv_mine = swap(kv_mine, TREES).reshape(pair * experts * own_kv, 2 * piece)
        kv_weight = gather(kv_mine, "line")
    out_mine, small = lax.optimization_barrier((w_out[0], small))
    out_weight = gather(out_mine, "line")

    small = jnp.transpose(small, (1, 0, 2)).reshape(-1, width)
    first_gain = small[0].astype(F32)
    second_gain = small[1].astype(F32)
    first_router = small[2 : 2 + experts]
    second_router = small[2 + experts : 2 + 2 * experts]

    residual = own_tokens.astype(F32)
    _, first_pull = jax.vjp(rms_scaled, residual, first_gain)
    table_shape = (experts, tok, half)
    tree_input, kv, first_logits = project(
        tree_tokens.reshape(rows, width),
        kv_weight,
        first_gain[None],
        first_router,
        cosine.reshape(table_shape),
        sine.reshape(table_shape),
        micro,
    )

    routes = integers[..., : tree * 2].reshape(pair, micro, experts, tok, 2)
    routes = jnp.transpose(routes, (0, 2, 1, 3, 4)).reshape(rows, 2)
    family = integers[..., tree * 2 :]
    bias = jax.vmap(jax.vmap(lambda parent: score_bias(parent, segment, places)))(family)

    kv = cube_gather(kv.reshape(2 * rows, piece), 1, 3)
    shape = (pair, experts, micro, tok, feats)
    kv = kv.reshape(experts, 2, pair, experts, micro, tok, piece)

    first_gates, first_gate_pull = jax.vjp(partial(mixture_gates, routes), first_logits)
    column = (jnp.arange(experts, dtype=jnp.int32) == position).astype(F32)
    own_gate = jnp.sum(first_gates * column[None, :], axis=1)

    raw = product(tree_input, query_weight)
    queries, heads_out = attend(raw.reshape(shape), kv, cosine, sine, bias, scale)
    heads_flat = heads_out.reshape(rows, feats)
    projected = product(heads_flat, out_weight)
    gated = (own_gate[:, None] * projected).astype(BF16)
    projected = projected.astype(BF16)
    attention = cube_reduce(gated.reshape(pair * experts, micro * tok, width), pair, 4).astype(F32)

    middle = residual + attention
    second_normed, second_pull = jax.vjp(rms_scaled, middle, second_gain)
    second_normed = second_normed.astype(BF16)
    picked = mlp_route[:, 0].reshape(micro * tok, 2)
    second_gates, second_gate_pull = jax.vjp(
        partial(mixture_gates, picked), product_nt(second_normed, second_router)
    )
    table = jax.vmap(partial(slot_table, experts=experts, capacity=capacity))(
        mlp_route[:, 0], fill_order[:, 0]
    )
    table_low = table.astype(BF16)
    grouped = second_normed.reshape(micro, tok, width)
    outgoing = jnp.einsum("mect,mtd->emcd", table_low, grouped, preferred_element_type=F32)
    top_grad = cotangent.reshape(micro, tok, width)
    slot_values = jnp.einsum("mect,mtd->emcd", table_low, top_grad, preferred_element_type=F32)
    slot_gates = jnp.einsum(
        "mect,mte->emc", table, second_gates.reshape(micro, tok, experts), precision=HIGHEST
    )
    slot_grad = (slot_gates[..., None] * slot_values).astype(BF16)
    slots = experts * micro * capacity
    outgoing = outgoing.astype(BF16).reshape(experts, micro * capacity, width)
    slot_grad = slot_grad.reshape(experts, micro * capacity, width)
    gate_weight, up_weight, down_weight = w_gate[0], w_up[0], w_down[0]
    if walk:
        returned, came_back, arrived, result_grad, inner, gate_grad, up_grad = feed_forward(
            outgoing, slot_grad, gate_weight, up_weight, down_weight, line, pair, 5
        )
        arrived, result_grad, inner, gate_grad, up_grad = (
            value.reshape(-1, value.shape[-1])
            for value in (arrived, result_grad, inner, gate_grad, up_grad)
        )
    else:
        arrived = gather(swap(outgoing, "expert").reshape(slots, width), DP)
        result_grad = gather(swap(slot_grad, "expert").reshape(slots, width), DP)
        gate_pre = product_nt(arrived, gate_weight)
        up_pre = product_nt(arrived, up_weight)
        sigma = jax.nn.sigmoid(gate_pre)
        inner = (gate_pre * sigma * up_pre).astype(BF16)
        returned = product(inner, down_weight).astype(BF16)
        inner_grad = product_nt(result_grad, down_weight)
        gate_grad = (inner_grad * up_pre * sigma * (1.0 + gate_pre * (1.0 - sigma))).astype(BF16)
        up_grad = (inner_grad * gate_pre * sigma).astype(BF16)
        came_back = (product(gate_grad, gate_weight) + product(up_grad, up_weight)).astype(BF16)
        back = (experts, micro * capacity, width)
        returned = swap(scatter(returned, DP).reshape(back), "expert")
        came_back = swap(scatter(came_back, DP).reshape(back), "expert")
    returned = returned.reshape(experts, micro, capacity, width)
    came_back = came_back.reshape(experts, micro, capacity, width)
    spread = jnp.einsum("mect,emcd->emtd", table_low, returned, preferred_element_type=F32)
    spread = spread.reshape(experts, micro * tok, width)
    mixed = jnp.sum(jnp.transpose(second_gates)[:, :, None] * spread, axis=0)
    layer_out = (middle + mixed).astype(BF16)
    dz = top_grad.reshape(micro * tok, width).astype(F32)
    second_gate_grad = jnp.transpose(jnp.sum(spread * dz[None], axis=-1))
    (second_logit_grad,) = second_gate_pull(second_gate_grad)
    hn_grad = jnp.einsum("mect,emcd->mtd", table_low, came_back, preferred_element_type=F32)
    hn_grad = hn_grad.reshape(micro * tok, width)
    second_router_wide = second_router.astype(F32)
    for expert in range(experts):
        hn_grad = hn_grad + second_logit_grad[:, expert : expert + 1] * second_router_wide[expert]
    grad_router_second = split_product(second_logit_grad, second_normed)
    middle_grad, grad_gain_second = second_pull(hn_grad)
    middle_grad = middle_grad + dz

    mix_grad = cube_gather(middle_grad.astype(BF16), pair, 7).reshape(rows, width).astype(F32)
    own_gate_grad = jnp.sum(mix_grad * projected.astype(F32), axis=-1)
    projected_grad = (own_gate[:, None] * mix_grad).astype(BF16)
    grad_output = product_tn(heads_flat, projected_grad).astype(BF16)
    grad_output, projected_grad = lax.optimization_barrier((grad_output, projected_grad))
    grad_output = scatter(grad_output, "line")
    heads_grad = product_nt(projected_grad, out_weight).astype(BF16).reshape(shape)
    query_pre, kv_pre = attend_back(queries, kv, heads_grad, cosine, sine, bias, scale)
    query_pre = query_pre.reshape(rows, feats)
    grad_query = product_tn(tree_input, query_pre).astype(BF16)
    grad_query, kv_pre = lax.optimization_barrier((grad_query, kv_pre))
    kv_sum = cube_reduce(kv_pre.reshape(experts, 2 * rows, piece), 1, 8)
    grad_query, grad_output, kv_sum = lax.optimization_barrier((grad_query, grad_output, kv_sum))
    (first_logit_grad,) = first_gate_pull(own_gate_grad[:, None] * column[None, :])
    kv_sum = kv_sum.reshape(2, rows, piece)
    grad_kv = jnp.concatenate(
        [product_tn(tree_input, kv_sum[0]), product_tn(tree_input, kv_sum[1])], axis=1
    ).astype(BF16)
    input_term = input_gradient(
        query_pre, query_weight, kv_sum, kv_weight, first_logit_grad, first_router.astype(F32)
    ).reshape(pair * experts, micro * tok, width)
    normed_grad = cube_reduce(input_term, pair, 9)
    if not walk:
        grad_kv = scatter(grad_kv, "line")
        grad_kv = swap(grad_kv.reshape(pair * experts, own_kv, 2 * piece), TREES)
        grad_kv = grad_kv.reshape(pair, experts, own_kv, 2, line // experts, part)
        grad_kv = jnp.transpose(grad_kv, (2, 3, 1, 4, 0, 5)).reshape(own_kv, 2, heads_total)
        grad_key, grad_value = grad_kv[:, 0].astype(F32), grad_kv[:, 1].astype(F32)
    grad_query = scatter(grad_query, "line")
    gate_grad, up_grad, inner, arrived, result_grad, normed_grad = lax.optimization_barrier(
        (gate_grad, up_grad, inner, arrived, result_grad, normed_grad)
    )
    grad_gate = product_tn(gate_grad, arrived)[None]
    grad_upward = product_tn(up_grad, arrived)[None]
    grad_downward = product_tn(inner, result_grad)[None]
    normed_grad = normed_grad.astype(F32)
    grad_router_first = split_product(first_logit_grad, tree_input)
    token_grad, grad_gain_first = first_pull(normed_grad)
    tokens_grad = token_grad + middle_grad

    sums = jnp.concatenate(
        [grad_gain_first[None], grad_gain_second[None], grad_router_first, grad_router_second],
        axis=0,
    )
    sums = jnp.transpose(sums.reshape(sums.shape[0], -1, own_kv), (1, 0, 2))
    if walk:
        sums, grad_query, grad_key, grad_value = last_exchange(
            sums, grad_query.reshape(pair, own_in, feats), grad_kv, sizes, 10
        )
        grad_query = grad_query[None]
    else:
        sums = small_exchange(sums, sizes, True, 10)
        grad_query = swap(grad_query.reshape(own_in * pair, line, part)[None], "pair", 1, 0)
        grad_query = jnp.transpose(grad_query, (1, 2, 0, 3)).reshape(1, own_in, heads_total)
    return (
        layer_out.reshape(micro, 1, tok, width),
        tokens_grad.reshape(micro, 1, tok, width),
        grad_query.astype(F32),
        grad_output[None].astype(F32),
        grad_key,
        grad_value,
        sums[0],
        jnp.transpose(sums[2 : 2 + experts]),
        sums[1],
        jnp.transpose(sums[2 + experts :]),
        grad_gate,
        grad_upward,
        grad_downward,
    )


def solution(mesh):
    line, experts = mesh.devices.shape
    pair = 2 if line % 2 == 0 and (HEADS % line == 0) else 1
    shaped = Mesh(mesh.devices.reshape(line // pair, pair, experts), ALL)
    in_specs = (
        P(None, DP, "expert", None),
        P("expert", DP, None),
        P("expert", DP, None),
        P(ALL, None),
        P(ALL, None),
        P(ALL),
        P(ALL, None),
        P(ALL),
        P(ALL, None),
        P("expert", DP, None),
        P("expert", DP, None),
        P("expert", DP, None),
        P(None, DP, None, None),
        P(None, DP, "expert", None),
        P(None, DP, "expert"),
        P(None, DP, None),
        P(None, DP, "expert", None),
    )
    out_specs = (
        P(None, DP, "expert", None),
        P(None, DP, "expert", None),
        P("expert", DP, None),
        P("expert", DP, None),
        P(ALL, None),
        P(ALL, None),
        P(ALL),
        P(ALL, None),
        P(ALL),
        P(ALL, None),
        P("expert", DP, None),
        P("expert", DP, None),
        P("expert", DP, None),
    )
    return jax.shard_map(body, mesh=shaped, in_specs=in_specs, out_specs=out_specs, check_vma=False)
```

```python
from functools import partial
import math

import jax
import jax.numpy as jnp
from jax import lax
from jax.experimental import pallas as pl
from jax.experimental.pallas import tpu as pltpu
from jax.sharding import Mesh, PartitionSpec as P

HEADS = 16
HDIM = 128
EPSILON = 1e-06
HIGHEST = lax.Precision.HIGHEST
BF16 = jnp.bfloat16
F32 = jnp.float32


def product(left, right):
    return jnp.dot(left, right, preferred_element_type=F32)


def product_tn(left, right):
    return lax.dot_general(left, right, (((0,), (0,)), ((), ())), preferred_element_type=F32)


def product_nt(left, right):
    return lax.dot_general(left, right, (((1,), (1,)), ((), ())), preferred_element_type=F32)


def split_product(values, rows):
    parts, rest = [], values
    for _ in range(3):
        parts.append(lax.reduce_precision(rest, 8, 7))
        rest = rest - parts[-1]
    count = values.shape[1]
    total = product_tn(jnp.concatenate(parts, axis=1).astype(BF16), rows)
    return total[:count] + total[count : 2 * count] + total[2 * count :]


def rms_scaled(values, gain):
    return values * lax.rsqrt(jnp.mean(values * values, axis=-1, keepdims=True) + EPSILON) * gain


def mixture_gates(picked, logits):
    labels = jnp.arange(logits.shape[1], dtype=jnp.int32)
    onehot = (picked[:, :, None] == labels[None, None, :]).astype(F32)
    chosen = jnp.sum(onehot * logits[:, None, :], axis=-1)
    weights = jax.nn.softmax(chosen, axis=-1)
    return jnp.sum(weights[:, :, None] * onehot, axis=1)


def tree_layout(segment_len, tree_len):
    places = jnp.arange(tree_len, dtype=jnp.int32)
    trunk_len = 4 * segment_len
    segment = jnp.where(
        places < trunk_len,
        0,
        jnp.where(
            places < 2 * trunk_len,
            1 + (places - trunk_len) // segment_len,
            5 + (places - 2 * trunk_len) // segment_len,
        ),
    )
    depth = jnp.where(
        places < trunk_len,
        places,
        jnp.where(
            places < 2 * trunk_len,
            trunk_len + (places - trunk_len) % segment_len,
            trunk_len + segment_len + (places - 2 * trunk_len) % segment_len,
        ),
    )
    return (places, segment, depth)


def ancestors(parent, segment):
    labels = jnp.arange(parent.shape[0], dtype=jnp.int32)
    first = jnp.where(labels > 0, parent, -1)
    lookup = jnp.maximum(first, 0)[:, None] == labels[None, :]
    second = jnp.where(first > 0, jnp.sum(jnp.where(lookup, parent[None, :], 0), axis=1), -1)
    member = segment[:, None] == labels[None, :]
    up_one = jnp.sum(jnp.where(member, first[None, :], 0), axis=1)
    up_two = jnp.sum(jnp.where(member, second[None, :], 0), axis=1)
    return (up_one, up_two)


def score_bias(parent, segment, places):
    up_one, up_two = ancestors(parent, segment)
    same = (segment[None, :] == segment[:, None]) & (places[None, :] <= places[:, None])
    seen = same | (segment[None, :] == up_one[:, None]) | (segment[None, :] == up_two[:, None])
    return jnp.where(seen, 0.0, -1e30).astype(F32)


def slot_table(picked, order, experts, capacity):
    labels = jnp.arange(experts, dtype=jnp.int32)
    chosen = jnp.sum((picked[:, :, None] == labels[None, None, :]).astype(F32), axis=1)
    earlier = (order[None, :] < order[:, None]).astype(F32)
    ranks = jnp.dot(earlier, chosen, precision=HIGHEST, preferred_element_type=F32)
    slots = jnp.arange(capacity, dtype=F32)
    return jnp.transpose(chosen)[:, None, :] * (
        jnp.transpose(ranks)[:, None, :] == slots[None, :, None]
    ).astype(F32)


def turn(values, cosine, sine):
    half = values.shape[-1] // 2
    first = values[:, :half]
    second = values[:, half:]
    return jnp.concatenate(
        [first * cosine - second * sine, second * cosine + first * sine], axis=-1
    )


def softmax_rows(queries, keys, bias, scale):
    scores = product_nt(queries, keys) * scale + bias
    highest = jnp.max(scores, axis=-1, keepdims=True)
    weights = jnp.exp(scores - highest)
    return weights / jnp.sum(weights, axis=-1, keepdims=True)


def attend_kernel(heads, scale, raw_ref, kv_ref, cos_ref, sin_ref, bias_ref, query_ref, out_ref):
    quarter, tok = raw_ref.shape[1], raw_ref.shape[3]
    rows = quarter * tok
    cosine, sine, bias = cos_ref[...], sin_ref[...], bias_ref[0, 0]
    for head in range(heads):
        cols = slice(head * HDIM, (head + 1) * HDIM)
        raw = raw_ref[0, :, 0, :, cols].reshape(rows, HDIM)
        keys = kv_ref[0, 0, 0, :, 0, :, cols].reshape(rows, HDIM)
        values = kv_ref[0, 1, 0, :, 0, :, cols].reshape(rows, HDIM)
        queries = turn(raw, cosine, sine).astype(BF16)
        probs = softmax_rows(queries, keys, bias, scale).astype(BF16)
        query_ref[0, :, 0, :, cols] = queries.reshape(quarter, tok, HDIM)
        out_ref[0, :, 0, :, cols] = product(probs, values).astype(BF16).reshape(quarter, tok, HDIM)


def attend_back_kernel(
    heads, scale, query_ref, kv_ref, grad_ref, cos_ref, sin_ref, bias_ref, dq_ref, dkv_ref
):
    quarter, tok = query_ref.shape[1], query_ref.shape[3]
    rows = quarter * tok
    cosine, sine, bias = cos_ref[...], sin_ref[...], bias_ref[0, 0]
    for head in range(heads):
        cols = slice(head * HDIM, (head + 1) * HDIM)
        queries = query_ref[0, :, 0, :, cols].reshape(rows, HDIM)
        keys = kv_ref[0, 0, 0, :, 0, :, cols].reshape(rows, HDIM)
        values = kv_ref[0, 1, 0, :, 0, :, cols].reshape(rows, HDIM)
        grad = grad_ref[0, :, 0, :, cols].reshape(rows, HDIM)
        probs = softmax_rows(queries, keys, bias, scale)
        prob_grad = product_nt(grad, values)
        centre = jnp.sum(prob_grad * probs, axis=-1, keepdims=True)
        score_grad = (probs * (prob_grad - centre) * scale).astype(BF16)
        query_grad = turn(product(score_grad, keys), cosine, -sine).astype(BF16)
        key_grad = turn(product_tn(score_grad, queries), cosine, -sine).astype(BF16)
        value_grad = product_tn(probs.astype(BF16), grad).astype(BF16)
        dq_ref[0, :, 0, :, cols] = query_grad.reshape(quarter, tok, HDIM)
        dkv_ref[0, 0, 0, :, 0, :, cols] = key_grad.reshape(quarter, tok, HDIM)
        dkv_ref[0, 1, 0, :, 0, :, cols] = value_grad.reshape(quarter, tok, HDIM)


def attention_specs(shape, slices):
    pair, quarter, micro, tok, feats = shape
    part = feats // slices
    rows = quarter * tok
    grid = (pair, micro, slices)
    flat = pl.BlockSpec((1, quarter, 1, tok, part), lambda i, m, s: (i, 0, m, 0, s))
    both = pl.BlockSpec(
        (1, 2, 1, quarter, 1, tok, part), lambda i, m, s: (s, 0, i, 0, m, 0, 0)
    )
    angle = pl.BlockSpec((rows, HDIM // 2), lambda i, m, s: (0, 0))
    bias = pl.BlockSpec((1, 1, rows, rows), lambda i, m, s: (i, m, 0, 0))
    return grid, part, flat, both, angle, bias


def attend(raw, kv, cosine, sine, bias, scale):
    slices = kv.shape[0]
    grid, part, flat, both, angle, bias_spec = attention_specs(raw.shape, slices)
    out = jax.ShapeDtypeStruct(raw.shape, BF16)
    return pl.pallas_call(
        partial(attend_kernel, part // HDIM, scale),
        grid=grid,
        in_specs=[flat, both, angle, angle, bias_spec],
        out_specs=[flat, flat],
        out_shape=[out, out],
        cost_estimate=pl.CostEstimate(
            flops=4 * raw.size * cosine.shape[0],
            bytes_accessed=12 * raw.size,
            transcendentals=raw.size * 2,
        ),
        name="attend",
    )(raw, kv, cosine, sine, bias)


def attend_back(queries, kv, grad, cosine, sine, bias, scale):
    slices = kv.shape[0]
    grid, part, flat, both, angle, bias_spec = attention_specs(queries.shape, slices)
    return pl.pallas_call(
        partial(attend_back_kernel, part // HDIM, scale),
        grid=grid,
        in_specs=[flat, both, flat, angle, angle, bias_spec],
        out_specs=[flat, both],
        out_shape=[
            jax.ShapeDtypeStruct(queries.shape, BF16),
            jax.ShapeDtypeStruct(kv.shape, BF16),
        ],
        cost_estimate=pl.CostEstimate(
            flops=10 * queries.size * cosine.shape[0],
            bytes_accessed=14 * queries.size,
            transcendentals=queries.size * 2,
        ),
        name="attend_back",
    )(queries, kv, grad, cosine, sine, bias)


MESH = pl.DeviceIdType.MESH
ANY = pl.BlockSpec(memory_space=pl.ANY)
VMEM = pl.BlockSpec(memory_space=pltpu.VMEM)
DMA = pltpu.SemaphoreType.DMA


def remote(src, dst, send, recv, target):
    return pltpu.make_async_remote_copy(
        src_ref=src, dst_ref=dst, send_sem=send, recv_sem=recv, device_id=target, device_id_type=MESH
    )


def greet(targets):
    barrier = pltpu.get_barrier_semaphore()
    for target in targets:
        pl.semaphore_signal(barrier, inc=1, device_id=target, device_id_type=MESH)
    pl.semaphore_wait(barrier, len(targets))


def params(number, limit=None):
    return pltpu.CompilerParams(
        collective_id=number, has_side_effects=True, vmem_limit_bytes=limit
    )


def add_into(target, sources, rows):
    step = 1
    while step * 2 <= rows and step * 2 * target.shape[-1] <= 65536 and rows % (step * 2) == 0:
        step *= 2

    def one(index, carry):
        where = pl.ds(pl.multiple_of(index * step, step), step)
        total = sources[0][where].astype(F32)
        for source in sources[1:]:
            total = total + source[where].astype(F32)
        target[where] = total.astype(target.dtype)
        return carry

    lax.fori_loop(0, rows // step, one, 0)


def cube_reduce_kernel(pairs, x_ref, o_ref, half, quarter, got_core, got_side, got_pair, send, recv):
    p = lax.axis_index("pair") if pairs == 2 else 0
    e = lax.axis_index("expert")
    c, y = lax.rem(e, 2), lax.div(e, 2)
    core = {"expert": e + 1 - 2 * c}
    side = {"expert": e + 2 - 4 * y}
    other = {"pair": lax.rem(p + 1, pairs)}
    greet([core, side] + ([other] if pairs == 2 else []))
    rows = x_ref.shape[3]
    shifts = (1, 0) if pairs == 2 else (0,)
    order = [(dx, dy) for dy in (1, 0) for dx in shifts]
    copies = []

    def push(source, place, slot, target):
        copy = remote(source, place, send.at[slot], recv.at[slot], target)
        copy.start()
        copies.append(copy)
        return copy

    first = []
    for slot, (dx, dy) in enumerate(order):
        px, yy = lax.rem(p + dx, pairs), lax.rem(y + dy, 2)
        first.append(push(x_ref.at[px, yy, 1 - c], got_core.at[slot], slot, core))
    base = len(order)
    cut = rows // 2 if pairs == 2 else rows
    upper, lower = pl.ds(0, cut), pl.ds(cut, rows - cut)
    to_side, to_other = {}, {}
    for slot, (dx, dy) in enumerate(order):
        px, yy = lax.rem(p + dx, pairs), lax.rem(y + dy, 2)
        first[slot].wait_recv()
        add_into(half.at[slot], [x_ref.at[px, yy, c], got_core.at[slot]], rows)
        if dy == 1:
            to_side[dx] = push(
                half.at[slot, upper], got_side.at[dx, upper], base + dx, side
            )
        if dx == 1:
            to_other[dy] = push(
                half.at[slot, lower], got_pair.at[dy, lower], base + 2 + dy, other
            )
    own = half.at[order.index((0, 0))]
    if pairs == 2:
        to_side[1].wait_recv()
        add_into(
            quarter.at[upper],
            [half.at[order.index((1, 0)), upper], got_side.at[1, upper]],
            cut,
        )
        to_pair = push(quarter.at[upper], got_pair.at[0, upper], base + 4, other)
        to_other[1].wait_recv()
        add_into(
            quarter.at[lower],
            [half.at[order.index((0, 1)), lower], got_pair.at[1, lower]],
            rows - cut,
        )
        to_flank = push(quarter.at[lower], got_side.at[0, lower], base + 5, side)
        to_side[0].wait_recv()
        to_pair.wait_recv()
        add_into(
            o_ref.at[upper], [own.at[upper], got_side.at[0, upper], got_pair.at[0, upper]], cut
        )
        to_other[0].wait_recv()
        to_flank.wait_recv()
        add_into(
            o_ref.at[lower],
            [own.at[lower], got_side.at[0, lower], got_pair.at[0, lower]],
            rows - cut,
        )
    else:
        to_side[0].wait_recv()
        add_into(o_ref, [own, got_side.at[0]], rows)
    for copy in copies:
        copy.wait_send()


def cube_reduce(value, pairs, number):
    _, rows, cols = value.shape
    value = value.reshape(pairs, 2, 2, rows, cols)
    slots = 2 * pairs
    block = jax.ShapeDtypeStruct((rows, cols), value.dtype)
    return pl.pallas_call(
        partial(cube_reduce_kernel, pairs),
        in_specs=[VMEM],
        out_specs=VMEM,
        out_shape=block,
        scratch_shapes=[
            pltpu.VMEM((slots, rows, cols), value.dtype),
            pltpu.VMEM((rows, cols), value.dtype),
            pltpu.VMEM((slots, rows, cols), value.dtype),
            pltpu.VMEM((2, rows, cols), value.dtype),
            pltpu.VMEM((2, rows, cols), value.dtype),
            DMA((slots + 6,)),
            DMA((slots + 6,)),
        ],
        compiler_params=params(number, 48 * 2**20),
        cost_estimate=pl.CostEstimate(flops=0, bytes_accessed=0, transcendentals=0),
        name="cube_reduce",
    )(value)


def cube_gather_kernel(pairs, x_ref, o_ref, send, recv, local):
    p = lax.axis_index("pair") if pairs == 2 else 0
    e = lax.axis_index("expert")
    c, y = lax.rem(e, 2), lax.div(e, 2)
    core = {"expert": e + 1 - 2 * c}
    side = {"expert": e + 2 - 4 * y}
    other = {"pair": lax.rem(p + 1, pairs)}
    greet([core, side] + ([other] if pairs == 2 else []))
    q, w = lax.rem(p + 1, pairs), 1 - y
    own = o_ref.at[p, y, c]
    keep = pltpu.make_async_copy(x_ref, own, local)
    keep.start()
    copies = []

    def push(slot, source, place, target):
        copy = remote(source, place, send.at[slot], recv.at[slot], target)
        copy.start()
        copies.append(copy)
        return copy

    rows = x_ref.shape[0]
    cut = rows // 2
    upper, lower = pl.ds(0, cut), pl.ds(cut, rows - cut)
    to_side = push(0, x_ref, own, side)
    to_other = push(1, x_ref, own, other) if pairs == 2 else None
    to_core = push(2, x_ref, own, core)
    waits = [to_core]
    if pairs == 2:
        to_other.wait_recv()
        block = o_ref.at[q, y, c]
        far = [push(3, block.at[upper], block.at[upper], side)]
        waits.append(push(4, block, block, core))
    to_side.wait_recv()
    block = o_ref.at[p, w, c]
    if pairs == 2:
        far.append(push(7, block.at[lower], block.at[lower], other))
    waits.append(push(5, block, block, core))
    if pairs == 2:
        for copy in far:
            copy.wait_recv()
        block = o_ref.at[q, w, c]
        waits.append(push(6, block, block, core))
    for copy in waits:
        copy.wait_recv()
    for copy in copies:
        copy.wait_send()
    keep.wait()


def cube_gather(value, pairs, number):
    return pl.pallas_call(
        partial(cube_gather_kernel, pairs),
        in_specs=[VMEM],
        out_specs=VMEM,
        out_shape=jax.ShapeDtypeStruct((pairs, 2, 2) + value.shape, value.dtype),
        scratch_shapes=[DMA((8,)), DMA((8,)), DMA(())],
        compiler_params=params(number, 48 * 2**20),
        cost_estimate=pl.CostEstimate(
            flops=0, bytes_accessed=80 * value.size, transcendentals=0
        ),
        name="cube_gather",
    )(value)


def place_of(index, sizes):
    line, pairs, experts = sizes
    return {
        "line": index // (pairs * experts),
        "pair": (index // experts) % pairs,
        "expert": index % experts,
    }


def small_kernel(sizes, reduce, x_ref, o_ref, got, send, recv):
    line, pairs, experts = sizes
    count = line * pairs * experts
    me = (
        lax.axis_index("line") * (pairs * experts)
        + lax.axis_index("pair") * experts
        + lax.axis_index("expert")
    )
    barrier = pltpu.get_barrier_semaphore()

    def greet_one(offset, carry):
        target = place_of((me + offset) % count, sizes)
        pl.semaphore_signal(barrier, inc=1, device_id=target, device_id_type=MESH)
        return carry

    lax.fori_loop(1, count, greet_one, 0)
    pl.semaphore_wait(barrier, count - 1)

    def copy_to(offset):
        peer = (me + offset) % count
        source = x_ref.at[peer] if reduce else x_ref
        return remote(source, got.at[offset], send.at[offset], recv.at[offset], place_of(peer, sizes))

    def start(offset, carry):
        copy_to(offset).start()
        return carry

    lax.fori_loop(1, count, start, 0)
    got[0] = x_ref[me] if reduce else x_ref[...]

    def finish(offset, carry):
        copy_to(offset).wait()
        return carry

    lax.fori_loop(1, count, finish, 0)
    if reduce:
        o_ref[...] = jnp.sum(got[...], axis=0)
    else:

        def order(offset, carry):
            o_ref[(me - offset + count) % count] = got[offset]
            return carry

        lax.fori_loop(0, count, order, 0)


def small_exchange(value, sizes, reduce, number):
    count = sizes[0] * sizes[1] * sizes[2]
    block = value.shape[1:] if reduce else value.shape
    return pl.pallas_call(
        partial(small_kernel, sizes, reduce),
        in_specs=[VMEM],
        out_specs=VMEM,
        out_shape=jax.ShapeDtypeStruct(block if reduce else (count,) + block, value.dtype),
        scratch_shapes=[pltpu.VMEM((count,) + block, value.dtype), DMA((count,)), DMA((count,))],
        compiler_params=params(number),
        cost_estimate=pl.CostEstimate(flops=0, bytes_accessed=2**24, transcendentals=0),
        name="small_reduce" if reduce else "small_gather",
    )(value)


def ff_kernel(
    a_in, b_in, gate_hbm, up_hbm, down_hbm,
    a_out, b_out, a_save, b_save, inner_save, dgate_save, dup_save,
    a_buf, b_buf, side, hop, extra, w_gate, w_up, w_down, mid, acc,
    send, recv, load, store, local,
):
    z, p, e = lax.axis_index("line"), lax.axis_index("pair"), lax.axis_index("expert")
    line, _, rows, width = a_buf.shape
    experts, size = a_in.shape[0], a_in.shape[1]
    q = 1 - p
    twin = z + 1 - 2 * (z % 2)
    up, down, other, across = {"line": z + 1}, {"line": z - 1}, {"pair": q}, {"line": twin}
    ins, bufs, outs, saves = (a_in, b_in), (a_buf, b_buf), (a_out, b_out), (a_save, b_save)
    high = z // 2
    near = z + high * (line - 1 - 2 * z)

    def order(t):
        j = t + near * (1 - t // 2) * (1 - 2 * t)
        return j + high * (line - 1 - 2 * j)

    weights = [
        pltpu.make_async_copy(src, dst, load.at[i])
        for i, (src, dst) in enumerate(((gate_hbm, w_gate), (up_hbm, w_up), (down_hbm, w_down)))
    ]
    for copy in weights:
        copy.start()

    barrier = pltpu.get_barrier_semaphore()
    for shift in range(1, experts):
        pl.semaphore_signal(
            barrier, inc=1, device_id={"expert": (e + shift) % experts}, device_id_type=MESH
        )
    pl.semaphore_signal(barrier, inc=1, device_id=other, device_id_type=MESH)

    @pl.when(z > 0)
    def _():
        pl.semaphore_signal(barrier, inc=1, device_id=down, device_id_type=MESH)

    @pl.when(z < line - 1)
    def _():
        pl.semaphore_signal(barrier, inc=1, device_id=up, device_id_type=MESH)

    below, above = (z + line - 1) // line, (2 * line - 2 - z) // line
    pl.semaphore_wait(barrier, experts + below + above)

    UP, DOWN, SIDE, SUMUP, SUMDOWN, SUMSIDE = (i * line for i in range(6))
    SUMTWIN, SWAP = 6 * line, 6 * line + 1
    BACK = SWAP + experts

    def push(src, dst, kind, use, target):
        return remote(src, dst, send.at[kind, use], recv.at[kind, use], target)

    def to_up(kind, j):
        return push(bufs[kind].at[j, p], bufs[kind].at[j, p], kind, UP + j, up)

    def to_down(kind, j):
        return push(bufs[kind].at[j, p], bufs[kind].at[j, p], kind, DOWN + j, down)

    def to_other(kind, j):
        return push(bufs[kind].at[j, p], bufs[kind].at[j, p], kind, SIDE + j, other)

    def sum_up(kind, j):
        return push(bufs[kind].at[j, p], hop.at[kind, j], kind, SUMUP + j, up)

    def sum_down(kind, j, slot):
        return push(bufs[kind].at[j, p], hop.at[kind, slot], kind, SUMDOWN + j, down)

    def sum_other(kind, j):
        return push(bufs[kind].at[j, q], side.at[kind, j], kind, SUMSIDE + j, other)

    def sum_twin():
        return push(bufs[1].at[twin, q], extra, 1, SUMTWIN, across)

    def piece(index):
        return pl.ds(pl.multiple_of(index * size, size), size)

    def save(kind, j, column):
        return pltpu.make_async_copy(
            bufs[kind].at[j, column], saves[kind].at[j, column], store.at[kind, j, column]
        )

    swaps = []
    for kind in range(2):
        home = bufs[kind].at[z, p, piece(e)]
        keep = pltpu.make_async_copy(ins[kind].at[e], home, local.at[kind])
        keep.start()
        group = []
        for shift in range(1, experts):
            peer = (e + shift) % experts
            copy = push(ins[kind].at[peer], home, kind, SWAP + shift, {"expert": peer})
            copy.start()
            group.append(copy)
        swaps.append((keep, group))

    def spread(t, first=False):
        j = order(t)
        for kind in range(2):
            if first:
                swaps[kind][0].wait()
                for copy in swaps[kind][1]:
                    copy.wait_recv()
            else:

                @pl.when(j < z)
                def _():
                    to_up(kind, j).wait_recv()

                @pl.when(j > z)
                def _():
                    to_down(kind, j).wait_recv()

            @pl.when((j <= z) & (z < line - 1))
            def _():
                to_up(kind, j).start()

            @pl.when((j >= z) & (z > 0))
            def _():
                to_down(kind, j).start()

            to_other(kind, j).start()
            save(kind, j, p).start()

    chunk = 512
    steps = width // chunk

    def first_half(j, column):
        for index in range(3):
            acc[index] = jnp.zeros(acc.shape[1:], F32)

        def one(k, carry):
            where = pl.ds(pl.multiple_of(k * chunk, chunk), chunk)
            left = a_buf[j, column, :, where]
            acc[0] += product_nt(left, w_gate[:, where])
            acc[1] += product_nt(left, w_up[:, where])
            acc[2] += product_nt(b_buf[j, column, :, where], w_down[:, where])
            return carry

        lax.fori_loop(0, steps, one, 0)
        part = 32

        def two(i, carry):
            where = pl.ds(pl.multiple_of(i * part, part), part)
            gate, lift, grad = acc[0, where], acc[1, where], acc[2, where]
            sigma = jax.nn.sigmoid(gate)
            mid[j, column, 0, where] = (gate * sigma * lift).astype(BF16)
            mid[j, column, 1, where] = (
                grad * lift * sigma * (1.0 + gate * (1.0 - sigma))
            ).astype(BF16)
            mid[j, column, 2, where] = (grad * gate * sigma).astype(BF16)
            return carry

        lax.fori_loop(0, rows // part, two, 0)

    def second_half(j, column):
        def one(k, carry):
            where = pl.ds(pl.multiple_of(k * chunk, chunk), chunk)
            a_buf[j, column, :, where] = product(mid[j, column, 0], w_down[:, where]).astype(BF16)
            b_buf[j, column, :, where] = (
                product(mid[j, column, 1], w_gate[:, where])
                + product(mid[j, column, 2], w_up[:, where])
            ).astype(BF16)
            return carry

        lax.fori_loop(0, steps, one, 0)

    def arrive(j):
        for kind in range(2):
            to_other(kind, j).wait_recv()
            save(kind, j, q).start()

    def emit(t):
        j = order(t)
        sum_other(0, j).start()

        @pl.when((j != twin) & (j != z))
        def _():
            sum_other(1, j).start()

    def step(s, carry):
        @pl.when(s == 0)
        def _():
            spread(0, True)
            for copy in weights:
                copy.wait()

        @pl.when(s == 1)
        def _():
            spread(1)
            spread(2)

        @pl.when(s == 3)
        def _():
            spread(3)

        @pl.when(s == line)
        def _():
            sum_twin().start()

        def half(c, inner_carry):
            t = s - c
            column = p + c * (q - p)

            @pl.when((t >= 0) & (t < line))
            def _():
                j = order(t)

                @pl.when(c == 1)
                def _():
                    arrive(j)

                first_half(j, column)

                @pl.when(c == 1)
                def _():
                    for kind in range(2):
                        save(kind, j, q).wait()
                    second_half(j, column)

            return inner_carry

        return lax.fori_loop(0, 2, half, carry)

    lax.fori_loop(0, line + 1, step, 0)

    for t in (3, 2, 1, 0):
        emit(t)

    for copy in (
        pltpu.make_async_copy(mid.at[:, :, 0], inner_save, local.at[2]),
        pltpu.make_async_copy(mid.at[:, :, 1], dgate_save, local.at[3]),
        pltpu.make_async_copy(mid.at[:, :, 2], dup_save, local.at[4]),
    ):
        copy.start()
    sum_twin().wait_recv()
    add_into(b_buf.at[z, q], [b_buf.at[z, q], extra], rows)
    sum_other(1, z).start()

    def back(kind):
        own = pltpu.make_async_copy(
            bufs[kind].at[z, p, piece(e)], outs[kind].at[e], local.at[kind]
        )
        return [own] + [
            push(
                bufs[kind].at[z, p, piece((e + shift) % experts)],
                outs[kind].at[e],
                kind,
                BACK + shift,
                {"expert": (e + shift) % experts},
            )
            for shift in range(1, experts)
        ]

    def fold(s, carry):
        t = line - 1 - s
        j = order(t)
        for kind in range(2):
            save(kind, j, p).wait()

            @pl.when((j <= z) & (z < line - 1))
            def _():
                to_up(kind, j).wait_send()

            @pl.when((j >= z) & (z > 0))
            def _():
                to_down(kind, j).wait_send()

            to_other(kind, j).wait_send()

        second_half(j, p)
        for kind in range(2):
            mine = bufs[kind].at[j, p]
            if kind == 0:
                sum_other(kind, j).wait_recv()
                add_into(mine, [mine, side.at[kind, j]], rows)
            else:

                @pl.when(j != twin)
                def _():
                    sum_other(kind, j).wait_recv()
                    add_into(mine, [mine, side.at[kind, j]], rows)

            @pl.when((j >= z) & (z > 0))
            def _():
                sum_up(kind, j).wait_recv()
                add_into(mine, [mine, hop.at[kind, j]], rows)

            @pl.when((j < z) & (z < line - 1))
            def _():
                sum_down(kind, j, j).wait_recv()
                add_into(mine, [mine, hop.at[kind, j]], rows)

            @pl.when((j == z) & (z < line - 1))
            def _():
                sum_down(kind, j, line).wait_recv()
                add_into(mine, [mine, hop.at[kind, line]], rows)

            @pl.when(j == z)
            def _():
                for copy in back(kind):
                    copy.start()

            @pl.when(j > z)
            def _():
                sum_up(kind, j).start()

            @pl.when((j < z) & (j != z - 1))
            def _():
                sum_down(kind, j, j).start()

            @pl.when((j < z) & (j == z - 1))
            def _():
                sum_down(kind, j, line).start()

        return carry

    lax.fori_loop(0, line, fold, 0)

    for kind in range(2):
        for copy in back(kind):
            copy.wait()

    def drain(j, carry):
        for kind in range(2):
            if kind == 0:
                sum_other(kind, j).wait_send()
            else:

                @pl.when(j != twin)
                def _():
                    sum_other(kind, j).wait_send()

            @pl.when(j > z)
            def _():
                sum_up(kind, j).wait_send()

            @pl.when(j < z)
            def _():
                sum_down(kind, j, j).wait_send()

        return carry

    lax.fori_loop(0, line, drain, 0)
    sum_twin().wait_send()
    for copy in (
        pltpu.make_async_copy(mid.at[:, :, 0], inner_save, local.at[2]),
        pltpu.make_async_copy(mid.at[:, :, 1], dgate_save, local.at[3]),
        pltpu.make_async_copy(mid.at[:, :, 2], dup_save, local.at[4]),
    ):
        copy.wait()
    for keep, group in swaps:
        for copy in group:
            copy.wait_send()


def feed_forward(first, second, w_gate, w_up, w_down, line, pairs, number):
    experts, size, width = first.shape
    hidden = w_gate.shape[0]
    rows = experts * size
    blocks = (line, pairs, rows)
    back = jax.ShapeDtypeStruct(first.shape, BF16)
    wide = jax.ShapeDtypeStruct(blocks + (width,), BF16)
    thin = jax.ShapeDtypeStruct(blocks + (hidden,), BF16)
    uses = 6 * line + 2 + 2 * experts
    total = line * pairs * rows
    return pl.pallas_call(
        ff_kernel,
        in_specs=[ANY] * 5,
        out_specs=[ANY] * 7,
        out_shape=[back, back, wide, wide, thin, thin, thin],
        scratch_shapes=[
            pltpu.VMEM(blocks + (width,), BF16),
            pltpu.VMEM(blocks + (width,), BF16),
            pltpu.VMEM((2, line, rows, width), BF16),
            pltpu.VMEM((2, line + 1, rows, width), BF16),
            pltpu.VMEM((rows, width), BF16),
            pltpu.VMEM((hidden, width), BF16),
            pltpu.VMEM((hidden, width), BF16),
            pltpu.VMEM((hidden, width), BF16),
            pltpu.VMEM((line, pairs, 3, rows, hidden), BF16),
            pltpu.VMEM((3, rows, hidden), F32),
            DMA((2, uses)),
            DMA((2, uses)),
            DMA((3,)),
            DMA((2, line, pairs)),
            DMA((5,)),
        ],
        compiler_params=params(number, 63 * 2**20),
        cost_estimate=pl.CostEstimate(
            flops=12 * total * hidden * width,
            bytes_accessed=12 * total * width,
            transcendentals=total * hidden,
        ),
        name="feed_forward",
    )(first, second, w_gate, w_up, w_down)


def last_kernel(
    sizes, x_ref, q_ref, g_hbm, o_ref, w_ref, key_ref, value_ref,
    got, side, g_ref, k_ref, hop, send, recv, peer_send, peer_recv, local,
):
    line, pairs, experts = sizes
    trees = pairs * experts
    count = line * trees
    z, p, e = lax.axis_index("line"), lax.axis_index("pair"), lax.axis_index("expert")
    mine = p * experts + e
    me = z * trees + mine
    span, piece = g_ref.shape[1], k_ref.shape[1]
    up, down = {"line": z + 1}, {"line": z - 1}
    high = z // 2
    near = z + high * (line - 1 - 2 * z)

    def order(t):
        j = t + near * (1 - t // 2) * (1 - 2 * t)
        return j + high * (line - 1 - 2 * j)

    fetch = pltpu.make_async_copy(g_hbm, g_ref, local)
    fetch.start()
    barrier = pltpu.get_barrier_semaphore()

    def greet_one(offset, carry):
        target = place_of((me + offset) % count, sizes)
        pl.semaphore_signal(barrier, inc=1, device_id=target, device_id_type=MESH)
        return carry

    lax.fori_loop(1, count, greet_one, 0)
    pl.semaphore_wait(barrier, count - 1)
    UP, DOWN, SWAP, PAIR = 0, line, 2 * line, 2 * line + trees

    def sum_up(j):
        return remote(g_ref.at[j], hop.at[j], send.at[UP + j], recv.at[UP + j], up)

    def sum_down(j, slot):
        return remote(g_ref.at[j], hop.at[slot], send.at[DOWN + j], recv.at[DOWN + j], down)

    def fold(t):
        j = order(t)
        own = g_ref.at[j]

        @pl.when((j >= z) & (z > 0))
        def _():
            sum_up(j).wait_recv()
            add_into(own, [own, hop.at[j]], span)

        @pl.when((j < z) & (z < line - 1))
        def _():
            sum_down(j, j).wait_recv()
            add_into(own, [own, hop.at[j]], span)

        @pl.when((j == z) & (z < line - 1))
        def _():
            sum_down(j, line).wait_recv()
            add_into(own, [own, hop.at[line]], span)

        @pl.when(j > z)
        def _():
            sum_up(j).start()

        @pl.when((j < z) & (j != z - 1))
        def _():
            sum_down(j, j).start()

        @pl.when((j < z) & (j == z - 1))
        def _():
            sum_down(j, line).start()

    fetch.wait()
    fold(3)
    swap = remote(q_ref.at[1 - p], side, send.at[PAIR], recv.at[PAIR], {"pair": 1 - p})
    swap.start()

    def copy_to(offset):
        peer = (me + offset) % count
        return remote(
            x_ref.at[peer],
            got.at[offset],
            peer_send.at[offset],
            peer_recv.at[offset],
            place_of(peer, sizes),
        )

    def start(offset, carry):
        copy_to(offset).start()
        return carry

    lax.fori_loop(1, count, start, 0)
    got[0] = x_ref[me]
    fold(2)
    part = q_ref.shape[2] // line

    def lay(block, source):
        for index in range(line):
            column = pl.multiple_of((index * pairs + source) * part, part)
            w_ref[:, pl.ds(column, part)] = block[:, index * part : (index + 1) * part].astype(F32)

    lay(q_ref.at[p], p)
    fold(1)
    swap.wait_recv()
    lay(side, 1 - p)

    def finish(offset, carry):
        copy_to(offset).wait()
        return carry

    lax.fori_loop(1, count, finish, 0)
    o_ref[...] = jnp.sum(got[...], axis=0)
    fold(0)

    def share_of(index):
        return g_ref.at[z, pl.ds(pl.multiple_of(index * piece, piece), piece)]

    keep = pltpu.make_async_copy(share_of(mine), k_ref.at[mine], local)
    keep.start()
    swaps = []
    for shift in range(1, trees):
        peer = (mine + shift) % trees
        copy = remote(
            share_of(peer),
            k_ref.at[mine],
            send.at[SWAP + shift],
            recv.at[SWAP + shift],
            {"pair": peer // experts, "expert": peer % experts},
        )
        copy.start()
        swaps.append(copy)
    keep.wait()
    for copy in swaps:
        copy.wait()
    share = k_ref.shape[2] // 2
    for source in range(trees):
        column = ((source % experts) * pairs + source // experts) * share
        for index, target in enumerate((key_ref, value_ref)):
            target[:, column : column + share] = k_ref[
                source, :, index * share : (index + 1) * share
            ].astype(F32)
    swap.wait_send()

    def drain(j, carry):
        @pl.when(j > z)
        def _():
            sum_up(j).wait_send()

        @pl.when(j < z)
        def _():
            sum_down(j, j).wait_send()

        return carry

    lax.fori_loop(0, line, drain, 0)


def last_exchange(sums, query, grads, sizes, number):
    line, pairs, experts = sizes
    trees = pairs * experts
    count, block = sums.shape[0], sums.shape[1:]
    _, rows, cols = query.shape
    span, thin = grads.shape[0] // line, grads.shape[1]
    uses = 2 * line + trees + 1
    wide = jax.ShapeDtypeStruct((span // trees, trees * thin // 2), F32)
    return pl.pallas_call(
        partial(last_kernel, sizes),
        in_specs=[VMEM, VMEM, ANY],
        out_specs=[VMEM] * 4,
        out_shape=[
            jax.ShapeDtypeStruct(block, F32),
            jax.ShapeDtypeStruct((rows, pairs * cols), F32),
            wide,
            wide,
        ],
        scratch_shapes=[
            pltpu.VMEM((count,) + block, F32),
            pltpu.VMEM((rows, cols), BF16),
            pltpu.VMEM((line, span, thin), BF16),
            pltpu.VMEM((trees, span // trees, thin), BF16),
            pltpu.VMEM((line + 1, span, thin), BF16),
            DMA((uses,)),
            DMA((uses,)),
            DMA((count,)),
            DMA((count,)),
            DMA(()),
        ],
        compiler_params=params(number, 48 * 2**20),
        cost_estimate=pl.CostEstimate(flops=0, bytes_accessed=0, transcendentals=0),
        name="last_exchange",
    )(sums, query, grads.reshape(line, span, thin))


def start_all_kernel(
    sizes, tok_ref, wq_ref, wk_ref, wv_ref, small_ref, int_ref,
    tok_out, q_out, kv_out, small_out, int_out,
    q_cut, kv_cut, send, recv, peer_send, peer_recv, local,
):
    line, pairs, experts = sizes
    z, p, e = lax.axis_index("line"), lax.axis_index("pair"), lax.axis_index("expert")
    c, y = e % 2, e // 2
    core, side = {"expert": e + 1 - 2 * c}, {"expert": e + 2 - 4 * y}
    other = {"pair": 1 - p}
    trees = pairs * experts
    count = line * trees
    mine = p * experts + e
    me = z * trees + mine
    barrier = pltpu.get_barrier_semaphore()

    def greet_one(offset, carry):
        target = place_of((me + offset) % count, sizes)
        pl.semaphore_signal(barrier, inc=1, device_id=target, device_id_type=MESH)
        return carry

    lax.fori_loop(1, count, greet_one, 0)
    part = wq_ref.shape[1] // (line * pairs)
    sub = line // experts
    for q in range(pairs):
        for d in range(experts):
            for index, ref in enumerate((wk_ref, wv_ref)):
                for h in range(sub):
                    column = ((d * sub + h) * pairs + q) * part
                    place = (index * sub + h) * part
                    kv_cut[q * experts + d, :, place : place + part] = ref[
                        :, column : column + part
                    ]
    for q in range(pairs):
        for index in range(line):
            column = (index * pairs + q) * part
            q_cut[q, :, index * part : (index + 1) * part] = wq_ref[:, column : column + part]
    pl.semaphore_wait(barrier, count - 1)

    copies, TOK, QSWAP, INTS, KV = [], 0, 7, 8, 9
    WALK = KV + trees

    def push(slot, source, place, target):
        copy = remote(source, place, send.at[slot], recv.at[slot], target)
        copy.start()
        copies.append(copy)
        return copy

    size = kv_cut.shape[1]
    kv_home = kv_out.at[z, pl.ds(pl.multiple_of(mine * size, size), size)]
    pieces = []
    for shift in range(1, trees):
        peer = (mine + shift) % trees
        pieces.append(
            push(
                KV + shift,
                kv_cut.at[peer],
                kv_home,
                {"pair": peer // experts, "expert": peer % experts},
            )
        )
    rows = q_cut.shape[1]
    q_home = q_out.at[z, pl.ds(pl.multiple_of(p * rows, rows), rows)]
    q_swap = push(QSWAP, q_cut.at[1 - p], q_home, other)
    keeps = [
        pltpu.make_async_copy(q_cut.at[p], q_home, local.at[0]),
        pltpu.make_async_copy(kv_cut.at[mine], kv_home, local.at[1]),
        pltpu.make_async_copy(tok_ref, tok_out.at[p, y, c], local.at[2]),
        pltpu.make_async_copy(small_ref, small_out.at[me], local.at[3]),
        pltpu.make_async_copy(int_ref, int_out.at[p], local.at[4]),
    ]
    for copy in keeps:
        copy.start()
    own = tok_out.at[p, y, c]
    to_side = push(TOK, tok_ref, own, side)
    to_other = push(TOK + 1, tok_ref, own, other)
    waits = [push(TOK + 2, tok_ref, own, core), push(INTS, int_ref, int_out.at[p], other)]

    def small_to(offset):
        return remote(
            small_ref,
            small_out.at[me],
            peer_send.at[offset],
            peer_recv.at[offset],
            place_of((me + offset) % count, sizes),
        )

    def small_start(offset, carry):
        small_to(offset).start()
        return carry

    lax.fori_loop(1, count, small_start, 0)

    def walker(ref, base):
        def to_up(j, d):
            return remote(
                ref.at[j], ref.at[j], send.at[base + d], recv.at[base + d], {"line": z + 1}
            )

        def to_down(j, d):
            at = base + line + d
            return remote(ref.at[j], ref.at[j], send.at[at], recv.at[at], {"line": z - 1})

        return to_up, to_down

    walkers = [walker(q_out, WALK), walker(kv_out, WALK + 2 * line + 2)]

    def begin(which):
        to_up, to_down = walkers[which]

        @pl.when(z < line - 1)
        def _():
            to_up(z, 1).start()

        @pl.when(z > 0)
        def _():
            to_down(z, 1).start()

    keeps[1].wait()
    for copy in pieces:
        copy.wait_recv()
    begin(1)
    keeps[0].wait()
    q_swap.wait_recv()
    begin(0)
    to_other.wait_recv()
    block = tok_out.at[1 - p, y, c]
    far = push(TOK + 3, block, block, side)
    waits.append(push(TOK + 4, block, block, core))
    to_side.wait_recv()
    block = tok_out.at[p, 1 - y, c]
    waits.append(push(TOK + 5, block, block, core))
    far.wait_recv()
    block = tok_out.at[1 - p, 1 - y, c]
    waits.append(push(TOK + 6, block, block, core))

    for d in range(1, line):
        for to_up, to_down in walkers[::-1]:

            @pl.when(z - d >= 0)
            def _():
                to_up(z - d, d).wait_recv()

                @pl.when(z < line - 1)
                def _():
                    to_up(z - d, d + 1).start()

            @pl.when(z + d < line)
            def _():
                to_down(z + d, d).wait_recv()

                @pl.when(z > 0)
                def _():
                    to_down(z + d, d + 1).start()

    for d in range(1, line):
        for to_up, to_down in walkers:

            @pl.when((z - d + 1 >= 0) & (z < line - 1))
            def _():
                to_up(z - d + 1, d).wait_send()

            @pl.when((z + d - 1 < line) & (z > 0))
            def _():
                to_down(z + d - 1, d).wait_send()

    for copy in waits:
        copy.wait_recv()
    for copy in copies:
        copy.wait_send()
    for copy in keeps[2:]:
        copy.wait()

    def small_finish(offset, carry):
        small_to(offset).wait()
        return carry

    lax.fori_loop(1, count, small_finish, 0)


def start_all(tokens, w_query, w_key, w_value, small, integers, sizes, number):
    line, pairs, experts = sizes
    trees = pairs * experts
    count = line * trees
    rows, width = w_query.shape
    size = w_key.shape[0]
    feats = width // pairs
    thin = 2 * feats // experts
    uses = 9 + trees + 4 * line + 4
    return pl.pallas_call(
        partial(start_all_kernel, sizes),
        in_specs=[VMEM] * 6,
        out_specs=[VMEM] * 5,
        out_shape=[
            jax.ShapeDtypeStruct((pairs, 2, 2) + tokens.shape, BF16),
            jax.ShapeDtypeStruct((line, pairs * rows, feats), BF16),
            jax.ShapeDtypeStruct((line, trees * size, thin), BF16),
            jax.ShapeDtypeStruct((count,) + small.shape, BF16),
            jax.ShapeDtypeStruct((pairs,) + integers.shape, jnp.int32),
        ],
        scratch_shapes=[
            pltpu.VMEM((pairs, rows, feats), BF16),
            pltpu.VMEM((trees, size, thin), BF16),
            DMA((uses,)),
            DMA((uses,)),
            DMA((count,)),
            DMA((count,)),
            DMA((5,)),
        ],
        compiler_params=params(number, 48 * 2**20),
        name="start_all",
    )(tokens, w_query, w_key, w_value, small, integers)


def input_kernel(dq_ref, wq_ref, kv_ref, wkv_ref, dl_ref, router_ref, o_ref):
    piece = kv_ref.shape[2]
    total = product_nt(dq_ref[...], wq_ref[...])
    total = total + product_nt(kv_ref[0], wkv_ref[:, :piece])
    total = total + product_nt(kv_ref[1], wkv_ref[:, piece:])
    for expert in range(router_ref.shape[0]):
        total = total + dl_ref[:, expert : expert + 1] * router_ref[expert : expert + 1, :]
    o_ref[...] = total.astype(BF16)


def input_gradient(query_pre, query_weight, kv_sum, kv_weight, logit_grad, router):
    rows, feats = query_pre.shape
    width = query_weight.shape[0]
    piece = kv_sum.shape[2]
    experts = router.shape[0]
    block, lanes = min(512, rows), 512
    return pl.pallas_call(
        input_kernel,
        grid=(width // lanes, rows // block),
        in_specs=[
            pl.BlockSpec((block, feats), lambda n, i: (i, 0)),
            pl.BlockSpec((lanes, feats), lambda n, i: (n, 0)),
            pl.BlockSpec((2, block, piece), lambda n, i: (0, i, 0)),
            pl.BlockSpec((lanes, 2 * piece), lambda n, i: (n, 0)),
            pl.BlockSpec((block, experts), lambda n, i: (i, 0)),
            pl.BlockSpec((experts, lanes), lambda n, i: (0, n)),
        ],
        out_specs=pl.BlockSpec((block, lanes), lambda n, i: (i, n)),
        out_shape=jax.ShapeDtypeStruct((rows, width), BF16),
        compiler_params=pltpu.CompilerParams(vmem_limit_bytes=40 * 2**20),
        cost_estimate=pl.CostEstimate(
            flops=2 * rows * width * (feats + 2 * piece), bytes_accessed=6 * rows * width, transcendentals=0
        ),
        name="input_gradient",
    )(query_pre, query_weight, kv_sum, kv_weight, logit_grad, router)


def project_kernel(micro, x_ref, w_ref, gain_ref, router_ref, cos_ref, sin_ref, n_ref, kv_ref, l_ref):
    x = x_ref[...].astype(F32)
    scale = lax.rsqrt(jnp.mean(x * x, axis=-1, keepdims=True) + EPSILON)
    normed = (x * scale * gain_ref[...]).astype(BF16)
    n_ref[...] = normed
    l_ref[...] = product_nt(normed, router_ref[...])
    raw = product(normed, w_ref[...])
    piece = kv_ref.shape[2]
    spread = lambda ref: jnp.concatenate(
        [ref[i] for i in range(ref.shape[0]) for _ in range(micro)], axis=0
    )
    cosine, sine = spread(cos_ref), spread(sin_ref)
    for head in range(piece // HDIM):
        cols = slice(head * HDIM, (head + 1) * HDIM)
        kv_ref[0, :, cols] = turn(raw[:, cols], cosine, sine).astype(BF16)
    kv_ref[1] = raw[:, piece:].astype(BF16)


def project(tokens, weight, gain, router, cosine, sine, micro):
    rows, width = tokens.shape
    piece = weight.shape[1] // 2
    experts, tok, half = cosine.shape
    block = 2 * micro * tok
    loops = experts // 2
    return pl.pallas_call(
        partial(project_kernel, micro),
        grid=(rows // block,),
        in_specs=[
            pl.BlockSpec((block, width), lambda i: (i, 0)),
            pl.BlockSpec(weight.shape, lambda i: (0, 0)),
            pl.BlockSpec((1, width), lambda i: (0, 0)),
            pl.BlockSpec(router.shape, lambda i: (0, 0)),
            pl.BlockSpec((2, tok, half), lambda i: (i % loops, 0, 0)),
            pl.BlockSpec((2, tok, half), lambda i: (i % loops, 0, 0)),
        ],
        out_specs=[
            pl.BlockSpec((block, width), lambda i: (i, 0)),
            pl.BlockSpec((2, block, piece), lambda i: (0, i, 0)),
            pl.BlockSpec((block, experts), lambda i: (i, 0)),
        ],
        out_shape=[
            jax.ShapeDtypeStruct((rows, width), BF16),
            jax.ShapeDtypeStruct((2, rows, piece), BF16),
            jax.ShapeDtypeStruct((rows, experts), F32),
        ],
        compiler_params=pltpu.CompilerParams(vmem_limit_bytes=40 * 2**20),
        cost_estimate=pl.CostEstimate(
            flops=2 * rows * width * weight.shape[1], bytes_accessed=5 * rows * width, transcendentals=0
        ),
        name="project",
    )(tokens, weight, gain, router, cosine, sine)


def gather(value, axes, axis=0):
    return lax.all_gather(value, axes, axis=axis, tiled=True)


def scatter(value, axes, axis=0):
    return lax.psum_scatter(value, axes, scatter_dimension=axis, tiled=True)


def swap(value, axes, split=0, concat=0):
    return lax.all_to_all(value, axes, split_axis=split, concat_axis=concat, tiled=True)


DP = ("line", "pair")
ALL = ("line", "pair", "expert")
TREES = ("pair", "expert")


def body(
    tokens,
    w_query,
    w_out,
    w_key,
    w_value,
    gain_attn,
    router_attn,
    gain_mlp,
    router_mlp,
    w_gate,
    w_up,
    w_down,
    attn_route,
    mlp_route,
    fill_order,
    parents,
    cotangent,
):
    experts = lax.axis_size("expert")
    pair = lax.axis_size("pair")
    line = lax.axis_size("line")
    position = lax.axis_index("expert")
    micro, _, tok, width = tokens.shape
    tree = experts * tok
    rows = pair * experts * micro * tok
    heads_total = w_query.shape[2]
    part = heads_total // (line * pair)
    feats = heads_total // pair
    piece = feats // experts
    own_in = w_query.shape[1]
    own_kv = w_key.shape[0]
    capacity = tok * mlp_route.shape[3] // experts
    scale = 1.0 / math.sqrt(HDIM)

    places, segment, depth = tree_layout(tree // 16, tree)
    half = HDIM // 2
    rates = 10000.0 ** (-jnp.arange(half, dtype=F32) / half)
    angle = depth.astype(F32)[:, None] * rates[None, :]
    cosine, sine = jnp.cos(angle), jnp.sin(angle)

    sizes = (line, pair, experts)
    walk = line == 4 and pair == 2 and experts == 4
    own_tokens = tokens.reshape(micro * tok, width)
    small = jnp.concatenate(
        [gain_attn[None], gain_mlp[None], router_attn.T, router_mlp.T], axis=0
    )
    integers = jnp.concatenate([attn_route[:, 0].reshape(micro, -1), parents[:, 0]], axis=1)
    if walk:
        flat = integers.reshape(-1)
        flat = jnp.pad(flat, (0, -flat.shape[0] % 1024)).reshape(-1, 128)
        tree_tokens, query_weight, kv_weight, small, flat = start_all(
            own_tokens, w_query[0], w_key, w_value, small, flat, sizes, 1
        )
        query_weight = query_weight.reshape(width, feats)
        kv_weight = kv_weight.reshape(width, 2 * piece)
        integers = flat.reshape(pair, -1)[:, : integers.size].reshape((pair,) + integers.shape)
    else:
        query_mine = w_query[0].reshape(own_in, line, pair, part)
        query_mine = jnp.transpose(query_mine, (2, 0, 1, 3)).reshape(pair, own_in, feats)
        if pair == 2:
            query_mine = swap(query_mine, "pair")
            integers = lax.all_gather(integers, "pair", axis=0)
        else:
            integers = integers[None]
        query_weight = gather(query_mine.reshape(pair * own_in, feats), "line")
        kv_mine = jnp.stack([w_key, w_value], axis=1).reshape(
            own_kv, 2, experts, line // experts, pair, part
        )
        kv_mine = jnp.transpose(kv_mine, (4, 2, 0, 1, 3, 5)).reshape(
            pair * experts, own_kv, 2 * piece
        )
        tree_tokens = cube_gather(own_tokens, pair, 1)
        small = small_exchange(small, sizes, False, 2)
        kv_mine = swap(kv_mine, TREES).reshape(pair * experts * own_kv, 2 * piece)
        kv_weight = gather(kv_mine, "line")
    out_mine, small = lax.optimization_barrier((w_out[0], small))
    out_weight = gather(out_mine, "line")

    small = jnp.transpose(small, (1, 0, 2)).reshape(-1, width)
    first_gain = small[0].astype(F32)
    second_gain = small[1].astype(F32)
    first_router = small[2 : 2 + experts]
    second_router = small[2 + experts : 2 + 2 * experts]

    residual = own_tokens.astype(F32)
    _, first_pull = jax.vjp(rms_scaled, residual, first_gain)
    table_shape = (experts, tok, half)
    tree_input, kv, first_logits = project(
        tree_tokens.reshape(rows, width),
        kv_weight,
        first_gain[None],
        first_router,
        cosine.reshape(table_shape),
        sine.reshape(table_shape),
        micro,
    )

    routes = integers[..., : tree * 2].reshape(pair, micro, experts, tok, 2)
    routes = jnp.transpose(routes, (0, 2, 1, 3, 4)).reshape(rows, 2)
    family = integers[..., tree * 2 :]
    bias = jax.vmap(jax.vmap(lambda parent: score_bias(parent, segment, places)))(family)

    kv = cube_gather(kv.reshape(2 * rows, piece), 1, 3)
    shape = (pair, experts, micro, tok, feats)
    kv = kv.reshape(experts, 2, pair, experts, micro, tok, piece)

    first_gates, first_gate_pull = jax.vjp(partial(mixture_gates, routes), first_logits)
    column = (jnp.arange(experts, dtype=jnp.int32) == position).astype(F32)
    own_gate = jnp.sum(first_gates * column[None, :], axis=1)

    raw = product(tree_input, query_weight)
    queries, heads_out = attend(raw.reshape(shape), kv, cosine, sine, bias, scale)
    heads_flat = heads_out.reshape(rows, feats)
    projected = product(heads_flat, out_weight)
    gated = (own_gate[:, None] * projected).astype(BF16)
    projected = projected.astype(BF16)
    attention = cube_reduce(gated.reshape(pair * experts, micro * tok, width), pair, 4).astype(F32)

    middle = residual + attention
    second_normed, second_pull = jax.vjp(rms_scaled, middle, second_gain)
    second_normed = second_normed.astype(BF16)
    picked = mlp_route[:, 0].reshape(micro * tok, 2)
    second_gates, second_gate_pull = jax.vjp(
        partial(mixture_gates, picked), product_nt(second_normed, second_router)
    )
    table = jax.vmap(partial(slot_table, experts=experts, capacity=capacity))(
        mlp_route[:, 0], fill_order[:, 0]
    )
    table_low = table.astype(BF16)
    grouped = second_normed.reshape(micro, tok, width)
    outgoing = jnp.einsum("mect,mtd->emcd", table_low, grouped, preferred_element_type=F32)
    top_grad = cotangent.reshape(micro, tok, width)
    slot_values = jnp.einsum("mect,mtd->emcd", table_low, top_grad, preferred_element_type=F32)
    slot_gates = jnp.einsum(
        "mect,mte->emc", table, second_gates.reshape(micro, tok, experts), precision=HIGHEST
    )
    slot_grad = (slot_gates[..., None] * slot_values).astype(BF16)
    slots = experts * micro * capacity
    outgoing = outgoing.astype(BF16).reshape(experts, micro * capacity, width)
    slot_grad = slot_grad.reshape(experts, micro * capacity, width)
    gate_weight, up_weight, down_weight = w_gate[0], w_up[0], w_down[0]
    if walk:
        returned, came_back, arrived, result_grad, inner, gate_grad, up_grad = feed_forward(
            outgoing, slot_grad, gate_weight, up_weight, down_weight, line, pair, 5
        )
        arrived, result_grad, inner, gate_grad, up_grad = (
            value.reshape(-1, value.shape[-1])
            for value in (arrived, result_grad, inner, gate_grad, up_grad)
        )
    else:
        arrived = gather(swap(outgoing, "expert").reshape(slots, width), DP)
        result_grad = gather(swap(slot_grad, "expert").reshape(slots, width), DP)
        gate_pre = product_nt(arrived, gate_weight)
        up_pre = product_nt(arrived, up_weight)
        sigma = jax.nn.sigmoid(gate_pre)
        inner = (gate_pre * sigma * up_pre).astype(BF16)
        returned = product(inner, down_weight).astype(BF16)
        inner_grad = product_nt(result_grad, down_weight)
        gate_grad = (inner_grad * up_pre * sigma * (1.0 + gate_pre * (1.0 - sigma))).astype(BF16)
        up_grad = (inner_grad * gate_pre * sigma).astype(BF16)
        came_back = (product(gate_grad, gate_weight) + product(up_grad, up_weight)).astype(BF16)
        back = (experts, micro * capacity, width)
        returned = swap(scatter(returned, DP).reshape(back), "expert")
        came_back = swap(scatter(came_back, DP).reshape(back), "expert")
    returned = returned.reshape(experts, micro, capacity, width)
    came_back = came_back.reshape(experts, micro, capacity, width)
    spread = jnp.einsum("mect,emcd->emtd", table_low, returned, preferred_element_type=F32)
    spread = spread.reshape(experts, micro * tok, width)
    mixed = jnp.sum(jnp.transpose(second_gates)[:, :, None] * spread, axis=0)
    layer_out = (middle + mixed).astype(BF16)
    dz = top_grad.reshape(micro * tok, width).astype(F32)
    second_gate_grad = jnp.transpose(jnp.sum(spread * dz[None], axis=-1))
    (second_logit_grad,) = second_gate_pull(second_gate_grad)
    hn_grad = jnp.einsum("mect,emcd->mtd", table_low, came_back, preferred_element_type=F32)
    hn_grad = hn_grad.reshape(micro * tok, width)
    second_router_wide = second_router.astype(F32)
    for expert in range(experts):
        hn_grad = hn_grad + second_logit_grad[:, expert : expert + 1] * second_router_wide[expert]
    grad_router_second = split_product(second_logit_grad, second_normed)
    middle_grad, grad_gain_second = second_pull(hn_grad)
    middle_grad = middle_grad + dz

    mix_grad = cube_gather(middle_grad.astype(BF16), pair, 7).reshape(rows, width).astype(F32)
    own_gate_grad = jnp.sum(mix_grad * projected.astype(F32), axis=-1)
    projected_grad = (own_gate[:, None] * mix_grad).astype(BF16)
    grad_output = product_tn(heads_flat, projected_grad).astype(BF16)
    grad_output, projected_grad = lax.optimization_barrier((grad_output, projected_grad))
    grad_output = scatter(grad_output, "line")
    heads_grad = product_nt(projected_grad, out_weight).astype(BF16).reshape(shape)
    query_pre, kv_pre = attend_back(queries, kv, heads_grad, cosine, sine, bias, scale)
    query_pre = query_pre.reshape(rows, feats)
    grad_query = product_tn(tree_input, query_pre).astype(BF16)
    grad_query, kv_pre = lax.optimization_barrier((grad_query, kv_pre))
    kv_sum = cube_reduce(kv_pre.reshape(experts, 2 * rows, piece), 1, 8)
    grad_query, grad_output, kv_sum = lax.optimization_barrier((grad_query, grad_output, kv_sum))
    (first_logit_grad,) = first_gate_pull(own_gate_grad[:, None] * column[None, :])
    kv_sum = kv_sum.reshape(2, rows, piece)
    grad_kv = jnp.concatenate(
        [product_tn(tree_input, kv_sum[0]), product_tn(tree_input, kv_sum[1])], axis=1
    ).astype(BF16)
    input_term = input_gradient(
        query_pre, query_weight, kv_sum, kv_weight, first_logit_grad, first_router.astype(F32)
    ).reshape(pair * experts, micro * tok, width)
    normed_grad = cube_reduce(input_term, pair, 9)
    if not walk:
        grad_kv = scatter(grad_kv, "line")
        grad_kv = swap(grad_kv.reshape(pair * experts, own_kv, 2 * piece), TREES)
        grad_kv = grad_kv.reshape(pair, experts, own_kv, 2, line // experts, part)
        grad_kv = jnp.transpose(grad_kv, (2, 3, 1, 4, 0, 5)).reshape(own_kv, 2, heads_total)
        grad_key, grad_value = grad_kv[:, 0].astype(F32), grad_kv[:, 1].astype(F32)
    grad_query = scatter(grad_query, "line")
    gate_grad, up_grad, inner, arrived, result_grad, normed_grad = lax.optimization_barrier(
        (gate_grad, up_grad, inner, arrived, result_grad, normed_grad)
    )
    grad_gate = product_tn(gate_grad, arrived)[None]
    grad_upward = product_tn(up_grad, arrived)[None]
    grad_downward = product_tn(inner, result_grad)[None]
    normed_grad = normed_grad.astype(F32)
    grad_router_first = split_product(first_logit_grad, tree_input)
    token_grad, grad_gain_first = first_pull(normed_grad)
    tokens_grad = token_grad + middle_grad

    sums = jnp.concatenate(
        [grad_gain_first[None], grad_gain_second[None], grad_router_first, grad_router_second],
        axis=0,
    )
    sums = jnp.transpose(sums.reshape(sums.shape[0], -1, own_kv), (1, 0, 2))
    if walk:
        sums, grad_query, grad_key, grad_value = last_exchange(
            sums, grad_query.reshape(pair, own_in, feats), grad_kv, sizes, 10
        )
        grad_query = grad_query[None]
    else:
        sums = small_exchange(sums, sizes, True, 10)
        grad_query = swap(grad_query.reshape(own_in * pair, line, part)[None], "pair", 1, 0)
        grad_query = jnp.transpose(grad_query, (1, 2, 0, 3)).reshape(1, own_in, heads_total)
    return (
        layer_out.reshape(micro, 1, tok, width),
        tokens_grad.reshape(micro, 1, tok, width),
        grad_query.astype(F32),
        grad_output[None].astype(F32),
        grad_key,
        grad_value,
        sums[0],
        jnp.transpose(sums[2 : 2 + experts]),
        sums[1],
        jnp.transpose(sums[2 + experts :]),
        grad_gate,
        grad_upward,
        grad_downward,
    )


def solution(mesh):
    line, experts = mesh.devices.shape
    pair = 2 if line % 2 == 0 and (HEADS % line == 0) else 1
    shaped = Mesh(mesh.devices.reshape(line // pair, pair, experts), ALL)
    in_specs = (
        P(None, DP, "expert", None),
        P("expert", DP, None),
        P("expert", DP, None),
        P(ALL, None),
        P(ALL, None),
        P(ALL),
        P(ALL, None),
        P(ALL),
        P(ALL, None),
        P("expert", DP, None),
        P("expert", DP, None),
        P("expert", DP, None),
        P(None, DP, None, None),
        P(None, DP, "expert", None),
        P(None, DP, "expert"),
        P(None, DP, None),
        P(None, DP, "expert", None),
    )
    out_specs = (
        P(None, DP, "expert", None),
        P(None, DP, "expert", None),
        P("expert", DP, None),
        P("expert", DP, None),
        P(ALL, None),
        P(ALL, None),
        P(ALL),
        P(ALL, None),
        P(ALL),
        P(ALL, None),
        P("expert", DP, None),
        P("expert", DP, None),
        P("expert", DP, None),
    )
    return jax.shard_map(body, mesh=shaped, in_specs=in_specs, out_specs=out_specs, check_vma=False)
```

```python
from functools import partial
import math

import jax
import jax.numpy as jnp
from jax import lax
from jax.experimental import pallas as pl
from jax.experimental.pallas import tpu as pltpu
from jax.sharding import Mesh, PartitionSpec as P

HEADS = 16
HDIM = 128
EPSILON = 1e-06
HIGHEST = lax.Precision.HIGHEST
BF16 = jnp.bfloat16
F32 = jnp.float32


def product(left, right):
    return jnp.dot(left, right, preferred_element_type=F32)


def product_tn(left, right):
    return lax.dot_general(left, right, (((0,), (0,)), ((), ())), preferred_element_type=F32)


def product_nt(left, right):
    return lax.dot_general(left, right, (((1,), (1,)), ((), ())), preferred_element_type=F32)


def split_product(values, rows):
    parts, rest = [], values
    for _ in range(3):
        parts.append(lax.reduce_precision(rest, 8, 7))
        rest = rest - parts[-1]
    count = values.shape[1]
    total = product_tn(jnp.concatenate(parts, axis=1).astype(BF16), rows)
    return total[:count] + total[count : 2 * count] + total[2 * count :]


def rms_scaled(values, gain):
    return values * lax.rsqrt(jnp.mean(values * values, axis=-1, keepdims=True) + EPSILON) * gain


def mixture_gates(picked, logits):
    labels = jnp.arange(logits.shape[1], dtype=jnp.int32)
    onehot = (picked[:, :, None] == labels[None, None, :]).astype(F32)
    chosen = jnp.sum(onehot * logits[:, None, :], axis=-1)
    weights = jax.nn.softmax(chosen, axis=-1)
    return jnp.sum(weights[:, :, None] * onehot, axis=1)


def tree_layout(segment_len, tree_len):
    places = jnp.arange(tree_len, dtype=jnp.int32)
    trunk_len = 4 * segment_len
    segment = jnp.where(
        places < trunk_len,
        0,
        jnp.where(
            places < 2 * trunk_len,
            1 + (places - trunk_len) // segment_len,
            5 + (places - 2 * trunk_len) // segment_len,
        ),
    )
    depth = jnp.where(
        places < trunk_len,
        places,
        jnp.where(
            places < 2 * trunk_len,
            trunk_len + (places - trunk_len) % segment_len,
            trunk_len + segment_len + (places - 2 * trunk_len) % segment_len,
        ),
    )
    return (places, segment, depth)


def ancestors(parent, segment):
    labels = jnp.arange(parent.shape[0], dtype=jnp.int32)
    first = jnp.where(labels > 0, parent, -1)
    lookup = jnp.maximum(first, 0)[:, None] == labels[None, :]
    second = jnp.where(first > 0, jnp.sum(jnp.where(lookup, parent[None, :], 0), axis=1), -1)
    member = segment[:, None] == labels[None, :]
    up_one = jnp.sum(jnp.where(member, first[None, :], 0), axis=1)
    up_two = jnp.sum(jnp.where(member, second[None, :], 0), axis=1)
    return (up_one, up_two)


def score_bias(parent, segment, places):
    up_one, up_two = ancestors(parent, segment)
    same = (segment[None, :] == segment[:, None]) & (places[None, :] <= places[:, None])
    seen = same | (segment[None, :] == up_one[:, None]) | (segment[None, :] == up_two[:, None])
    return jnp.where(seen, 0.0, -1e30).astype(F32)


def slot_table(picked, order, experts, capacity):
    labels = jnp.arange(experts, dtype=jnp.int32)
    chosen = jnp.sum((picked[:, :, None] == labels[None, None, :]).astype(F32), axis=1)
    earlier = (order[None, :] < order[:, None]).astype(F32)
    ranks = jnp.dot(earlier, chosen, precision=HIGHEST, preferred_element_type=F32)
    slots = jnp.arange(capacity, dtype=F32)
    return jnp.transpose(chosen)[:, None, :] * (
        jnp.transpose(ranks)[:, None, :] == slots[None, :, None]
    ).astype(F32)


def turn(values, cosine, sine):
    half = values.shape[-1] // 2
    first = values[:, :half]
    second = values[:, half:]
    return jnp.concatenate(
        [first * cosine - second * sine, second * cosine + first * sine], axis=-1
    )


def softmax_rows(queries, keys, bias, scale):
    scores = product_nt(queries, keys) * scale + bias
    highest = jnp.max(scores, axis=-1, keepdims=True)
    weights = jnp.exp(scores - highest)
    return weights / jnp.sum(weights, axis=-1, keepdims=True)


def attend_kernel(heads, scale, raw_ref, kv_ref, cos_ref, sin_ref, bias_ref, query_ref, out_ref):
    quarter, tok = raw_ref.shape[1], raw_ref.shape[3]
    rows = quarter * tok
    cosine, sine, bias = cos_ref[...], sin_ref[...], bias_ref[0, 0]
    for head in range(heads):
        cols = slice(head * HDIM, (head + 1) * HDIM)
        raw = raw_ref[0, :, 0, :, cols].reshape(rows, HDIM)
        keys = kv_ref[0, 0, 0, :, 0, :, cols].reshape(rows, HDIM)
        values = kv_ref[0, 1, 0, :, 0, :, cols].reshape(rows, HDIM)
        queries = turn(raw, cosine, sine).astype(BF16)
        probs = softmax_rows(queries, keys, bias, scale).astype(BF16)
        query_ref[0, :, 0, :, cols] = queries.reshape(quarter, tok, HDIM)
        out_ref[0, :, 0, :, cols] = product(probs, values).astype(BF16).reshape(quarter, tok, HDIM)


def attend_back_kernel(
    heads, scale, query_ref, kv_ref, grad_ref, cos_ref, sin_ref, bias_ref, dq_ref, dkv_ref
):
    quarter, tok = query_ref.shape[1], query_ref.shape[3]
    rows = quarter * tok
    cosine, sine, bias = cos_ref[...], sin_ref[...], bias_ref[0, 0]
    for head in range(heads):
        cols = slice(head * HDIM, (head + 1) * HDIM)
        queries = query_ref[0, :, 0, :, cols].reshape(rows, HDIM)
        keys = kv_ref[0, 0, 0, :, 0, :, cols].reshape(rows, HDIM)
        values = kv_ref[0, 1, 0, :, 0, :, cols].reshape(rows, HDIM)
        grad = grad_ref[0, :, 0, :, cols].reshape(rows, HDIM)
        probs = softmax_rows(queries, keys, bias, scale)
        prob_grad = product_nt(grad, values)
        centre = jnp.sum(prob_grad * probs, axis=-1, keepdims=True)
        score_grad = (probs * (prob_grad - centre) * scale).astype(BF16)
        query_grad = turn(product(score_grad, keys), cosine, -sine).astype(BF16)
        key_grad = turn(product_tn(score_grad, queries), cosine, -sine).astype(BF16)
        value_grad = product_tn(probs.astype(BF16), grad).astype(BF16)
        dq_ref[0, :, 0, :, cols] = query_grad.reshape(quarter, tok, HDIM)
        dkv_ref[0, 0, 0, :, 0, :, cols] = key_grad.reshape(quarter, tok, HDIM)
        dkv_ref[0, 1, 0, :, 0, :, cols] = value_grad.reshape(quarter, tok, HDIM)


def attention_specs(shape, slices):
    pair, quarter, micro, tok, feats = shape
    part = feats // slices
    rows = quarter * tok
    grid = (pair, micro, slices)
    flat = pl.BlockSpec((1, quarter, 1, tok, part), lambda i, m, s: (i, 0, m, 0, s))
    both = pl.BlockSpec(
        (1, 2, 1, quarter, 1, tok, part), lambda i, m, s: (s, 0, i, 0, m, 0, 0)
    )
    angle = pl.BlockSpec((rows, HDIM // 2), lambda i, m, s: (0, 0))
    bias = pl.BlockSpec((1, 1, rows, rows), lambda i, m, s: (i, m, 0, 0))
    return grid, part, flat, both, angle, bias


def attend(raw, kv, cosine, sine, bias, scale):
    slices = kv.shape[0]
    grid, part, flat, both, angle, bias_spec = attention_specs(raw.shape, slices)
    out = jax.ShapeDtypeStruct(raw.shape, BF16)
    return pl.pallas_call(
        partial(attend_kernel, part // HDIM, scale),
        grid=grid,
        in_specs=[flat, both, angle, angle, bias_spec],
        out_specs=[flat, flat],
        out_shape=[out, out],
        cost_estimate=pl.CostEstimate(
            flops=4 * raw.size * cosine.shape[0],
            bytes_accessed=12 * raw.size,
            transcendentals=raw.size * 2,
        ),
        name="attend",
    )(raw, kv, cosine, sine, bias)


def attend_back(queries, kv, grad, cosine, sine, bias, scale):
    slices = kv.shape[0]
    grid, part, flat, both, angle, bias_spec = attention_specs(queries.shape, slices)
    return pl.pallas_call(
        partial(attend_back_kernel, part // HDIM, scale),
        grid=grid,
        in_specs=[flat, both, flat, angle, angle, bias_spec],
        out_specs=[flat, both],
        out_shape=[
            jax.ShapeDtypeStruct(queries.shape, BF16),
            jax.ShapeDtypeStruct(kv.shape, BF16),
        ],
        cost_estimate=pl.CostEstimate(
            flops=10 * queries.size * cosine.shape[0],
            bytes_accessed=14 * queries.size,
            transcendentals=queries.size * 2,
        ),
        name="attend_back",
    )(queries, kv, grad, cosine, sine, bias)


MESH = pl.DeviceIdType.MESH
ANY = pl.BlockSpec(memory_space=pl.ANY)
VMEM = pl.BlockSpec(memory_space=pltpu.VMEM)
DMA = pltpu.SemaphoreType.DMA


def remote(src, dst, send, recv, target):
    return pltpu.make_async_remote_copy(
        src_ref=src, dst_ref=dst, send_sem=send, recv_sem=recv, device_id=target, device_id_type=MESH
    )


def greet(targets):
    barrier = pltpu.get_barrier_semaphore()
    for target in targets:
        pl.semaphore_signal(barrier, inc=1, device_id=target, device_id_type=MESH)
    pl.semaphore_wait(barrier, len(targets))


def params(number, limit=None):
    return pltpu.CompilerParams(
        collective_id=number, has_side_effects=True, vmem_limit_bytes=limit
    )


def add_into(target, sources, rows):
    step = 1
    while step * 2 <= rows and step * 2 * target.shape[-1] <= 65536 and rows % (step * 2) == 0:
        step *= 2

    def one(index, carry):
        where = pl.ds(pl.multiple_of(index * step, step), step)
        total = sources[0][where].astype(F32)
        for source in sources[1:]:
            total = total + source[where].astype(F32)
        target[where] = total.astype(target.dtype)
        return carry

    lax.fori_loop(0, rows // step, one, 0)


def cube_reduce_kernel(pairs, x_ref, o_ref, half, quarter, got_core, got_side, got_pair, send, recv):
    p = lax.axis_index("pair") if pairs == 2 else 0
    e = lax.axis_index("expert")
    c, y = lax.rem(e, 2), lax.div(e, 2)
    core = {"expert": e + 1 - 2 * c}
    side = {"expert": e + 2 - 4 * y}
    other = {"pair": lax.rem(p + 1, pairs)}
    greet([core, side] + ([other] if pairs == 2 else []))
    rows = x_ref.shape[3]
    shifts = (1, 0) if pairs == 2 else (0,)
    order = [(dx, dy) for dy in (1, 0) for dx in shifts]
    copies = []

    def push(source, place, slot, target):
        copy = remote(source, place, send.at[slot], recv.at[slot], target)
        copy.start()
        copies.append(copy)
        return copy

    first = []
    for slot, (dx, dy) in enumerate(order):
        px, yy = lax.rem(p + dx, pairs), lax.rem(y + dy, 2)
        first.append(push(x_ref.at[px, yy, 1 - c], got_core.at[slot], slot, core))
    base = len(order)
    cut = rows // 2 if pairs == 2 else rows
    upper, lower = pl.ds(0, cut), pl.ds(cut, rows - cut)
    to_side, to_other = {}, {}
    for slot, (dx, dy) in enumerate(order):
        px, yy = lax.rem(p + dx, pairs), lax.rem(y + dy, 2)
        first[slot].wait_recv()
        add_into(half.at[slot], [x_ref.at[px, yy, c], got_core.at[slot]], rows)
        if dy == 1:
            to_side[dx] = push(
                half.at[slot, upper], got_side.at[dx, upper], base + dx, side
            )
        if dx == 1:
            to_other[dy] = push(
                half.at[slot, lower], got_pair.at[dy, lower], base + 2 + dy, other
            )
    own = half.at[order.index((0, 0))]
    if pairs == 2:
        to_side[1].wait_recv()
        add_into(
            quarter.at[upper],
            [half.at[order.index((1, 0)), upper], got_side.at[1, upper]],
            cut,
        )
        to_pair = push(quarter.at[upper], got_pair.at[0, upper], base + 4, other)
        to_other[1].wait_recv()
        add_into(
            quarter.at[lower],
            [half.at[order.index((0, 1)), lower], got_pair.at[1, lower]],
            rows - cut,
        )
        to_flank = push(quarter.at[lower], got_side.at[0, lower], base + 5, side)
        to_side[0].wait_recv()
        to_pair.wait_recv()
        add_into(
            o_ref.at[upper], [own.at[upper], got_side.at[0, upper], got_pair.at[0, upper]], cut
        )
        to_other[0].wait_recv()
        to_flank.wait_recv()
        add_into(
            o_ref.at[lower],
            [own.at[lower], got_side.at[0, lower], got_pair.at[0, lower]],
            rows - cut,
        )
    else:
        to_side[0].wait_recv()
        add_into(o_ref, [own, got_side.at[0]], rows)
    for copy in copies:
        copy.wait_send()


def cube_reduce(value, pairs, number):
    _, rows, cols = value.shape
    value = value.reshape(pairs, 2, 2, rows, cols)
    slots = 2 * pairs
    block = jax.ShapeDtypeStruct((rows, cols), value.dtype)
    return pl.pallas_call(
        partial(cube_reduce_kernel, pairs),
        in_specs=[VMEM],
        out_specs=VMEM,
        out_shape=block,
        scratch_shapes=[
            pltpu.VMEM((slots, rows, cols), value.dtype),
            pltpu.VMEM((rows, cols), value.dtype),
            pltpu.VMEM((slots, rows, cols), value.dtype),
            pltpu.VMEM((2, rows, cols), value.dtype),
            pltpu.VMEM((2, rows, cols), value.dtype),
            DMA((slots + 6,)),
            DMA((slots + 6,)),
        ],
        compiler_params=params(number, 48 * 2**20),
        cost_estimate=pl.CostEstimate(flops=0, bytes_accessed=0, transcendentals=0),
        name="cube_reduce",
    )(value)


def cube_gather_kernel(pairs, x_ref, o_ref, send, recv, local):
    p = lax.axis_index("pair") if pairs == 2 else 0
    e = lax.axis_index("expert")
    c, y = lax.rem(e, 2), lax.div(e, 2)
    core = {"expert": e + 1 - 2 * c}
    side = {"expert": e + 2 - 4 * y}
    other = {"pair": lax.rem(p + 1, pairs)}
    greet([core, side] + ([other] if pairs == 2 else []))
    q, w = lax.rem(p + 1, pairs), 1 - y
    own = o_ref.at[p, y, c]
    keep = pltpu.make_async_copy(x_ref, own, local)
    keep.start()
    copies = []

    def push(slot, source, place, target):
        copy = remote(source, place, send.at[slot], recv.at[slot], target)
        copy.start()
        copies.append(copy)
        return copy

    rows = x_ref.shape[0]
    cut = rows // 2
    upper, lower = pl.ds(0, cut), pl.ds(cut, rows - cut)
    to_side = push(0, x_ref, own, side)
    to_other = push(1, x_ref, own, other) if pairs == 2 else None
    to_core = push(2, x_ref, own, core)
    waits = [to_core]
    if pairs == 2:
        to_other.wait_recv()
        block = o_ref.at[q, y, c]
        far = [push(3, block.at[upper], block.at[upper], side)]
        waits.append(push(4, block, block, core))
    to_side.wait_recv()
    block = o_ref.at[p, w, c]
    if pairs == 2:
        far.append(push(7, block.at[lower], block.at[lower], other))
    waits.append(push(5, block, block, core))
    if pairs == 2:
        for copy in far:
            copy.wait_recv()
        block = o_ref.at[q, w, c]
        waits.append(push(6, block, block, core))
    for copy in waits:
        copy.wait_recv()
    for copy in copies:
        copy.wait_send()
    keep.wait()


def cube_gather(value, pairs, number):
    return pl.pallas_call(
        partial(cube_gather_kernel, pairs),
        in_specs=[VMEM],
        out_specs=VMEM,
        out_shape=jax.ShapeDtypeStruct((pairs, 2, 2) + value.shape, value.dtype),
        scratch_shapes=[DMA((8,)), DMA((8,)), DMA(())],
        compiler_params=params(number, 48 * 2**20),
        cost_estimate=pl.CostEstimate(
            flops=0, bytes_accessed=80 * value.size, transcendentals=0
        ),
        name="cube_gather",
    )(value)


def place_of(index, sizes):
    line, pairs, experts = sizes
    return {
        "line": index // (pairs * experts),
        "pair": (index // experts) % pairs,
        "expert": index % experts,
    }


def small_kernel(sizes, reduce, x_ref, o_ref, got, send, recv):
    line, pairs, experts = sizes
    count = line * pairs * experts
    me = (
        lax.axis_index("line") * (pairs * experts)
        + lax.axis_index("pair") * experts
        + lax.axis_index("expert")
    )
    barrier = pltpu.get_barrier_semaphore()

    def greet_one(offset, carry):
        target = place_of((me + offset) % count, sizes)
        pl.semaphore_signal(barrier, inc=1, device_id=target, device_id_type=MESH)
        return carry

    lax.fori_loop(1, count, greet_one, 0)
    pl.semaphore_wait(barrier, count - 1)

    def copy_to(offset):
        peer = (me + offset) % count
        source = x_ref.at[peer] if reduce else x_ref
        return remote(source, got.at[offset], send.at[offset], recv.at[offset], place_of(peer, sizes))

    def start(offset, carry):
        copy_to(offset).start()
        return carry

    lax.fori_loop(1, count, start, 0)
    got[0] = x_ref[me] if reduce else x_ref[...]

    def finish(offset, carry):
        copy_to(offset).wait()
        return carry

    lax.fori_loop(1, count, finish, 0)
    if reduce:
        o_ref[...] = jnp.sum(got[...], axis=0)
    else:

        def order(offset, carry):
            o_ref[(me - offset + count) % count] = got[offset]
            return carry

        lax.fori_loop(0, count, order, 0)


def small_exchange(value, sizes, reduce, number):
    count = sizes[0] * sizes[1] * sizes[2]
    block = value.shape[1:] if reduce else value.shape
    return pl.pallas_call(
        partial(small_kernel, sizes, reduce),
        in_specs=[VMEM],
        out_specs=VMEM,
        out_shape=jax.ShapeDtypeStruct(block if reduce else (count,) + block, value.dtype),
        scratch_shapes=[pltpu.VMEM((count,) + block, value.dtype), DMA((count,)), DMA((count,))],
        compiler_params=params(number),
        cost_estimate=pl.CostEstimate(flops=0, bytes_accessed=2**24, transcendentals=0),
        name="small_reduce" if reduce else "small_gather",
    )(value)


def ff_kernel(
    a_in, b_in, gate_hbm, up_hbm, down_hbm,
    a_out, b_out, a_save, b_save, inner_save, dgate_save, dup_save,
    a_buf, b_buf, side, hop, extra, w_gate, w_up, w_down, mid, acc,
    send, recv, load, store, local,
):
    z, p, e = lax.axis_index("line"), lax.axis_index("pair"), lax.axis_index("expert")
    line, _, rows, width = a_buf.shape
    experts, size = a_in.shape[0], a_in.shape[1]
    q = 1 - p
    twin = z + 1 - 2 * (z % 2)
    up, down, other, across = {"line": z + 1}, {"line": z - 1}, {"pair": q}, {"line": twin}
    ins, bufs, outs, saves = (a_in, b_in), (a_buf, b_buf), (a_out, b_out), (a_save, b_save)
    high = z // 2
    near = z + high * (line - 1 - 2 * z)

    def order(t):
        j = t + near * (1 - t // 2) * (1 - 2 * t)
        return j + high * (line - 1 - 2 * j)

    weights = [
        pltpu.make_async_copy(src, dst, load.at[i])
        for i, (src, dst) in enumerate(((gate_hbm, w_gate), (up_hbm, w_up), (down_hbm, w_down)))
    ]
    for copy in weights:
        copy.start()

    barrier = pltpu.get_barrier_semaphore()
    for shift in range(1, experts):
        pl.semaphore_signal(
            barrier, inc=1, device_id={"expert": (e + shift) % experts}, device_id_type=MESH
        )
    pl.semaphore_signal(barrier, inc=1, device_id=other, device_id_type=MESH)

    @pl.when(z > 0)
    def _():
        pl.semaphore_signal(barrier, inc=1, device_id=down, device_id_type=MESH)

    @pl.when(z < line - 1)
    def _():
        pl.semaphore_signal(barrier, inc=1, device_id=up, device_id_type=MESH)

    below, above = (z + line - 1) // line, (2 * line - 2 - z) // line
    pl.semaphore_wait(barrier, experts + below + above)

    UP, DOWN, SIDE, SUMUP, SUMDOWN, SUMSIDE = (i * line for i in range(6))
    SUMTWIN, SWAP = 6 * line, 6 * line + 1
    BACK = SWAP + experts
    PART = BACK + experts
    EARLY = PART + experts

    def push(src, dst, kind, use, target):
        return remote(src, dst, send.at[kind, use], recv.at[kind, use], target)

    def to_up(kind, j):
        return push(bufs[kind].at[j, p], bufs[kind].at[j, p], kind, UP + j, up)

    def to_down(kind, j):
        return push(bufs[kind].at[j, p], bufs[kind].at[j, p], kind, DOWN + j, down)

    def to_other(kind, j):
        return push(bufs[kind].at[j, p], bufs[kind].at[j, p], kind, SIDE + j, other)

    def early(kind, shift):
        ref = bufs[kind].at[z, p, piece((e + experts - shift) % experts)]
        return push(ref, ref, kind, EARLY + shift, other)

    def sum_up(kind, j):
        return push(bufs[kind].at[j, p], hop.at[kind, j], kind, SUMUP + j, up)

    def sum_down(kind, j, slot):
        return push(bufs[kind].at[j, p], hop.at[kind, slot], kind, SUMDOWN + j, down)

    def sum_other(kind, j):
        return push(bufs[kind].at[j, q], side.at[kind, j], kind, SUMSIDE + j, other)

    def piece(index):
        return pl.ds(pl.multiple_of(index * size, size), size)

    far_expert = (e + 2) % experts
    queue = (far_expert, far_expert + 1 - 2 * (far_expert % 2), e + 1 - 2 * (e % 2), e)

    def sum_part(i):
        return push(
            b_buf.at[z, q, piece(queue[i])],
            side.at[1, z, piece(queue[i])],
            1,
            PART + i,
            other,
        )

    def sum_twin():
        return push(bufs[1].at[twin, q], extra, 1, SUMTWIN, across)

    def save(kind, j, column):
        return pltpu.make_async_copy(
            bufs[kind].at[j, column], saves[kind].at[j, column], store.at[kind, j, column]
        )

    swaps = []
    for kind in range(2):
        home = bufs[kind].at[z, p, piece(e)]
        keep = pltpu.make_async_copy(ins[kind].at[e], home, local.at[kind])
        keep.start()
        group = []
        for shift in range(1, experts):
            peer = (e + shift) % experts
            copy = push(ins[kind].at[peer], home, kind, SWAP + shift, {"expert": peer})
            copy.start()
            group.append(copy)
        swaps.append((keep, group))

    def spread(t, first=False):
        j = order(t)
        for kind in range(2):
            if first:
                swaps[kind][0].wait()
                early(kind, 0).start()
                for shift in range(experts - 1, 0, -1):
                    swaps[kind][1][shift - 1].wait_recv()
                    early(kind, shift).start()
            else:

                @pl.when(j < z)
                def _():
                    to_up(kind, j).wait_recv()

                @pl.when(j > z)
                def _():
                    to_down(kind, j).wait_recv()

            @pl.when((j <= z) & (z < line - 1))
            def _():
                to_up(kind, j).start()

            @pl.when((j >= z) & (z > 0))
            def _():
                to_down(kind, j).start()

            if not first:
                to_other(kind, j).start()
            save(kind, j, p).start()

    chunk = 512
    steps = width // chunk

    def first_half(j, column):
        for index in range(3):
            acc[index] = jnp.zeros(acc.shape[1:], F32)

        def one(k, carry):
            where = pl.ds(pl.multiple_of(k * chunk, chunk), chunk)
            left = a_buf[j, column, :, where]
            acc[0] += product_nt(left, w_gate[:, where])
            acc[1] += product_nt(left, w_up[:, where])
            acc[2] += product_nt(b_buf[j, column, :, where], w_down[:, where])
            return carry

        lax.fori_loop(0, steps, one, 0)
        part = 32

        def two(i, carry):
            where = pl.ds(pl.multiple_of(i * part, part), part)
            gate, lift, grad = acc[0, where], acc[1, where], acc[2, where]
            sigma = jax.nn.sigmoid(gate)
            mid[j, column, 0, where] = (gate * sigma * lift).astype(BF16)
            mid[j, column, 1, where] = (
                grad * lift * sigma * (1.0 + gate * (1.0 - sigma))
            ).astype(BF16)
            mid[j, column, 2, where] = (grad * gate * sigma).astype(BF16)
            return carry

        lax.fori_loop(0, rows // part, two, 0)

    def second_half(j, column):
        def one(k, carry):
            where = pl.ds(pl.multiple_of(k * chunk, chunk), chunk)
            a_buf[j, column, :, where] = product(mid[j, column, 0], w_down[:, where]).astype(BF16)
            b_buf[j, column, :, where] = (
                product(mid[j, column, 1], w_gate[:, where])
                + product(mid[j, column, 2], w_up[:, where])
            ).astype(BF16)
            return carry

        lax.fori_loop(0, steps, one, 0)

    def arrive(j):
        for kind in range(2):
            @pl.when(j == z)
            def _():
                for shift in range(experts):
                    early(kind, shift).wait_recv()

            @pl.when(j != z)
            def _():
                to_other(kind, j).wait_recv()

            save(kind, j, q).start()

    def emit(t):
        j = order(t)
        sum_other(0, j).start()

        @pl.when((j != twin) & (j != z))
        def _():
            sum_other(1, j).start()

    def step(s, carry):
        @pl.when(s == 0)
        def _():
            spread(0, True)
            for copy in weights:
                copy.wait()

        @pl.when(s == 1)
        def _():
            spread(1)
            spread(2)

        @pl.when(s == 3)
        def _():
            spread(3)

        @pl.when(s == line)
        def _():
            sum_twin().start()

        def half(c, inner_carry):
            t = s - c
            column = p + c * (q - p)

            @pl.when((t >= 0) & (t < line))
            def _():
                j = order(t)

                @pl.when(c == 1)
                def _():
                    arrive(j)

                first_half(j, column)

                @pl.when(c == 1)
                def _():
                    for kind in range(2):
                        save(kind, j, q).wait()
                    second_half(j, column)

            return inner_carry

        return lax.fori_loop(0, 2, half, carry)

    lax.fori_loop(0, line + 1, step, 0)

    for t in (3, 2, 1, 0):
        emit(t)

    for copy in (
        pltpu.make_async_copy(mid.at[:, :, 0], inner_save, local.at[2]),
        pltpu.make_async_copy(mid.at[:, :, 1], dgate_save, local.at[3]),
        pltpu.make_async_copy(mid.at[:, :, 2], dup_save, local.at[4]),
    ):
        copy.start()
    sum_twin().wait_recv()
    for i in range(experts):
        part = b_buf.at[z, q, piece(queue[i])]
        add_into(part, [part, extra.at[piece(queue[i])]], size)
        sum_part(i).start()

    def back(kind):
        own = pltpu.make_async_copy(
            bufs[kind].at[z, p, piece(e)], outs[kind].at[e], local.at[kind]
        )
        return [own] + [
            push(
                bufs[kind].at[z, p, piece((e + shift) % experts)],
                outs[kind].at[e],
                kind,
                BACK + shift,
                {"expert": (e + shift) % experts},
            )
            for shift in range(1, experts)
        ]

    def back_part(i):
        source = b_buf.at[z, p, piece(queue[i])]
        if i == experts - 1:
            return pltpu.make_async_copy(source, b_out.at[e], local.at[1])
        return push(source, b_out.at[e], 1, BACK + 1 + i, {"expert": queue[i]})

    def fold(s, carry):
        t = line - 1 - s
        j = order(t)
        for kind in range(2):
            save(kind, j, p).wait()

            @pl.when((j <= z) & (z < line - 1))
            def _():
                to_up(kind, j).wait_send()

            @pl.when((j >= z) & (z > 0))
            def _():
                to_down(kind, j).wait_send()

            @pl.when(j == z)
            def _():
                for shift in range(experts):
                    early(kind, shift).wait_send()

            @pl.when(j != z)
            def _():
                to_other(kind, j).wait_send()

        second_half(j, p)
        for kind in range(2):
            mine = bufs[kind].at[j, p]
            if kind == 0:
                sum_other(kind, j).wait_recv()
                add_into(mine, [mine, side.at[kind, j]], rows)
            else:

                @pl.when((j != twin) & (j != z))
                def _():
                    sum_other(kind, j).wait_recv()
                    add_into(mine, [mine, side.at[kind, j]], rows)

            @pl.when((j >= z) & (z > 0))
            def _():
                sum_up(kind, j).wait_recv()
                add_into(mine, [mine, hop.at[kind, j]], rows)

            @pl.when((j < z) & (z < line - 1))
            def _():
                sum_down(kind, j, j).wait_recv()
                add_into(mine, [mine, hop.at[kind, j]], rows)

            @pl.when((j == z) & (z < line - 1))
            def _():
                sum_down(kind, j, line).wait_recv()
                add_into(mine, [mine, hop.at[kind, line]], rows)

            @pl.when(j == z)
            def _():
                if kind == 0:
                    for copy in back(0):
                        copy.start()
                else:
                    for i in range(experts):
                        part = b_buf.at[z, p, piece(queue[i])]
                        sum_part(i).wait_recv()
                        add_into(part, [part, side.at[1, z, piece(queue[i])]], size)
                        back_part(i).start()

            @pl.when(j > z)
            def _():
                sum_up(kind, j).start()

            @pl.when((j < z) & (j != z - 1))
            def _():
                sum_down(kind, j, j).start()

            @pl.when((j < z) & (j == z - 1))
            def _():
                sum_down(kind, j, line).start()

        return carry

    lax.fori_loop(0, line, fold, 0)

    for copy in back(0):
        copy.wait()
    for i in range(experts):
        back_part(i).wait()

    def drain(j, carry):
        for kind in range(2):
            if kind == 0:
                sum_other(kind, j).wait_send()
            else:

                @pl.when((j != twin) & (j != z))
                def _():
                    sum_other(kind, j).wait_send()

            @pl.when(j > z)
            def _():
                sum_up(kind, j).wait_send()

            @pl.when(j < z)
            def _():
                sum_down(kind, j, j).wait_send()

        return carry

    lax.fori_loop(0, line, drain, 0)
    sum_twin().wait_send()
    for i in range(experts):
        sum_part(i).wait_send()
    for copy in (
        pltpu.make_async_copy(mid.at[:, :, 0], inner_save, local.at[2]),
        pltpu.make_async_copy(mid.at[:, :, 1], dgate_save, local.at[3]),
        pltpu.make_async_copy(mid.at[:, :, 2], dup_save, local.at[4]),
    ):
        copy.wait()
    for keep, group in swaps:
        for copy in group:
            copy.wait_send()


def feed_forward(first, second, w_gate, w_up, w_down, line, pairs, number):
    experts, size, width = first.shape
    hidden = w_gate.shape[0]
    rows = experts * size
    blocks = (line, pairs, rows)
    back = jax.ShapeDtypeStruct(first.shape, BF16)
    wide = jax.ShapeDtypeStruct(blocks + (width,), BF16)
    thin = jax.ShapeDtypeStruct(blocks + (hidden,), BF16)
    uses = 6 * line + 2 + 4 * experts
    total = line * pairs * rows
    return pl.pallas_call(
        ff_kernel,
        in_specs=[ANY] * 5,
        out_specs=[ANY] * 7,
        out_shape=[back, back, wide, wide, thin, thin, thin],
        scratch_shapes=[
            pltpu.VMEM(blocks + (width,), BF16),
            pltpu.VMEM(blocks + (width,), BF16),
            pltpu.VMEM((2, line, rows, width), BF16),
            pltpu.VMEM((2, line + 1, rows, width), BF16),
            pltpu.VMEM((rows, width), BF16),
            pltpu.VMEM((hidden, width), BF16),
            pltpu.VMEM((hidden, width), BF16),
            pltpu.VMEM((hidden, width), BF16),
            pltpu.VMEM((line, pairs, 3, rows, hidden), BF16),
            pltpu.VMEM((3, rows, hidden), F32),
            DMA((2, uses)),
            DMA((2, uses)),
            DMA((3,)),
            DMA((2, line, pairs)),
            DMA((5,)),
        ],
        compiler_params=params(number, 63 * 2**20),
        cost_estimate=pl.CostEstimate(
            flops=12 * total * hidden * width,
            bytes_accessed=12 * total * width,
            transcendentals=total * hidden,
        ),
        name="feed_forward",
    )(first, second, w_gate, w_up, w_down)


def last_kernel(
    sizes, x_ref, q_ref, g_hbm, o_ref, w_ref, key_ref, value_ref,
    got, side, g_ref, k_ref, hop, send, recv, peer_send, peer_recv, local,
):
    line, pairs, experts = sizes
    trees = pairs * experts
    count = line * trees
    z, p, e = lax.axis_index("line"), lax.axis_index("pair"), lax.axis_index("expert")
    mine = p * experts + e
    me = z * trees + mine
    span, piece = g_ref.shape[1], k_ref.shape[1]
    up, down = {"line": z + 1}, {"line": z - 1}
    high = z // 2
    near = z + high * (line - 1 - 2 * z)

    def order(t):
        j = t + near * (1 - t // 2) * (1 - 2 * t)
        return j + high * (line - 1 - 2 * j)

    fetch = pltpu.make_async_copy(g_hbm, g_ref, local)
    fetch.start()
    barrier = pltpu.get_barrier_semaphore()

    def greet_one(offset, carry):
        target = place_of((me + offset) % count, sizes)
        pl.semaphore_signal(barrier, inc=1, device_id=target, device_id_type=MESH)
        return carry

    lax.fori_loop(1, count, greet_one, 0)
    pl.semaphore_wait(barrier, count - 1)
    UP, DOWN, SWAP, PAIR = 0, line, 2 * line, 2 * line + trees

    def sum_up(j):
        return remote(g_ref.at[j], hop.at[j], send.at[UP + j], recv.at[UP + j], up)

    def sum_down(j, slot):
        return remote(g_ref.at[j], hop.at[slot], send.at[DOWN + j], recv.at[DOWN + j], down)

    def fold(t):
        j = order(t)
        own = g_ref.at[j]

        @pl.when((j >= z) & (z > 0))
        def _():
            sum_up(j).wait_recv()
            add_into(own, [own, hop.at[j]], span)

        @pl.when((j < z) & (z < line - 1))
        def _():
            sum_down(j, j).wait_recv()
            add_into(own, [own, hop.at[j]], span)

        @pl.when((j == z) & (z < line - 1))
        def _():
            sum_down(j, line).wait_recv()
            add_into(own, [own, hop.at[line]], span)

        @pl.when(j > z)
        def _():
            sum_up(j).start()

        @pl.when((j < z) & (j != z - 1))
        def _():
            sum_down(j, j).start()

        @pl.when((j < z) & (j == z - 1))
        def _():
            sum_down(j, line).start()

    fetch.wait()
    fold(3)
    swap = remote(q_ref.at[1 - p], side, send.at[PAIR], recv.at[PAIR], {"pair": 1 - p})
    swap.start()

    def copy_to(offset):
        peer = (me + offset) % count
        return remote(
            x_ref.at[peer],
            got.at[offset],
            peer_send.at[offset],
            peer_recv.at[offset],
            place_of(peer, sizes),
        )

    def start(offset, carry):
        copy_to(offset).start()
        return carry

    lax.fori_loop(1, count, start, 0)
    got[0] = x_ref[me]
    fold(2)
    part = q_ref.shape[2] // line

    def lay(block, source):
        for index in range(line):
            column = pl.multiple_of((index * pairs + source) * part, part)
            w_ref[:, pl.ds(column, part)] = block[:, index * part : (index + 1) * part].astype(F32)

    lay(q_ref.at[p], p)
    fold(1)
    swap.wait_recv()
    lay(side, 1 - p)

    def finish(offset, carry):
        copy_to(offset).wait()
        return carry

    lax.fori_loop(1, count, finish, 0)
    o_ref[...] = jnp.sum(got[...], axis=0)
    fold(0)

    def share_of(index):
        return g_ref.at[z, pl.ds(pl.multiple_of(index * piece, piece), piece)]

    keep = pltpu.make_async_copy(share_of(mine), k_ref.at[mine], local)
    keep.start()
    swaps = []
    for shift in range(1, trees):
        peer = (mine + shift) % trees
        copy = remote(
            share_of(peer),
            k_ref.at[mine],
            send.at[SWAP + shift],
            recv.at[SWAP + shift],
            {"pair": peer // experts, "expert": peer % experts},
        )
        copy.start()
        swaps.append(copy)
    keep.wait()
    for copy in swaps:
        copy.wait()
    share = k_ref.shape[2] // 2
    for source in range(trees):
        column = ((source % experts) * pairs + source // experts) * share
        for index, target in enumerate((key_ref, value_ref)):
            target[:, column : column + share] = k_ref[
                source, :, index * share : (index + 1) * share
            ].astype(F32)
    swap.wait_send()

    def drain(j, carry):
        @pl.when(j > z)
        def _():
            sum_up(j).wait_send()

        @pl.when(j < z)
        def _():
            sum_down(j, j).wait_send()

        return carry

    lax.fori_loop(0, line, drain, 0)


def last_exchange(sums, query, grads, sizes, number):
    line, pairs, experts = sizes
    trees = pairs * experts
    count, block = sums.shape[0], sums.shape[1:]
    _, rows, cols = query.shape
    span, thin = grads.shape[0] // line, grads.shape[1]
    uses = 2 * line + trees + 1
    wide = jax.ShapeDtypeStruct((span // trees, trees * thin // 2), F32)
    return pl.pallas_call(
        partial(last_kernel, sizes),
        in_specs=[VMEM, VMEM, ANY],
        out_specs=[VMEM] * 4,
        out_shape=[
            jax.ShapeDtypeStruct(block, F32),
            jax.ShapeDtypeStruct((rows, pairs * cols), F32),
            wide,
            wide,
        ],
        scratch_shapes=[
            pltpu.VMEM((count,) + block, F32),
            pltpu.VMEM((rows, cols), BF16),
            pltpu.VMEM((line, span, thin), BF16),
            pltpu.VMEM((trees, span // trees, thin), BF16),
            pltpu.VMEM((line + 1, span, thin), BF16),
            DMA((uses,)),
            DMA((uses,)),
            DMA((count,)),
            DMA((count,)),
            DMA(()),
        ],
        compiler_params=params(number, 48 * 2**20),
        cost_estimate=pl.CostEstimate(flops=0, bytes_accessed=0, transcendentals=0),
        name="last_exchange",
    )(sums, query, grads.reshape(line, span, thin))


def start_all_kernel(
    sizes, tok_ref, wq_ref, wk_ref, wv_ref, small_ref, int_ref,
    tok_out, q_out, kv_out, small_out, int_out,
    q_cut, kv_cut, send, recv, peer_send, peer_recv, local,
):
    line, pairs, experts = sizes
    z, p, e = lax.axis_index("line"), lax.axis_index("pair"), lax.axis_index("expert")
    c, y = e % 2, e // 2
    core, side = {"expert": e + 1 - 2 * c}, {"expert": e + 2 - 4 * y}
    other = {"pair": 1 - p}
    trees = pairs * experts
    count = line * trees
    mine = p * experts + e
    me = z * trees + mine
    barrier = pltpu.get_barrier_semaphore()

    def greet_one(offset, carry):
        target = place_of((me + offset) % count, sizes)
        pl.semaphore_signal(barrier, inc=1, device_id=target, device_id_type=MESH)
        return carry

    lax.fori_loop(1, count, greet_one, 0)
    part = wq_ref.shape[1] // (line * pairs)
    sub = line // experts
    for q in range(pairs):
        for d in range(experts):
            for index, ref in enumerate((wk_ref, wv_ref)):
                for h in range(sub):
                    column = ((d * sub + h) * pairs + q) * part
                    place = (index * sub + h) * part
                    kv_cut[q * experts + d, :, place : place + part] = ref[
                        :, column : column + part
                    ]
    for q in range(pairs):
        for index in range(line):
            column = (index * pairs + q) * part
            q_cut[q, :, index * part : (index + 1) * part] = wq_ref[:, column : column + part]
    pl.semaphore_wait(barrier, count - 1)

    copies, TOK, QSWAP, INTS, KV = [], 0, 7, 8, 9
    WALK = KV + trees

    def push(slot, source, place, target):
        copy = remote(source, place, send.at[slot], recv.at[slot], target)
        copy.start()
        copies.append(copy)
        return copy

    size = kv_cut.shape[1]
    kv_home = kv_out.at[z, pl.ds(pl.multiple_of(mine * size, size), size)]
    pieces = []
    for shift in range(1, trees):
        peer = (mine + shift) % trees
        pieces.append(
            push(
                KV + shift,
                kv_cut.at[peer],
                kv_home,
                {"pair": peer // experts, "expert": peer % experts},
            )
        )
    rows = q_cut.shape[1]
    q_home = q_out.at[z, pl.ds(pl.multiple_of(p * rows, rows), rows)]
    q_swap = push(QSWAP, q_cut.at[1 - p], q_home, other)
    keeps = [
        pltpu.make_async_copy(q_cut.at[p], q_home, local.at[0]),
        pltpu.make_async_copy(kv_cut.at[mine], kv_home, local.at[1]),
        pltpu.make_async_copy(tok_ref, tok_out.at[p, y, c], local.at[2]),
        pltpu.make_async_copy(small_ref, small_out.at[me], local.at[3]),
        pltpu.make_async_copy(int_ref, int_out.at[p], local.at[4]),
    ]
    for copy in keeps:
        copy.start()
    def walker(block, base):
        def to_up(j, d):
            ref = block(j)
            return remote(ref, ref, send.at[base + d], recv.at[base + d], {"line": z + 1})

        def to_down(j, d):
            ref, at = block(j), base + line + d
            return remote(ref, ref, send.at[at], recv.at[at], {"line": z - 1})

        return to_up, to_down

    def q_rows(member):
        return lambda j: q_out.at[j, pl.ds(pl.multiple_of(member * rows, rows), rows)]

    stride = 2 * line + 2
    walkers = [
        walker(q_rows(p), WALK),
        walker(lambda j: kv_out.at[j], WALK + stride),
        walker(q_rows(1 - p), WALK + 2 * stride),
    ]

    def begin(which):
        to_up, to_down = walkers[which]

        @pl.when(z < line - 1)
        def _():
            to_up(z, 1).start()

        @pl.when(z > 0)
        def _():
            to_down(z, 1).start()

    keeps[0].wait()
    begin(0)
    own = tok_out.at[p, y, c]
    to_side = push(TOK, tok_ref, own, side)
    to_other = push(TOK + 1, tok_ref, own, other)
    waits = [push(TOK + 2, tok_ref, own, core), push(INTS, int_ref, int_out.at[p], other)]

    def small_to(offset):
        return remote(
            small_ref,
            small_out.at[me],
            peer_send.at[offset],
            peer_recv.at[offset],
            place_of((me + offset) % count, sizes),
        )

    def small_start(offset, carry):
        small_to(offset).start()
        return carry

    lax.fori_loop(1, count, small_start, 0)

    keeps[1].wait()
    for copy in pieces:
        copy.wait_recv()
    begin(1)
    q_swap.wait_recv()
    begin(2)
    to_other.wait_recv()
    block = tok_out.at[1 - p, y, c]
    far = push(TOK + 3, block, block, side)
    waits.append(push(TOK + 4, block, block, core))
    to_side.wait_recv()
    block = tok_out.at[p, 1 - y, c]
    waits.append(push(TOK + 5, block, block, core))
    far.wait_recv()
    block = tok_out.at[1 - p, 1 - y, c]
    waits.append(push(TOK + 6, block, block, core))

    for d in range(1, line):
        for to_up, to_down in walkers:

            @pl.when(z - d >= 0)
            def _():
                to_up(z - d, d).wait_recv()

                @pl.when(z < line - 1)
                def _():
                    to_up(z - d, d + 1).start()

            @pl.when(z + d < line)
            def _():
                to_down(z + d, d).wait_recv()

                @pl.when(z > 0)
                def _():
                    to_down(z + d, d + 1).start()

    for d in range(1, line):
        for to_up, to_down in walkers:

            @pl.when((z - d + 1 >= 0) & (z < line - 1))
            def _():
                to_up(z - d + 1, d).wait_send()

            @pl.when((z + d - 1 < line) & (z > 0))
            def _():
                to_down(z + d - 1, d).wait_send()

    for copy in waits:
        copy.wait_recv()
    for copy in copies:
        copy.wait_send()
    for copy in keeps[2:]:
        copy.wait()

    def small_finish(offset, carry):
        small_to(offset).wait()
        return carry

    lax.fori_loop(1, count, small_finish, 0)


def start_all(tokens, w_query, w_key, w_value, small, integers, sizes, number):
    line, pairs, experts = sizes
    trees = pairs * experts
    count = line * trees
    rows, width = w_query.shape
    size = w_key.shape[0]
    feats = width // pairs
    thin = 2 * feats // experts
    uses = 9 + trees + 6 * line + 6
    return pl.pallas_call(
        partial(start_all_kernel, sizes),
        in_specs=[VMEM] * 6,
        out_specs=[VMEM] * 5,
        out_shape=[
            jax.ShapeDtypeStruct((pairs, 2, 2) + tokens.shape, BF16),
            jax.ShapeDtypeStruct((line, pairs * rows, feats), BF16),
            jax.ShapeDtypeStruct((line, trees * size, thin), BF16),
            jax.ShapeDtypeStruct((count,) + small.shape, BF16),
            jax.ShapeDtypeStruct((pairs,) + integers.shape, jnp.int32),
        ],
        scratch_shapes=[
            pltpu.VMEM((pairs, rows, feats), BF16),
            pltpu.VMEM((trees, size, thin), BF16),
            DMA((uses,)),
            DMA((uses,)),
            DMA((count,)),
            DMA((count,)),
            DMA((5,)),
        ],
        compiler_params=params(number, 48 * 2**20),
        name="start_all",
    )(tokens, w_query, w_key, w_value, small, integers)


def input_kernel(dq_ref, wq_ref, kv_ref, wkv_ref, dl_ref, router_ref, o_ref):
    piece = kv_ref.shape[2]
    total = product_nt(dq_ref[...], wq_ref[...])
    total = total + product_nt(kv_ref[0], wkv_ref[:, :piece])
    total = total + product_nt(kv_ref[1], wkv_ref[:, piece:])
    for expert in range(router_ref.shape[0]):
        total = total + dl_ref[:, expert : expert + 1] * router_ref[expert : expert + 1, :]
    o_ref[...] = total.astype(BF16)


def input_gradient(query_pre, query_weight, kv_sum, kv_weight, logit_grad, router):
    rows, feats = query_pre.shape
    width = query_weight.shape[0]
    piece = kv_sum.shape[2]
    experts = router.shape[0]
    block, lanes = min(512, rows), 512
    return pl.pallas_call(
        input_kernel,
        grid=(width // lanes, rows // block),
        in_specs=[
            pl.BlockSpec((block, feats), lambda n, i: (i, 0)),
            pl.BlockSpec((lanes, feats), lambda n, i: (n, 0)),
            pl.BlockSpec((2, block, piece), lambda n, i: (0, i, 0)),
            pl.BlockSpec((lanes, 2 * piece), lambda n, i: (n, 0)),
            pl.BlockSpec((block, experts), lambda n, i: (i, 0)),
            pl.BlockSpec((experts, lanes), lambda n, i: (0, n)),
        ],
        out_specs=pl.BlockSpec((block, lanes), lambda n, i: (i, n)),
        out_shape=jax.ShapeDtypeStruct((rows, width), BF16),
        compiler_params=pltpu.CompilerParams(vmem_limit_bytes=40 * 2**20),
        cost_estimate=pl.CostEstimate(
            flops=2 * rows * width * (feats + 2 * piece), bytes_accessed=6 * rows * width, transcendentals=0
        ),
        name="input_gradient",
    )(query_pre, query_weight, kv_sum, kv_weight, logit_grad, router)


def project_kernel(micro, x_ref, w_ref, gain_ref, router_ref, cos_ref, sin_ref, n_ref, kv_ref, l_ref):
    x = x_ref[...].astype(F32)
    scale = lax.rsqrt(jnp.mean(x * x, axis=-1, keepdims=True) + EPSILON)
    normed = (x * scale * gain_ref[...]).astype(BF16)
    n_ref[...] = normed
    l_ref[...] = product_nt(normed, router_ref[...])
    raw = product(normed, w_ref[...])
    piece = kv_ref.shape[2]
    spread = lambda ref: jnp.concatenate(
        [ref[i] for i in range(ref.shape[0]) for _ in range(micro)], axis=0
    )
    cosine, sine = spread(cos_ref), spread(sin_ref)
    for head in range(piece // HDIM):
        cols = slice(head * HDIM, (head + 1) * HDIM)
        kv_ref[0, :, cols] = turn(raw[:, cols], cosine, sine).astype(BF16)
    kv_ref[1] = raw[:, piece:].astype(BF16)


def project(tokens, weight, gain, router, cosine, sine, micro):
    rows, width = tokens.shape
    piece = weight.shape[1] // 2
    experts, tok, half = cosine.shape
    block = 2 * micro * tok
    loops = experts // 2
    return pl.pallas_call(
        partial(project_kernel, micro),
        grid=(rows // block,),
        in_specs=[
            pl.BlockSpec((block, width), lambda i: (i, 0)),
            pl.BlockSpec(weight.shape, lambda i: (0, 0)),
            pl.BlockSpec((1, width), lambda i: (0, 0)),
            pl.BlockSpec(router.shape, lambda i: (0, 0)),
            pl.BlockSpec((2, tok, half), lambda i: (i % loops, 0, 0)),
            pl.BlockSpec((2, tok, half), lambda i: (i % loops, 0, 0)),
        ],
        out_specs=[
            pl.BlockSpec((block, width), lambda i: (i, 0)),
            pl.BlockSpec((2, block, piece), lambda i: (0, i, 0)),
            pl.BlockSpec((block, experts), lambda i: (i, 0)),
        ],
        out_shape=[
            jax.ShapeDtypeStruct((rows, width), BF16),
            jax.ShapeDtypeStruct((2, rows, piece), BF16),
            jax.ShapeDtypeStruct((rows, experts), F32),
        ],
        compiler_params=pltpu.CompilerParams(vmem_limit_bytes=40 * 2**20),
        cost_estimate=pl.CostEstimate(
            flops=2 * rows * width * weight.shape[1], bytes_accessed=5 * rows * width, transcendentals=0
        ),
        name="project",
    )(tokens, weight, gain, router, cosine, sine)


def gather(value, axes, axis=0):
    return lax.all_gather(value, axes, axis=axis, tiled=True)


def scatter(value, axes, axis=0):
    return lax.psum_scatter(value, axes, scatter_dimension=axis, tiled=True)


def swap(value, axes, split=0, concat=0):
    return lax.all_to_all(value, axes, split_axis=split, concat_axis=concat, tiled=True)


DP = ("line", "pair")
ALL = ("line", "pair", "expert")
TREES = ("pair", "expert")


def body(
    tokens,
    w_query,
    w_out,
    w_key,
    w_value,
    gain_attn,
    router_attn,
    gain_mlp,
    router_mlp,
    w_gate,
    w_up,
    w_down,
    attn_route,
    mlp_route,
    fill_order,
    parents,
    cotangent,
):
    experts = lax.axis_size("expert")
    pair = lax.axis_size("pair")
    line = lax.axis_size("line")
    position = lax.axis_index("expert")
    micro, _, tok, width = tokens.shape
    tree = experts * tok
    rows = pair * experts * micro * tok
    heads_total = w_query.shape[2]
    part = heads_total // (line * pair)
    feats = heads_total // pair
    piece = feats // experts
    own_in = w_query.shape[1]
    own_kv = w_key.shape[0]
    capacity = tok * mlp_route.shape[3] // experts
    scale = 1.0 / math.sqrt(HDIM)

    places, segment, depth = tree_layout(tree // 16, tree)
    half = HDIM // 2
    rates = 10000.0 ** (-jnp.arange(half, dtype=F32) / half)
    angle = depth.astype(F32)[:, None] * rates[None, :]
    cosine, sine = jnp.cos(angle), jnp.sin(angle)

    sizes = (line, pair, experts)
    walk = line == 4 and pair == 2 and experts == 4
    own_tokens = tokens.reshape(micro * tok, width)
    small = jnp.concatenate(
        [gain_attn[None], gain_mlp[None], router_attn.T, router_mlp.T], axis=0
    )
    integers = jnp.concatenate([attn_route[:, 0].reshape(micro, -1), parents[:, 0]], axis=1)
    if walk:
        flat = integers.reshape(-1)
        flat = jnp.pad(flat, (0, -flat.shape[0] % 1024)).reshape(-1, 128)
        tree_tokens, query_weight, kv_weight, small, flat = start_all(
            own_tokens, w_query[0], w_key, w_value, small, flat, sizes, 1
        )
        query_weight = query_weight.reshape(width, feats)
        kv_weight = kv_weight.reshape(width, 2 * piece)
        integers = flat.reshape(pair, -1)[:, : integers.size].reshape((pair,) + integers.shape)
    else:
        query_mine = w_query[0].reshape(own_in, line, pair, part)
        query_mine = jnp.transpose(query_mine, (2, 0, 1, 3)).reshape(pair, own_in, feats)
        if pair == 2:
            query_mine = swap(query_mine, "pair")
            integers = lax.all_gather(integers, "pair", axis=0)
        else:
            integers = integers[None]
        query_weight = gather(query_mine.reshape(pair * own_in, feats), "line")
        kv_mine = jnp.stack([w_key, w_value], axis=1).reshape(
            own_kv, 2, experts, line // experts, pair, part
        )
        kv_mine = jnp.transpose(kv_mine, (4, 2, 0, 1, 3, 5)).reshape(
            pair * experts, own_kv, 2 * piece
        )
        tree_tokens = cube_gather(own_tokens, pair, 1)
        small = small_exchange(small, sizes, False, 2)
        kv_mine = swap(kv_mine, TREES).reshape(pair * experts * own_kv, 2 * piece)
        kv_weight = gather(kv_mine, "line")
    out_mine, small = lax.optimization_barrier((w_out[0], small))
    out_weight = gather(out_mine, "line")

    small = jnp.transpose(small, (1, 0, 2)).reshape(-1, width)
    first_gain = small[0].astype(F32)
    second_gain = small[1].astype(F32)
    first_router = small[2 : 2 + experts]
    second_router = small[2 + experts : 2 + 2 * experts]

    residual = own_tokens.astype(F32)
    _, first_pull = jax.vjp(rms_scaled, residual, first_gain)
    table_shape = (experts, tok, half)
    tree_input, kv, first_logits = project(
        tree_tokens.reshape(rows, width),
        kv_weight,
        first_gain[None],
        first_router,
        cosine.reshape(table_shape),
        sine.reshape(table_shape),
        micro,
    )

    routes = integers[..., : tree * 2].reshape(pair, micro, experts, tok, 2)
    routes = jnp.transpose(routes, (0, 2, 1, 3, 4)).reshape(rows, 2)
    family = integers[..., tree * 2 :]
    bias = jax.vmap(jax.vmap(lambda parent: score_bias(parent, segment, places)))(family)

    kv = cube_gather(kv.reshape(2 * rows, piece), 1, 3)
    shape = (pair, experts, micro, tok, feats)
    kv = kv.reshape(experts, 2, pair, experts, micro, tok, piece)

    first_gates, first_gate_pull = jax.vjp(partial(mixture_gates, routes), first_logits)
    column = (jnp.arange(experts, dtype=jnp.int32) == position).astype(F32)
    own_gate = jnp.sum(first_gates * column[None, :], axis=1)

    raw = product(tree_input, query_weight)
    queries, heads_out = attend(raw.reshape(shape), kv, cosine, sine, bias, scale)
    heads_flat = heads_out.reshape(rows, feats)
    projected = product(heads_flat, out_weight)
    gated = (own_gate[:, None] * projected).astype(BF16)
    projected = projected.astype(BF16)
    attention = cube_reduce(gated.reshape(pair * experts, micro * tok, width), pair, 4).astype(F32)

    middle = residual + attention
    second_normed, second_pull = jax.vjp(rms_scaled, middle, second_gain)
    second_normed = second_normed.astype(BF16)
    picked = mlp_route[:, 0].reshape(micro * tok, 2)
    second_gates, second_gate_pull = jax.vjp(
        partial(mixture_gates, picked), product_nt(second_normed, second_router)
    )
    table = jax.vmap(partial(slot_table, experts=experts, capacity=capacity))(
        mlp_route[:, 0], fill_order[:, 0]
    )
    table_low = table.astype(BF16)
    grouped = second_normed.reshape(micro, tok, width)
    outgoing = jnp.einsum("mect,mtd->emcd", table_low, grouped, preferred_element_type=F32)
    top_grad = cotangent.reshape(micro, tok, width)
    slot_values = jnp.einsum("mect,mtd->emcd", table_low, top_grad, preferred_element_type=F32)
    slot_gates = jnp.einsum(
        "mect,mte->emc", table, second_gates.reshape(micro, tok, experts), precision=HIGHEST
    )
    slot_grad = (slot_gates[..., None] * slot_values).astype(BF16)
    slots = experts * micro * capacity
    outgoing = outgoing.astype(BF16).reshape(experts, micro * capacity, width)
    slot_grad = slot_grad.reshape(experts, micro * capacity, width)
    gate_weight, up_weight, down_weight = w_gate[0], w_up[0], w_down[0]
    if walk:
        returned, came_back, arrived, result_grad, inner, gate_grad, up_grad = feed_forward(
            outgoing, slot_grad, gate_weight, up_weight, down_weight, line, pair, 5
        )
        arrived, result_grad, inner, gate_grad, up_grad = (
            value.reshape(-1, value.shape[-1])
            for value in (arrived, result_grad, inner, gate_grad, up_grad)
        )
    else:
        arrived = gather(swap(outgoing, "expert").reshape(slots, width), DP)
        result_grad = gather(swap(slot_grad, "expert").reshape(slots, width), DP)
        gate_pre = product_nt(arrived, gate_weight)
        up_pre = product_nt(arrived, up_weight)
        sigma = jax.nn.sigmoid(gate_pre)
        inner = (gate_pre * sigma * up_pre).astype(BF16)
        returned = product(inner, down_weight).astype(BF16)
        inner_grad = product_nt(result_grad, down_weight)
        gate_grad = (inner_grad * up_pre * sigma * (1.0 + gate_pre * (1.0 - sigma))).astype(BF16)
        up_grad = (inner_grad * gate_pre * sigma).astype(BF16)
        came_back = (product(gate_grad, gate_weight) + product(up_grad, up_weight)).astype(BF16)
        back = (experts, micro * capacity, width)
        returned = swap(scatter(returned, DP).reshape(back), "expert")
        came_back = swap(scatter(came_back, DP).reshape(back), "expert")
    returned = returned.reshape(experts, micro, capacity, width)
    came_back = came_back.reshape(experts, micro, capacity, width)
    spread = jnp.einsum("mect,emcd->emtd", table_low, returned, preferred_element_type=F32)
    spread = spread.reshape(experts, micro * tok, width)
    mixed = jnp.sum(jnp.transpose(second_gates)[:, :, None] * spread, axis=0)
    layer_out = (middle + mixed).astype(BF16)
    dz = top_grad.reshape(micro * tok, width).astype(F32)
    second_gate_grad = jnp.transpose(jnp.sum(spread * dz[None], axis=-1))
    (second_logit_grad,) = second_gate_pull(second_gate_grad)
    hn_grad = jnp.einsum("mect,emcd->mtd", table_low, came_back, preferred_element_type=F32)
    hn_grad = hn_grad.reshape(micro * tok, width)
    second_router_wide = second_router.astype(F32)
    for expert in range(experts):
        hn_grad = hn_grad + second_logit_grad[:, expert : expert + 1] * second_router_wide[expert]
    grad_router_second = split_product(second_logit_grad, second_normed)
    middle_grad, grad_gain_second = second_pull(hn_grad)
    middle_grad = middle_grad + dz

    mix_grad = cube_gather(middle_grad.astype(BF16), pair, 7).reshape(rows, width).astype(F32)
    own_gate_grad = jnp.sum(mix_grad * projected.astype(F32), axis=-1)
    projected_grad = (own_gate[:, None] * mix_grad).astype(BF16)
    grad_output = product_tn(heads_flat, projected_grad).astype(BF16)
    grad_output, projected_grad = lax.optimization_barrier((grad_output, projected_grad))
    grad_output = scatter(grad_output, "line")
    heads_grad = product_nt(projected_grad, out_weight).astype(BF16).reshape(shape)
    query_pre, kv_pre = attend_back(queries, kv, heads_grad, cosine, sine, bias, scale)
    query_pre = query_pre.reshape(rows, feats)
    grad_query = product_tn(tree_input, query_pre).astype(BF16)
    grad_query, kv_pre = lax.optimization_barrier((grad_query, kv_pre))
    kv_sum = cube_reduce(kv_pre.reshape(experts, 2 * rows, piece), 1, 8)
    grad_query, grad_output, kv_sum = lax.optimization_barrier((grad_query, grad_output, kv_sum))
    (first_logit_grad,) = first_gate_pull(own_gate_grad[:, None] * column[None, :])
    kv_sum = kv_sum.reshape(2, rows, piece)
    grad_kv = jnp.concatenate(
        [product_tn(tree_input, kv_sum[0]), product_tn(tree_input, kv_sum[1])], axis=1
    ).astype(BF16)
    input_term = input_gradient(
        query_pre, query_weight, kv_sum, kv_weight, first_logit_grad, first_router.astype(F32)
    ).reshape(pair * experts, micro * tok, width)
    normed_grad = cube_reduce(input_term, pair, 9)
    if not walk:
        grad_kv = scatter(grad_kv, "line")
        grad_kv = swap(grad_kv.reshape(pair * experts, own_kv, 2 * piece), TREES)
        grad_kv = grad_kv.reshape(pair, experts, own_kv, 2, line // experts, part)
        grad_kv = jnp.transpose(grad_kv, (2, 3, 1, 4, 0, 5)).reshape(own_kv, 2, heads_total)
        grad_key, grad_value = grad_kv[:, 0].astype(F32), grad_kv[:, 1].astype(F32)
    grad_query = scatter(grad_query, "line")
    gate_grad, up_grad, inner, arrived, result_grad, normed_grad = lax.optimization_barrier(
        (gate_grad, up_grad, inner, arrived, result_grad, normed_grad)
    )
    grad_gate = product_tn(gate_grad, arrived)[None]
    grad_upward = product_tn(up_grad, arrived)[None]
    grad_downward = product_tn(inner, result_grad)[None]
    normed_grad = normed_grad.astype(F32)
    grad_router_first = split_product(first_logit_grad, tree_input)
    token_grad, grad_gain_first = first_pull(normed_grad)
    tokens_grad = token_grad + middle_grad

    sums = jnp.concatenate(
        [grad_gain_first[None], grad_gain_second[None], grad_router_first, grad_router_second],
        axis=0,
    )
    sums = jnp.transpose(sums.reshape(sums.shape[0], -1, own_kv), (1, 0, 2))
    if walk:
        sums, grad_query, grad_key, grad_value = last_exchange(
            sums, grad_query.reshape(pair, own_in, feats), grad_kv, sizes, 10
        )
        grad_query = grad_query[None]
    else:
        sums = small_exchange(sums, sizes, True, 10)
        grad_query = swap(grad_query.reshape(own_in * pair, line, part)[None], "pair", 1, 0)
        grad_query = jnp.transpose(grad_query, (1, 2, 0, 3)).reshape(1, own_in, heads_total)
    return (
        layer_out.reshape(micro, 1, tok, width),
        tokens_grad.reshape(micro, 1, tok, width),
        grad_query.astype(F32),
        grad_output[None].astype(F32),
        grad_key,
        grad_value,
        sums[0],
        jnp.transpose(sums[2 : 2 + experts]),
        sums[1],
        jnp.transpose(sums[2 + experts :]),
        grad_gate,
        grad_upward,
        grad_downward,
    )


def solution(mesh):
    line, experts = mesh.devices.shape
    pair = 2 if line % 2 == 0 and (HEADS % line == 0) else 1
    shaped = Mesh(mesh.devices.reshape(line // pair, pair, experts), ALL)
    in_specs = (
        P(None, DP, "expert", None),
        P("expert", DP, None),
        P("expert", DP, None),
        P(ALL, None),
        P(ALL, None),
        P(ALL),
        P(ALL, None),
        P(ALL),
        P(ALL, None),
        P("expert", DP, None),
        P("expert", DP, None),
        P("expert", DP, None),
        P(None, DP, None, None),
        P(None, DP, "expert", None),
        P(None, DP, "expert"),
        P(None, DP, None),
        P(None, DP, "expert", None),
    )
    out_specs = (
        P(None, DP, "expert", None),
        P(None, DP, "expert", None),
        P("expert", DP, None),
        P("expert", DP, None),
        P(ALL, None),
        P(ALL, None),
        P(ALL),
        P(ALL, None),
        P(ALL),
        P(ALL, None),
        P("expert", DP, None),
        P("expert", DP, None),
        P("expert", DP, None),
    )
    return jax.shard_map(body, mesh=shaped, in_specs=in_specs, out_specs=out_specs, check_vma=False)
```

```python
from functools import partial
import math

import jax
import jax.numpy as jnp
from jax import lax
from jax.experimental import pallas as pl
from jax.experimental.pallas import tpu as pltpu
from jax.sharding import Mesh, PartitionSpec as P

HEADS = 16
HDIM = 128
EPSILON = 1e-06
HIGHEST = lax.Precision.HIGHEST
BF16 = jnp.bfloat16
F32 = jnp.float32


def product(left, right):
    return jnp.dot(left, right, preferred_element_type=F32)


def product_tn(left, right):
    return lax.dot_general(left, right, (((0,), (0,)), ((), ())), preferred_element_type=F32)


def product_nt(left, right):
    return lax.dot_general(left, right, (((1,), (1,)), ((), ())), preferred_element_type=F32)


def split_product(values, rows):
    parts, rest = [], values
    for _ in range(3):
        parts.append(lax.reduce_precision(rest, 8, 7))
        rest = rest - parts[-1]
    count = values.shape[1]
    total = product_tn(jnp.concatenate(parts, axis=1).astype(BF16), rows)
    return total[:count] + total[count : 2 * count] + total[2 * count :]


def rms_scaled(values, gain):
    return values * lax.rsqrt(jnp.mean(values * values, axis=-1, keepdims=True) + EPSILON) * gain


def mixture_gates(picked, logits):
    labels = jnp.arange(logits.shape[1], dtype=jnp.int32)
    onehot = (picked[:, :, None] == labels[None, None, :]).astype(F32)
    chosen = jnp.sum(onehot * logits[:, None, :], axis=-1)
    weights = jax.nn.softmax(chosen, axis=-1)
    return jnp.sum(weights[:, :, None] * onehot, axis=1)


def tree_layout(segment_len, tree_len):
    places = jnp.arange(tree_len, dtype=jnp.int32)
    trunk_len = 4 * segment_len
    segment = jnp.where(
        places < trunk_len,
        0,
        jnp.where(
            places < 2 * trunk_len,
            1 + (places - trunk_len) // segment_len,
            5 + (places - 2 * trunk_len) // segment_len,
        ),
    )
    depth = jnp.where(
        places < trunk_len,
        places,
        jnp.where(
            places < 2 * trunk_len,
            trunk_len + (places - trunk_len) % segment_len,
            trunk_len + segment_len + (places - 2 * trunk_len) % segment_len,
        ),
    )
    return (places, segment, depth)


def ancestors(parent, segment):
    labels = jnp.arange(parent.shape[0], dtype=jnp.int32)
    first = jnp.where(labels > 0, parent, -1)
    lookup = jnp.maximum(first, 0)[:, None] == labels[None, :]
    second = jnp.where(first > 0, jnp.sum(jnp.where(lookup, parent[None, :], 0), axis=1), -1)
    member = segment[:, None] == labels[None, :]
    up_one = jnp.sum(jnp.where(member, first[None, :], 0), axis=1)
    up_two = jnp.sum(jnp.where(member, second[None, :], 0), axis=1)
    return (up_one, up_two)


def score_bias(parent, segment, places):
    up_one, up_two = ancestors(parent, segment)
    same = (segment[None, :] == segment[:, None]) & (places[None, :] <= places[:, None])
    seen = same | (segment[None, :] == up_one[:, None]) | (segment[None, :] == up_two[:, None])
    return jnp.where(seen, 0.0, -1e30).astype(F32)


def slot_table(picked, order, experts, capacity):
    labels = jnp.arange(experts, dtype=jnp.int32)
    chosen = jnp.sum((picked[:, :, None] == labels[None, None, :]).astype(F32), axis=1)
    earlier = (order[None, :] < order[:, None]).astype(F32)
    ranks = jnp.dot(earlier, chosen, precision=HIGHEST, preferred_element_type=F32)
    slots = jnp.arange(capacity, dtype=F32)
    return jnp.transpose(chosen)[:, None, :] * (
        jnp.transpose(ranks)[:, None, :] == slots[None, :, None]
    ).astype(F32)


def turn(values, cosine, sine):
    half = values.shape[-1] // 2
    first = values[:, :half]
    second = values[:, half:]
    return jnp.concatenate(
        [first * cosine - second * sine, second * cosine + first * sine], axis=-1
    )


def softmax_rows(queries, keys, bias, scale):
    scores = product_nt(queries, keys) * scale + bias
    highest = jnp.max(scores, axis=-1, keepdims=True)
    weights = jnp.exp(scores - highest)
    return weights / jnp.sum(weights, axis=-1, keepdims=True)


def attend_kernel(heads, scale, raw_ref, kv_ref, cos_ref, sin_ref, bias_ref, query_ref, out_ref):
    quarter, tok = raw_ref.shape[1], raw_ref.shape[3]
    rows = quarter * tok
    cosine, sine, bias = cos_ref[...], sin_ref[...], bias_ref[0, 0]
    for head in range(heads):
        cols = slice(head * HDIM, (head + 1) * HDIM)
        raw = raw_ref[0, :, 0, :, cols].reshape(rows, HDIM)
        keys = kv_ref[0, 0, 0, :, 0, :, cols].reshape(rows, HDIM)
        values = kv_ref[0, 1, 0, :, 0, :, cols].reshape(rows, HDIM)
        queries = turn(raw, cosine, sine).astype(BF16)
        probs = softmax_rows(queries, keys, bias, scale).astype(BF16)
        query_ref[0, :, 0, :, cols] = queries.reshape(quarter, tok, HDIM)
        out_ref[0, :, 0, :, cols] = product(probs, values).astype(BF16).reshape(quarter, tok, HDIM)


def attend_back_kernel(
    heads, scale, query_ref, kv_ref, grad_ref, cos_ref, sin_ref, bias_ref, dq_ref, dkv_ref
):
    quarter, tok = query_ref.shape[1], query_ref.shape[3]
    rows = quarter * tok
    cosine, sine, bias = cos_ref[...], sin_ref[...], bias_ref[0, 0]
    for head in range(heads):
        cols = slice(head * HDIM, (head + 1) * HDIM)
        queries = query_ref[0, :, 0, :, cols].reshape(rows, HDIM)
        keys = kv_ref[0, 0, 0, :, 0, :, cols].reshape(rows, HDIM)
        values = kv_ref[0, 1, 0, :, 0, :, cols].reshape(rows, HDIM)
        grad = grad_ref[0, :, 0, :, cols].reshape(rows, HDIM)
        probs = softmax_rows(queries, keys, bias, scale)
        prob_grad = product_nt(grad, values)
        centre = jnp.sum(prob_grad * probs, axis=-1, keepdims=True)
        score_grad = (probs * (prob_grad - centre) * scale).astype(BF16)
        query_grad = turn(product(score_grad, keys), cosine, -sine).astype(BF16)
        key_grad = turn(product_tn(score_grad, queries), cosine, -sine).astype(BF16)
        value_grad = product_tn(probs.astype(BF16), grad).astype(BF16)
        dq_ref[0, :, 0, :, cols] = query_grad.reshape(quarter, tok, HDIM)
        dkv_ref[0, 0, 0, :, 0, :, cols] = key_grad.reshape(quarter, tok, HDIM)
        dkv_ref[0, 1, 0, :, 0, :, cols] = value_grad.reshape(quarter, tok, HDIM)


def attention_specs(shape, slices):
    pair, quarter, micro, tok, feats = shape
    part = feats // slices
    rows = quarter * tok
    grid = (pair, micro, slices)
    flat = pl.BlockSpec((1, quarter, 1, tok, part), lambda i, m, s: (i, 0, m, 0, s))
    both = pl.BlockSpec(
        (1, 2, 1, quarter, 1, tok, part), lambda i, m, s: (s, 0, i, 0, m, 0, 0)
    )
    angle = pl.BlockSpec((rows, HDIM // 2), lambda i, m, s: (0, 0))
    bias = pl.BlockSpec((1, 1, rows, rows), lambda i, m, s: (i, m, 0, 0))
    return grid, part, flat, both, angle, bias


def attend(raw, kv, cosine, sine, bias, scale):
    slices = kv.shape[0]
    grid, part, flat, both, angle, bias_spec = attention_specs(raw.shape, slices)
    out = jax.ShapeDtypeStruct(raw.shape, BF16)
    return pl.pallas_call(
        partial(attend_kernel, part // HDIM, scale),
        grid=grid,
        in_specs=[flat, both, angle, angle, bias_spec],
        out_specs=[flat, flat],
        out_shape=[out, out],
        cost_estimate=pl.CostEstimate(
            flops=4 * raw.size * cosine.shape[0],
            bytes_accessed=12 * raw.size,
            transcendentals=raw.size * 2,
        ),
        name="attend",
    )(raw, kv, cosine, sine, bias)


def attend_back(queries, kv, grad, cosine, sine, bias, scale):
    slices = kv.shape[0]
    grid, part, flat, both, angle, bias_spec = attention_specs(queries.shape, slices)
    return pl.pallas_call(
        partial(attend_back_kernel, part // HDIM, scale),
        grid=grid,
        in_specs=[flat, both, flat, angle, angle, bias_spec],
        out_specs=[flat, both],
        out_shape=[
            jax.ShapeDtypeStruct(queries.shape, BF16),
            jax.ShapeDtypeStruct(kv.shape, BF16),
        ],
        cost_estimate=pl.CostEstimate(
            flops=10 * queries.size * cosine.shape[0],
            bytes_accessed=14 * queries.size,
            transcendentals=queries.size * 2,
        ),
        name="attend_back",
    )(queries, kv, grad, cosine, sine, bias)


MESH = pl.DeviceIdType.MESH
ANY = pl.BlockSpec(memory_space=pl.ANY)
VMEM = pl.BlockSpec(memory_space=pltpu.VMEM)
DMA = pltpu.SemaphoreType.DMA


def remote(src, dst, send, recv, target):
    return pltpu.make_async_remote_copy(
        src_ref=src, dst_ref=dst, send_sem=send, recv_sem=recv, device_id=target, device_id_type=MESH
    )


def greet(targets):
    barrier = pltpu.get_barrier_semaphore()
    for target in targets:
        pl.semaphore_signal(barrier, inc=1, device_id=target, device_id_type=MESH)
    pl.semaphore_wait(barrier, len(targets))


def params(number, limit=None):
    return pltpu.CompilerParams(
        collective_id=number, has_side_effects=True, vmem_limit_bytes=limit
    )


def add_into(target, sources, rows):
    step = 1
    while step * 2 <= rows and step * 2 * target.shape[-1] <= 65536 and rows % (step * 2) == 0:
        step *= 2

    def one(index, carry):
        where = pl.ds(pl.multiple_of(index * step, step), step)
        total = sources[0][where].astype(F32)
        for source in sources[1:]:
            total = total + source[where].astype(F32)
        target[where] = total.astype(target.dtype)
        return carry

    lax.fori_loop(0, rows // step, one, 0)


def cube_reduce_kernel(pairs, x_ref, o_ref, half, quarter, got_core, got_side, got_pair, send, recv):
    p = lax.axis_index("pair") if pairs == 2 else 0
    e = lax.axis_index("expert")
    c, y = lax.rem(e, 2), lax.div(e, 2)
    core = {"expert": e + 1 - 2 * c}
    side = {"expert": e + 2 - 4 * y}
    other = {"pair": lax.rem(p + 1, pairs)}
    greet([core, side] + ([other] if pairs == 2 else []))
    rows = x_ref.shape[3]
    shifts = (1, 0) if pairs == 2 else (0,)
    order = [(dx, dy) for dy in (1, 0) for dx in shifts]
    copies = []

    def push(source, place, slot, target):
        copy = remote(source, place, send.at[slot], recv.at[slot], target)
        copy.start()
        copies.append(copy)
        return copy

    first = []
    for slot, (dx, dy) in enumerate(order):
        px, yy = lax.rem(p + dx, pairs), lax.rem(y + dy, 2)
        first.append(push(x_ref.at[px, yy, 1 - c], got_core.at[slot], slot, core))
    base = len(order)
    cut = rows // 2 if pairs == 2 else rows
    upper, lower = pl.ds(0, cut), pl.ds(cut, rows - cut)
    to_side, to_other = {}, {}
    for slot, (dx, dy) in enumerate(order):
        px, yy = lax.rem(p + dx, pairs), lax.rem(y + dy, 2)
        first[slot].wait_recv()
        add_into(half.at[slot], [x_ref.at[px, yy, c], got_core.at[slot]], rows)
        if dy == 1:
            to_side[dx] = push(
                half.at[slot, upper], got_side.at[dx, upper], base + dx, side
            )
        if dx == 1:
            to_other[dy] = push(
                half.at[slot, lower], got_pair.at[dy, lower], base + 2 + dy, other
            )
    own = half.at[order.index((0, 0))]
    if pairs == 2:
        to_side[1].wait_recv()
        add_into(
            quarter.at[upper],
            [half.at[order.index((1, 0)), upper], got_side.at[1, upper]],
            cut,
        )
        to_pair = push(quarter.at[upper], got_pair.at[0, upper], base + 4, other)
        to_other[1].wait_recv()
        add_into(
            quarter.at[lower],
            [half.at[order.index((0, 1)), lower], got_pair.at[1, lower]],
            rows - cut,
        )
        to_flank = push(quarter.at[lower], got_side.at[0, lower], base + 5, side)
        to_side[0].wait_recv()
        to_pair.wait_recv()
        add_into(
            o_ref.at[upper], [own.at[upper], got_side.at[0, upper], got_pair.at[0, upper]], cut
        )
        to_other[0].wait_recv()
        to_flank.wait_recv()
        add_into(
            o_ref.at[lower],
            [own.at[lower], got_side.at[0, lower], got_pair.at[0, lower]],
            rows - cut,
        )
    else:
        to_side[0].wait_recv()
        add_into(o_ref, [own, got_side.at[0]], rows)
    for copy in copies:
        copy.wait_send()


def cube_reduce(value, pairs, number):
    _, rows, cols = value.shape
    value = value.reshape(pairs, 2, 2, rows, cols)
    slots = 2 * pairs
    block = jax.ShapeDtypeStruct((rows, cols), value.dtype)
    return pl.pallas_call(
        partial(cube_reduce_kernel, pairs),
        in_specs=[VMEM],
        out_specs=VMEM,
        out_shape=block,
        scratch_shapes=[
            pltpu.VMEM((slots, rows, cols), value.dtype),
            pltpu.VMEM((rows, cols), value.dtype),
            pltpu.VMEM((slots, rows, cols), value.dtype),
            pltpu.VMEM((2, rows, cols), value.dtype),
            pltpu.VMEM((2, rows, cols), value.dtype),
            DMA((slots + 6,)),
            DMA((slots + 6,)),
        ],
        compiler_params=params(number, 48 * 2**20),
        cost_estimate=pl.CostEstimate(flops=0, bytes_accessed=0, transcendentals=0),
        name="cube_reduce",
    )(value)


def cube_gather_kernel(pairs, x_ref, o_ref, send, recv, local):
    p = lax.axis_index("pair") if pairs == 2 else 0
    e = lax.axis_index("expert")
    c, y = lax.rem(e, 2), lax.div(e, 2)
    core = {"expert": e + 1 - 2 * c}
    side = {"expert": e + 2 - 4 * y}
    other = {"pair": lax.rem(p + 1, pairs)}
    greet([core, side] + ([other] if pairs == 2 else []))
    q, w = lax.rem(p + 1, pairs), 1 - y
    own = o_ref.at[p, y, c]
    keep = pltpu.make_async_copy(x_ref, own, local)
    keep.start()
    copies = []

    def push(slot, source, place, target):
        copy = remote(source, place, send.at[slot], recv.at[slot], target)
        copy.start()
        copies.append(copy)
        return copy

    rows = x_ref.shape[0]
    cut = rows // 2
    upper, lower = pl.ds(0, cut), pl.ds(cut, rows - cut)
    to_side = push(0, x_ref, own, side)
    to_other = push(1, x_ref, own, other) if pairs == 2 else None
    to_core = push(2, x_ref, own, core)
    waits = [to_core]
    if pairs == 2:
        to_other.wait_recv()
        block = o_ref.at[q, y, c]
        far = [push(3, block.at[upper], block.at[upper], side)]
        waits.append(push(4, block, block, core))
    to_side.wait_recv()
    block = o_ref.at[p, w, c]
    if pairs == 2:
        far.append(push(7, block.at[lower], block.at[lower], other))
    waits.append(push(5, block, block, core))
    if pairs == 2:
        for copy in far:
            copy.wait_recv()
        block = o_ref.at[q, w, c]
        waits.append(push(6, block, block, core))
    for copy in waits:
        copy.wait_recv()
    for copy in copies:
        copy.wait_send()
    keep.wait()


def cube_gather(value, pairs, number):
    return pl.pallas_call(
        partial(cube_gather_kernel, pairs),
        in_specs=[VMEM],
        out_specs=VMEM,
        out_shape=jax.ShapeDtypeStruct((pairs, 2, 2) + value.shape, value.dtype),
        scratch_shapes=[DMA((8,)), DMA((8,)), DMA(())],
        compiler_params=params(number, 48 * 2**20),
        cost_estimate=pl.CostEstimate(
            flops=0, bytes_accessed=80 * value.size, transcendentals=0
        ),
        name="cube_gather",
    )(value)


def place_of(index, sizes):
    line, pairs, experts = sizes
    return {
        "line": index // (pairs * experts),
        "pair": (index // experts) % pairs,
        "expert": index % experts,
    }


def small_kernel(sizes, reduce, x_ref, o_ref, got, send, recv):
    line, pairs, experts = sizes
    count = line * pairs * experts
    me = (
        lax.axis_index("line") * (pairs * experts)
        + lax.axis_index("pair") * experts
        + lax.axis_index("expert")
    )
    barrier = pltpu.get_barrier_semaphore()

    def greet_one(offset, carry):
        target = place_of((me + offset) % count, sizes)
        pl.semaphore_signal(barrier, inc=1, device_id=target, device_id_type=MESH)
        return carry

    lax.fori_loop(1, count, greet_one, 0)
    pl.semaphore_wait(barrier, count - 1)

    def copy_to(offset):
        peer = (me + offset) % count
        source = x_ref.at[peer] if reduce else x_ref
        return remote(source, got.at[offset], send.at[offset], recv.at[offset], place_of(peer, sizes))

    def start(offset, carry):
        copy_to(offset).start()
        return carry

    lax.fori_loop(1, count, start, 0)
    got[0] = x_ref[me] if reduce else x_ref[...]

    def finish(offset, carry):
        copy_to(offset).wait()
        return carry

    lax.fori_loop(1, count, finish, 0)
    if reduce:
        o_ref[...] = jnp.sum(got[...], axis=0)
    else:

        def order(offset, carry):
            o_ref[(me - offset + count) % count] = got[offset]
            return carry

        lax.fori_loop(0, count, order, 0)


def small_exchange(value, sizes, reduce, number):
    count = sizes[0] * sizes[1] * sizes[2]
    block = value.shape[1:] if reduce else value.shape
    return pl.pallas_call(
        partial(small_kernel, sizes, reduce),
        in_specs=[VMEM],
        out_specs=VMEM,
        out_shape=jax.ShapeDtypeStruct(block if reduce else (count,) + block, value.dtype),
        scratch_shapes=[pltpu.VMEM((count,) + block, value.dtype), DMA((count,)), DMA((count,))],
        compiler_params=params(number),
        cost_estimate=pl.CostEstimate(flops=0, bytes_accessed=2**24, transcendentals=0),
        name="small_reduce" if reduce else "small_gather",
    )(value)


def ff_kernel(
    a_in, b_in, gate_hbm, up_hbm, down_hbm,
    a_out, b_out, a_save, b_save, inner_save, dgate_save, dup_save,
    a_buf, b_buf, side, hop, extra, w_gate, w_up, w_down, mid, acc,
    send, recv, load, store, local,
):
    z, p, e = lax.axis_index("line"), lax.axis_index("pair"), lax.axis_index("expert")
    line, _, rows, width = a_buf.shape
    experts, size = a_in.shape[0], a_in.shape[1]
    q = 1 - p
    twin = z + 1 - 2 * (z % 2)
    up, down, other, across = {"line": z + 1}, {"line": z - 1}, {"pair": q}, {"line": twin}
    ins, bufs, outs, saves = (a_in, b_in), (a_buf, b_buf), (a_out, b_out), (a_save, b_save)
    high = z // 2
    near = z + high * (line - 1 - 2 * z)

    def order(t):
        j = t + near * (1 - t // 2) * (1 - 2 * t)
        return j + high * (line - 1 - 2 * j)

    weights = [
        pltpu.make_async_copy(src, dst, load.at[i])
        for i, (src, dst) in enumerate(((gate_hbm, w_gate), (up_hbm, w_up), (down_hbm, w_down)))
    ]
    for copy in weights:
        copy.start()

    barrier = pltpu.get_barrier_semaphore()
    for shift in range(1, experts):
        pl.semaphore_signal(
            barrier, inc=1, device_id={"expert": (e + shift) % experts}, device_id_type=MESH
        )
    pl.semaphore_signal(barrier, inc=1, device_id=other, device_id_type=MESH)

    @pl.when(z > 0)
    def _():
        pl.semaphore_signal(barrier, inc=1, device_id=down, device_id_type=MESH)

    @pl.when(z < line - 1)
    def _():
        pl.semaphore_signal(barrier, inc=1, device_id=up, device_id_type=MESH)

    below, above = (z + line - 1) // line, (2 * line - 2 - z) // line
    pl.semaphore_wait(barrier, experts + below + above)

    UP, DOWN, SIDE, SUMUP, SUMDOWN, SUMSIDE = (i * line for i in range(6))
    SUMTWIN, SWAP = 6 * line, 6 * line + 1
    BACK = SWAP + experts
    PART = BACK + experts
    EARLY = PART + experts

    def push(src, dst, kind, use, target):
        return remote(src, dst, send.at[kind, use], recv.at[kind, use], target)

    def to_up(kind, j):
        return push(bufs[kind].at[j, p], bufs[kind].at[j, p], kind, UP + j, up)

    def to_down(kind, j):
        return push(bufs[kind].at[j, p], bufs[kind].at[j, p], kind, DOWN + j, down)

    def to_other(kind, j):
        return push(bufs[kind].at[j, p], bufs[kind].at[j, p], kind, SIDE + j, other)

    def early(kind, shift):
        ref = bufs[kind].at[z, p, piece((e + experts - shift) % experts)]
        return push(ref, ref, kind, EARLY + shift, other)

    def sum_up(kind, j):
        return push(bufs[kind].at[j, p], hop.at[kind, j], kind, SUMUP + j, up)

    def sum_down(kind, j, slot):
        return push(bufs[kind].at[j, p], hop.at[kind, slot], kind, SUMDOWN + j, down)

    def sum_other(kind, j):
        return push(bufs[kind].at[j, q], side.at[kind, j], kind, SUMSIDE + j, other)

    def piece(index):
        return pl.ds(pl.multiple_of(index * size, size), size)

    far_expert = (e + 2) % experts
    queue = (far_expert, far_expert + 1 - 2 * (far_expert % 2), e + 1 - 2 * (e % 2), e)

    def sum_part(i):
        return push(
            b_buf.at[z, q, piece(queue[i])],
            side.at[1, z, piece(queue[i])],
            1,
            PART + i,
            other,
        )

    def sum_twin():
        return push(bufs[1].at[twin, q], extra, 1, SUMTWIN, across)

    def save(kind, j, column):
        return pltpu.make_async_copy(
            bufs[kind].at[j, column], saves[kind].at[j, column], store.at[kind, j, column]
        )

    swaps = []
    for kind in range(2):
        home = bufs[kind].at[z, p, piece(e)]
        keep = pltpu.make_async_copy(ins[kind].at[e], home, local.at[kind])
        keep.start()
        group = []
        for shift in range(1, experts):
            peer = (e + shift) % experts
            copy = push(ins[kind].at[peer], home, kind, SWAP + shift, {"expert": peer})
            copy.start()
            group.append(copy)
        swaps.append((keep, group))

    def spread(t, first=False):
        j = order(t)
        for kind in range(2):
            if first:
                swaps[kind][0].wait()
                early(kind, 0).start()
                for shift in range(experts - 1, 0, -1):
                    swaps[kind][1][shift - 1].wait_recv()
                    early(kind, shift).start()
            else:

                @pl.when(j < z)
                def _():
                    to_up(kind, j).wait_recv()

                @pl.when(j > z)
                def _():
                    to_down(kind, j).wait_recv()

            @pl.when((j <= z) & (z < line - 1))
            def _():
                to_up(kind, j).start()

            @pl.when((j >= z) & (z > 0))
            def _():
                to_down(kind, j).start()

            if not first:
                to_other(kind, j).start()
            save(kind, j, p).start()

    chunk = 512
    steps = width // chunk

    part = 32

    def rows_half(j, column):
        for index in range(2):
            acc[index] = jnp.zeros(acc.shape[1:], F32)

        def one(n, carry):
            where = pl.ds(pl.multiple_of(n * chunk, chunk), chunk)
            left = a_buf[j, column, :, where]
            acc[0] += product_nt(left, w_gate[:, where])
            acc[1] += product_nt(left, w_up[:, where])
            return carry

        lax.fori_loop(0, steps, one, 0)

        def two(i, carry):
            where = pl.ds(pl.multiple_of(i * part, part), part)
            gate = acc[0, where]
            mid[j, column, 0, where] = (gate * jax.nn.sigmoid(gate) * acc[1, where]).astype(BF16)
            return carry

        lax.fori_loop(0, rows // part, two, 0)

    def grads_half(j, column):
        acc[2] = jnp.zeros(acc.shape[1:], F32)

        def one(n, carry):
            where = pl.ds(pl.multiple_of(n * chunk, chunk), chunk)
            acc[2] += product_nt(b_buf[j, column, :, where], w_down[:, where])
            return carry

        lax.fori_loop(0, steps, one, 0)

        def two(i, carry):
            where = pl.ds(pl.multiple_of(i * part, part), part)
            gate, lift, grad = acc[0, where], acc[1, where], acc[2, where]
            sigma = jax.nn.sigmoid(gate)
            mid[j, column, 1, where] = (
                grad * lift * sigma * (1.0 + gate * (1.0 - sigma))
            ).astype(BF16)
            mid[j, column, 2, where] = (grad * gate * sigma).astype(BF16)
            return carry

        lax.fori_loop(0, rows // part, two, 0)

    def out_half(j, column):
        def one(n, carry):
            where = pl.ds(pl.multiple_of(n * chunk, chunk), chunk)
            a_buf[j, column, :, where] = product(mid[j, column, 0], w_down[:, where]).astype(BF16)
            return carry

        lax.fori_loop(0, steps, one, 0)

    def back_half(j, column):
        def one(n, carry):
            where = pl.ds(pl.multiple_of(n * chunk, chunk), chunk)
            b_buf[j, column, :, where] = (
                product(mid[j, column, 1], w_gate[:, where])
                + product(mid[j, column, 2], w_up[:, where])
            ).astype(BF16)
            return carry

        lax.fori_loop(0, steps, one, 0)

    def arrive(kind, j):
        @pl.when(j == z)
        def _():
            for shift in range(experts):
                early(kind, shift).wait_recv()

        @pl.when(j != z)
        def _():
            to_other(kind, j).wait_recv()

        save(kind, j, q).start()

    def emit(t):
        j = order(t)
        sum_other(0, j).start()

        @pl.when((j != twin) & (j != z))
        def _():
            sum_other(1, j).start()

    def step(s, carry):
        @pl.when(s == 0)
        def _():
            spread(0, True)
            for copy in weights:
                copy.wait()

        @pl.when(s == 1)
        def _():
            spread(1)
            spread(2)

        @pl.when(s == 3)
        def _():
            spread(3)

        @pl.when(s == line)
        def _():
            sum_twin().start()

        def half(c, inner_carry):
            t = s - c
            column = p + c * (q - p)

            @pl.when((t >= 0) & (t < line))
            def _():
                j = order(t)

                @pl.when(c == 1)
                def _():
                    arrive(0, j)

                rows_half(j, column)

                @pl.when(c == 1)
                def _():
                    save(0, j, q).wait()
                    out_half(j, q)

                    @pl.when(t == line - 1)
                    def _():
                        sum_other(0, j).start()

                    arrive(1, j)

                grads_half(j, column)

                @pl.when(c == 1)
                def _():
                    save(1, j, q).wait()
                    back_half(j, q)

                    @pl.when(t == line - 1)
                    def _():
                        sum_other(1, j).start()

            return inner_carry

        return lax.fori_loop(0, 2, half, carry)

    lax.fori_loop(0, line + 1, step, 0)

    for t in (2, 1, 0):
        emit(t)

    for copy in (
        pltpu.make_async_copy(mid.at[:, :, 0], inner_save, local.at[2]),
        pltpu.make_async_copy(mid.at[:, :, 1], dgate_save, local.at[3]),
        pltpu.make_async_copy(mid.at[:, :, 2], dup_save, local.at[4]),
    ):
        copy.start()
    sum_twin().wait_recv()
    for i in range(experts):
        part = b_buf.at[z, q, piece(queue[i])]
        add_into(part, [part, extra.at[piece(queue[i])]], size)
        sum_part(i).start()

    def back(kind):
        own = pltpu.make_async_copy(
            bufs[kind].at[z, p, piece(e)], outs[kind].at[e], local.at[kind]
        )
        return [own] + [
            push(
                bufs[kind].at[z, p, piece((e + shift) % experts)],
                outs[kind].at[e],
                kind,
                BACK + shift,
                {"expert": (e + shift) % experts},
            )
            for shift in range(1, experts)
        ]

    def back_part(i):
        source = b_buf.at[z, p, piece(queue[i])]
        if i == experts - 1:
            return pltpu.make_async_copy(source, b_out.at[e], local.at[1])
        return push(source, b_out.at[e], 1, BACK + 1 + i, {"expert": queue[i]})

    def fold(s, carry):
        t = line - 1 - s
        j = order(t)
        for kind in range(2):
            save(kind, j, p).wait()

            @pl.when((j <= z) & (z < line - 1))
            def _():
                to_up(kind, j).wait_send()

            @pl.when((j >= z) & (z > 0))
            def _():
                to_down(kind, j).wait_send()

            @pl.when(j == z)
            def _():
                for shift in range(experts):
                    early(kind, shift).wait_send()

            @pl.when(j != z)
            def _():
                to_other(kind, j).wait_send()

        for kind in range(2):
            (out_half, back_half)[kind](j, p)
            mine = bufs[kind].at[j, p]
            if kind == 0:
                sum_other(kind, j).wait_recv()
                add_into(mine, [mine, side.at[kind, j]], rows)
            else:

                @pl.when((j != twin) & (j != z))
                def _():
                    sum_other(kind, j).wait_recv()
                    add_into(mine, [mine, side.at[kind, j]], rows)

            @pl.when((j >= z) & (z > 0))
            def _():
                sum_up(kind, j).wait_recv()
                add_into(mine, [mine, hop.at[kind, j]], rows)

            @pl.when((j < z) & (z < line - 1))
            def _():
                sum_down(kind, j, j).wait_recv()
                add_into(mine, [mine, hop.at[kind, j]], rows)

            @pl.when((j == z) & (z < line - 1))
            def _():
                sum_down(kind, j, line).wait_recv()
                add_into(mine, [mine, hop.at[kind, line]], rows)

            @pl.when(j == z)
            def _():
                if kind == 0:
                    for copy in back(0):
                        copy.start()
                else:
                    for i in range(experts):
                        part = b_buf.at[z, p, piece(queue[i])]
                        sum_part(i).wait_recv()
                        add_into(part, [part, side.at[1, z, piece(queue[i])]], size)
                        back_part(i).start()

            @pl.when(j > z)
            def _():
                sum_up(kind, j).start()

            @pl.when((j < z) & (j != z - 1))
            def _():
                sum_down(kind, j, j).start()

            @pl.when((j < z) & (j == z - 1))
            def _():
                sum_down(kind, j, line).start()

        return carry

    lax.fori_loop(0, line, fold, 0)

    for copy in back(0):
        copy.wait()
    for i in range(experts):
        back_part(i).wait()

    def drain(j, carry):
        for kind in range(2):
            if kind == 0:
                sum_other(kind, j).wait_send()
            else:

                @pl.when((j != twin) & (j != z))
                def _():
                    sum_other(kind, j).wait_send()

            @pl.when(j > z)
            def _():
                sum_up(kind, j).wait_send()

            @pl.when(j < z)
            def _():
                sum_down(kind, j, j).wait_send()

        return carry

    lax.fori_loop(0, line, drain, 0)
    sum_twin().wait_send()
    for i in range(experts):
        sum_part(i).wait_send()
    for copy in (
        pltpu.make_async_copy(mid.at[:, :, 0], inner_save, local.at[2]),
        pltpu.make_async_copy(mid.at[:, :, 1], dgate_save, local.at[3]),
        pltpu.make_async_copy(mid.at[:, :, 2], dup_save, local.at[4]),
    ):
        copy.wait()
    for keep, group in swaps:
        for copy in group:
            copy.wait_send()


def feed_forward(first, second, w_gate, w_up, w_down, line, pairs, number):
    experts, size, width = first.shape
    hidden = w_gate.shape[0]
    rows = experts * size
    blocks = (line, pairs, rows)
    back = jax.ShapeDtypeStruct(first.shape, BF16)
    wide = jax.ShapeDtypeStruct(blocks + (width,), BF16)
    thin = jax.ShapeDtypeStruct(blocks + (hidden,), BF16)
    uses = 6 * line + 2 + 4 * experts
    total = line * pairs * rows
    return pl.pallas_call(
        ff_kernel,
        in_specs=[ANY] * 5,
        out_specs=[ANY] * 7,
        out_shape=[back, back, wide, wide, thin, thin, thin],
        scratch_shapes=[
            pltpu.VMEM(blocks + (width,), BF16),
            pltpu.VMEM(blocks + (width,), BF16),
            pltpu.VMEM((2, line, rows, width), BF16),
            pltpu.VMEM((2, line + 1, rows, width), BF16),
            pltpu.VMEM((rows, width), BF16),
            pltpu.VMEM((hidden, width), BF16),
            pltpu.VMEM((hidden, width), BF16),
            pltpu.VMEM((hidden, width), BF16),
            pltpu.VMEM((line, pairs, 3, rows, hidden), BF16),
            pltpu.VMEM((3, rows, hidden), F32),
            DMA((2, uses)),
            DMA((2, uses)),
            DMA((3,)),
            DMA((2, line, pairs)),
            DMA((5,)),
        ],
        compiler_params=params(number, 63 * 2**20),
        cost_estimate=pl.CostEstimate(
            flops=12 * total * hidden * width,
            bytes_accessed=12 * total * width,
            transcendentals=total * hidden,
        ),
        name="feed_forward",
    )(first, second, w_gate, w_up, w_down)


def last_kernel(
    sizes, x_ref, q_ref, g_hbm, o_ref, w_ref, key_ref, value_ref,
    got, side, g_ref, k_ref, hop, send, recv, peer_send, peer_recv, local,
):
    line, pairs, experts = sizes
    trees = pairs * experts
    count = line * trees
    z, p, e = lax.axis_index("line"), lax.axis_index("pair"), lax.axis_index("expert")
    mine = p * experts + e
    me = z * trees + mine
    span, piece = g_ref.shape[1], k_ref.shape[1]
    up, down = {"line": z + 1}, {"line": z - 1}
    high = z // 2
    near = z + high * (line - 1 - 2 * z)

    def order(t):
        j = t + near * (1 - t // 2) * (1 - 2 * t)
        return j + high * (line - 1 - 2 * j)

    fetch = pltpu.make_async_copy(g_hbm, g_ref, local)
    fetch.start()
    barrier = pltpu.get_barrier_semaphore()

    def greet_one(offset, carry):
        target = place_of((me + offset) % count, sizes)
        pl.semaphore_signal(barrier, inc=1, device_id=target, device_id_type=MESH)
        return carry

    lax.fori_loop(1, count, greet_one, 0)
    pl.semaphore_wait(barrier, count - 1)
    UP, DOWN, SWAP, PAIR = 0, line, 2 * line, 2 * line + trees

    def sum_up(j):
        return remote(g_ref.at[j], hop.at[j], send.at[UP + j], recv.at[UP + j], up)

    def sum_down(j, slot):
        return remote(g_ref.at[j], hop.at[slot], send.at[DOWN + j], recv.at[DOWN + j], down)

    def fold(t):
        j = order(t)
        own = g_ref.at[j]

        @pl.when((j >= z) & (z > 0))
        def _():
            sum_up(j).wait_recv()
            add_into(own, [own, hop.at[j]], span)

        @pl.when((j < z) & (z < line - 1))
        def _():
            sum_down(j, j).wait_recv()
            add_into(own, [own, hop.at[j]], span)

        @pl.when((j == z) & (z < line - 1))
        def _():
            sum_down(j, line).wait_recv()
            add_into(own, [own, hop.at[line]], span)

        @pl.when(j > z)
        def _():
            sum_up(j).start()

        @pl.when((j < z) & (j != z - 1))
        def _():
            sum_down(j, j).start()

        @pl.when((j < z) & (j == z - 1))
        def _():
            sum_down(j, line).start()

    fetch.wait()
    fold(3)
    swap = remote(q_ref.at[1 - p], side, send.at[PAIR], recv.at[PAIR], {"pair": 1 - p})
    swap.start()

    def copy_to(offset):
        peer = (me + offset) % count
        return remote(
            x_ref.at[peer],
            got.at[offset],
            peer_send.at[offset],
            peer_recv.at[offset],
            place_of(peer, sizes),
        )

    def start(offset, carry):
        copy_to(offset).start()
        return carry

    lax.fori_loop(1, count, start, 0)
    got[0] = x_ref[me]
    fold(2)
    part = q_ref.shape[2] // line

    def lay(block, source):
        for index in range(line):
            column = pl.multiple_of((index * pairs + source) * part, part)
            w_ref[:, pl.ds(column, part)] = block[:, index * part : (index + 1) * part].astype(F32)

    lay(q_ref.at[p], p)
    fold(1)
    swap.wait_recv()
    lay(side, 1 - p)

    def finish(offset, carry):
        copy_to(offset).wait()
        return carry

    lax.fori_loop(1, count, finish, 0)
    o_ref[...] = jnp.sum(got[...], axis=0)
    fold(0)

    def share_of(index):
        return g_ref.at[z, pl.ds(pl.multiple_of(index * piece, piece), piece)]

    keep = pltpu.make_async_copy(share_of(mine), k_ref.at[mine], local)
    keep.start()
    swaps = []
    for shift in range(1, trees):
        peer = (mine + shift) % trees
        copy = remote(
            share_of(peer),
            k_ref.at[mine],
            send.at[SWAP + shift],
            recv.at[SWAP + shift],
            {"pair": peer // experts, "expert": peer % experts},
        )
        copy.start()
        swaps.append(copy)
    keep.wait()
    for copy in swaps:
        copy.wait()
    share = k_ref.shape[2] // 2
    for source in range(trees):
        column = ((source % experts) * pairs + source // experts) * share
        for index, target in enumerate((key_ref, value_ref)):
            target[:, column : column + share] = k_ref[
                source, :, index * share : (index + 1) * share
            ].astype(F32)
    swap.wait_send()

    def drain(j, carry):
        @pl.when(j > z)
        def _():
            sum_up(j).wait_send()

        @pl.when(j < z)
        def _():
            sum_down(j, j).wait_send()

        return carry

    lax.fori_loop(0, line, drain, 0)


def last_exchange(sums, query, grads, sizes, number):
    line, pairs, experts = sizes
    trees = pairs * experts
    count, block = sums.shape[0], sums.shape[1:]
    _, rows, cols = query.shape
    span, thin = grads.shape[0] // line, grads.shape[1]
    uses = 2 * line + trees + 1
    wide = jax.ShapeDtypeStruct((span // trees, trees * thin // 2), F32)
    return pl.pallas_call(
        partial(last_kernel, sizes),
        in_specs=[VMEM, VMEM, ANY],
        out_specs=[VMEM] * 4,
        out_shape=[
            jax.ShapeDtypeStruct(block, F32),
            jax.ShapeDtypeStruct((rows, pairs * cols), F32),
            wide,
            wide,
        ],
        scratch_shapes=[
            pltpu.VMEM((count,) + block, F32),
            pltpu.VMEM((rows, cols), BF16),
            pltpu.VMEM((line, span, thin), BF16),
            pltpu.VMEM((trees, span // trees, thin), BF16),
            pltpu.VMEM((line + 1, span, thin), BF16),
            DMA((uses,)),
            DMA((uses,)),
            DMA((count,)),
            DMA((count,)),
            DMA(()),
        ],
        compiler_params=params(number, 48 * 2**20),
        cost_estimate=pl.CostEstimate(flops=0, bytes_accessed=0, transcendentals=0),
        name="last_exchange",
    )(sums, query, grads.reshape(line, span, thin))


def start_all_kernel(
    sizes, tok_ref, wq_ref, wk_ref, wv_ref, small_ref, int_ref,
    tok_out, q_out, kv_out, small_out, int_out,
    q_cut, kv_cut, send, recv, peer_send, peer_recv, local,
):
    line, pairs, experts = sizes
    z, p, e = lax.axis_index("line"), lax.axis_index("pair"), lax.axis_index("expert")
    c, y = e % 2, e // 2
    core, side = {"expert": e + 1 - 2 * c}, {"expert": e + 2 - 4 * y}
    other = {"pair": 1 - p}
    trees = pairs * experts
    count = line * trees
    mine = p * experts + e
    me = z * trees + mine
    barrier = pltpu.get_barrier_semaphore()

    def greet_one(offset, carry):
        target = place_of((me + offset) % count, sizes)
        pl.semaphore_signal(barrier, inc=1, device_id=target, device_id_type=MESH)
        return carry

    lax.fori_loop(1, count, greet_one, 0)
    part = wq_ref.shape[1] // (line * pairs)
    sub = line // experts
    for q in range(pairs):
        for d in range(experts):
            for index, ref in enumerate((wk_ref, wv_ref)):
                for h in range(sub):
                    column = ((d * sub + h) * pairs + q) * part
                    place = (index * sub + h) * part
                    kv_cut[q * experts + d, :, place : place + part] = ref[
                        :, column : column + part
                    ]
    for q in range(pairs):
        for index in range(line):
            column = (index * pairs + q) * part
            q_cut[q, :, index * part : (index + 1) * part] = wq_ref[:, column : column + part]
    pl.semaphore_wait(barrier, count - 1)

    copies, TOK, QSWAP, INTS, KV = [], 0, 7, 8, 9
    WALK = KV + trees

    def push(slot, source, place, target):
        copy = remote(source, place, send.at[slot], recv.at[slot], target)
        copy.start()
        copies.append(copy)
        return copy

    size = kv_cut.shape[1]
    kv_home = kv_out.at[z, pl.ds(pl.multiple_of(mine * size, size), size)]
    pieces = []
    for shift in range(1, trees):
        peer = (mine + shift) % trees
        pieces.append(
            push(
                KV + shift,
                kv_cut.at[peer],
                kv_home,
                {"pair": peer // experts, "expert": peer % experts},
            )
        )
    rows = q_cut.shape[1]
    q_home = q_out.at[z, pl.ds(pl.multiple_of(p * rows, rows), rows)]
    q_swap = push(QSWAP, q_cut.at[1 - p], q_home, other)
    keeps = [
        pltpu.make_async_copy(q_cut.at[p], q_home, local.at[0]),
        pltpu.make_async_copy(kv_cut.at[mine], kv_home, local.at[1]),
        pltpu.make_async_copy(tok_ref, tok_out.at[p, y, c], local.at[2]),
        pltpu.make_async_copy(small_ref, small_out.at[me], local.at[3]),
        pltpu.make_async_copy(int_ref, int_out.at[p], local.at[4]),
    ]
    for copy in keeps:
        copy.start()
    def walker(block, base):
        def to_up(j, d):
            ref = block(j)
            return remote(ref, ref, send.at[base + d], recv.at[base + d], {"line": z + 1})

        def to_down(j, d):
            ref, at = block(j), base + line + d
            return remote(ref, ref, send.at[at], recv.at[at], {"line": z - 1})

        return to_up, to_down

    def q_rows(member):
        return lambda j: q_out.at[j, pl.ds(pl.multiple_of(member * rows, rows), rows)]

    stride = 2 * line + 2
    walkers = [
        walker(q_rows(p), WALK),
        walker(lambda j: kv_out.at[j], WALK + stride),
        walker(q_rows(1 - p), WALK + 2 * stride),
    ]

    def begin(which):
        to_up, to_down = walkers[which]

        @pl.when(z < line - 1)
        def _():
            to_up(z, 1).start()

        @pl.when(z > 0)
        def _():
            to_down(z, 1).start()

    keeps[0].wait()
    begin(0)
    own = tok_out.at[p, y, c]
    to_side = push(TOK, tok_ref, own, side)
    to_other = push(TOK + 1, tok_ref, own, other)
    waits = [push(TOK + 2, tok_ref, own, core), push(INTS, int_ref, int_out.at[p], other)]

    def small_to(offset):
        return remote(
            small_ref,
            small_out.at[me],
            peer_send.at[offset],
            peer_recv.at[offset],
            place_of((me + offset) % count, sizes),
        )

    def small_start(offset, carry):
        small_to(offset).start()
        return carry

    lax.fori_loop(1, count, small_start, 0)

    keeps[1].wait()
    for copy in pieces:
        copy.wait_recv()
    begin(1)
    q_swap.wait_recv()
    begin(2)
    to_other.wait_recv()
    block = tok_out.at[1 - p, y, c]
    far = push(TOK + 3, block, block, side)
    waits.append(push(TOK + 4, block, block, core))
    to_side.wait_recv()
    block = tok_out.at[p, 1 - y, c]
    waits.append(push(TOK + 5, block, block, core))
    far.wait_recv()
    block = tok_out.at[1 - p, 1 - y, c]
    waits.append(push(TOK + 6, block, block, core))

    for d in range(1, line):
        for to_up, to_down in walkers:

            @pl.when(z - d >= 0)
            def _():
                to_up(z - d, d).wait_recv()

                @pl.when(z < line - 1)
                def _():
                    to_up(z - d, d + 1).start()

            @pl.when(z + d < line)
            def _():
                to_down(z + d, d).wait_recv()

                @pl.when(z > 0)
                def _():
                    to_down(z + d, d + 1).start()

    for d in range(1, line):
        for to_up, to_down in walkers:

            @pl.when((z - d + 1 >= 0) & (z < line - 1))
            def _():
                to_up(z - d + 1, d).wait_send()

            @pl.when((z + d - 1 < line) & (z > 0))
            def _():
                to_down(z + d - 1, d).wait_send()

    for copy in waits:
        copy.wait_recv()
    for copy in copies:
        copy.wait_send()
    for copy in keeps[2:]:
        copy.wait()

    def small_finish(offset, carry):
        small_to(offset).wait()
        return carry

    lax.fori_loop(1, count, small_finish, 0)


def start_all(tokens, w_query, w_key, w_value, small, integers, sizes, number):
    line, pairs, experts = sizes
    trees = pairs * experts
    count = line * trees
    rows, width = w_query.shape
    size = w_key.shape[0]
    feats = width // pairs
    thin = 2 * feats // experts
    uses = 9 + trees + 6 * line + 6
    return pl.pallas_call(
        partial(start_all_kernel, sizes),
        in_specs=[VMEM] * 6,
        out_specs=[VMEM] * 5,
        out_shape=[
            jax.ShapeDtypeStruct((pairs, 2, 2) + tokens.shape, BF16),
            jax.ShapeDtypeStruct((line, pairs * rows, feats), BF16),
            jax.ShapeDtypeStruct((line, trees * size, thin), BF16),
            jax.ShapeDtypeStruct((count,) + small.shape, BF16),
            jax.ShapeDtypeStruct((pairs,) + integers.shape, jnp.int32),
        ],
        scratch_shapes=[
            pltpu.VMEM((pairs, rows, feats), BF16),
            pltpu.VMEM((trees, size, thin), BF16),
            DMA((uses,)),
            DMA((uses,)),
            DMA((count,)),
            DMA((count,)),
            DMA((5,)),
        ],
        compiler_params=params(number, 48 * 2**20),
        name="start_all",
    )(tokens, w_query, w_key, w_value, small, integers)


def input_kernel(dq_ref, wq_ref, kv_ref, wkv_ref, dl_ref, router_ref, o_ref):
    piece = kv_ref.shape[2]
    total = product_nt(dq_ref[...], wq_ref[...])
    total = total + product_nt(kv_ref[0], wkv_ref[:, :piece])
    total = total + product_nt(kv_ref[1], wkv_ref[:, piece:])
    for expert in range(router_ref.shape[0]):
        total = total + dl_ref[:, expert : expert + 1] * router_ref[expert : expert + 1, :]
    o_ref[...] = total.astype(BF16)


def input_gradient(query_pre, query_weight, kv_sum, kv_weight, logit_grad, router):
    rows, feats = query_pre.shape
    width = query_weight.shape[0]
    piece = kv_sum.shape[2]
    experts = router.shape[0]
    block, lanes = min(512, rows), 512
    return pl.pallas_call(
        input_kernel,
        grid=(width // lanes, rows // block),
        in_specs=[
            pl.BlockSpec((block, feats), lambda n, i: (i, 0)),
            pl.BlockSpec((lanes, feats), lambda n, i: (n, 0)),
            pl.BlockSpec((2, block, piece), lambda n, i: (0, i, 0)),
            pl.BlockSpec((lanes, 2 * piece), lambda n, i: (n, 0)),
            pl.BlockSpec((block, experts), lambda n, i: (i, 0)),
            pl.BlockSpec((experts, lanes), lambda n, i: (0, n)),
        ],
        out_specs=pl.BlockSpec((block, lanes), lambda n, i: (i, n)),
        out_shape=jax.ShapeDtypeStruct((rows, width), BF16),
        compiler_params=pltpu.CompilerParams(vmem_limit_bytes=40 * 2**20),
        cost_estimate=pl.CostEstimate(
            flops=2 * rows * width * (feats + 2 * piece), bytes_accessed=6 * rows * width, transcendentals=0
        ),
        name="input_gradient",
    )(query_pre, query_weight, kv_sum, kv_weight, logit_grad, router)


def project_kernel(micro, x_ref, w_ref, gain_ref, router_ref, cos_ref, sin_ref, n_ref, kv_ref, l_ref):
    x = x_ref[...].astype(F32)
    scale = lax.rsqrt(jnp.mean(x * x, axis=-1, keepdims=True) + EPSILON)
    normed = (x * scale * gain_ref[...]).astype(BF16)
    n_ref[...] = normed
    l_ref[...] = product_nt(normed, router_ref[...])
    raw = product(normed, w_ref[...])
    piece = kv_ref.shape[2]
    spread = lambda ref: jnp.concatenate(
        [ref[i] for i in range(ref.shape[0]) for _ in range(micro)], axis=0
    )
    cosine, sine = spread(cos_ref), spread(sin_ref)
    for head in range(piece // HDIM):
        cols = slice(head * HDIM, (head + 1) * HDIM)
        kv_ref[0, :, cols] = turn(raw[:, cols], cosine, sine).astype(BF16)
    kv_ref[1] = raw[:, piece:].astype(BF16)


def project(tokens, weight, gain, router, cosine, sine, micro):
    rows, width = tokens.shape
    piece = weight.shape[1] // 2
    experts, tok, half = cosine.shape
    block = 2 * micro * tok
    loops = experts // 2
    return pl.pallas_call(
        partial(project_kernel, micro),
        grid=(rows // block,),
        in_specs=[
            pl.BlockSpec((block, width), lambda i: (i, 0)),
            pl.BlockSpec(weight.shape, lambda i: (0, 0)),
            pl.BlockSpec((1, width), lambda i: (0, 0)),
            pl.BlockSpec(router.shape, lambda i: (0, 0)),
            pl.BlockSpec((2, tok, half), lambda i: (i % loops, 0, 0)),
            pl.BlockSpec((2, tok, half), lambda i: (i % loops, 0, 0)),
        ],
        out_specs=[
            pl.BlockSpec((block, width), lambda i: (i, 0)),
            pl.BlockSpec((2, block, piece), lambda i: (0, i, 0)),
            pl.BlockSpec((block, experts), lambda i: (i, 0)),
        ],
        out_shape=[
            jax.ShapeDtypeStruct((rows, width), BF16),
            jax.ShapeDtypeStruct((2, rows, piece), BF16),
            jax.ShapeDtypeStruct((rows, experts), F32),
        ],
        compiler_params=pltpu.CompilerParams(vmem_limit_bytes=40 * 2**20),
        cost_estimate=pl.CostEstimate(
            flops=2 * rows * width * weight.shape[1], bytes_accessed=5 * rows * width, transcendentals=0
        ),
        name="project",
    )(tokens, weight, gain, router, cosine, sine)


def gather(value, axes, axis=0):
    return lax.all_gather(value, axes, axis=axis, tiled=True)


def scatter(value, axes, axis=0):
    return lax.psum_scatter(value, axes, scatter_dimension=axis, tiled=True)


def swap(value, axes, split=0, concat=0):
    return lax.all_to_all(value, axes, split_axis=split, concat_axis=concat, tiled=True)


DP = ("line", "pair")
ALL = ("line", "pair", "expert")
TREES = ("pair", "expert")


def body(
    tokens,
    w_query,
    w_out,
    w_key,
    w_value,
    gain_attn,
    router_attn,
    gain_mlp,
    router_mlp,
    w_gate,
    w_up,
    w_down,
    attn_route,
    mlp_route,
    fill_order,
    parents,
    cotangent,
):
    experts = lax.axis_size("expert")
    pair = lax.axis_size("pair")
    line = lax.axis_size("line")
    position = lax.axis_index("expert")
    micro, _, tok, width = tokens.shape
    tree = experts * tok
    rows = pair * experts * micro * tok
    heads_total = w_query.shape[2]
    part = heads_total // (line * pair)
    feats = heads_total // pair
    piece = feats // experts
    own_in = w_query.shape[1]
    own_kv = w_key.shape[0]
    capacity = tok * mlp_route.shape[3] // experts
    scale = 1.0 / math.sqrt(HDIM)

    places, segment, depth = tree_layout(tree // 16, tree)
    half = HDIM // 2
    rates = 10000.0 ** (-jnp.arange(half, dtype=F32) / half)
    angle = depth.astype(F32)[:, None] * rates[None, :]
    cosine, sine = jnp.cos(angle), jnp.sin(angle)

    sizes = (line, pair, experts)
    walk = line == 4 and pair == 2 and experts == 4
    own_tokens = tokens.reshape(micro * tok, width)
    small = jnp.concatenate(
        [gain_attn[None], gain_mlp[None], router_attn.T, router_mlp.T], axis=0
    )
    integers = jnp.concatenate([attn_route[:, 0].reshape(micro, -1), parents[:, 0]], axis=1)
    if walk:
        flat = integers.reshape(-1)
        flat = jnp.pad(flat, (0, -flat.shape[0] % 1024)).reshape(-1, 128)
        tree_tokens, query_weight, kv_weight, small, flat = start_all(
            own_tokens, w_query[0], w_key, w_value, small, flat, sizes, 1
        )
        query_weight = query_weight.reshape(width, feats)
        kv_weight = kv_weight.reshape(width, 2 * piece)
        integers = flat.reshape(pair, -1)[:, : integers.size].reshape((pair,) + integers.shape)
    else:
        query_mine = w_query[0].reshape(own_in, line, pair, part)
        query_mine = jnp.transpose(query_mine, (2, 0, 1, 3)).reshape(pair, own_in, feats)
        if pair == 2:
            query_mine = swap(query_mine, "pair")
            integers = lax.all_gather(integers, "pair", axis=0)
        else:
            integers = integers[None]
        query_weight = gather(query_mine.reshape(pair * own_in, feats), "line")
        kv_mine = jnp.stack([w_key, w_value], axis=1).reshape(
            own_kv, 2, experts, line // experts, pair, part
        )
        kv_mine = jnp.transpose(kv_mine, (4, 2, 0, 1, 3, 5)).reshape(
            pair * experts, own_kv, 2 * piece
        )
        tree_tokens = cube_gather(own_tokens, pair, 1)
        small = small_exchange(small, sizes, False, 2)
        kv_mine = swap(kv_mine, TREES).reshape(pair * experts * own_kv, 2 * piece)
        kv_weight = gather(kv_mine, "line")
    out_mine, small = lax.optimization_barrier((w_out[0], small))
    out_weight = gather(out_mine, "line")

    small = jnp.transpose(small, (1, 0, 2)).reshape(-1, width)
    first_gain = small[0].astype(F32)
    second_gain = small[1].astype(F32)
    first_router = small[2 : 2 + experts]
    second_router = small[2 + experts : 2 + 2 * experts]

    residual = own_tokens.astype(F32)
    _, first_pull = jax.vjp(rms_scaled, residual, first_gain)
    table_shape = (experts, tok, half)
    tree_input, kv, first_logits = project(
        tree_tokens.reshape(rows, width),
        kv_weight,
        first_gain[None],
        first_router,
        cosine.reshape(table_shape),
        sine.reshape(table_shape),
        micro,
    )

    routes = integers[..., : tree * 2].reshape(pair, micro, experts, tok, 2)
    routes = jnp.transpose(routes, (0, 2, 1, 3, 4)).reshape(rows, 2)
    family = integers[..., tree * 2 :]
    bias = jax.vmap(jax.vmap(lambda parent: score_bias(parent, segment, places)))(family)

    kv = cube_gather(kv.reshape(2 * rows, piece), 1, 3)
    shape = (pair, experts, micro, tok, feats)
    kv = kv.reshape(experts, 2, pair, experts, micro, tok, piece)

    first_gates, first_gate_pull = jax.vjp(partial(mixture_gates, routes), first_logits)
    column = (jnp.arange(experts, dtype=jnp.int32) == position).astype(F32)
    own_gate = jnp.sum(first_gates * column[None, :], axis=1)

    raw = product(tree_input, query_weight)
    queries, heads_out = attend(raw.reshape(shape), kv, cosine, sine, bias, scale)
    heads_flat = heads_out.reshape(rows, feats)
    projected = product(heads_flat, out_weight)
    gated = (own_gate[:, None] * projected).astype(BF16)
    projected = projected.astype(BF16)
    attention = cube_reduce(gated.reshape(pair * experts, micro * tok, width), pair, 4).astype(F32)

    middle = residual + attention
    second_normed, second_pull = jax.vjp(rms_scaled, middle, second_gain)
    second_normed = second_normed.astype(BF16)
    picked = mlp_route[:, 0].reshape(micro * tok, 2)
    second_gates, second_gate_pull = jax.vjp(
        partial(mixture_gates, picked), product_nt(second_normed, second_router)
    )
    table = jax.vmap(partial(slot_table, experts=experts, capacity=capacity))(
        mlp_route[:, 0], fill_order[:, 0]
    )
    table_low = table.astype(BF16)
    grouped = second_normed.reshape(micro, tok, width)
    outgoing = jnp.einsum("mect,mtd->emcd", table_low, grouped, preferred_element_type=F32)
    top_grad = cotangent.reshape(micro, tok, width)
    slot_values = jnp.einsum("mect,mtd->emcd", table_low, top_grad, preferred_element_type=F32)
    slot_gates = jnp.einsum(
        "mect,mte->emc", table, second_gates.reshape(micro, tok, experts), precision=HIGHEST
    )
    slot_grad = (slot_gates[..., None] * slot_values).astype(BF16)
    slots = experts * micro * capacity
    outgoing = outgoing.astype(BF16).reshape(experts, micro * capacity, width)
    slot_grad = slot_grad.reshape(experts, micro * capacity, width)
    gate_weight, up_weight, down_weight = w_gate[0], w_up[0], w_down[0]
    if walk:
        returned, came_back, arrived, result_grad, inner, gate_grad, up_grad = feed_forward(
            outgoing, slot_grad, gate_weight, up_weight, down_weight, line, pair, 5
        )
        arrived, result_grad, inner, gate_grad, up_grad = (
            value.reshape(-1, value.shape[-1])
            for value in (arrived, result_grad, inner, gate_grad, up_grad)
        )
    else:
        arrived = gather(swap(outgoing, "expert").reshape(slots, width), DP)
        result_grad = gather(swap(slot_grad, "expert").reshape(slots, width), DP)
        gate_pre = product_nt(arrived, gate_weight)
        up_pre = product_nt(arrived, up_weight)
        sigma = jax.nn.sigmoid(gate_pre)
        inner = (gate_pre * sigma * up_pre).astype(BF16)
        returned = product(inner, down_weight).astype(BF16)
        inner_grad = product_nt(result_grad, down_weight)
        gate_grad = (inner_grad * up_pre * sigma * (1.0 + gate_pre * (1.0 - sigma))).astype(BF16)
        up_grad = (inner_grad * gate_pre * sigma).astype(BF16)
        came_back = (product(gate_grad, gate_weight) + product(up_grad, up_weight)).astype(BF16)
        back = (experts, micro * capacity, width)
        returned = swap(scatter(returned, DP).reshape(back), "expert")
        came_back = swap(scatter(came_back, DP).reshape(back), "expert")
    returned = returned.reshape(experts, micro, capacity, width)
    came_back = came_back.reshape(experts, micro, capacity, width)
    spread = jnp.einsum("mect,emcd->emtd", table_low, returned, preferred_element_type=F32)
    spread = spread.reshape(experts, micro * tok, width)
    mixed = jnp.sum(jnp.transpose(second_gates)[:, :, None] * spread, axis=0)
    layer_out = (middle + mixed).astype(BF16)
    dz = top_grad.reshape(micro * tok, width).astype(F32)
    second_gate_grad = jnp.transpose(jnp.sum(spread * dz[None], axis=-1))
    (second_logit_grad,) = second_gate_pull(second_gate_grad)
    hn_grad = jnp.einsum("mect,emcd->mtd", table_low, came_back, preferred_element_type=F32)
    hn_grad = hn_grad.reshape(micro * tok, width)
    second_router_wide = second_router.astype(F32)
    for expert in range(experts):
        hn_grad = hn_grad + second_logit_grad[:, expert : expert + 1] * second_router_wide[expert]
    grad_router_second = split_product(second_logit_grad, second_normed)
    middle_grad, grad_gain_second = second_pull(hn_grad)
    middle_grad = middle_grad + dz

    mix_grad = cube_gather(middle_grad.astype(BF16), pair, 7).reshape(rows, width).astype(F32)
    own_gate_grad = jnp.sum(mix_grad * projected.astype(F32), axis=-1)
    projected_grad = (own_gate[:, None] * mix_grad).astype(BF16)
    grad_output = product_tn(heads_flat, projected_grad).astype(BF16)
    grad_output, projected_grad = lax.optimization_barrier((grad_output, projected_grad))
    grad_output = scatter(grad_output, "line")
    heads_grad = product_nt(projected_grad, out_weight).astype(BF16).reshape(shape)
    query_pre, kv_pre = attend_back(queries, kv, heads_grad, cosine, sine, bias, scale)
    query_pre = query_pre.reshape(rows, feats)
    grad_query = product_tn(tree_input, query_pre).astype(BF16)
    grad_query, kv_pre = lax.optimization_barrier((grad_query, kv_pre))
    kv_sum = cube_reduce(kv_pre.reshape(experts, 2 * rows, piece), 1, 8)
    grad_query, grad_output, kv_sum = lax.optimization_barrier((grad_query, grad_output, kv_sum))
    (first_logit_grad,) = first_gate_pull(own_gate_grad[:, None] * column[None, :])
    kv_sum = kv_sum.reshape(2, rows, piece)
    grad_kv = jnp.concatenate(
        [product_tn(tree_input, kv_sum[0]), product_tn(tree_input, kv_sum[1])], axis=1
    ).astype(BF16)
    input_term = input_gradient(
        query_pre, query_weight, kv_sum, kv_weight, first_logit_grad, first_router.astype(F32)
    ).reshape(pair * experts, micro * tok, width)
    normed_grad = cube_reduce(input_term, pair, 9)
    if not walk:
        grad_kv = scatter(grad_kv, "line")
        grad_kv = swap(grad_kv.reshape(pair * experts, own_kv, 2 * piece), TREES)
        grad_kv = grad_kv.reshape(pair, experts, own_kv, 2, line // experts, part)
        grad_kv = jnp.transpose(grad_kv, (2, 3, 1, 4, 0, 5)).reshape(own_kv, 2, heads_total)
        grad_key, grad_value = grad_kv[:, 0].astype(F32), grad_kv[:, 1].astype(F32)
    grad_query = scatter(grad_query, "line")
    gate_grad, up_grad, inner, arrived, result_grad, normed_grad = lax.optimization_barrier(
        (gate_grad, up_grad, inner, arrived, result_grad, normed_grad)
    )
    grad_gate = product_tn(gate_grad, arrived)[None]
    grad_upward = product_tn(up_grad, arrived)[None]
    grad_downward = product_tn(inner, result_grad)[None]
    normed_grad = normed_grad.astype(F32)
    grad_router_first = split_product(first_logit_grad, tree_input)
    token_grad, grad_gain_first = first_pull(normed_grad)
    tokens_grad = token_grad + middle_grad

    sums = jnp.concatenate(
        [grad_gain_first[None], grad_gain_second[None], grad_router_first, grad_router_second],
        axis=0,
    )
    sums = jnp.transpose(sums.reshape(sums.shape[0], -1, own_kv), (1, 0, 2))
    if walk:
        sums, grad_query, grad_key, grad_value = last_exchange(
            sums, grad_query.reshape(pair, own_in, feats), grad_kv, sizes, 10
        )
        grad_query = grad_query[None]
    else:
        sums = small_exchange(sums, sizes, True, 10)
        grad_query = swap(grad_query.reshape(own_in * pair, line, part)[None], "pair", 1, 0)
        grad_query = jnp.transpose(grad_query, (1, 2, 0, 3)).reshape(1, own_in, heads_total)
    return (
        layer_out.reshape(micro, 1, tok, width),
        tokens_grad.reshape(micro, 1, tok, width),
        grad_query.astype(F32),
        grad_output[None].astype(F32),
        grad_key,
        grad_value,
        sums[0],
        jnp.transpose(sums[2 : 2 + experts]),
        sums[1],
        jnp.transpose(sums[2 + experts :]),
        grad_gate,
        grad_upward,
        grad_downward,
    )


def solution(mesh):
    line, experts = mesh.devices.shape
    pair = 2 if line % 2 == 0 and (HEADS % line == 0) else 1
    shaped = Mesh(mesh.devices.reshape(line // pair, pair, experts), ALL)
    in_specs = (
        P(None, DP, "expert", None),
        P("expert", DP, None),
        P("expert", DP, None),
        P(ALL, None),
        P(ALL, None),
        P(ALL),
        P(ALL, None),
        P(ALL),
        P(ALL, None),
        P("expert", DP, None),
        P("expert", DP, None),
        P("expert", DP, None),
        P(None, DP, None, None),
        P(None, DP, "expert", None),
        P(None, DP, "expert"),
        P(None, DP, None),
        P(None, DP, "expert", None),
    )
    out_specs = (
        P(None, DP, "expert", None),
        P(None, DP, "expert", None),
        P("expert", DP, None),
        P("expert", DP, None),
        P(ALL, None),
        P(ALL, None),
        P(ALL),
        P(ALL, None),
        P(ALL),
        P(ALL, None),
        P("expert", DP, None),
        P("expert", DP, None),
        P("expert", DP, None),
    )
    return jax.shard_map(body, mesh=shaped, in_specs=in_specs, out_specs=out_specs, check_vma=False)
```

```python
from functools import partial
import math

import jax
import jax.numpy as jnp
from jax import lax
from jax.experimental import pallas as pl
from jax.experimental.pallas import tpu as pltpu
from jax.sharding import Mesh, PartitionSpec as P

HEADS = 16
HDIM = 128
EPSILON = 1e-06
HIGHEST = lax.Precision.HIGHEST
BF16 = jnp.bfloat16
F32 = jnp.float32


def product(left, right):
    return jnp.dot(left, right, preferred_element_type=F32)


def product_tn(left, right):
    return lax.dot_general(left, right, (((0,), (0,)), ((), ())), preferred_element_type=F32)


def product_nt(left, right):
    return lax.dot_general(left, right, (((1,), (1,)), ((), ())), preferred_element_type=F32)


def split_product(values, rows):
    parts, rest = [], values
    for _ in range(3):
        parts.append(lax.reduce_precision(rest, 8, 7))
        rest = rest - parts[-1]
    count = values.shape[1]
    total = product_tn(jnp.concatenate(parts, axis=1).astype(BF16), rows)
    return total[:count] + total[count : 2 * count] + total[2 * count :]


def rms_scaled(values, gain):
    return values * lax.rsqrt(jnp.mean(values * values, axis=-1, keepdims=True) + EPSILON) * gain


def mixture_gates(picked, logits):
    labels = jnp.arange(logits.shape[1], dtype=jnp.int32)
    onehot = (picked[:, :, None] == labels[None, None, :]).astype(F32)
    chosen = jnp.sum(onehot * logits[:, None, :], axis=-1)
    weights = jax.nn.softmax(chosen, axis=-1)
    return jnp.sum(weights[:, :, None] * onehot, axis=1)


def tree_layout(segment_len, tree_len):
    places = jnp.arange(tree_len, dtype=jnp.int32)
    trunk_len = 4 * segment_len
    segment = jnp.where(
        places < trunk_len,
        0,
        jnp.where(
            places < 2 * trunk_len,
            1 + (places - trunk_len) // segment_len,
            5 + (places - 2 * trunk_len) // segment_len,
        ),
    )
    depth = jnp.where(
        places < trunk_len,
        places,
        jnp.where(
            places < 2 * trunk_len,
            trunk_len + (places - trunk_len) % segment_len,
            trunk_len + segment_len + (places - 2 * trunk_len) % segment_len,
        ),
    )
    return (places, segment, depth)


def ancestors(parent, segment):
    labels = jnp.arange(parent.shape[0], dtype=jnp.int32)
    first = jnp.where(labels > 0, parent, -1)
    lookup = jnp.maximum(first, 0)[:, None] == labels[None, :]
    second = jnp.where(first > 0, jnp.sum(jnp.where(lookup, parent[None, :], 0), axis=1), -1)
    member = segment[:, None] == labels[None, :]
    up_one = jnp.sum(jnp.where(member, first[None, :], 0), axis=1)
    up_two = jnp.sum(jnp.where(member, second[None, :], 0), axis=1)
    return (up_one, up_two)


def score_bias(parent, segment, places):
    up_one, up_two = ancestors(parent, segment)
    same = (segment[None, :] == segment[:, None]) & (places[None, :] <= places[:, None])
    seen = same | (segment[None, :] == up_one[:, None]) | (segment[None, :] == up_two[:, None])
    return jnp.where(seen, 0.0, -1e30).astype(F32)


def slot_table(picked, order, experts, capacity):
    labels = jnp.arange(experts, dtype=jnp.int32)
    chosen = jnp.sum((picked[:, :, None] == labels[None, None, :]).astype(F32), axis=1)
    earlier = (order[None, :] < order[:, None]).astype(F32)
    ranks = jnp.dot(earlier, chosen, precision=HIGHEST, preferred_element_type=F32)
    slots = jnp.arange(capacity, dtype=F32)
    return jnp.transpose(chosen)[:, None, :] * (
        jnp.transpose(ranks)[:, None, :] == slots[None, :, None]
    ).astype(F32)


def turn(values, cosine, sine):
    half = values.shape[-1] // 2
    first = values[:, :half]
    second = values[:, half:]
    return jnp.concatenate(
        [first * cosine - second * sine, second * cosine + first * sine], axis=-1
    )


def softmax_rows(queries, keys, bias, scale):
    scores = product_nt(queries, keys) * scale + bias
    highest = jnp.max(scores, axis=-1, keepdims=True)
    weights = jnp.exp(scores - highest)
    return weights / jnp.sum(weights, axis=-1, keepdims=True)


def attend_kernel(heads, scale, raw_ref, kv_ref, cos_ref, sin_ref, bias_ref, query_ref, out_ref):
    quarter, tok = raw_ref.shape[1], raw_ref.shape[3]
    rows = quarter * tok
    cosine, sine, bias = cos_ref[...], sin_ref[...], bias_ref[0, 0]
    for head in range(heads):
        cols = slice(head * HDIM, (head + 1) * HDIM)
        raw = raw_ref[0, :, 0, :, cols].reshape(rows, HDIM)
        keys = kv_ref[0, 0, 0, :, 0, :, cols].reshape(rows, HDIM)
        values = kv_ref[0, 1, 0, :, 0, :, cols].reshape(rows, HDIM)
        queries = turn(raw, cosine, sine).astype(BF16)
        probs = softmax_rows(queries, keys, bias, scale).astype(BF16)
        query_ref[0, :, 0, :, cols] = queries.reshape(quarter, tok, HDIM)
        out_ref[0, :, 0, :, cols] = product(probs, values).astype(BF16).reshape(quarter, tok, HDIM)


def attend_back_kernel(
    heads, scale, query_ref, kv_ref, grad_ref, cos_ref, sin_ref, bias_ref, dq_ref, dkv_ref
):
    quarter, tok = query_ref.shape[1], query_ref.shape[3]
    rows = quarter * tok
    cosine, sine, bias = cos_ref[...], sin_ref[...], bias_ref[0, 0]
    for head in range(heads):
        cols = slice(head * HDIM, (head + 1) * HDIM)
        queries = query_ref[0, :, 0, :, cols].reshape(rows, HDIM)
        keys = kv_ref[0, 0, 0, :, 0, :, cols].reshape(rows, HDIM)
        values = kv_ref[0, 1, 0, :, 0, :, cols].reshape(rows, HDIM)
        grad = grad_ref[0, :, 0, :, cols].reshape(rows, HDIM)
        probs = softmax_rows(queries, keys, bias, scale)
        prob_grad = product_nt(grad, values)
        centre = jnp.sum(prob_grad * probs, axis=-1, keepdims=True)
        score_grad = (probs * (prob_grad - centre) * scale).astype(BF16)
        query_grad = turn(product(score_grad, keys), cosine, -sine).astype(BF16)
        key_grad = turn(product_tn(score_grad, queries), cosine, -sine).astype(BF16)
        value_grad = product_tn(probs.astype(BF16), grad).astype(BF16)
        dq_ref[0, :, 0, :, cols] = query_grad.reshape(quarter, tok, HDIM)
        dkv_ref[0, 0, 0, :, 0, :, cols] = key_grad.reshape(quarter, tok, HDIM)
        dkv_ref[0, 1, 0, :, 0, :, cols] = value_grad.reshape(quarter, tok, HDIM)


def attention_specs(shape, slices):
    pair, quarter, micro, tok, feats = shape
    part = feats // slices
    rows = quarter * tok
    grid = (pair, micro, slices)
    flat = pl.BlockSpec((1, quarter, 1, tok, part), lambda i, m, s: (i, 0, m, 0, s))
    both = pl.BlockSpec(
        (1, 2, 1, quarter, 1, tok, part), lambda i, m, s: (s, 0, i, 0, m, 0, 0)
    )
    angle = pl.BlockSpec((rows, HDIM // 2), lambda i, m, s: (0, 0))
    bias = pl.BlockSpec((1, 1, rows, rows), lambda i, m, s: (i, m, 0, 0))
    return grid, part, flat, both, angle, bias


def attend(raw, kv, cosine, sine, bias, scale):
    slices = kv.shape[0]
    grid, part, flat, both, angle, bias_spec = attention_specs(raw.shape, slices)
    out = jax.ShapeDtypeStruct(raw.shape, BF16)
    return pl.pallas_call(
        partial(attend_kernel, part // HDIM, scale),
        grid=grid,
        in_specs=[flat, both, angle, angle, bias_spec],
        out_specs=[flat, flat],
        out_shape=[out, out],
        cost_estimate=pl.CostEstimate(
            flops=4 * raw.size * cosine.shape[0],
            bytes_accessed=12 * raw.size,
            transcendentals=raw.size * 2,
        ),
        name="attend",
    )(raw, kv, cosine, sine, bias)


def attend_back(queries, kv, grad, cosine, sine, bias, scale):
    slices = kv.shape[0]
    grid, part, flat, both, angle, bias_spec = attention_specs(queries.shape, slices)
    return pl.pallas_call(
        partial(attend_back_kernel, part // HDIM, scale),
        grid=grid,
        in_specs=[flat, both, flat, angle, angle, bias_spec],
        out_specs=[flat, both],
        out_shape=[
            jax.ShapeDtypeStruct(queries.shape, BF16),
            jax.ShapeDtypeStruct(kv.shape, BF16),
        ],
        cost_estimate=pl.CostEstimate(
            flops=10 * queries.size * cosine.shape[0],
            bytes_accessed=14 * queries.size,
            transcendentals=queries.size * 2,
        ),
        name="attend_back",
    )(queries, kv, grad, cosine, sine, bias)


MESH = pl.DeviceIdType.MESH
ANY = pl.BlockSpec(memory_space=pl.ANY)
VMEM = pl.BlockSpec(memory_space=pltpu.VMEM)
DMA = pltpu.SemaphoreType.DMA


def remote(src, dst, send, recv, target):
    return pltpu.make_async_remote_copy(
        src_ref=src, dst_ref=dst, send_sem=send, recv_sem=recv, device_id=target, device_id_type=MESH
    )


def greet(targets):
    barrier = pltpu.get_barrier_semaphore()
    for target in targets:
        pl.semaphore_signal(barrier, inc=1, device_id=target, device_id_type=MESH)
    pl.semaphore_wait(barrier, len(targets))


def params(number, limit=None):
    return pltpu.CompilerParams(
        collective_id=number, has_side_effects=True, vmem_limit_bytes=limit
    )


def add_into(target, sources, rows):
    step = 1
    while step * 2 <= rows and step * 2 * target.shape[-1] <= 65536 and rows % (step * 2) == 0:
        step *= 2

    def one(index, carry):
        where = pl.ds(pl.multiple_of(index * step, step), step)
        total = sources[0][where].astype(F32)
        for source in sources[1:]:
            total = total + source[where].astype(F32)
        target[where] = total.astype(target.dtype)
        return carry

    lax.fori_loop(0, rows // step, one, 0)


def cube_reduce_kernel(pairs, x_ref, o_ref, half, quarter, got_core, got_side, got_pair, send, recv):
    p = lax.axis_index("pair") if pairs == 2 else 0
    e = lax.axis_index("expert")
    c, y = lax.rem(e, 2), lax.div(e, 2)
    core = {"expert": e + 1 - 2 * c}
    side = {"expert": e + 2 - 4 * y}
    other = {"pair": lax.rem(p + 1, pairs)}
    greet([core, side] + ([other] if pairs == 2 else []))
    rows = x_ref.shape[3]
    shifts = (1, 0) if pairs == 2 else (0,)
    order = [(dx, dy) for dy in (1, 0) for dx in shifts]
    copies = []

    def push(source, place, slot, target):
        copy = remote(source, place, send.at[slot], recv.at[slot], target)
        copy.start()
        copies.append(copy)
        return copy

    first = []
    for slot, (dx, dy) in enumerate(order):
        px, yy = lax.rem(p + dx, pairs), lax.rem(y + dy, 2)
        first.append(push(x_ref.at[px, yy, 1 - c], got_core.at[slot], slot, core))
    base = len(order)
    cut = rows // 2 if pairs == 2 else rows
    upper, lower = pl.ds(0, cut), pl.ds(cut, rows - cut)
    to_side, to_other = {}, {}
    for slot, (dx, dy) in enumerate(order):
        px, yy = lax.rem(p + dx, pairs), lax.rem(y + dy, 2)
        first[slot].wait_recv()
        add_into(half.at[slot], [x_ref.at[px, yy, c], got_core.at[slot]], rows)
        if dy == 1:
            to_side[dx] = push(
                half.at[slot, upper], got_side.at[dx, upper], base + dx, side
            )
        if dx == 1:
            to_other[dy] = push(
                half.at[slot, lower], got_pair.at[dy, lower], base + 2 + dy, other
            )
    own = half.at[order.index((0, 0))]
    if pairs == 2:
        to_side[1].wait_recv()
        add_into(
            quarter.at[upper],
            [half.at[order.index((1, 0)), upper], got_side.at[1, upper]],
            cut,
        )
        to_pair = push(quarter.at[upper], got_pair.at[0, upper], base + 4, other)
        to_other[1].wait_recv()
        add_into(
            quarter.at[lower],
            [half.at[order.index((0, 1)), lower], got_pair.at[1, lower]],
            rows - cut,
        )
        to_flank = push(quarter.at[lower], got_side.at[0, lower], base + 5, side)
        to_side[0].wait_recv()
        to_pair.wait_recv()
        add_into(
            o_ref.at[upper], [own.at[upper], got_side.at[0, upper], got_pair.at[0, upper]], cut
        )
        to_other[0].wait_recv()
        to_flank.wait_recv()
        add_into(
            o_ref.at[lower],
            [own.at[lower], got_side.at[0, lower], got_pair.at[0, lower]],
            rows - cut,
        )
    else:
        to_side[0].wait_recv()
        add_into(o_ref, [own, got_side.at[0]], rows)
    for copy in copies:
        copy.wait_send()


def cube_reduce(value, pairs, number):
    _, rows, cols = value.shape
    value = value.reshape(pairs, 2, 2, rows, cols)
    slots = 2 * pairs
    block = jax.ShapeDtypeStruct((rows, cols), value.dtype)
    return pl.pallas_call(
        partial(cube_reduce_kernel, pairs),
        in_specs=[VMEM],
        out_specs=VMEM,
        out_shape=block,
        scratch_shapes=[
            pltpu.VMEM((slots, rows, cols), value.dtype),
            pltpu.VMEM((rows, cols), value.dtype),
            pltpu.VMEM((slots, rows, cols), value.dtype),
            pltpu.VMEM((2, rows, cols), value.dtype),
            pltpu.VMEM((2, rows, cols), value.dtype),
            DMA((slots + 6,)),
            DMA((slots + 6,)),
        ],
        compiler_params=params(number, 48 * 2**20),
        cost_estimate=pl.CostEstimate(flops=0, bytes_accessed=0, transcendentals=0),
        name="cube_reduce",
    )(value)


def cube_gather_kernel(pairs, x_ref, o_ref, send, recv, local):
    p = lax.axis_index("pair") if pairs == 2 else 0
    e = lax.axis_index("expert")
    c, y = lax.rem(e, 2), lax.div(e, 2)
    core = {"expert": e + 1 - 2 * c}
    side = {"expert": e + 2 - 4 * y}
    other = {"pair": lax.rem(p + 1, pairs)}
    greet([core, side] + ([other] if pairs == 2 else []))
    q, w = lax.rem(p + 1, pairs), 1 - y
    own = o_ref.at[p, y, c]
    keep = pltpu.make_async_copy(x_ref, own, local)
    keep.start()
    copies = []

    def push(slot, source, place, target):
        copy = remote(source, place, send.at[slot], recv.at[slot], target)
        copy.start()
        copies.append(copy)
        return copy

    rows = x_ref.shape[0]
    cut = rows // 2
    upper, lower = pl.ds(0, cut), pl.ds(cut, rows - cut)
    to_side = push(0, x_ref, own, side)
    to_other = push(1, x_ref, own, other) if pairs == 2 else None
    to_core = push(2, x_ref, own, core)
    waits = [to_core]
    if pairs == 2:
        to_other.wait_recv()
        block = o_ref.at[q, y, c]
        far = [push(3, block.at[upper], block.at[upper], side)]
        waits.append(push(4, block, block, core))
    to_side.wait_recv()
    block = o_ref.at[p, w, c]
    if pairs == 2:
        far.append(push(7, block.at[lower], block.at[lower], other))
    waits.append(push(5, block, block, core))
    if pairs == 2:
        for copy in far:
            copy.wait_recv()
        block = o_ref.at[q, w, c]
        waits.append(push(6, block, block, core))
    for copy in waits:
        copy.wait_recv()
    for copy in copies:
        copy.wait_send()
    keep.wait()


def cube_gather(value, pairs, number):
    return pl.pallas_call(
        partial(cube_gather_kernel, pairs),
        in_specs=[VMEM],
        out_specs=VMEM,
        out_shape=jax.ShapeDtypeStruct((pairs, 2, 2) + value.shape, value.dtype),
        scratch_shapes=[DMA((8,)), DMA((8,)), DMA(())],
        compiler_params=params(number, 48 * 2**20),
        cost_estimate=pl.CostEstimate(
            flops=0, bytes_accessed=80 * value.size, transcendentals=0
        ),
        name="cube_gather",
    )(value)


def place_of(index, sizes):
    line, pairs, experts = sizes
    return {
        "line": index // (pairs * experts),
        "pair": (index // experts) % pairs,
        "expert": index % experts,
    }


def small_kernel(sizes, reduce, x_ref, o_ref, got, send, recv):
    line, pairs, experts = sizes
    count = line * pairs * experts
    me = (
        lax.axis_index("line") * (pairs * experts)
        + lax.axis_index("pair") * experts
        + lax.axis_index("expert")
    )
    barrier = pltpu.get_barrier_semaphore()

    def greet_one(offset, carry):
        target = place_of((me + offset) % count, sizes)
        pl.semaphore_signal(barrier, inc=1, device_id=target, device_id_type=MESH)
        return carry

    lax.fori_loop(1, count, greet_one, 0)
    pl.semaphore_wait(barrier, count - 1)

    def copy_to(offset):
        peer = (me + offset) % count
        source = x_ref.at[peer] if reduce else x_ref
        return remote(source, got.at[offset], send.at[offset], recv.at[offset], place_of(peer, sizes))

    def start(offset, carry):
        copy_to(offset).start()
        return carry

    lax.fori_loop(1, count, start, 0)
    got[0] = x_ref[me] if reduce else x_ref[...]

    def finish(offset, carry):
        copy_to(offset).wait()
        return carry

    lax.fori_loop(1, count, finish, 0)
    if reduce:
        o_ref[...] = jnp.sum(got[...], axis=0)
    else:

        def order(offset, carry):
            o_ref[(me - offset + count) % count] = got[offset]
            return carry

        lax.fori_loop(0, count, order, 0)


def small_exchange(value, sizes, reduce, number):
    count = sizes[0] * sizes[1] * sizes[2]
    block = value.shape[1:] if reduce else value.shape
    return pl.pallas_call(
        partial(small_kernel, sizes, reduce),
        in_specs=[VMEM],
        out_specs=VMEM,
        out_shape=jax.ShapeDtypeStruct(block if reduce else (count,) + block, value.dtype),
        scratch_shapes=[pltpu.VMEM((count,) + block, value.dtype), DMA((count,)), DMA((count,))],
        compiler_params=params(number),
        cost_estimate=pl.CostEstimate(flops=0, bytes_accessed=2**24, transcendentals=0),
        name="small_reduce" if reduce else "small_gather",
    )(value)


def ff_kernel(
    a_in, b_in, gate_hbm, up_hbm, down_hbm,
    a_out, b_out, a_save, b_save, inner_save, dgate_save, dup_save,
    a_buf, b_buf, side, hop, extra, w_gate, w_up, w_down, mid, acc,
    send, recv, load, store, local,
):
    z, p, e = lax.axis_index("line"), lax.axis_index("pair"), lax.axis_index("expert")
    line, _, rows, width = a_buf.shape
    experts, size = a_in.shape[0], a_in.shape[1]
    q = 1 - p
    twin = z + 1 - 2 * (z % 2)
    up, down, other, across = {"line": z + 1}, {"line": z - 1}, {"pair": q}, {"line": twin}
    ins, bufs, outs, saves = (a_in, b_in), (a_buf, b_buf), (a_out, b_out), (a_save, b_save)
    high = z // 2
    near = z + high * (line - 1 - 2 * z)

    def order(t):
        j = t + near * (1 - t // 2) * (1 - 2 * t)
        return j + high * (line - 1 - 2 * j)

    weights = [
        pltpu.make_async_copy(src, dst, load.at[i])
        for i, (src, dst) in enumerate(((gate_hbm, w_gate), (up_hbm, w_up), (down_hbm, w_down)))
    ]
    for copy in weights:
        copy.start()

    barrier = pltpu.get_barrier_semaphore()
    for shift in range(1, experts):
        pl.semaphore_signal(
            barrier, inc=1, device_id={"expert": (e + shift) % experts}, device_id_type=MESH
        )
    pl.semaphore_signal(barrier, inc=1, device_id=other, device_id_type=MESH)

    @pl.when(z > 0)
    def _():
        pl.semaphore_signal(barrier, inc=1, device_id=down, device_id_type=MESH)

    @pl.when(z < line - 1)
    def _():
        pl.semaphore_signal(barrier, inc=1, device_id=up, device_id_type=MESH)

    below, above = (z + line - 1) // line, (2 * line - 2 - z) // line
    pl.semaphore_wait(barrier, experts + below + above)

    UP, DOWN, SIDE, SUMUP, SUMDOWN, SUMSIDE = (i * line for i in range(6))
    SUMTWIN, SWAP = 6 * line, 6 * line + 1
    BACK = SWAP + experts
    PART = BACK + experts
    EARLY = PART + experts

    def push(src, dst, kind, use, target):
        return remote(src, dst, send.at[kind, use], recv.at[kind, use], target)

    def to_up(kind, j):
        return push(bufs[kind].at[j, p], bufs[kind].at[j, p], kind, UP + j, up)

    def to_down(kind, j):
        return push(bufs[kind].at[j, p], bufs[kind].at[j, p], kind, DOWN + j, down)

    def to_other(kind, j):
        return push(bufs[kind].at[j, p], bufs[kind].at[j, p], kind, SIDE + j, other)

    def early(kind, shift):
        ref = bufs[kind].at[z, p, piece((e + experts - shift) % experts)]
        return push(ref, ref, kind, EARLY + shift, other)

    def sum_up(kind, j):
        return push(bufs[kind].at[j, p], hop.at[kind, j], kind, SUMUP + j, up)

    def sum_down(kind, j, slot):
        return push(bufs[kind].at[j, p], hop.at[kind, slot], kind, SUMDOWN + j, down)

    def sum_other(kind, j):
        return push(bufs[kind].at[j, q], side.at[kind, j], kind, SUMSIDE + j, other)

    def piece(index):
        return pl.ds(pl.multiple_of(index * size, size), size)

    far_expert = (e + 2) % experts
    queue = (far_expert, far_expert + 1 - 2 * (far_expert % 2), e + 1 - 2 * (e % 2), e)

    def sum_part(i):
        return push(
            b_buf.at[z, q, piece(queue[i])],
            side.at[1, z, piece(queue[i])],
            1,
            PART + i,
            other,
        )

    def sum_twin():
        return push(bufs[1].at[twin, q], extra, 1, SUMTWIN, across)

    def save(kind, j, column):
        return pltpu.make_async_copy(
            bufs[kind].at[j, column], saves[kind].at[j, column], store.at[kind, j, column]
        )

    swaps = []
    for kind in range(2):
        home = bufs[kind].at[z, p, piece(e)]
        keep = pltpu.make_async_copy(ins[kind].at[e], home, local.at[kind])
        keep.start()
        group = []
        for shift in range(1, experts):
            peer = (e + shift) % experts
            copy = push(ins[kind].at[peer], home, kind, SWAP + shift, {"expert": peer})
            copy.start()
            group.append(copy)
        swaps.append((keep, group))

    def spread(t, first=False):
        j = order(t)
        for kind in range(2):
            if first:
                swaps[kind][0].wait()
                early(kind, 0).start()
                for shift in range(experts - 1, 0, -1):
                    swaps[kind][1][shift - 1].wait_recv()
                    early(kind, shift).start()
            else:

                @pl.when(j < z)
                def _():
                    to_up(kind, j).wait_recv()

                @pl.when(j > z)
                def _():
                    to_down(kind, j).wait_recv()

            @pl.when((j <= z) & (z < line - 1))
            def _():
                to_up(kind, j).start()

            @pl.when((j >= z) & (z > 0))
            def _():
                to_down(kind, j).start()

            if not first:
                to_other(kind, j).start()
            save(kind, j, p).start()

    chunk = 512
    steps = width // chunk

    part = 32

    def rows_half(j, column):
        for index in range(2):
            acc[index] = jnp.zeros(acc.shape[1:], F32)

        def one(n, carry):
            where = pl.ds(pl.multiple_of(n * chunk, chunk), chunk)
            left = a_buf[j, column, :, where]
            acc[0] += product_nt(left, w_gate[:, where])
            acc[1] += product_nt(left, w_up[:, where])
            return carry

        lax.fori_loop(0, steps, one, 0)

        def two(i, carry):
            where = pl.ds(pl.multiple_of(i * part, part), part)
            gate = acc[0, where]
            mid[j, column, 0, where] = (gate * jax.nn.sigmoid(gate) * acc[1, where]).astype(BF16)
            return carry

        lax.fori_loop(0, rows // part, two, 0)

    def grads_half(j, column):
        acc[2] = jnp.zeros(acc.shape[1:], F32)

        def one(n, carry):
            where = pl.ds(pl.multiple_of(n * chunk, chunk), chunk)
            acc[2] += product_nt(b_buf[j, column, :, where], w_down[:, where])
            return carry

        lax.fori_loop(0, steps, one, 0)

        def two(i, carry):
            where = pl.ds(pl.multiple_of(i * part, part), part)
            gate, lift, grad = acc[0, where], acc[1, where], acc[2, where]
            sigma = jax.nn.sigmoid(gate)
            mid[j, column, 1, where] = (
                grad * lift * sigma * (1.0 + gate * (1.0 - sigma))
            ).astype(BF16)
            mid[j, column, 2, where] = (grad * gate * sigma).astype(BF16)
            return carry

        lax.fori_loop(0, rows // part, two, 0)

    def out_half(j, column):
        def one(n, carry):
            where = pl.ds(pl.multiple_of(n * chunk, chunk), chunk)
            a_buf[j, column, :, where] = product(mid[j, column, 0], w_down[:, where]).astype(BF16)
            return carry

        lax.fori_loop(0, steps, one, 0)

    def back_half(j, column):
        def one(n, carry):
            where = pl.ds(pl.multiple_of(n * chunk, chunk), chunk)
            b_buf[j, column, :, where] = (
                product(mid[j, column, 1], w_gate[:, where])
                + product(mid[j, column, 2], w_up[:, where])
            ).astype(BF16)
            return carry

        lax.fori_loop(0, steps, one, 0)

    def arrive(kind, j):
        @pl.when(j == z)
        def _():
            for shift in range(experts):
                early(kind, shift).wait_recv()

        @pl.when(j != z)
        def _():
            to_other(kind, j).wait_recv()

        save(kind, j, q).start()

    def emit(t):
        j = order(t)
        sum_other(0, j).start()

        @pl.when((j != twin) & (j != z))
        def _():
            sum_other(1, j).start()

    def step(s, carry):
        @pl.when(s == 0)
        def _():
            spread(0, True)
            for copy in weights:
                copy.wait()

        @pl.when(s == 1)
        def _():
            spread(1)
            spread(2)

        @pl.when(s == 3)
        def _():
            spread(3)

        @pl.when(s == line)
        def _():
            sum_twin().start()

        def half(c, inner_carry):
            t = s - c
            column = p + c * (q - p)

            @pl.when((t >= 0) & (t < line))
            def _():
                j = order(t)

                @pl.when(c == 1)
                def _():
                    arrive(0, j)

                rows_half(j, column)

                @pl.when(c == 1)
                def _():
                    save(0, j, q).wait()
                    out_half(j, q)

                    @pl.when(t == line - 1)
                    def _():
                        sum_other(0, j).start()

                    arrive(1, j)

                grads_half(j, column)

                @pl.when(c == 1)
                def _():
                    save(1, j, q).wait()
                    back_half(j, q)

                    @pl.when(t == line - 1)
                    def _():
                        sum_other(1, j).start()

            return inner_carry

        return lax.fori_loop(0, 2, half, carry)

    lax.fori_loop(0, line + 1, step, 0)

    for t in (2, 1, 0):
        emit(t)

    for copy in (
        pltpu.make_async_copy(mid.at[:, :, 0], inner_save, local.at[2]),
        pltpu.make_async_copy(mid.at[:, :, 1], dgate_save, local.at[3]),
        pltpu.make_async_copy(mid.at[:, :, 2], dup_save, local.at[4]),
    ):
        copy.start()
    sum_twin().wait_recv()
    for i in range(experts):
        part = b_buf.at[z, q, piece(queue[i])]
        add_into(part, [part, extra.at[piece(queue[i])]], size)
        sum_part(i).start()

    def back(kind):
        own = pltpu.make_async_copy(
            bufs[kind].at[z, p, piece(e)], outs[kind].at[e], local.at[kind]
        )
        return [own] + [
            push(
                bufs[kind].at[z, p, piece((e + shift) % experts)],
                outs[kind].at[e],
                kind,
                BACK + shift,
                {"expert": (e + shift) % experts},
            )
            for shift in range(1, experts)
        ]

    def back_part(i):
        source = b_buf.at[z, p, piece(queue[i])]
        if i == experts - 1:
            return pltpu.make_async_copy(source, b_out.at[e], local.at[1])
        return push(source, b_out.at[e], 1, BACK + 1 + i, {"expert": queue[i]})

    def fold(s, carry):
        t = line - 1 - s
        j = order(t)
        for kind in range(2):
            save(kind, j, p).wait()

            @pl.when((j <= z) & (z < line - 1))
            def _():
                to_up(kind, j).wait_send()

            @pl.when((j >= z) & (z > 0))
            def _():
                to_down(kind, j).wait_send()

            @pl.when(j == z)
            def _():
                for shift in range(experts):
                    early(kind, shift).wait_send()

            @pl.when(j != z)
            def _():
                to_other(kind, j).wait_send()

        for kind in range(2):
            (out_half, back_half)[kind](j, p)
            mine = bufs[kind].at[j, p]
            if kind == 0:
                sum_other(kind, j).wait_recv()
                add_into(mine, [mine, side.at[kind, j]], rows)
            else:

                @pl.when((j != twin) & (j != z))
                def _():
                    sum_other(kind, j).wait_recv()
                    add_into(mine, [mine, side.at[kind, j]], rows)

            @pl.when((j >= z) & (z > 0))
            def _():
                sum_up(kind, j).wait_recv()
                add_into(mine, [mine, hop.at[kind, j]], rows)

            @pl.when((j < z) & (z < line - 1))
            def _():
                sum_down(kind, j, j).wait_recv()
                add_into(mine, [mine, hop.at[kind, j]], rows)

            @pl.when((j == z) & (z < line - 1))
            def _():
                sum_down(kind, j, line).wait_recv()
                add_into(mine, [mine, hop.at[kind, line]], rows)

            @pl.when(j == z)
            def _():
                if kind == 0:
                    for copy in back(0):
                        copy.start()
                else:
                    for i in range(experts):
                        part = b_buf.at[z, p, piece(queue[i])]
                        sum_part(i).wait_recv()
                        add_into(part, [part, side.at[1, z, piece(queue[i])]], size)
                        back_part(i).start()

            @pl.when(j > z)
            def _():
                sum_up(kind, j).start()

            @pl.when((j < z) & (j != z - 1))
            def _():
                sum_down(kind, j, j).start()

            @pl.when((j < z) & (j == z - 1))
            def _():
                sum_down(kind, j, line).start()

        return carry

    lax.fori_loop(0, line, fold, 0)

    for copy in back(0):
        copy.wait()
    for i in range(experts):
        back_part(i).wait()

    def drain(j, carry):
        for kind in range(2):
            if kind == 0:
                sum_other(kind, j).wait_send()
            else:

                @pl.when((j != twin) & (j != z))
                def _():
                    sum_other(kind, j).wait_send()

            @pl.when(j > z)
            def _():
                sum_up(kind, j).wait_send()

            @pl.when(j < z)
            def _():
                sum_down(kind, j, j).wait_send()

        return carry

    lax.fori_loop(0, line, drain, 0)
    sum_twin().wait_send()
    for i in range(experts):
        sum_part(i).wait_send()
    for copy in (
        pltpu.make_async_copy(mid.at[:, :, 0], inner_save, local.at[2]),
        pltpu.make_async_copy(mid.at[:, :, 1], dgate_save, local.at[3]),
        pltpu.make_async_copy(mid.at[:, :, 2], dup_save, local.at[4]),
    ):
        copy.wait()
    for keep, group in swaps:
        for copy in group:
            copy.wait_send()


def feed_forward(first, second, w_gate, w_up, w_down, line, pairs, number):
    experts, size, width = first.shape
    hidden = w_gate.shape[0]
    rows = experts * size
    blocks = (line, pairs, rows)
    back = jax.ShapeDtypeStruct(first.shape, BF16)
    wide = jax.ShapeDtypeStruct(blocks + (width,), BF16)
    thin = jax.ShapeDtypeStruct(blocks + (hidden,), BF16)
    uses = 6 * line + 2 + 4 * experts
    total = line * pairs * rows
    return pl.pallas_call(
        ff_kernel,
        in_specs=[ANY] * 5,
        out_specs=[ANY] * 7,
        out_shape=[back, back, wide, wide, thin, thin, thin],
        scratch_shapes=[
            pltpu.VMEM(blocks + (width,), BF16),
            pltpu.VMEM(blocks + (width,), BF16),
            pltpu.VMEM((2, line, rows, width), BF16),
            pltpu.VMEM((2, line + 1, rows, width), BF16),
            pltpu.VMEM((rows, width), BF16),
            pltpu.VMEM((hidden, width), BF16),
            pltpu.VMEM((hidden, width), BF16),
            pltpu.VMEM((hidden, width), BF16),
            pltpu.VMEM((line, pairs, 3, rows, hidden), BF16),
            pltpu.VMEM((3, rows, hidden), F32),
            DMA((2, uses)),
            DMA((2, uses)),
            DMA((3,)),
            DMA((2, line, pairs)),
            DMA((5,)),
        ],
        compiler_params=params(number, 63 * 2**20),
        cost_estimate=pl.CostEstimate(
            flops=12 * total * hidden * width,
            bytes_accessed=12 * total * width,
            transcendentals=total * hidden,
        ),
        name="feed_forward",
    )(first, second, w_gate, w_up, w_down)


def last_kernel(
    sizes, x_ref, q_ref, g_hbm, o_ref, w_ref, key_ref, value_ref,
    got, side, g_ref, k_ref, hop, send, recv, peer_send, peer_recv, local,
):
    line, pairs, experts = sizes
    trees = pairs * experts
    count = line * trees
    z, p, e = lax.axis_index("line"), lax.axis_index("pair"), lax.axis_index("expert")
    mine = p * experts + e
    me = z * trees + mine
    span, piece = g_ref.shape[1], k_ref.shape[1]
    up, down = {"line": z + 1}, {"line": z - 1}
    high = z // 2
    near = z + high * (line - 1 - 2 * z)

    def order(t):
        j = t + near * (1 - t // 2) * (1 - 2 * t)
        return j + high * (line - 1 - 2 * j)

    fetch = pltpu.make_async_copy(g_hbm, g_ref, local)
    fetch.start()
    barrier = pltpu.get_barrier_semaphore()

    def greet_one(offset, carry):
        target = place_of((me + offset) % count, sizes)
        pl.semaphore_signal(barrier, inc=1, device_id=target, device_id_type=MESH)
        return carry

    lax.fori_loop(1, count, greet_one, 0)
    pl.semaphore_wait(barrier, count - 1)
    UP, DOWN, SWAP, PAIR = 0, pairs * line, 2 * pairs * line, 2 * pairs * line + trees
    size = span // pairs

    def sum_up(j, h):
        where, use = pl.ds(h * size, size), UP + pairs * j + h
        return remote(g_ref.at[j, where], hop.at[j, where], send.at[use], recv.at[use], up)

    def sum_down(j, slot, h):
        where, use = pl.ds(h * size, size), DOWN + pairs * j + h
        return remote(g_ref.at[j, where], hop.at[slot, where], send.at[use], recv.at[use], down)

    def fold(t, done=None):
        j = order(t)
        for h in range(pairs):
            where = pl.ds(h * size, size)
            own = g_ref.at[j, where]

            @pl.when((j >= z) & (z > 0))
            def _():
                sum_up(j, h).wait_recv()
                add_into(own, [own, hop.at[j, where]], size)

            @pl.when((j < z) & (z < line - 1))
            def _():
                sum_down(j, j, h).wait_recv()
                add_into(own, [own, hop.at[j, where]], size)

            @pl.when((j == z) & (z < line - 1))
            def _():
                sum_down(j, line, h).wait_recv()
                add_into(own, [own, hop.at[line, where]], size)

            @pl.when(j > z)
            def _():
                sum_up(j, h).start()

            @pl.when((j < z) & (j != z - 1))
            def _():
                sum_down(j, j, h).start()

            @pl.when((j < z) & (j == z - 1))
            def _():
                sum_down(j, line, h).start()

            if done is not None:
                done(h)

    fetch.wait()
    fold(3)
    swap = remote(q_ref.at[1 - p], side, send.at[PAIR], recv.at[PAIR], {"pair": 1 - p})
    swap.start()

    def copy_to(offset):
        peer = (me + offset) % count
        return remote(
            x_ref.at[peer],
            got.at[offset],
            peer_send.at[offset],
            peer_recv.at[offset],
            place_of(peer, sizes),
        )

    def start(offset, carry):
        copy_to(offset).start()
        return carry

    lax.fori_loop(1, count, start, 0)
    got[0] = x_ref[me]
    fold(2)
    part = q_ref.shape[2] // line

    def lay(block, source):
        for index in range(line):
            column = pl.multiple_of((index * pairs + source) * part, part)
            w_ref[:, pl.ds(column, part)] = block[:, index * part : (index + 1) * part].astype(F32)

    lay(q_ref.at[p], p)
    fold(1)
    swap.wait_recv()
    lay(side, 1 - p)

    def finish(offset, carry):
        copy_to(offset).wait()
        return carry

    lax.fori_loop(1, count, finish, 0)
    o_ref[...] = jnp.sum(got[...], axis=0)
    def share_of(index):
        return g_ref.at[z, pl.ds(pl.multiple_of(index * piece, piece), piece)]

    keep = pltpu.make_async_copy(share_of(mine), k_ref.at[mine], local)

    def deal(index):
        use = SWAP + (index + trees - mine) % trees
        return remote(
            share_of(index),
            k_ref.at[mine],
            send.at[use],
            recv.at[use],
            {"pair": index // experts, "expert": index % experts},
        )

    def leave(h):
        for index in range(h * experts, (h + 1) * experts):

            @pl.when(mine == index)
            def _():
                keep.start()

            @pl.when(mine != index)
            def _():
                deal(index).start()

    fold(0, leave)
    keep.wait()
    for shift in range(1, trees):
        deal((mine + shift) % trees).wait()
    share = k_ref.shape[2] // 2
    for source in range(trees):
        column = ((source % experts) * pairs + source // experts) * share
        for index, target in enumerate((key_ref, value_ref)):
            target[:, column : column + share] = k_ref[
                source, :, index * share : (index + 1) * share
            ].astype(F32)
    swap.wait_send()

    def drain(j, carry):
        for h in range(pairs):

            @pl.when(j > z)
            def _():
                sum_up(j, h).wait_send()

            @pl.when(j < z)
            def _():
                sum_down(j, j, h).wait_send()

        return carry

    lax.fori_loop(0, line, drain, 0)


def last_exchange(sums, query, grads, sizes, number):
    line, pairs, experts = sizes
    trees = pairs * experts
    count, block = sums.shape[0], sums.shape[1:]
    _, rows, cols = query.shape
    span, thin = grads.shape[0] // line, grads.shape[1]
    uses = 2 * pairs * line + trees + 1
    wide = jax.ShapeDtypeStruct((span // trees, trees * thin // 2), F32)
    return pl.pallas_call(
        partial(last_kernel, sizes),
        in_specs=[VMEM, VMEM, ANY],
        out_specs=[VMEM] * 4,
        out_shape=[
            jax.ShapeDtypeStruct(block, F32),
            jax.ShapeDtypeStruct((rows, pairs * cols), F32),
            wide,
            wide,
        ],
        scratch_shapes=[
            pltpu.VMEM((count,) + block, F32),
            pltpu.VMEM((rows, cols), BF16),
            pltpu.VMEM((line, span, thin), BF16),
            pltpu.VMEM((trees, span // trees, thin), BF16),
            pltpu.VMEM((line + 1, span, thin), BF16),
            DMA((uses,)),
            DMA((uses,)),
            DMA((count,)),
            DMA((count,)),
            DMA(()),
        ],
        compiler_params=params(number, 48 * 2**20),
        cost_estimate=pl.CostEstimate(flops=0, bytes_accessed=0, transcendentals=0),
        name="last_exchange",
    )(sums, query, grads.reshape(line, span, thin))


def start_all_kernel(
    sizes, tok_ref, wq_ref, wk_ref, wv_ref, small_ref, int_ref,
    tok_out, q_out, kv_out, small_out, int_out,
    q_cut, kv_cut, send, recv, peer_send, peer_recv, local,
):
    line, pairs, experts = sizes
    z, p, e = lax.axis_index("line"), lax.axis_index("pair"), lax.axis_index("expert")
    c, y = e % 2, e // 2
    core, side = {"expert": e + 1 - 2 * c}, {"expert": e + 2 - 4 * y}
    other = {"pair": 1 - p}
    trees = pairs * experts
    count = line * trees
    mine = p * experts + e
    me = z * trees + mine
    barrier = pltpu.get_barrier_semaphore()

    def greet_one(offset, carry):
        target = place_of((me + offset) % count, sizes)
        pl.semaphore_signal(barrier, inc=1, device_id=target, device_id_type=MESH)
        return carry

    lax.fori_loop(1, count, greet_one, 0)
    part = wq_ref.shape[1] // (line * pairs)
    sub = line // experts
    for q in range(pairs):
        for d in range(experts):
            for index, ref in enumerate((wk_ref, wv_ref)):
                for h in range(sub):
                    column = ((d * sub + h) * pairs + q) * part
                    place = (index * sub + h) * part
                    kv_cut[q * experts + d, :, place : place + part] = ref[
                        :, column : column + part
                    ]
    for q in range(pairs):
        for index in range(line):
            column = (index * pairs + q) * part
            q_cut[q, :, index * part : (index + 1) * part] = wq_ref[:, column : column + part]
    pl.semaphore_wait(barrier, count - 1)

    copies, TOK, QSWAP, INTS, KV = [], 0, 7, 8, 9
    WALK = KV + trees

    def push(slot, source, place, target):
        copy = remote(source, place, send.at[slot], recv.at[slot], target)
        copy.start()
        copies.append(copy)
        return copy

    size = kv_cut.shape[1]
    kv_home = kv_out.at[z, pl.ds(pl.multiple_of(mine * size, size), size)]
    pieces = []
    for shift in range(1, trees):
        peer = (mine + shift) % trees
        pieces.append(
            push(
                KV + shift,
                kv_cut.at[peer],
                kv_home,
                {"pair": peer // experts, "expert": peer % experts},
            )
        )
    rows = q_cut.shape[1]
    q_home = q_out.at[z, pl.ds(pl.multiple_of(p * rows, rows), rows)]
    q_swap = push(QSWAP, q_cut.at[1 - p], q_home, other)
    keeps = [
        pltpu.make_async_copy(q_cut.at[p], q_home, local.at[0]),
        pltpu.make_async_copy(kv_cut.at[mine], kv_home, local.at[1]),
        pltpu.make_async_copy(tok_ref, tok_out.at[p, y, c], local.at[2]),
        pltpu.make_async_copy(small_ref, small_out.at[me], local.at[3]),
        pltpu.make_async_copy(int_ref, int_out.at[p], local.at[4]),
    ]
    for copy in keeps:
        copy.start()
    def walker(block, base):
        def to_up(j, d):
            ref = block(j)
            return remote(ref, ref, send.at[base + d], recv.at[base + d], {"line": z + 1})

        def to_down(j, d):
            ref, at = block(j), base + line + d
            return remote(ref, ref, send.at[at], recv.at[at], {"line": z - 1})

        return to_up, to_down

    def q_rows(member):
        return lambda j: q_out.at[j, pl.ds(pl.multiple_of(member * rows, rows), rows)]

    stride = 2 * line + 2
    walkers = [
        walker(q_rows(p), WALK),
        walker(lambda j: kv_out.at[j], WALK + stride),
        walker(q_rows(1 - p), WALK + 2 * stride),
    ]

    def begin(which):
        to_up, to_down = walkers[which]

        @pl.when(z < line - 1)
        def _():
            to_up(z, 1).start()

        @pl.when(z > 0)
        def _():
            to_down(z, 1).start()

    keeps[0].wait()
    begin(0)
    own = tok_out.at[p, y, c]
    to_side = push(TOK, tok_ref, own, side)
    to_other = push(TOK + 1, tok_ref, own, other)
    waits = [push(TOK + 2, tok_ref, own, core), push(INTS, int_ref, int_out.at[p], other)]

    def small_to(offset):
        return remote(
            small_ref,
            small_out.at[me],
            peer_send.at[offset],
            peer_recv.at[offset],
            place_of((me + offset) % count, sizes),
        )

    def small_start(offset, carry):
        small_to(offset).start()
        return carry

    lax.fori_loop(1, count, small_start, 0)

    keeps[1].wait()
    for copy in pieces:
        copy.wait_recv()
    begin(1)
    q_swap.wait_recv()
    begin(2)
    to_other.wait_recv()
    block = tok_out.at[1 - p, y, c]
    far = push(TOK + 3, block, block, side)
    waits.append(push(TOK + 4, block, block, core))
    to_side.wait_recv()
    block = tok_out.at[p, 1 - y, c]
    waits.append(push(TOK + 5, block, block, core))
    far.wait_recv()
    block = tok_out.at[1 - p, 1 - y, c]
    waits.append(push(TOK + 6, block, block, core))

    for d in range(1, line):
        for to_up, to_down in walkers:

            @pl.when(z - d >= 0)
            def _():
                to_up(z - d, d).wait_recv()

                @pl.when(z < line - 1)
                def _():
                    to_up(z - d, d + 1).start()

            @pl.when(z + d < line)
            def _():
                to_down(z + d, d).wait_recv()

                @pl.when(z > 0)
                def _():
                    to_down(z + d, d + 1).start()

    for d in range(1, line):
        for to_up, to_down in walkers:

            @pl.when((z - d + 1 >= 0) & (z < line - 1))
            def _():
                to_up(z - d + 1, d).wait_send()

            @pl.when((z + d - 1 < line) & (z > 0))
            def _():
                to_down(z + d - 1, d).wait_send()

    for copy in waits:
        copy.wait_recv()
    for copy in copies:
        copy.wait_send()
    for copy in keeps[2:]:
        copy.wait()

    def small_finish(offset, carry):
        small_to(offset).wait()
        return carry

    lax.fori_loop(1, count, small_finish, 0)


def start_all(tokens, w_query, w_key, w_value, small, integers, sizes, number):
    line, pairs, experts = sizes
    trees = pairs * experts
    count = line * trees
    rows, width = w_query.shape
    size = w_key.shape[0]
    feats = width // pairs
    thin = 2 * feats // experts
    uses = 9 + trees + 6 * line + 6
    return pl.pallas_call(
        partial(start_all_kernel, sizes),
        in_specs=[VMEM] * 6,
        out_specs=[VMEM] * 5,
        out_shape=[
            jax.ShapeDtypeStruct((pairs, 2, 2) + tokens.shape, BF16),
            jax.ShapeDtypeStruct((line, pairs * rows, feats), BF16),
            jax.ShapeDtypeStruct((line, trees * size, thin), BF16),
            jax.ShapeDtypeStruct((count,) + small.shape, BF16),
            jax.ShapeDtypeStruct((pairs,) + integers.shape, jnp.int32),
        ],
        scratch_shapes=[
            pltpu.VMEM((pairs, rows, feats), BF16),
            pltpu.VMEM((trees, size, thin), BF16),
            DMA((uses,)),
            DMA((uses,)),
            DMA((count,)),
            DMA((count,)),
            DMA((5,)),
        ],
        compiler_params=params(number, 48 * 2**20),
        name="start_all",
    )(tokens, w_query, w_key, w_value, small, integers)


def input_kernel(dq_ref, wq_ref, kv_ref, wkv_ref, dl_ref, router_ref, o_ref):
    piece = kv_ref.shape[2]
    total = product_nt(dq_ref[...], wq_ref[...])
    total = total + product_nt(kv_ref[0], wkv_ref[:, :piece])
    total = total + product_nt(kv_ref[1], wkv_ref[:, piece:])
    for expert in range(router_ref.shape[0]):
        total = total + dl_ref[:, expert : expert + 1] * router_ref[expert : expert + 1, :]
    o_ref[...] = total.astype(BF16)


def input_gradient(query_pre, query_weight, kv_sum, kv_weight, logit_grad, router):
    rows, feats = query_pre.shape
    width = query_weight.shape[0]
    piece = kv_sum.shape[2]
    experts = router.shape[0]
    block, lanes = min(512, rows), 512
    return pl.pallas_call(
        input_kernel,
        grid=(width // lanes, rows // block),
        in_specs=[
            pl.BlockSpec((block, feats), lambda n, i: (i, 0)),
            pl.BlockSpec((lanes, feats), lambda n, i: (n, 0)),
            pl.BlockSpec((2, block, piece), lambda n, i: (0, i, 0)),
            pl.BlockSpec((lanes, 2 * piece), lambda n, i: (n, 0)),
            pl.BlockSpec((block, experts), lambda n, i: (i, 0)),
            pl.BlockSpec((experts, lanes), lambda n, i: (0, n)),
        ],
        out_specs=pl.BlockSpec((block, lanes), lambda n, i: (i, n)),
        out_shape=jax.ShapeDtypeStruct((rows, width), BF16),
        compiler_params=pltpu.CompilerParams(vmem_limit_bytes=40 * 2**20),
        cost_estimate=pl.CostEstimate(
            flops=2 * rows * width * (feats + 2 * piece), bytes_accessed=6 * rows * width, transcendentals=0
        ),
        name="input_gradient",
    )(query_pre, query_weight, kv_sum, kv_weight, logit_grad, router)


def project_kernel(micro, x_ref, w_ref, gain_ref, router_ref, cos_ref, sin_ref, n_ref, kv_ref, l_ref):
    x = x_ref[...].astype(F32)
    scale = lax.rsqrt(jnp.mean(x * x, axis=-1, keepdims=True) + EPSILON)
    normed = (x * scale * gain_ref[...]).astype(BF16)
    n_ref[...] = normed
    l_ref[...] = product_nt(normed, router_ref[...])
    raw = product(normed, w_ref[...])
    piece = kv_ref.shape[2]
    spread = lambda ref: jnp.concatenate(
        [ref[i] for i in range(ref.shape[0]) for _ in range(micro)], axis=0
    )
    cosine, sine = spread(cos_ref), spread(sin_ref)
    for head in range(piece // HDIM):
        cols = slice(head * HDIM, (head + 1) * HDIM)
        kv_ref[0, :, cols] = turn(raw[:, cols], cosine, sine).astype(BF16)
    kv_ref[1] = raw[:, piece:].astype(BF16)


def project(tokens, weight, gain, router, cosine, sine, micro):
    rows, width = tokens.shape
    piece = weight.shape[1] // 2
    experts, tok, half = cosine.shape
    block = 2 * micro * tok
    loops = experts // 2
    return pl.pallas_call(
        partial(project_kernel, micro),
        grid=(rows // block,),
        in_specs=[
            pl.BlockSpec((block, width), lambda i: (i, 0)),
            pl.BlockSpec(weight.shape, lambda i: (0, 0)),
            pl.BlockSpec((1, width), lambda i: (0, 0)),
            pl.BlockSpec(router.shape, lambda i: (0, 0)),
            pl.BlockSpec((2, tok, half), lambda i: (i % loops, 0, 0)),
            pl.BlockSpec((2, tok, half), lambda i: (i % loops, 0, 0)),
        ],
        out_specs=[
            pl.BlockSpec((block, width), lambda i: (i, 0)),
            pl.BlockSpec((2, block, piece), lambda i: (0, i, 0)),
            pl.BlockSpec((block, experts), lambda i: (i, 0)),
        ],
        out_shape=[
            jax.ShapeDtypeStruct((rows, width), BF16),
            jax.ShapeDtypeStruct((2, rows, piece), BF16),
            jax.ShapeDtypeStruct((rows, experts), F32),
        ],
        compiler_params=pltpu.CompilerParams(vmem_limit_bytes=40 * 2**20),
        cost_estimate=pl.CostEstimate(
            flops=2 * rows * width * weight.shape[1], bytes_accessed=5 * rows * width, transcendentals=0
        ),
        name="project",
    )(tokens, weight, gain, router, cosine, sine)


def gather(value, axes, axis=0):
    return lax.all_gather(value, axes, axis=axis, tiled=True)


def scatter(value, axes, axis=0):
    return lax.psum_scatter(value, axes, scatter_dimension=axis, tiled=True)


def swap(value, axes, split=0, concat=0):
    return lax.all_to_all(value, axes, split_axis=split, concat_axis=concat, tiled=True)


DP = ("line", "pair")
ALL = ("line", "pair", "expert")
TREES = ("pair", "expert")


def body(
    tokens,
    w_query,
    w_out,
    w_key,
    w_value,
    gain_attn,
    router_attn,
    gain_mlp,
    router_mlp,
    w_gate,
    w_up,
    w_down,
    attn_route,
    mlp_route,
    fill_order,
    parents,
    cotangent,
):
    experts = lax.axis_size("expert")
    pair = lax.axis_size("pair")
    line = lax.axis_size("line")
    position = lax.axis_index("expert")
    micro, _, tok, width = tokens.shape
    tree = experts * tok
    rows = pair * experts * micro * tok
    heads_total = w_query.shape[2]
    part = heads_total // (line * pair)
    feats = heads_total // pair
    piece = feats // experts
    own_in = w_query.shape[1]
    own_kv = w_key.shape[0]
    capacity = tok * mlp_route.shape[3] // experts
    scale = 1.0 / math.sqrt(HDIM)

    places, segment, depth = tree_layout(tree // 16, tree)
    half = HDIM // 2
    rates = 10000.0 ** (-jnp.arange(half, dtype=F32) / half)
    angle = depth.astype(F32)[:, None] * rates[None, :]
    cosine, sine = jnp.cos(angle), jnp.sin(angle)

    sizes = (line, pair, experts)
    walk = line == 4 and pair == 2 and experts == 4
    own_tokens = tokens.reshape(micro * tok, width)
    small = jnp.concatenate(
        [gain_attn[None], gain_mlp[None], router_attn.T, router_mlp.T], axis=0
    )
    integers = jnp.concatenate([attn_route[:, 0].reshape(micro, -1), parents[:, 0]], axis=1)
    if walk:
        flat = integers.reshape(-1)
        flat = jnp.pad(flat, (0, -flat.shape[0] % 1024)).reshape(-1, 128)
        tree_tokens, query_weight, kv_weight, small, flat = start_all(
            own_tokens, w_query[0], w_key, w_value, small, flat, sizes, 1
        )
        query_weight = query_weight.reshape(width, feats)
        kv_weight = kv_weight.reshape(width, 2 * piece)
        integers = flat.reshape(pair, -1)[:, : integers.size].reshape((pair,) + integers.shape)
    else:
        query_mine = w_query[0].reshape(own_in, line, pair, part)
        query_mine = jnp.transpose(query_mine, (2, 0, 1, 3)).reshape(pair, own_in, feats)
        if pair == 2:
            query_mine = swap(query_mine, "pair")
            integers = lax.all_gather(integers, "pair", axis=0)
        else:
            integers = integers[None]
        query_weight = gather(query_mine.reshape(pair * own_in, feats), "line")
        kv_mine = jnp.stack([w_key, w_value], axis=1).reshape(
            own_kv, 2, experts, line // experts, pair, part
        )
        kv_mine = jnp.transpose(kv_mine, (4, 2, 0, 1, 3, 5)).reshape(
            pair * experts, own_kv, 2 * piece
        )
        tree_tokens = cube_gather(own_tokens, pair, 1)
        small = small_exchange(small, sizes, False, 2)
        kv_mine = swap(kv_mine, TREES).reshape(pair * experts * own_kv, 2 * piece)
        kv_weight = gather(kv_mine, "line")
    out_mine, small = lax.optimization_barrier((w_out[0], small))
    out_weight = gather(out_mine, "line")

    small = jnp.transpose(small, (1, 0, 2)).reshape(-1, width)
    first_gain = small[0].astype(F32)
    second_gain = small[1].astype(F32)
    first_router = small[2 : 2 + experts]
    second_router = small[2 + experts : 2 + 2 * experts]

    residual = own_tokens.astype(F32)
    _, first_pull = jax.vjp(rms_scaled, residual, first_gain)
    table_shape = (experts, tok, half)
    tree_input, kv, first_logits = project(
        tree_tokens.reshape(rows, width),
        kv_weight,
        first_gain[None],
        first_router,
        cosine.reshape(table_shape),
        sine.reshape(table_shape),
        micro,
    )

    routes = integers[..., : tree * 2].reshape(pair, micro, experts, tok, 2)
    routes = jnp.transpose(routes, (0, 2, 1, 3, 4)).reshape(rows, 2)
    family = integers[..., tree * 2 :]
    bias = jax.vmap(jax.vmap(lambda parent: score_bias(parent, segment, places)))(family)

    kv = cube_gather(kv.reshape(2 * rows, piece), 1, 3)
    shape = (pair, experts, micro, tok, feats)
    kv = kv.reshape(experts, 2, pair, experts, micro, tok, piece)

    first_gates, first_gate_pull = jax.vjp(partial(mixture_gates, routes), first_logits)
    column = (jnp.arange(experts, dtype=jnp.int32) == position).astype(F32)
    own_gate = jnp.sum(first_gates * column[None, :], axis=1)

    raw = product(tree_input, query_weight)
    queries, heads_out = attend(raw.reshape(shape), kv, cosine, sine, bias, scale)
    heads_flat = heads_out.reshape(rows, feats)
    projected = product(heads_flat, out_weight)
    gated = (own_gate[:, None] * projected).astype(BF16)
    projected = projected.astype(BF16)
    attention = cube_reduce(gated.reshape(pair * experts, micro * tok, width), pair, 4).astype(F32)

    middle = residual + attention
    second_normed, second_pull = jax.vjp(rms_scaled, middle, second_gain)
    second_normed = second_normed.astype(BF16)
    picked = mlp_route[:, 0].reshape(micro * tok, 2)
    second_gates, second_gate_pull = jax.vjp(
        partial(mixture_gates, picked), product_nt(second_normed, second_router)
    )
    table = jax.vmap(partial(slot_table, experts=experts, capacity=capacity))(
        mlp_route[:, 0], fill_order[:, 0]
    )
    table_low = table.astype(BF16)
    grouped = second_normed.reshape(micro, tok, width)
    outgoing = jnp.einsum("mect,mtd->emcd", table_low, grouped, preferred_element_type=F32)
    top_grad = cotangent.reshape(micro, tok, width)
    slot_values = jnp.einsum("mect,mtd->emcd", table_low, top_grad, preferred_element_type=F32)
    slot_gates = jnp.einsum(
        "mect,mte->emc", table, second_gates.reshape(micro, tok, experts), precision=HIGHEST
    )
    slot_grad = (slot_gates[..., None] * slot_values).astype(BF16)
    slots = experts * micro * capacity
    outgoing = outgoing.astype(BF16).reshape(experts, micro * capacity, width)
    slot_grad = slot_grad.reshape(experts, micro * capacity, width)
    gate_weight, up_weight, down_weight = w_gate[0], w_up[0], w_down[0]
    if walk:
        returned, came_back, arrived, result_grad, inner, gate_grad, up_grad = feed_forward(
            outgoing, slot_grad, gate_weight, up_weight, down_weight, line, pair, 5
        )
        arrived, result_grad, inner, gate_grad, up_grad = (
            value.reshape(-1, value.shape[-1])
            for value in (arrived, result_grad, inner, gate_grad, up_grad)
        )
    else:
        arrived = gather(swap(outgoing, "expert").reshape(slots, width), DP)
        result_grad = gather(swap(slot_grad, "expert").reshape(slots, width), DP)
        gate_pre = product_nt(arrived, gate_weight)
        up_pre = product_nt(arrived, up_weight)
        sigma = jax.nn.sigmoid(gate_pre)
        inner = (gate_pre * sigma * up_pre).astype(BF16)
        returned = product(inner, down_weight).astype(BF16)
        inner_grad = product_nt(result_grad, down_weight)
        gate_grad = (inner_grad * up_pre * sigma * (1.0 + gate_pre * (1.0 - sigma))).astype(BF16)
        up_grad = (inner_grad * gate_pre * sigma).astype(BF16)
        came_back = (product(gate_grad, gate_weight) + product(up_grad, up_weight)).astype(BF16)
        back = (experts, micro * capacity, width)
        returned = swap(scatter(returned, DP).reshape(back), "expert")
        came_back = swap(scatter(came_back, DP).reshape(back), "expert")
    returned = returned.reshape(experts, micro, capacity, width)
    came_back = came_back.reshape(experts, micro, capacity, width)
    spread = jnp.einsum("mect,emcd->emtd", table_low, returned, preferred_element_type=F32)
    spread = spread.reshape(experts, micro * tok, width)
    mixed = jnp.sum(jnp.transpose(second_gates)[:, :, None] * spread, axis=0)
    layer_out = (middle + mixed).astype(BF16)
    dz = top_grad.reshape(micro * tok, width).astype(F32)
    second_gate_grad = jnp.transpose(jnp.sum(spread * dz[None], axis=-1))
    (second_logit_grad,) = second_gate_pull(second_gate_grad)
    hn_grad = jnp.einsum("mect,emcd->mtd", table_low, came_back, preferred_element_type=F32)
    hn_grad = hn_grad.reshape(micro * tok, width)
    second_router_wide = second_router.astype(F32)
    for expert in range(experts):
        hn_grad = hn_grad + second_logit_grad[:, expert : expert + 1] * second_router_wide[expert]
    grad_router_second = split_product(second_logit_grad, second_normed)
    middle_grad, grad_gain_second = second_pull(hn_grad)
    middle_grad = middle_grad + dz

    mix_grad = cube_gather(middle_grad.astype(BF16), pair, 7).reshape(rows, width).astype(F32)
    own_gate_grad = jnp.sum(mix_grad * projected.astype(F32), axis=-1)
    projected_grad = (own_gate[:, None] * mix_grad).astype(BF16)
    grad_output = product_tn(heads_flat, projected_grad).astype(BF16)
    grad_output, projected_grad = lax.optimization_barrier((grad_output, projected_grad))
    grad_output = scatter(grad_output, "line")
    heads_grad = product_nt(projected_grad, out_weight).astype(BF16).reshape(shape)
    query_pre, kv_pre = attend_back(queries, kv, heads_grad, cosine, sine, bias, scale)
    query_pre = query_pre.reshape(rows, feats)
    grad_query = product_tn(tree_input, query_pre).astype(BF16)
    grad_query, kv_pre = lax.optimization_barrier((grad_query, kv_pre))
    kv_sum = cube_reduce(kv_pre.reshape(experts, 2 * rows, piece), 1, 8)
    grad_query, grad_output, kv_sum = lax.optimization_barrier((grad_query, grad_output, kv_sum))
    (first_logit_grad,) = first_gate_pull(own_gate_grad[:, None] * column[None, :])
    kv_sum = kv_sum.reshape(2, rows, piece)
    grad_kv = jnp.concatenate(
        [product_tn(tree_input, kv_sum[0]), product_tn(tree_input, kv_sum[1])], axis=1
    ).astype(BF16)
    input_term = input_gradient(
        query_pre, query_weight, kv_sum, kv_weight, first_logit_grad, first_router.astype(F32)
    ).reshape(pair * experts, micro * tok, width)
    normed_grad = cube_reduce(input_term, pair, 9)
    if not walk:
        grad_kv = scatter(grad_kv, "line")
        grad_kv = swap(grad_kv.reshape(pair * experts, own_kv, 2 * piece), TREES)
        grad_kv = grad_kv.reshape(pair, experts, own_kv, 2, line // experts, part)
        grad_kv = jnp.transpose(grad_kv, (2, 3, 1, 4, 0, 5)).reshape(own_kv, 2, heads_total)
        grad_key, grad_value = grad_kv[:, 0].astype(F32), grad_kv[:, 1].astype(F32)
    grad_query = scatter(grad_query, "line")
    gate_grad, up_grad, inner, arrived, result_grad, normed_grad = lax.optimization_barrier(
        (gate_grad, up_grad, inner, arrived, result_grad, normed_grad)
    )
    grad_gate = product_tn(gate_grad, arrived)[None]
    grad_upward = product_tn(up_grad, arrived)[None]
    grad_downward = product_tn(inner, result_grad)[None]
    normed_grad = normed_grad.astype(F32)
    grad_router_first = split_product(first_logit_grad, tree_input)
    token_grad, grad_gain_first = first_pull(normed_grad)
    tokens_grad = token_grad + middle_grad

    sums = jnp.concatenate(
        [grad_gain_first[None], grad_gain_second[None], grad_router_first, grad_router_second],
        axis=0,
    )
    sums = jnp.transpose(sums.reshape(sums.shape[0], -1, own_kv), (1, 0, 2))
    if walk:
        sums, grad_query, grad_key, grad_value = last_exchange(
            sums, grad_query.reshape(pair, own_in, feats), grad_kv, sizes, 10
        )
        grad_query = grad_query[None]
    else:
        sums = small_exchange(sums, sizes, True, 10)
        grad_query = swap(grad_query.reshape(own_in * pair, line, part)[None], "pair", 1, 0)
        grad_query = jnp.transpose(grad_query, (1, 2, 0, 3)).reshape(1, own_in, heads_total)
    return (
        layer_out.reshape(micro, 1, tok, width),
        tokens_grad.reshape(micro, 1, tok, width),
        grad_query.astype(F32),
        grad_output[None].astype(F32),
        grad_key,
        grad_value,
        sums[0],
        jnp.transpose(sums[2 : 2 + experts]),
        sums[1],
        jnp.transpose(sums[2 + experts :]),
        grad_gate,
        grad_upward,
        grad_downward,
    )


def solution(mesh):
    line, experts = mesh.devices.shape
    pair = 2 if line % 2 == 0 and (HEADS % line == 0) else 1
    shaped = Mesh(mesh.devices.reshape(line // pair, pair, experts), ALL)
    in_specs = (
        P(None, DP, "expert", None),
        P("expert", DP, None),
        P("expert", DP, None),
        P(ALL, None),
        P(ALL, None),
        P(ALL),
        P(ALL, None),
        P(ALL),
        P(ALL, None),
        P("expert", DP, None),
        P("expert", DP, None),
        P("expert", DP, None),
        P(None, DP, None, None),
        P(None, DP, "expert", None),
        P(None, DP, "expert"),
        P(None, DP, None),
        P(None, DP, "expert", None),
    )
    out_specs = (
        P(None, DP, "expert", None),
        P(None, DP, "expert", None),
        P("expert", DP, None),
        P("expert", DP, None),
        P(ALL, None),
        P(ALL, None),
        P(ALL),
        P(ALL, None),
        P(ALL),
        P(ALL, None),
        P("expert", DP, None),
        P("expert", DP, None),
        P("expert", DP, None),
    )
    return jax.shard_map(body, mesh=shaped, in_specs=in_specs, out_specs=out_specs, check_vma=False)
```
